256 devices in a mesh: gz: 64 (over z, x, core), gx: 4 (over y).
Axes of the slice: x: 4, y: 4, z: 8, core: 2. Of those that a mesh axis runs over, the one named last changes fastest.
Arguments:
- d_field: float32 [3, 512, 128, 128], P(None, 'gz', 'gx'), may hold values from -6 to 6
- e_field: float32 [3, 512, 128, 128], P(None, 'gz', 'gx'), may hold values from -6 to 6
- h_field: float32 [3, 512, 128, 128], P(None, 'gz', 'gx'), may hold values from -6 to 6
- permittivity: float32 [512, 128, 128], P('gz', 'gx'), may hold values from 1 to 4
- kerr_coeff: float32 [512, 128, 128], P('gz', 'gx'), may hold values from 0.05 to 0.3
- classes: int32 [2, 128, 128], P(None, 'gx'), may hold values from 0 to 7
- eps_table: float32 [8], replicated, may hold values from 1 to 6
- chi_table: float32 [8], replicated, may hold values from 0.02 to 0.4
Outputs:
- d_out: float32 [3, 512, 128, 128], P(None, 'gz', 'gx')
- e_out: float32 [3, 512, 128, 128], P(None, 'gz', 'gx')
- h_out: float32 [3, 512, 128, 128], P(None, 'gz', 'gx')
- eps_out: float32 [512, 128, 128], P('gz', 'gx')
- chi_out: float32 [512, 128, 128], P('gz', 'gx')
The draws below stay inside these ranges and needn't reach their ends.
All inputs are finite; a program needn't handle non-finite values.
Results may differ from the reference program's by a relative error of at most 0.00002.
Values sent between devices are 32-bit elements; how exact they have to be, the bound alone decides.
No kernel may reach another device: no remote copies, remote signals or barrier semaphores. Data moves between devices by JAX's collectives and lax.ppermute only.
A program may use at most 64 MiB of HBM per device.

```python
import math
import jax
import jax.numpy as jnp
from jax import lax

NX = 128
NY = 128
STEPS = 4
KERR = 3
ADVANCE = 2
CLASSES = 8
NZ = 512


def plant(result, key, smallest, top_value):
    extent = result.shape
    index_at = [jax.random.randint(jax.random.fold_in(key, axis), (), 0, extent[axis]) for axis in range(len(extent))]
    result = result.at[tuple(index_at)].set(smallest)
    longest = extent.index(max(extent))
    index_at[longest] = (index_at[longest] + 1) % extent[longest]
    return result.at[tuple(index_at)].set(top_value)


def block_levels(own_key, shape, pieces, smallest, top_value):
    loudness = 1.0
    for position, shards_of in pieces:
        steps = jax.random.uniform(jax.random.fold_in(jax.random.fold_in(own_key, 6), position), (shards_of,), jnp.float32, smallest / len(pieces), top_value / len(pieces))
        loudness = loudness * jnp.repeat(jnp.exp(steps), shape[position] // shards_of).reshape((-1,) + (1,) * (len(shape) - 1 - position))
    return loudness


def normal_values(stream_key, extent, scale, most, cuts=(), held_as=jnp.bfloat16):
    factor_of = block_levels(stream_key, extent, cuts, -0.22, 0.18) if cuts else 1.0
    result = jax.random.normal(stream_key, extent, jnp.float32) * scale * factor_of
    return jnp.minimum(jnp.maximum(result, -most), most).astype(held_as)


def setup_inputs(seed: int = 0) -> dict:
    key_list = jax.random.split(jax.random.key(seed), 9)
    d_field = normal_values(key_list[0], (3, NZ, NX, NY), 1.0, 6.0, ((1, 64), (2, 4)), jnp.float32)
    e_field = normal_values(key_list[1], (3, NZ, NX, NY), 1.0, 6.0, ((1, 64), (2, 4)), jnp.float32)
    h_field = normal_values(key_list[2], (3, NZ, NX, NY), 1.0, 6.0, ((1, 64), (2, 4)), jnp.float32)
    permittivity = jnp.clip(jnp.exp(math.log(4.0) - 1.3862944 * jax.random.uniform(key_list[3], (NZ, NX, NY), jnp.float32) ** block_levels(key_list[3], (NZ, NX, NY), ((0, 64), (1, 4)), -0.2, 0.2)), 1.0, 4.0)
    kerr_coeff = jnp.clip(0.05 + 0.25 * jax.random.uniform(key_list[4], (NZ, NX, NY), jnp.float32) ** block_levels(key_list[4], (NZ, NX, NY), ((0, 64), (1, 4)), -0.2, 0.2), 0.05, 0.3)
    classes = plant(jax.random.randint(key_list[5], (ADVANCE, NX, NY), 0, CLASSES), jax.random.fold_in(key_list[5], 1), 0, CLASSES - 1).astype(jnp.int32)
    eps_table = jnp.clip(jnp.exp(jax.random.uniform(key_list[6], (CLASSES,), jnp.float32, math.log(1.0), math.log(6.0))), 1.0, 6.0)
    chi_table = jnp.clip(jax.random.uniform(key_list[7], (CLASSES,), jnp.float32, 0.02, 0.4), 0.02, 0.4)
    return {"d_field": d_field, "e_field": e_field, "h_field": h_field, "permittivity": permittivity, "kerr_coeff": kerr_coeff, "classes": classes, "eps_table": eps_table, "chi_table": chi_table}


courant = 0.5


def ahead(values, along):
    size = values.shape[along]
    tail = lax.slice_in_dim(values, 1, size, axis=along)
    zeros = jnp.zeros_like(lax.slice_in_dim(values, 0, 1, axis=along))
    return jnp.concatenate([tail, zeros], axis=along)


def behind(values, along):
    size = values.shape[along]
    head = lax.slice_in_dim(values, 0, size - 1, axis=along)
    zeros = jnp.zeros_like(lax.slice_in_dim(values, 0, 1, axis=along))
    return jnp.concatenate([zeros, head], axis=along)


def curl_ahead(field):
    curl_x = (ahead(field[2], 2) - field[2]) - (ahead(field[1], 0) - field[1])
    curl_y = (ahead(field[0], 0) - field[0]) - (ahead(field[2], 1) - field[2])
    curl_z = (ahead(field[1], 1) - field[1]) - (ahead(field[0], 2) - field[0])
    return jnp.stack([curl_x, curl_y, curl_z])


def curl_behind(field):
    curl_x = (field[2] - behind(field[2], 2)) - (field[1] - behind(field[1], 0))
    curl_y = (field[0] - behind(field[0], 0)) - (field[2] - behind(field[2], 1))
    curl_z = (field[1] - behind(field[1], 1)) - (field[0] - behind(field[0], 2))
    return jnp.stack([curl_x, curl_y, curl_z])


def lookup(classes, table):
    labels = jnp.arange(table.shape[0], dtype=jnp.int32).reshape(-1, 1, 1, 1)
    picked = jnp.where(classes[None] == labels, table.reshape(-1, 1, 1, 1), jnp.float32(0.0))
    return jnp.sum(picked, axis=0)


def reference(d_field, e_field, h_field, permittivity, kerr_coeff, classes, eps_table, chi_table):
    displace, electric, magnetic = d_field, e_field, h_field
    for sweep in range(STEPS):
        magnetic = magnetic - courant * curl_ahead(electric)
        displace = displace + courant * curl_behind(magnetic)
        for inner in range(KERR):
            energy = electric[0] * electric[0] + electric[1] * electric[1] + electric[2] * electric[2]
            electric = displace / (permittivity + kerr_coeff * energy)[None]
    zeros = jnp.zeros((3, ADVANCE) + d_field.shape[2:], jnp.float32)
    d_out = jnp.concatenate([displace[:, ADVANCE:], zeros], axis=1)
    e_out = jnp.concatenate([electric[:, ADVANCE:], zeros], axis=1)
    h_out = jnp.concatenate([magnetic[:, ADVANCE:], zeros], axis=1)
    eps_out = jnp.concatenate([permittivity[ADVANCE:], lookup(classes, eps_table)], axis=0)
    chi_out = jnp.concatenate([kerr_coeff[ADVANCE:], lookup(classes, chi_table)], axis=0)
    return d_out, e_out, h_out, eps_out, chi_out
```

```python
import jax
import jax.numpy as jnp
from jax import lax
from jax.experimental import pallas as pl
from jax.experimental.pallas import tpu as pltpu
from jax.sharding import PartitionSpec as P

STEPS = 4
KERR = 3
ADVANCE = 2
HALF = 0.5

D, E, H, EPS, CHI = 0, 3, 6, 9, 10
NZL, NXL, NY = 8, 32, 128
XH = 4
ROWS = NXL + 2 * XH

ZHI = {(c, p): c * 5 + p for c in range(11) for p in range(5)}
ZHI.update({(E, 5): 55, (E + 1, 5): 56})
ZLO = {}
for _c in (D, D + 1, D + 2, H, H + 1, H + 2, E, E + 1, E + 2, EPS, CHI):
    ZLO[(_c, 7)] = len(ZLO)
for _c in (E, E + 1, E + 2, H, H + 1):
    ZLO[(_c, 6)] = len(ZLO)

VM = pl.BlockSpec(memory_space=pltpu.VMEM)
ANY = pl.BlockSpec(memory_space=pltpu.HBM)
SM = pl.BlockSpec(memory_space=pltpu.SMEM)


def shape(*dims):
    return jax.ShapeDtypeStruct(dims, jnp.float32)


def pack_zhi(d, e, h, eps, chi, out, sems):
    moves = []
    for base, ref in ((D, d), (E, e), (H, h)):
        for c in range(3):
            moves.append((ref.at[c, pl.ds(0, 5)], out.at[pl.ds((base + c) * 5, 5)]))
    moves.append((eps.at[pl.ds(0, 5)], out.at[pl.ds(EPS * 5, 5)]))
    moves.append((chi.at[pl.ds(0, 5)], out.at[pl.ds(CHI * 5, 5)]))
    for c in range(2):
        moves.append((e.at[c, pl.ds(5, 1)], out.at[pl.ds(55 + c, 1)]))
    copies = [pltpu.make_async_copy(a, b, sems.at[i]) for i, (a, b) in enumerate(moves)]
    for c in copies:
        c.start()
    for c in copies:
        c.wait()


def pick(d, e, h, eps, chi, comp, plane):
    if comp < E:
        return d[comp, plane]
    if comp < H:
        return e[comp - E, plane]
    if comp < EPS:
        return h[comp - H, plane]
    return eps[plane] if comp == EPS else chi[plane]


def pack_rest(d, e, h, eps, chi, xhi, xlo, zlo):
    for comp in range(11):
        for plane in range(NZL):
            v = pick(d, e, h, eps, chi, comp, plane)
            xhi[comp, plane] = v[0:XH]
            xlo[comp, plane] = v[NXL - XH :]
    for (comp, plane), i in ZLO.items():
        zlo[i] = pick(d, e, h, eps, chi, comp, plane)


def pack_corners(xhi, xlo, xt, czhi, czlo):
    for comp in range(11):
        for plane in range(NZL):
            t = jnp.concatenate([xhi[comp, plane], xlo[comp, plane]], axis=0)
            xt[comp, plane] = t
            if (comp, plane) in ZHI:
                czhi[ZHI[(comp, plane)]] = t
            if (comp, plane) in ZLO:
                czlo[ZLO[(comp, plane)]] = t


def advance(d, e, h, eps, chi, xt, zhi, zlo, czhi, czlo, classes, eps_table, chi_table, d_out, e_out, h_out, eps_out, chi_out, ds, es, hs):
    gz, gx = lax.axis_index("gz"), lax.axis_index("gx")
    last_z = gz == lax.axis_size("gz") - 1
    up = jnp.where(last_z, 0.0, 1.0).astype(jnp.float32)
    down = jnp.where(gz == 0, 0.0, 1.0).astype(jnp.float32)
    right = jnp.where(gx == lax.axis_size("gx") - 1, 0.0, 1.0).astype(jnp.float32)
    left = jnp.where(gx == 0, 0.0, 1.0).astype(jnp.float32)
    row = lax.broadcasted_iota(jnp.int32, (8, NY), 0)
    lane = lax.broadcasted_iota(jnp.int32, (ROWS, NY), 1)
    edge = jnp.where(row < XH, right, left)
    last_y, first_y = lane == NY - 1, lane == 0

    def inside(plane):
        return up if plane >= NZL else (down if plane < 0 else None)

    def factor(plane):
        z = inside(plane)
        main = jnp.full((NXL, NY), HALF, jnp.float32)
        tile = edge * HALF
        if z is not None:
            main, tile = main * z, tile * z
        return jnp.concatenate([main, tile], axis=0)

    def start(comp, plane):
        if plane >= NZL:
            i = ZHI[(comp, plane - NZL)]
            return jnp.concatenate([zhi[i], czhi[i]], axis=0)
        if plane < 0:
            i = ZLO[(comp, plane + NZL)]
            return jnp.concatenate([zlo[i], czlo[i]], axis=0)
        return jnp.concatenate([pick(d, e, h, eps, chi, comp, plane), xt[comp, plane]], axis=0)

    def medium(plane):
        a, b = start(EPS, plane), start(CHI, plane)
        z = inside(plane)
        if z is None:
            fill = jnp.concatenate([jnp.zeros((NXL, NY), jnp.float32), 1.0 - edge], axis=0)
        else:
            fill = jnp.concatenate([jnp.full((NXL, NY), 1.0 - z, jnp.float32), 1.0 - edge * z], axis=0)
        return a + fill, b

    def get(step, comp, plane):
        if step == 0:
            return start(comp, plane)
        ref, c = ((ds, comp), (es, comp - E), (hs, comp - H))[comp // 3]
        return ref[c, plane + 2]

    def next_y(v):
        return jnp.where(last_y, 0.0, pltpu.roll(v, NY - 1, 1))

    def prev_y(v):
        return jnp.where(first_y, 0.0, pltpu.roll(v, 1, 1))

    def next_x(v):
        return pltpu.roll(v, ROWS - 1, 0)

    def prev_x(v):
        return pltpu.roll(v, 1, 0)

    for n in range(1, STEPS + 1):
        for plane in range(n - 3, 14 - n):
            f = factor(plane)
            ex, ey, ez = (get(n - 1, E + c, plane) for c in range(3))
            exn, eyn = (get(n - 1, E + c, plane + 1) for c in range(2))
            below = plane == n - 3
            hx = get(n - 1, H, plane) - f * ((next_y(ez) - ez) - (eyn - ey))
            hy = get(n - 1, H + 1, plane) - f * ((exn - ex) - (next_x(ez) - ez))
            hs[0, plane + 2] = hx
            hs[1, plane + 2] = hy
            if below:
                continue
            hz = get(n - 1, H + 2, plane) - f * ((next_x(ey) - ey) - (next_y(ex) - ex))
            hs[2, plane + 2] = hz
            hxp, hyp = hs[0, plane + 1], hs[1, plane + 1]
            dx = get(n - 1, D, plane) + f * ((hz - prev_y(hz)) - (hy - hyp))
            dy = get(n - 1, D + 1, plane) + f * ((hx - hxp) - (hz - prev_x(hz)))
            dz = get(n - 1, D + 2, plane) + f * ((hy - prev_x(hy)) - (hx - prev_y(hx)))
            eps_p, chi_p = medium(plane)
            last = n == STEPS
            if last:
                dx, dy, dz, ex, ey, ez, eps_p, chi_p = (v[:NXL] for v in (dx, dy, dz, ex, ey, ez, eps_p, chi_p))
            inverse = 1.0 / (eps_p + chi_p * (ex * ex + ey * ey + ez * ez))
            squares = chi_p * (dx * dx + dy * dy + dz * dz)
            for _ in range(KERR - 1):
                inverse = 1.0 / (eps_p + squares * (inverse * inverse))
            if last:
                o = plane - ADVANCE
                for c, (dv, hv) in enumerate(((dx, hx), (dy, hy), (dz, hz))):
                    d_out[c, o] = dv
                    e_out[c, o] = dv * inverse
                    h_out[c, o] = hv[:NXL]
            else:
                for c, dv in enumerate((dx, dy, dz)):
                    ds[c, plane + 2] = dv
                    es[c, plane + 2] = dv * inverse

    for ref, comp, out, table in ((eps, EPS, eps_out, eps_table), (chi, CHI, chi_out, chi_table)):
        for plane in range(ADVANCE, NZL):
            out[plane - ADVANCE] = ref[plane]
        for k in range(ADVANCE):
            picked = jnp.zeros((NXL, NY), jnp.float32)
            for label in range(table.shape[0]):
                picked = jnp.where(classes[k] == label, table[label], picked)
            out[NZL - ADVANCE + k] = jnp.where(last_z, picked, zhi[ZHI[(comp, k)]])


def passed_along(shard, axis, by):
    devices = lax.axis_size(axis)
    pairs = [(i, i + by) for i in range(devices) if 0 <= i + by < devices]
    return lax.ppermute(shard, axis, pairs)


def on_device(d_field, e_field, h_field, permittivity, kerr_coeff, classes, eps_table, chi_table):
    fields = (d_field, e_field, h_field, permittivity, kerr_coeff)
    zhi = pl.pallas_call(
        pack_zhi,
        out_shape=shape(57, NXL, NY),
        in_specs=[ANY] * 5,
        out_specs=VM,
        scratch_shapes=[pltpu.SemaphoreType.DMA((13,))],
        name="pack_zhi", compiler_params=pltpu.CompilerParams(vmem_limit_bytes=4 << 20),
    )(*fields)
    zhi = passed_along(zhi, "gz", -1)
    xhi, xlo, zlo = pl.pallas_call(
        pack_rest,
        out_shape=(shape(11, NZL, XH, NY), shape(11, NZL, XH, NY), shape(16, NXL, NY)),
        in_specs=[VM] * 5,
        out_specs=(VM, VM, VM),
        name="pack_rest", compiler_params=pltpu.CompilerParams(vmem_limit_bytes=8 << 20),
    )(*fields)
    xhi = passed_along(xhi, "gx", -1)
    xlo = passed_along(xlo, "gx", 1)
    zlo = passed_along(zlo, "gz", 1)
    xt, czhi, czlo = pl.pallas_call(
        pack_corners,
        out_shape=(shape(11, NZL, 8, NY), shape(57, 8, NY), shape(16, 8, NY)),
        in_specs=[VM] * 2,
        out_specs=(VM, VM, VM),
        name="pack_corners", compiler_params=pltpu.CompilerParams(vmem_limit_bytes=8 << 20),
    )(xhi, xlo)
    czhi = passed_along(czhi, "gz", -1)
    czlo = passed_along(czlo, "gz", 1)
    state = pltpu.VMEM((3, 16, ROWS, NY), jnp.float32)
    field = shape(3, NZL, NXL, NY)
    medium = shape(NZL, NXL, NY)
    return pl.pallas_call(
        advance,
        out_shape=(field, field, field, medium, medium),
        in_specs=[VM] * 11 + [SM, SM],
        out_specs=(VM,) * 5,
        scratch_shapes=[state, state, state],
        name="advance", compiler_params=pltpu.CompilerParams(vmem_limit_bytes=24 << 20),
    )(*fields, xt, zhi, zlo, czhi, czlo, classes, eps_table, chi_table)


def solution(mesh):
    placed = (
        P(None, "gz", "gx", None),
        P(None, "gz", "gx", None),
        P(None, "gz", "gx", None),
        P("gz", "gx", None),
        P("gz", "gx", None),
        P(None, "gx", None),
        P(),
        P(),
    )
    return jax.shard_map(
        on_device,
        mesh=mesh,
        in_specs=placed,
        out_specs=placed[:5],
        check_vma=False,
    )
```

```python
import functools

import jax
import jax.numpy as jnp
from jax import lax
from jax.experimental import pallas as pl
from jax.experimental.pallas import tpu as pltpu
from jax.sharding import PartitionSpec as P

STEPS = 4
KERR = 3
ADVANCE = 2
HALF = 0.5

D, E, H, EPS, CHI = 0, 3, 6, 9, 10
ALL = range(11)
NZL, NXL, NY = 8, 32, 128
XH = 4
ROWS = NXL + 2 * XH
EDGE = 24

HI = [(c, p) for p in range(3) for c in ALL]
LO = [(c, 7) for c in ALL] + [(H, 6), (H + 1, 6)]
HI_AT = {k: i for i, k in enumerate(HI)}
LO_AT = {k: i for i, k in enumerate(LO)}
NS = len(HI)

VM = pl.BlockSpec(memory_space=pltpu.VMEM)
HBM = pl.BlockSpec(memory_space=pltpu.HBM)
SM = pl.BlockSpec(memory_space=pltpu.SMEM)


def shape(*dims):
    return jax.ShapeDtypeStruct(dims, jnp.float32)


def rows(*parts):
    return jnp.concatenate(parts, axis=0)


def scalar(condition):
    return jnp.where(condition, 1.0, 0.0).astype(jnp.float32)


def position():
    gz, gx = lax.axis_index("gz"), lax.axis_index("gx")
    return gz, gx, lax.axis_size("gz") - 1, lax.axis_size("gx") - 1


def halo_row():
    return lax.broadcasted_iota(jnp.int32, (8, NY), 0)


def inside_x():
    _, gx, _, last = position()
    return jnp.where(halo_row() < XH, scalar(gx != last), scalar(gx != 0))


class Grid:
    def __init__(self, size, factor, fill):
        self.size, self.factor, self.fill = size, factor, fill
        self.where, self.level = {}, {}
        lane = lax.broadcasted_iota(jnp.int32, (size, NY), 1)
        self.last_y, self.first_y = lane == NY - 1, lane == 0

    def hold(self, comp, plane, read, level=0):
        self.where[(comp, plane)] = read
        self.level[(comp, plane)] = level

    def get(self, comp, plane, level=None):
        assert level is None or self.level[(comp, plane)] == level, (comp, plane)
        return self.where[(comp, plane)]()

    def put(self, ref, index, comp, plane, value, level):
        ref[index] = value
        self.hold(comp, plane, lambda: ref[index], level)

    def next_y(self, v):
        return jnp.where(self.last_y, 0.0, pltpu.roll(v, NY - 1, 1))

    def prev_y(self, v):
        return jnp.where(self.first_y, 0.0, pltpu.roll(v, 1, 1))

    def next_x(self, v):
        return pltpu.roll(v, self.size - 1, 0)

    def prev_x(self, v):
        return pltpu.roll(v, 1, 0)

    def step_h(self, n, p, comps, put):
        f = self.factor(p)
        ex, ey, ez = (self.get(E + c, p, n - 1) for c in range(3))
        new = {}
        if 0 in comps:
            eyn = self.get(E + 1, p + 1, n - 1)
            new[0] = (self.next_y(ez) - ez) - (eyn - ey)
        if 1 in comps:
            exn = self.get(E, p + 1, n - 1)
            new[1] = (exn - ex) - (self.next_x(ez) - ez)
        if 2 in comps:
            new[2] = (self.next_x(ey) - ey) - (self.next_y(ex) - ex)
        for c, curl in new.items():
            put(H + c, p, self.get(H + c, p, n - 1) - f * curl, n)

    def step_de(self, n, p, put):
        f = self.factor(p)
        hx, hy, hz = (self.get(H + c, p, n) for c in range(3))
        hxp, hyp = (self.get(H + c, p - 1, n) for c in range(2))
        dx = self.get(D, p, n - 1) + f * ((hz - self.prev_y(hz)) - (hy - hyp))
        dy = self.get(D + 1, p, n - 1) + f * ((hx - hxp) - (hz - self.prev_x(hz)))
        dz = self.get(D + 2, p, n - 1) + f * ((hy - self.prev_x(hy)) - (hx - self.prev_y(hx)))
        ex, ey, ez = (self.get(E + c, p, n - 1) for c in range(3))
        eps, chi = self.get(EPS, p), self.get(CHI, p)
        fill = self.fill(p)
        if fill is not None:
            eps = eps + fill
        if n == STEPS:
            dx, dy, dz, ex, ey, ez, eps, chi = (v[:NXL] for v in (dx, dy, dz, ex, ey, ez, eps, chi))
        inverse = 1.0 / (eps + chi * (ex * ex + ey * ey + ez * ez))
        squares = chi * (dx * dx + dy * dy + dz * dz)
        for _ in range(KERR - 1):
            inverse = 1.0 / (eps + squares * (inverse * inverse))
        for c, v in enumerate((dx, dy, dz)):
            put(D + c, p, v, n)
            put(E + c, p, v * inverse, n)

    def sweep(self, n, h_planes, de_planes, put):
        for p in range(-2, 11):
            if p in h_planes:
                self.step_h(n, p, range(3), put)
            if p in de_planes:
                self.step_de(n, p, put)


def own(fields, comp, plane):
    d, e, h, eps, chi = fields
    if comp < E:
        return d[comp, plane]
    if comp < H:
        return e[comp - E, plane]
    if comp < EPS:
        return h[comp - H, plane]
    return eps[plane] if comp == EPS else chi[plane]


def load(d, e, h, eps, chi, dv, ev, hv, epsv, chiv, ya, yb, sems):
    moves = [(a.at[c], b.at[c]) for a, b in ((d, dv), (e, ev), (h, hv)) for c in range(3)] + [(eps, epsv), (chi, chiv)]
    copies = [pltpu.make_async_copy(a, b, sems.at[i]) for i, (a, b) in enumerate(moves)]
    for c in copies:
        c.start()
    _, gx, _, last = position()
    even = lax.rem(gx, 2) == 0
    keep = scalar(jnp.logical_and(gx != 0, gx != last))
    for comp in ALL:
        copies[comp].wait()
        for plane in range(NZL):
            v = own((dv, ev, hv, epsv, chiv), comp, plane)
            low, high = v[:XH], v[NXL - XH :]
            ya[comp, plane] = jnp.where(even, high, low)
            yb[comp, plane] = jnp.where(even, low, high) * keep


def early(grid, put):
    grid.sweep(1, range(0, 5), range(1, 5), put)
    grid.sweep(2, range(1, 4), range(2, 4), put)
    grid.sweep(3, range(2, 3), (), put)


def sent(grid, side, i):
    comp, plane = side[i]
    return grid.get(comp, plane)


def inner(d, e, h, eps, chi, fd, fe, fh, lo, out):
    fields = (d, e, h, eps, chi)
    grid = Grid(NXL, lambda p: HALF, lambda p: None)
    for comp in ALL:
        for p in range(NZL):
            grid.hold(comp, p, functools.partial(own, fields, comp, p))
    grid.step_h(1, 6, range(2), lambda c, p, v, n: grid.put(lo, c - H, c, p, v, n))

    def put(c, p, v, n):
        ref = (fd, fe, fh)[c // 3]
        grid.put(ref, (c % 3, p), c, p, v, n)

    early(grid, put)
    gz, _, last, _ = position()
    first_core = lax.rem(gz, 2) == 0
    keep = scalar(jnp.logical_and(gz != 0, gz != last))
    half = halo_row() < XH
    for i in range(NS):
        v = sent(grid, HI, i)
        if i < len(LO):
            v = jnp.where(first_core, v, sent(grid, LO, i))
        v = v * keep
        out[i, 0:8] = jnp.where(half, v[24:32], v[0:8])
        out[i, 8:24] = v[8:24]


def edges(d, e, h, eps, chi, id_, ie, ih, ilo, ra, rb, xt, fd, fe, fh, flo, cross, chip, sd, se, sh, slo):
    fields = (d, e, h, eps, chi)
    _, gx, _, _ = position()
    even = lax.rem(gx, 2) == 0
    for comp in ALL:
        for p in range(NZL):
            a, b = ra[comp, p], rb[comp, p]
            xt[comp, p] = rows(jnp.where(even, a, b), jnp.where(even, b, a))
    edge = inside_x()
    f = rows(jnp.full((8, NY), HALF), edge * HALF, jnp.full((8, NY), HALF))
    none = jnp.zeros((8, NY), jnp.float32)
    fill = rows(none, 1.0 - edge, none)
    grid = Grid(EDGE, lambda p: f, lambda p: fill)

    def read(comp, p):
        v = own(fields, comp, p)
        return rows(v[24:32], xt[comp, p], v[0:8])

    for comp in ALL:
        for p in range(NZL):
            grid.hold(comp, p, functools.partial(read, comp, p))
    grid.step_h(1, 6, range(2), lambda c, p, v, n: grid.put(slo, c - H, c, p, v, n))

    def put(c, p, v, n):
        ref = (sd, se, sh)[c // 3]
        grid.put(ref, (c % 3, p), c, p, v, n)

    early(grid, put)
    half = halo_row() < XH

    def merged(v, w):
        return rows(jnp.where(half, w[16:24], v[0:8]), v[8:24], jnp.where(half, v[24:32], w[0:8]), w[8:16])

    whole = {}
    for (comp, p), level in grid.level.items():
        if comp < EPS and (level or comp >= H and (comp, p) in ((H, 6), (H + 1, 6))):
            if p == 6:
                v, w, ref, index = ilo[comp - H], slo[comp - H], flo, comp - H
            else:
                k = comp // 3
                index = (comp % 3, p)
                v, w, ref = (id_, ie, ih)[k][index], (sd, se, sh)[k][index], (fd, fe, fh)[k]
            ref[index] = merged(v, w)
            whole[(comp, p)] = (ref, index)

    gz, _, last, _ = position()
    first_core = lax.rem(gz, 2) == 0
    keep = scalar(jnp.logical_and(gz != 0, gz != last))

    def frame(comp, p):
        if (comp, p) in whole:
            ref, index = whole[(comp, p)]
            return ref[index]
        return rows(own(fields, comp, p), xt[comp, p])

    for i in range(NS):
        hi = frame(*HI[i])
        if i < len(LO):
            lo = frame(*LO[i])
            there, here = jnp.where(first_core, hi, lo), jnp.where(first_core, lo, hi)
        else:
            there, here = hi, hi
        chip[i] = here
        there = there * keep
        cross[i, 0:8] = jnp.where(half, there[0:8], there[24:32])
        cross[i, 8:16] = there[32:40]


def full_grid():
    gz, _, last, _ = position()
    up, down = scalar(gz != last), scalar(gz != 0)
    edge = inside_x()

    def inside(p):
        return up if p >= NZL else (down if p < 0 else None)

    def factor(p):
        z = inside(p)
        main, tile = jnp.full((NXL, NY), HALF, jnp.float32), edge * HALF
        return rows(main, tile) if z is None else rows(main * z, tile * z)

    def fill(p):
        z = inside(p)
        if z is None:
            return rows(jnp.zeros((NXL, NY), jnp.float32), 1.0 - edge)
        return rows(jnp.full((NXL, NY), 1.0 - z, jnp.float32), 1.0 - edge * z)

    return Grid(ROWS, factor, fill)


def hold_own(grid, fields, xt):
    for comp in ALL:
        for p in range(NZL):
            grid.hold(comp, p, functools.partial(lambda c, q: rows(own(fields, c, q), xt[c, q]), comp, p))


def hold_frames(grid, refs, levels):
    for k, ref in enumerate(refs):
        for p, level in levels[k].items():
            for c in range(3):
                grid.hold(3 * k + c, p, functools.partial(lambda r, a, b: r[a, b], ref, c, p), level)


EARLY = ({1: 1, 2: 2, 3: 2, 4: 1}, {1: 1, 2: 2, 3: 2, 4: 1}, {0: 1, 1: 2, 2: 3, 3: 2, 4: 1})
MIDDLE = ({3: 3, 4: 3, 5: 2, 6: 1}, {3: 3, 4: 3, 5: 2, 6: 1}, {3: 4, 4: 3, 5: 2, 6: 1})


def middle(d, e, h, eps, chi, xt, fd, fe, fh, gd, ge, gh):
    grid = full_grid()
    hold_own(grid, (d, e, h, eps, chi), xt)
    hold_frames(grid, (fd, fe, fh), EARLY)

    def put(c, p, v, n):
        grid.put((gd, ge, gh)[c // 3], (c % 3, p), c, p, v, n)

    grid.sweep(1, (5, 6), (5, 6), put)
    grid.sweep(2, (4, 5), (4, 5), put)
    grid.sweep(3, (3, 4), (3, 4), put)
    grid.sweep(4, (3,), (), put)


def finish(d, e, h, eps, chi, xt, fd, fe, fh, gd, ge, gh, ca, cb, cc, classes, eps_table, chi_table, d_out, e_out, h_out, eps_out, chi_out, sd, se, sh):
    gz, _, last, _ = position()
    first_core = lax.rem(gz, 2) == 0
    last_z = gz == last
    half = halo_row() < XH
    grid = full_grid()
    hold_own(grid, (d, e, h, eps, chi), xt)
    hold_frames(grid, (fd, fe, fh), EARLY)
    hold_frames(grid, (gd, ge, gh), MIDDLE)

    def cross(i):
        m, x = ca[i, 0:8], cb[i, 0:8]
        return rows(jnp.where(half, x, m), ca[i, 8:24], jnp.where(half, m, x), cb[i, 8:16])

    def above(i):
        return jnp.where(first_core, cc[i], cross(i))

    def below(i):
        return jnp.where(first_core, cross(i), cc[i])

    for (comp, p), i in HI_AT.items():
        level = p + 1 if H <= comp < EPS else p
        grid.hold(comp, p + NZL, functools.partial(above, i), level)
    for (comp, p), i in LO_AT.items():
        grid.hold(comp, p - NZL, functools.partial(below, i), 1 if p == 6 else 0)

    def put(c, p, v, n):
        k = c // 3
        if n == STEPS:
            o = p - ADVANCE
            if o >= 0:
                (d_out, e_out, h_out)[k][c % 3, o] = v[:NXL]
            if k < 2:
                return
        grid.put((sd, se, sh)[k], (c % 3, p + 2), c, p, v, n)

    grid.sweep(1, (-1,), (-1, 0), put)
    grid.sweep(2, (-1, 0), (0, 1), put)
    grid.sweep(3, (0, 1), (1, 2), put)
    grid.sweep(4, (1, 2), (2, 3), put)
    for c in range(3):
        h_out[c, 3 - ADVANCE] = grid.get(H + c, 3, 4)[:NXL]
    grid.sweep(1, (7,), (7, 8), put)
    grid.sweep(2, range(6, 9), range(6, 10), put)
    grid.sweep(3, range(5, 10), range(5, 11), put)
    grid.sweep(4, range(4, 10), range(4, 10), put)

    for ref, comp, out, table in ((eps, EPS, eps_out, eps_table), (chi, CHI, chi_out, chi_table)):
        for plane in range(ADVANCE, NZL):
            out[plane - ADVANCE] = ref[plane]
        for k in range(ADVANCE):
            picked = jnp.zeros((NXL, NY), jnp.float32)
            for label in range(table.shape[0]):
                picked = jnp.where(classes[k] == label, table[label], picked)
            out[NZL - ADVANCE + k] = jnp.where(last_z, picked, grid.get(comp, NZL + k)[:NXL])


def pairs(axis, first):
    n = lax.axis_size(axis)
    out = []
    for i in range(first, n, 2):
        j = (i + 1) % n
        out += [(i, j), (j, i)]
    return out


def swapped(shard, axis, first):
    return lax.ppermute(shard, axis, pairs(axis, first))


def call(body, name, inputs, out_shape, scratch=(), vmem=8, specs=None):
    return pl.pallas_call(
        body,
        out_shape=out_shape,
        in_specs=[VM] * len(inputs) if specs is None else specs,
        out_specs=jax.tree.map(lambda _: VM, out_shape),
        scratch_shapes=list(scratch),
        compiler_params=pltpu.CompilerParams(vmem_limit_bytes=vmem << 20),
        name=name,
    )(*inputs)


def on_device(d_field, e_field, h_field, permittivity, kerr_coeff, classes, eps_table, chi_table):
    field, medium = shape(3, NZL, NXL, NY), shape(NZL, NXL, NY)
    halo = shape(11, NZL, XH, NY)
    *fields, ya, yb = call(
        load,
        "load",
        [pltpu.with_memory_space_constraint(a, pltpu.HBM) for a in (d_field, e_field, h_field, permittivity, kerr_coeff)],
        (field, field, field, medium, medium, halo, halo),
        [pltpu.SemaphoreType.DMA((11,))],
        specs=[HBM] * 5,
    )
    ra, rb = swapped(ya, "gx", 0), swapped(yb, "gx", 1)
    frames = [shape(3, 5, NXL, NY)] * 3
    lo = shape(2, NXL, NY)
    *inside, za = call(inner, "inner", fields, (*frames, lo, shape(NS, 24, NY)))
    ca = swapped(za, "gz", 1)
    frames = [shape(3, 5, ROWS, NY)] * 3
    scratch = [pltpu.VMEM((3, 5, EDGE, NY), jnp.float32)] * 3 + [pltpu.VMEM((2, EDGE, NY), jnp.float32)]
    xt, *frames, _, zb, zc = call(
        edges,
        "edges",
        [*fields, *inside, ra, rb],
        (shape(11, NZL, 8, NY), *frames, shape(2, ROWS, NY), shape(NS, 16, NY), shape(NS, ROWS, NY)),
        scratch,
    )
    cb, cc = swapped(zb, "gz", 1), swapped(zc, "gz", 0)
    more = call(middle, "middle", [*fields, xt, *frames], (shape(3, 7, ROWS, NY),) * 3)
    state = pltpu.VMEM((3, 13, ROWS, NY), jnp.float32)
    inputs = [*fields, xt, *frames, *more, ca, cb, cc, classes, eps_table, chi_table]
    return call(
        finish,
        "finish",
        inputs,
        (field, field, field, medium, medium),
        [state] * 3,
        vmem=16,
        specs=[VM] * (len(inputs) - 2) + [SM, SM],
    )


def solution(mesh):
    placed = (
        P(None, "gz", "gx", None),
        P(None, "gz", "gx", None),
        P(None, "gz", "gx", None),
        P("gz", "gx", None),
        P("gz", "gx", None),
        P(None, "gx", None),
        P(),
        P(),
    )
    return jax.shard_map(
        on_device,
        mesh=mesh,
        in_specs=placed,
        out_specs=placed[:5],
        check_vma=False,
    )
```

```python
import functools

import jax
import jax.numpy as jnp
from jax import lax
from jax.experimental import pallas as pl
from jax.experimental.pallas import tpu as pltpu
from jax.sharding import PartitionSpec as P


STEPS = 4
KERR = 3
ADVANCE = 2
HALF = 0.5

D, E, H, EPS, CHI = 0, 3, 6, 9, 10
ALL = range(11)
NZL, NXL, NY = 8, 32, 128
XH = 4
ROWS = NXL + 2 * XH
EDGE = 24

HI = [(c, p) for p in range(3) for c in ALL]
LO = [(c, 7) for c in ALL] + [(H, 6), (H + 1, 6)]
HI_AT = {k: i for i, k in enumerate(HI)}
LO_AT = {k: i for i, k in enumerate(LO)}
NS = len(HI)

VM = pl.BlockSpec(memory_space=pltpu.VMEM)
HBM = pl.BlockSpec(memory_space=pltpu.HBM)
SM = pl.BlockSpec(memory_space=pltpu.SMEM)


def shape(*dims):
    return jax.ShapeDtypeStruct(dims, jnp.float32)


def rows(*parts):
    return jnp.concatenate(parts, axis=0)


def scalar(condition):
    return jnp.where(condition, 1.0, 0.0).astype(jnp.float32)


def position():
    gz, gx = lax.axis_index("gz"), lax.axis_index("gx")
    return gz, gx, lax.axis_size("gz") - 1, lax.axis_size("gx") - 1


def halo_row():
    return lax.broadcasted_iota(jnp.int32, (8, NY), 0)


def inside_x():
    _, gx, _, last = position()
    return jnp.where(halo_row() < XH, scalar(gx != last), scalar(gx != 0))


class Grid:
    def __init__(self, size, factor, fill):
        self.size, self.factor, self.fill = size, factor, fill
        self.where, self.level = {}, {}
        lane = lax.broadcasted_iota(jnp.int32, (size, NY), 1)
        self.last_y, self.first_y = lane == NY - 1, lane == 0

    def hold(self, comp, plane, read, level=0):
        self.where[(comp, plane)] = read
        self.level[(comp, plane)] = level

    def get(self, comp, plane, level=None):
        assert level is None or self.level[(comp, plane)] == level, (comp, plane)
        return self.where[(comp, plane)]()

    def put(self, ref, index, comp, plane, value, level):
        ref[index] = value
        self.hold(comp, plane, lambda: ref[index], level)

    def next_y(self, v):
        return jnp.where(self.last_y, 0.0, pltpu.roll(v, NY - 1, 1))

    def prev_y(self, v):
        return jnp.where(self.first_y, 0.0, pltpu.roll(v, 1, 1))

    def next_x(self, v):
        return pltpu.roll(v, self.size - 1, 0)

    def prev_x(self, v):
        return pltpu.roll(v, 1, 0)

    def step_h(self, n, p, comps, put):
        f = self.factor(p)
        ex, ey, ez = (self.get(E + c, p, n - 1) for c in range(3))
        new = {}
        if 0 in comps:
            eyn = self.get(E + 1, p + 1, n - 1)
            new[0] = (self.next_y(ez) - ez) - (eyn - ey)
        if 1 in comps:
            exn = self.get(E, p + 1, n - 1)
            new[1] = (exn - ex) - (self.next_x(ez) - ez)
        if 2 in comps:
            new[2] = (self.next_x(ey) - ey) - (self.next_y(ex) - ex)
        for c, curl in new.items():
            put(H + c, p, self.get(H + c, p, n - 1) - f * curl, n)

    def step_de(self, n, p, put):
        f = self.factor(p)
        hx, hy, hz = (self.get(H + c, p, n) for c in range(3))
        hxp, hyp = (self.get(H + c, p - 1, n) for c in range(2))
        dx = self.get(D, p, n - 1) + f * ((hz - self.prev_y(hz)) - (hy - hyp))
        dy = self.get(D + 1, p, n - 1) + f * ((hx - hxp) - (hz - self.prev_x(hz)))
        dz = self.get(D + 2, p, n - 1) + f * ((hy - self.prev_x(hy)) - (hx - self.prev_y(hx)))
        ex, ey, ez = (self.get(E + c, p, n - 1) for c in range(3))
        eps, chi = self.get(EPS, p), self.get(CHI, p)
        fill = self.fill(p)
        if fill is not None:
            eps = eps + fill
        if n == STEPS:
            dx, dy, dz, ex, ey, ez, eps, chi = (v[:NXL] for v in (dx, dy, dz, ex, ey, ez, eps, chi))
        inverse = 1.0 / (eps + chi * (ex * ex + ey * ey + ez * ez))
        squares = chi * (dx * dx + dy * dy + dz * dz)
        for _ in range(KERR - 1):
            inverse = 1.0 / (eps + squares * (inverse * inverse))
        for c, v in enumerate((dx, dy, dz)):
            put(D + c, p, v, n)
            put(E + c, p, v * inverse, n)

    def sweep(self, n, h_planes, de_planes, put):
        for p in range(-2, 11):
            if p in h_planes:
                self.step_h(n, p, range(3), put)
            if p in de_planes:
                self.step_de(n, p, put)


def own(fields, comp, plane):
    d, e, h, eps, chi = fields
    if comp < E:
        return d[comp, plane]
    if comp < H:
        return e[comp - E, plane]
    if comp < EPS:
        return h[comp - H, plane]
    return eps[plane] if comp == EPS else chi[plane]


def load(d, e, h, eps, chi, dv, ev, hv, epsv, chiv, ya, yb, sems):
    moves = [(a.at[c], b.at[c]) for a, b in ((d, dv), (e, ev), (h, hv)) for c in range(3)] + [(eps, epsv), (chi, chiv)]
    copies = [pltpu.make_async_copy(a, b, sems.at[i]) for i, (a, b) in enumerate(moves)]
    for c in copies:
        c.start()
    _, gx, _, last = position()
    even = lax.rem(gx, 2) == 0
    keep = scalar(jnp.logical_and(gx != 0, gx != last))
    for comp in ALL:
        copies[comp].wait()
        for plane in range(NZL):
            v = own((dv, ev, hv, epsv, chiv), comp, plane)
            low, high = v[:XH], v[NXL - XH :]
            ya[comp, plane] = jnp.where(even, high, low)
            yb[comp, plane] = jnp.where(even, low, high) * keep


def early(grid, put):
    grid.sweep(1, range(0, 5), range(1, 5), put)
    grid.sweep(2, range(1, 4), range(2, 4), put)
    grid.sweep(3, range(2, 3), (), put)


def lookup(classes, eps_table, chi_table, eps_in, chi_in):
    for out, table in ((eps_in, eps_table), (chi_in, chi_table)):
        for k in range(ADVANCE):
            picked = jnp.zeros((NXL, NY), jnp.float32)
            for label in range(table.shape[0]):
                picked = jnp.where(classes[k] == label, table[label], picked)
            out[k] = picked


def sent(grid, side, i):
    comp, plane = side[i]
    return grid.get(comp, plane)


def inner(d, e, h, eps, chi, fd, fe, fh, lo, out):
    fields = (d, e, h, eps, chi)
    grid = Grid(NXL, lambda p: HALF, lambda p: None)
    for comp in ALL:
        for p in range(NZL):
            grid.hold(comp, p, functools.partial(own, fields, comp, p))
    grid.step_h(1, 6, range(2), lambda c, p, v, n: grid.put(lo, c - H, c, p, v, n))

    def put(c, p, v, n):
        ref = (fd, fe, fh)[c // 3]
        grid.put(ref, (c % 3, p), c, p, v, n)

    early(grid, put)
    gz, _, _, _ = position()
    first_core = lax.rem(gz, 2) == 0
    half = halo_row() < XH
    for i in range(NS):
        v = sent(grid, HI, i)
        if i < len(LO):
            v = jnp.where(first_core, v, sent(grid, LO, i))
        out[i, 0:8] = jnp.where(half, v[24:32], v[0:8])
        out[i, 8:24] = v[8:24]


def edges(d, e, h, eps, chi, id_, ie, ih, ilo, ra, rb, xt, fd, fe, fh, flo, cross, chip, sd, se, sh, slo):
    fields = (d, e, h, eps, chi)
    _, gx, _, _ = position()
    even = lax.rem(gx, 2) == 0
    for comp in ALL:
        for p in range(NZL):
            a, b = ra[comp, p], rb[comp, p]
            xt[comp, p] = rows(jnp.where(even, a, b), jnp.where(even, b, a))
    edge = inside_x()
    f = rows(jnp.full((8, NY), HALF), edge * HALF, jnp.full((8, NY), HALF))
    none = jnp.zeros((8, NY), jnp.float32)
    fill = rows(none, 1.0 - edge, none)
    grid = Grid(EDGE, lambda p: f, lambda p: fill)

    def read(comp, p):
        v = own(fields, comp, p)
        return rows(v[24:32], xt[comp, p], v[0:8])

    for comp in ALL:
        for p in range(NZL):
            grid.hold(comp, p, functools.partial(read, comp, p))
    grid.step_h(1, 6, range(2), lambda c, p, v, n: grid.put(slo, c - H, c, p, v, n))

    def put(c, p, v, n):
        ref = (sd, se, sh)[c // 3]
        grid.put(ref, (c % 3, p), c, p, v, n)

    early(grid, put)
    half = halo_row() < XH

    def merged(v, w):
        return rows(jnp.where(half, w[16:24], v[0:8]), v[8:24], jnp.where(half, v[24:32], w[0:8]), w[8:16])

    whole = {}
    for (comp, p), level in grid.level.items():
        if comp < EPS and (level or comp >= H and (comp, p) in ((H, 6), (H + 1, 6))):
            if p == 6:
                v, w, ref, index = ilo[comp - H], slo[comp - H], flo, comp - H
            else:
                k = comp // 3
                index = (comp % 3, p)
                v, w, ref = (id_, ie, ih)[k][index], (sd, se, sh)[k][index], (fd, fe, fh)[k]
            ref[index] = merged(v, w)
            whole[(comp, p)] = (ref, index)

    gz, _, _, _ = position()
    first_core = lax.rem(gz, 2) == 0

    def frame(comp, p):
        if (comp, p) in whole:
            ref, index = whole[(comp, p)]
            return ref[index]
        return rows(own(fields, comp, p), xt[comp, p])

    for i in range(NS):
        hi = frame(*HI[i])
        if i < len(LO):
            lo = frame(*LO[i])
            there, here = jnp.where(first_core, hi, lo), jnp.where(first_core, lo, hi)
        else:
            there, here = hi, hi
        chip[i] = here
        cross[i, 0:8] = jnp.where(half, there[0:8], there[24:32])
        cross[i, 8:16] = there[32:40]


def full_grid():
    gz, _, last, _ = position()
    up, down = scalar(gz != last), scalar(gz != 0)
    edge = inside_x()

    def inside(p):
        return up if p >= NZL else (down if p < 0 else None)

    def factor(p):
        z = inside(p)
        main, tile = jnp.full((NXL, NY), HALF, jnp.float32), edge * HALF
        return rows(main, tile) if z is None else rows(main * z, tile * z)

    def fill(p):
        z = inside(p)
        if z is None:
            return rows(jnp.zeros((NXL, NY), jnp.float32), 1.0 - edge)
        return rows(jnp.full((NXL, NY), 1.0 - z, jnp.float32), 1.0 - edge * z)

    return Grid(ROWS, factor, fill)


def hold_own(grid, fields, xt):
    for comp in ALL:
        for p in range(NZL):
            grid.hold(comp, p, functools.partial(lambda c, q: rows(own(fields, c, q), xt[c, q]), comp, p))


def hold_frames(grid, refs, levels):
    for k, ref in enumerate(refs):
        for p, level in levels[k].items():
            for c in range(3):
                grid.hold(3 * k + c, p, functools.partial(lambda r, a, b: r[a, b], ref, c, p), level)


EARLY = ({1: 1, 2: 2, 3: 2, 4: 1}, {1: 1, 2: 2, 3: 2, 4: 1}, {0: 1, 1: 2, 2: 3, 3: 2, 4: 1})
MIDDLE = ({3: 3, 4: 3, 5: 2, 6: 1}, {3: 3, 4: 3, 5: 2, 6: 1}, {3: 4, 4: 3, 5: 2, 6: 1})


def middle(d, e, h, eps, chi, xt, fd, fe, fh, gd, ge, gh):
    grid = full_grid()
    hold_own(grid, (d, e, h, eps, chi), xt)
    hold_frames(grid, (fd, fe, fh), EARLY)

    def put(c, p, v, n):
        grid.put((gd, ge, gh)[c // 3], (c % 3, p), c, p, v, n)

    grid.sweep(1, (5, 6), (5, 6), put)
    grid.sweep(2, (4, 5), (4, 5), put)
    grid.sweep(3, (3, 4), (3, 4), put)
    grid.sweep(4, (3,), (), put)


def finish(d, e, h, eps, chi, xt, fd, fe, fh, gd, ge, gh, ca, cb, cc, eps_in, chi_in, d_out, e_out, h_out, eps_out, chi_out, sd, se, sh):
    gz, _, last, _ = position()
    first_core = lax.rem(gz, 2) == 0
    last_z = gz == last
    half = halo_row() < XH
    grid = full_grid()
    hold_own(grid, (d, e, h, eps, chi), xt)
    hold_frames(grid, (fd, fe, fh), EARLY)
    hold_frames(grid, (gd, ge, gh), MIDDLE)

    def cross(i):
        m, x = ca[i, 0:8], cb[i, 0:8]
        return rows(jnp.where(half, x, m), ca[i, 8:24], jnp.where(half, m, x), cb[i, 8:16])

    def above(i):
        return jnp.where(first_core, cc[i], cross(i))

    def below(i):
        return jnp.where(first_core, cross(i), cc[i])

    for (comp, p), i in HI_AT.items():
        level = p + 1 if H <= comp < EPS else p
        grid.hold(comp, p + NZL, functools.partial(above, i), level)
    for (comp, p), i in LO_AT.items():
        grid.hold(comp, p - NZL, functools.partial(below, i), 1 if p == 6 else 0)

    def put(c, p, v, n):
        k = c // 3
        if n == STEPS:
            o = p - ADVANCE
            if o >= 0:
                (d_out, e_out, h_out)[k][c % 3, o] = v[:NXL]
            if k < 2:
                return
        grid.put((sd, se, sh)[k], (c % 3, p + 2), c, p, v, n)

    grid.sweep(1, (-1,), (-1, 0), put)
    grid.sweep(2, (-1, 0), (0, 1), put)
    grid.sweep(3, (0, 1), (1, 2), put)
    grid.sweep(4, (1, 2), (2, 3), put)
    for c in range(3):
        h_out[c, 3 - ADVANCE] = grid.get(H + c, 3, 4)[:NXL]
    grid.sweep(1, (7,), (7, 8), put)
    grid.sweep(2, range(6, 9), range(6, 10), put)
    grid.sweep(3, range(5, 10), range(5, 11), put)
    grid.sweep(4, range(4, 10), range(4, 10), put)

    for ref, comp, out, new in ((eps, EPS, eps_out, eps_in), (chi, CHI, chi_out, chi_in)):
        for plane in range(ADVANCE, NZL):
            out[plane - ADVANCE] = ref[plane]
        for k in range(ADVANCE):
            out[NZL - ADVANCE + k] = jnp.where(last_z, new[k], grid.get(comp, NZL + k)[:NXL])


def swapped(shard, axis, first):
    n = {a: lax.axis_size(a) for a in ("gz", "gx")}
    moves = []
    for z in range(n["gz"]):
        for x in range(n["gx"]):
            at = z if axis == "gz" else x
            to = at + 1 if at % 2 == first else at - 1
            if 0 <= to < n[axis]:
                other = (to, x) if axis == "gz" else (z, to)
            elif axis == "gx":
                other = (z ^ 1, x)
            else:
                continue
            moves.append((z * n["gx"] + x, other[0] * n["gx"] + other[1]))
    return lax.ppermute(shard, ("gz", "gx"), moves)


def call(body, inputs, out_shape, scratch=(), vmem=8, specs=None):
    return pl.pallas_call(
        body,
        out_shape=out_shape,
        in_specs=[VM] * len(inputs) if specs is None else specs,
        out_specs=jax.tree.map(lambda _: VM, out_shape),
        scratch_shapes=list(scratch),
        compiler_params=pltpu.CompilerParams(vmem_limit_bytes=vmem << 20),
    )(*inputs)


def on_device(d_field, e_field, h_field, permittivity, kerr_coeff, classes, eps_table, chi_table):
    field, medium = shape(3, NZL, NXL, NY), shape(NZL, NXL, NY)
    halo = shape(11, NZL, XH, NY)
    *fields, ya, yb = call(
        load,
        [pltpu.with_memory_space_constraint(a, pltpu.HBM) for a in (d_field, e_field, h_field, permittivity, kerr_coeff)],
        (field, field, field, medium, medium, halo, halo),
        [pltpu.SemaphoreType.DMA((11,))],
        specs=[HBM] * 5,
    )
    ra, rb = swapped(ya, "gx", 0), swapped(yb, "gx", 1)
    frames = [shape(3, 5, NXL, NY)] * 3
    lo = shape(2, NXL, NY)
    *inside, za = call(inner, fields, (*frames, lo, shape(NS, 24, NY)))
    ca = swapped(za, "gz", 1)
    coming = call(lookup, [classes, eps_table, chi_table], (shape(ADVANCE, NXL, NY),) * 2, specs=[VM, SM, SM])
    frames = [shape(3, 5, ROWS, NY)] * 3
    scratch = [pltpu.VMEM((3, 5, EDGE, NY), jnp.float32)] * 3 + [pltpu.VMEM((2, EDGE, NY), jnp.float32)]
    xt, *frames, _, zb, zc = call(
        edges,
        [*fields, *inside, ra, rb],
        (shape(11, NZL, 8, NY), *frames, shape(2, ROWS, NY), shape(NS, 16, NY), shape(NS, ROWS, NY)),
        scratch,
    )
    cb, cc = swapped(zb, "gz", 1), swapped(zc, "gz", 0)
    more = call(middle, [*fields, xt, *frames], (shape(3, 7, ROWS, NY),) * 3)
    state = pltpu.VMEM((3, 13, ROWS, NY), jnp.float32)
    inputs = [*fields, xt, *frames, *more, ca, cb, cc, *coming]
    return call(finish, inputs, (field, field, field, medium, medium), [state] * 3, vmem=16)


def solution(mesh):
    placed = (
        P(None, "gz", "gx", None),
        P(None, "gz", "gx", None),
        P(None, "gz", "gx", None),
        P("gz", "gx", None),
        P("gz", "gx", None),
        P(None, "gx", None),
        P(),
        P(),
    )
    return jax.shard_map(
        on_device,
        mesh=mesh,
        in_specs=placed,
        out_specs=placed[:5],
        check_vma=False,
    )
```

```python
import functools

import jax
import jax.numpy as jnp
from jax import lax
from jax.experimental import pallas as pl
from jax.experimental.pallas import tpu as pltpu
from jax.sharding import PartitionSpec as P


STEPS = 4
KERR = 3
ADVANCE = 2
HALF = 0.5

D, E, H, EPS, CHI = 0, 3, 6, 9, 10
ALL = range(11)
NZL, NXL, NY = 8, 32, 128
XH = 4
ROWS = NXL + 2 * XH
EDGE = 24

HI = [(c, p) for p in range(3) for c in ALL]
LO = [(c, 7) for c in ALL] + [(H, 6), (H + 1, 6)]
HI_AT = {k: i for i, k in enumerate(HI)}
LO_AT = {k: i for i, k in enumerate(LO)}
NS = len(HI)

VM = pl.BlockSpec(memory_space=pltpu.VMEM)
HBM = pl.BlockSpec(memory_space=pltpu.HBM)
SM = pl.BlockSpec(memory_space=pltpu.SMEM)


def shape(*dims):
    return jax.ShapeDtypeStruct(dims, jnp.float32)


def rows(*parts):
    return jnp.concatenate(parts, axis=0)


def scalar(condition):
    return jnp.where(condition, 1.0, 0.0).astype(jnp.float32)


def position():
    gz, gx = lax.axis_index("gz"), lax.axis_index("gx")
    return gz, gx, lax.axis_size("gz") - 1, lax.axis_size("gx") - 1


def halo_row():
    return lax.broadcasted_iota(jnp.int32, (8, NY), 0)


def inside_x():
    _, gx, _, last = position()
    return jnp.where(halo_row() < XH, scalar(gx != last), scalar(gx != 0))


class Grid:
    def __init__(self, size, factor, fill):
        self.size, self.factor, self.fill = size, factor, fill
        self.where, self.level = {}, {}
        lane = lax.broadcasted_iota(jnp.int32, (size, NY), 1)
        self.last_y, self.first_y = lane == NY - 1, lane == 0

    def hold(self, comp, plane, read, level=0):
        self.where[(comp, plane)] = read
        self.level[(comp, plane)] = level

    def get(self, comp, plane, level=None):
        assert level is None or self.level[(comp, plane)] == level, (comp, plane)
        return self.where[(comp, plane)]()

    def put(self, ref, index, comp, plane, value, level):
        ref[index] = value
        self.hold(comp, plane, lambda: ref[index], level)

    def next_y(self, v):
        return jnp.where(self.last_y, 0.0, pltpu.roll(v, NY - 1, 1))

    def prev_y(self, v):
        return jnp.where(self.first_y, 0.0, pltpu.roll(v, 1, 1))

    def next_x(self, v):
        return pltpu.roll(v, self.size - 1, 0)

    def prev_x(self, v):
        return pltpu.roll(v, 1, 0)

    def step_h(self, n, p, comps, put):
        f = self.factor(p)
        ex, ey, ez = (self.get(E + c, p, n - 1) for c in range(3))
        new = {}
        if 0 in comps:
            eyn = self.get(E + 1, p + 1, n - 1)
            new[0] = (self.next_y(ez) - ez) - (eyn - ey)
        if 1 in comps:
            exn = self.get(E, p + 1, n - 1)
            new[1] = (exn - ex) - (self.next_x(ez) - ez)
        if 2 in comps:
            new[2] = (self.next_x(ey) - ey) - (self.next_y(ex) - ex)
        for c, curl in new.items():
            put(H + c, p, self.get(H + c, p, n - 1) - f * curl, n)

    def step_de(self, n, p, put):
        f = self.factor(p)
        hx, hy, hz = (self.get(H + c, p, n) for c in range(3))
        hxp, hyp = (self.get(H + c, p - 1, n) for c in range(2))
        dx = self.get(D, p, n - 1) + f * ((hz - self.prev_y(hz)) - (hy - hyp))
        dy = self.get(D + 1, p, n - 1) + f * ((hx - hxp) - (hz - self.prev_x(hz)))
        dz = self.get(D + 2, p, n - 1) + f * ((hy - self.prev_x(hy)) - (hx - self.prev_y(hx)))
        ex, ey, ez = (self.get(E + c, p, n - 1) for c in range(3))
        eps, chi = self.get(EPS, p), self.get(CHI, p)
        fill = self.fill(p)
        if fill is not None:
            eps = eps + fill
        if n == STEPS:
            dx, dy, dz, ex, ey, ez, eps, chi = (v[:NXL] for v in (dx, dy, dz, ex, ey, ez, eps, chi))
        inverse = 1.0 / (eps + chi * (ex * ex + ey * ey + ez * ez))
        squares = chi * (dx * dx + dy * dy + dz * dz)
        for _ in range(KERR - 1):
            inverse = 1.0 / (eps + squares * (inverse * inverse))
        for c, v in enumerate((dx, dy, dz)):
            put(D + c, p, v, n)
            put(E + c, p, v * inverse, n)

    def sweep(self, n, h_planes, de_planes, put):
        for p in range(-2, 11):
            if p in h_planes:
                self.step_h(n, p, range(3), put)
            if p in de_planes:
                self.step_de(n, p, put)


def own(fields, comp, plane):
    d, e, h, eps, chi = fields
    if comp < E:
        return d[comp, plane]
    if comp < H:
        return e[comp - E, plane]
    if comp < EPS:
        return h[comp - H, plane]
    return eps[plane] if comp == EPS else chi[plane]


def load(d, e, h, eps, chi, dv, ev, hv, epsv, chiv, ya, yb, sems):
    moves = [(a.at[c], b.at[c]) for a, b in ((d, dv), (e, ev), (h, hv)) for c in range(3)] + [(eps, epsv), (chi, chiv)]
    copies = [pltpu.make_async_copy(a, b, sems.at[i]) for i, (a, b) in enumerate(moves)]
    for c in copies:
        c.start()
    _, gx, _, last = position()
    even = lax.rem(gx, 2) == 0
    keep = scalar(jnp.logical_and(gx != 0, gx != last))
    for comp in ALL:
        copies[comp].wait()
        for plane in range(NZL):
            v = own((dv, ev, hv, epsv, chiv), comp, plane)
            low, high = v[:XH], v[NXL - XH :]
            ya[comp, plane] = jnp.where(even, high, low)
            yb[comp, plane] = jnp.where(even, low, high) * keep


def early(grid, put):
    grid.sweep(1, range(0, 5), range(1, 5), put)
    grid.sweep(2, range(1, 4), range(2, 4), put)
    grid.sweep(3, range(2, 3), (), put)


def lookup(classes, eps_table, chi_table, eps_in, chi_in):
    for out, table in ((eps_in, eps_table), (chi_in, chi_table)):
        for k in range(ADVANCE):
            picked = jnp.zeros((NXL, NY), jnp.float32)
            for label in range(table.shape[0]):
                picked = jnp.where(classes[k] == label, table[label], picked)
            out[k] = picked


def sent(grid, side, i):
    comp, plane = side[i]
    return grid.get(comp, plane)


def inner(d, e, h, eps, chi, fd, fe, fh, lo, out):
    fields = (d, e, h, eps, chi)
    grid = Grid(NXL, lambda p: HALF, lambda p: None)
    for comp in ALL:
        for p in range(NZL):
            grid.hold(comp, p, functools.partial(own, fields, comp, p))
    grid.step_h(1, 6, range(2), lambda c, p, v, n: grid.put(lo, c - H, c, p, v, n))

    def put(c, p, v, n):
        ref = (fd, fe, fh)[c // 3]
        grid.put(ref, (c % 3, p), c, p, v, n)

    early(grid, put)
    gz, _, last, _ = position()
    first_core = lax.rem(gz, 2) == 0
    keep = scalar(jnp.logical_and(gz != 0, gz != last))
    half = halo_row() < XH
    for i in range(NS):
        v = sent(grid, HI, i)
        if i < len(LO):
            v = jnp.where(first_core, v, sent(grid, LO, i))
        v = v * keep
        out[i, 0:8] = jnp.where(half, v[24:32], v[0:8])
        out[i, 8:24] = v[8:24]


def edges(d, e, h, eps, chi, ra, rb, xt, sd, se, sh, slo, cross):
    fields = (d, e, h, eps, chi)
    _, gx, _, _ = position()
    even = lax.rem(gx, 2) == 0
    for comp in ALL:
        for p in range(NZL):
            a, b = ra[comp, p], rb[comp, p]
            xt[comp, p] = rows(jnp.where(even, a, b), jnp.where(even, b, a))
    edge = inside_x()
    f = rows(jnp.full((8, NY), HALF), edge * HALF, jnp.full((8, NY), HALF))
    none = jnp.zeros((8, NY), jnp.float32)
    fill = rows(none, 1.0 - edge, none)
    grid = Grid(EDGE, lambda p: f, lambda p: fill)

    def read(comp, p):
        v = own(fields, comp, p)
        return rows(v[24:32], xt[comp, p], v[0:8])

    for comp in ALL:
        for p in range(NZL):
            grid.hold(comp, p, functools.partial(read, comp, p))
    grid.step_h(1, 6, range(2), lambda c, p, v, n: grid.put(slo, c - H, c, p, v, n))

    def put(c, p, v, n):
        grid.put((sd, se, sh)[c // 3], (c % 3, p), c, p, v, n)

    early(grid, put)
    half = halo_row() < XH
    gz, _, last, _ = position()
    first_core = lax.rem(gz, 2) == 0
    keep = scalar(jnp.logical_and(gz != 0, gz != last))
    for i in range(NS):
        v = sent(grid, HI, i)
        if i < len(LO):
            v = jnp.where(first_core, v, sent(grid, LO, i))
        v = v * keep
        cross[i, 0:8] = jnp.where(half, v[16:24], v[0:8])
        cross[i, 8:16] = v[8:16]


def merge(d, e, h, eps, chi, id_, ie, ih, ilo, sd, se, sh, slo, xt, fd, fe, fh, chip):
    fields = (d, e, h, eps, chi)
    half = halo_row() < XH

    def merged(v, w):
        return rows(jnp.where(half, w[16:24], v[0:8]), v[8:24], jnp.where(half, v[24:32], w[0:8]), w[8:16])

    grid = Grid(ROWS, None, None)
    hold_own(grid, fields, xt)
    for k, (v, w, ref) in enumerate(((id_, sd, fd), (ie, se, fe), (ih, sh, fh))):
        for p in EARLY[k]:
            for c in range(3):
                grid.put(ref, (c, p), 3 * k + c, p, merged(v[c, p], w[c, p]), 1)
    for c in range(2):
        grid.hold(H + c, 6, functools.partial(lambda a: merged(ilo[a], slo[a]), c))
    gz, _, _, _ = position()
    first_core = lax.rem(gz, 2) == 0
    for i in range(NS):
        v = sent(grid, HI, i)
        if i < len(LO):
            v = jnp.where(first_core, sent(grid, LO, i), v)
        chip[i] = v


def full_grid():
    gz, _, last, _ = position()
    up, down = scalar(gz != last), scalar(gz != 0)
    edge = inside_x()

    def inside(p):
        return up if p >= NZL else (down if p < 0 else None)

    def factor(p):
        z = inside(p)
        main, tile = jnp.full((NXL, NY), HALF, jnp.float32), edge * HALF
        return rows(main, tile) if z is None else rows(main * z, tile * z)

    def fill(p):
        z = inside(p)
        if z is None:
            return rows(jnp.zeros((NXL, NY), jnp.float32), 1.0 - edge)
        return rows(jnp.full((NXL, NY), 1.0 - z, jnp.float32), 1.0 - edge * z)

    return Grid(ROWS, factor, fill)


def hold_own(grid, fields, xt):
    for comp in ALL:
        for p in range(NZL):
            grid.hold(comp, p, functools.partial(lambda c, q: rows(own(fields, c, q), xt[c, q]), comp, p))


def hold_frames(grid, refs, levels):
    for k, ref in enumerate(refs):
        for p, level in levels[k].items():
            for c in range(3):
                grid.hold(3 * k + c, p, functools.partial(lambda r, a, b: r[a, b], ref, c, p), level)


EARLY = ({1: 1, 2: 2, 3: 2, 4: 1}, {1: 1, 2: 2, 3: 2, 4: 1}, {0: 1, 1: 2, 2: 3, 3: 2, 4: 1})
MIDDLE = ({3: 3, 4: 3, 5: 2, 6: 1}, {3: 3, 4: 3, 5: 2, 6: 1}, {3: 4, 4: 3, 5: 2, 6: 1})


def middle(d, e, h, eps, chi, xt, fd, fe, fh, gd, ge, gh):
    grid = full_grid()
    hold_own(grid, (d, e, h, eps, chi), xt)
    hold_frames(grid, (fd, fe, fh), EARLY)

    def put(c, p, v, n):
        grid.put((gd, ge, gh)[c // 3], (c % 3, p), c, p, v, n)

    grid.sweep(1, (5, 6), (5, 6), put)
    grid.sweep(2, (4, 5), (4, 5), put)
    grid.sweep(3, (3, 4), (3, 4), put)
    grid.sweep(4, (3,), (), put)


def complete(own_refs, xt, frames, more, above, below, scratch, outs, sems, coming):
    fields = own_refs
    grid = full_grid()
    hold_own(grid, fields, xt)
    hold_frames(grid, frames, EARLY)
    hold_frames(grid, more, MIDDLE)
    for side, at, shift in ((above, HI_AT, NZL), (below, LO_AT, -NZL)):
        if side is not None:
            for (comp, p), i in at.items():
                level = (p + (H <= comp < EPS)) if shift > 0 else int(p == 6)
                grid.hold(comp, p + shift, functools.partial(side, i), level)
    state, staged = scratch[:3], scratch[3:6]
    copies = []

    def send(o):
        for k in range(3):
            copies.append(pltpu.make_async_copy(staged[k].at[:, pl.ds(o, 1)], outs[k].at[:, pl.ds(o, 1)], sems.at[k, o]))
            copies[-1].start()

    def put(c, p, v, n):
        k = c // 3
        if n == STEPS and p >= ADVANCE:
            staged[k][c % 3, p - ADVANCE] = v[:NXL]
        if n < STEPS or k == 2:
            grid.put(state[k], (c % 3, p + 2), c, p, v, n)

    def last_sweep(h_planes, de_planes):
        for p in sorted(set(h_planes) | set(de_planes)):
            if p in h_planes:
                grid.step_h(STEPS, p, range(3), put)
            if p in de_planes:
                if p not in h_planes:
                    for c in range(3):
                        staged[2][c, p - ADVANCE] = grid.get(H + c, p, STEPS)[:NXL]
                grid.step_de(STEPS, p, put)
                send(p - ADVANCE)

    if below is not None:
        grid.sweep(1, (-1,), (-1, 0), put)
        grid.sweep(2, (-1, 0), (0, 1), put)
        grid.sweep(3, (0, 1), (1, 2), put)
        last_sweep((1, 2), (2, 3))
    if above is not None:
        for k, (comp, new) in enumerate(((EPS, coming and coming[0]), (CHI, coming and coming[1]))):
            for o in range(ADVANCE):
                v = grid.get(comp, NZL + o)[:NXL]
                if new is not None:
                    gz, _, last, _ = position()
                    v = jnp.where(gz == last, new[o], v)
                scratch[6 + k][o] = v
            copies.append(pltpu.make_async_copy(scratch[6 + k], outs[3 + k].at[pl.ds(NZL - ADVANCE, ADVANCE)], sems.at[3, k]))
            copies[-1].start()
        grid.sweep(1, (7,), (7, 8), put)
        grid.sweep(2, range(6, 9), range(6, 10), put)
        grid.sweep(3, range(5, 10), range(5, 11), put)
        last_sweep(range(4, 10), range(4, 10))
    for c in copies:
        c.wait()


def near(d, e, h, eps, chi, xt, fd, fe, fh, gd, ge, gh, cc, d_out, e_out, h_out, eps_out, chi_out, *rest):
    *scratch, sems = rest
    fields, frames, more = (d, e, h, eps, chi), (fd, fe, fh), (gd, ge, gh)
    outs = (d_out, e_out, h_out, eps_out, chi_out)
    gz, _, _, _ = position()
    keep = NZL - ADVANCE
    media = [
        pltpu.make_async_copy(a.at[pl.ds(ADVANCE, keep)], b.at[pl.ds(0, keep)], sems.at[3, 2 + k])
        for k, (a, b) in enumerate(((eps, eps_out), (chi, chi_out)))
    ]
    for c in media:
        c.start()

    @pl.when(lax.rem(gz, 2) == 0)
    def _():
        complete(fields, xt, frames, more, lambda i: cc[i], None, scratch, outs, sems, None)

    @pl.when(lax.rem(gz, 2) == 1)
    def _():
        complete(fields, xt, frames, more, None, lambda i: cc[i], scratch, outs, sems, None)

    for c in media:
        c.wait()


def far(d, e, h, eps, chi, xt, fd, fe, fh, gd, ge, gh, ca, cb, eps_in, chi_in, *rest):
    outs, scratch, sems = rest[5:10], rest[10:-1], rest[-1]
    fields, frames, more = (d, e, h, eps, chi), (fd, fe, fh), (gd, ge, gh)
    half = halo_row() < XH
    gz, _, _, _ = position()

    def cross(i):
        m, x = ca[i, 0:8], cb[i, 0:8]
        return rows(jnp.where(half, x, m), ca[i, 8:24], jnp.where(half, m, x), cb[i, 8:16])

    @pl.when(lax.rem(gz, 2) == 0)
    def _():
        complete(fields, xt, frames, more, None, cross, scratch, outs, sems, None)

    @pl.when(lax.rem(gz, 2) == 1)
    def _():
        complete(fields, xt, frames, more, cross, None, scratch, outs, sems, (eps_in, chi_in))


def swapped(shard, axis, first):
    n = {a: lax.axis_size(a) for a in ("gz", "gx")}
    moves = []
    for z in range(n["gz"]):
        for x in range(n["gx"]):
            at = z if axis == "gz" else x
            to = at + 1 if at % 2 == first else at - 1
            if 0 <= to < n[axis]:
                other = (to, x) if axis == "gz" else (z, to)
            else:
                other = (z ^ 1, x) if axis == "gx" else (z, x ^ 1)
            moves.append((z * n["gx"] + x, other[0] * n["gx"] + other[1]))
    return lax.ppermute(shard, ("gz", "gx"), moves)


def call(body, inputs, out_shape, scratch=(), vmem=8, specs=None, out=VM, aliases=None):
    return pl.pallas_call(
        body,
        out_shape=out_shape,
        in_specs=[VM] * len(inputs) if specs is None else specs,
        out_specs=jax.tree.map(lambda _: out, out_shape),
        input_output_aliases=aliases or {},
        scratch_shapes=list(scratch),
        compiler_params=pltpu.CompilerParams(vmem_limit_bytes=vmem << 20),
    )(*inputs)


def on_device(d_field, e_field, h_field, permittivity, kerr_coeff, classes, eps_table, chi_table):
    field, medium = shape(3, NZL, NXL, NY), shape(NZL, NXL, NY)
    halo = shape(11, NZL, XH, NY)
    *fields, ya, yb = call(
        load,
        [pltpu.with_memory_space_constraint(a, pltpu.HBM) for a in (d_field, e_field, h_field, permittivity, kerr_coeff)],
        (field, field, field, medium, medium, halo, halo),
        [pltpu.SemaphoreType.DMA((11,))],
        specs=[HBM] * 5,
    )
    ra, rb = swapped(ya, "gx", 0), swapped(yb, "gx", 1)
    frames = [shape(3, 5, NXL, NY)] * 3
    lo = shape(2, NXL, NY)
    *inside, za = call(inner, fields, (*frames, lo, shape(NS, 24, NY)))
    ca = swapped(za, "gz", 1)
    coming = call(lookup, [classes, eps_table, chi_table], (shape(ADVANCE, NXL, NY),) * 2, specs=[VM, SM, SM])
    thin = [shape(3, 5, EDGE, NY)] * 3
    xt, *outside, zb = call(
        edges, [*fields, ra, rb], (shape(11, NZL, 8, NY), *thin, shape(2, EDGE, NY), shape(NS, 16, NY))
    )
    cb = swapped(zb, "gz", 1)
    frames = [shape(3, 5, ROWS, NY)] * 3
    *frames, zc = call(merge, [*fields, *inside, *outside, xt], (*frames, shape(NS, ROWS, NY)))
    cc = swapped(zc, "gz", 0)
    more = call(middle, [*fields, xt, *frames], (shape(3, 7, ROWS, NY),) * 3)
    scratch = [pltpu.VMEM((3, 13, ROWS, NY), jnp.float32)] * 3 + [pltpu.VMEM((3, NZL, NXL, NY), jnp.float32)] * 3
    scratch += [pltpu.VMEM((ADVANCE, NXL, NY), jnp.float32)] * 2 + [pltpu.SemaphoreType.DMA((4, NZL))]
    given = [*fields, xt, *frames, *more]
    results = (field, field, field, medium, medium)
    outs = call(near, [*given, cc], results, scratch, vmem=16, out=HBM)
    given += [ca, cb, *coming]
    n = len(given)
    return call(
        far,
        [*given, *outs],
        results,
        scratch,
        vmem=16,
        specs=[VM] * n + [HBM] * 5,
        out=HBM,
        aliases={n + k: k for k in range(5)},
    )


def solution(mesh):
    placed = (
        P(None, "gz", "gx", None),
        P(None, "gz", "gx", None),
        P(None, "gz", "gx", None),
        P("gz", "gx", None),
        P("gz", "gx", None),
        P(None, "gx", None),
        P(),
        P(),
    )
    return jax.shard_map(
        on_device,
        mesh=mesh,
        in_specs=placed,
        out_specs=placed[:5],
        check_vma=False,
    )
```

```python
import functools

import jax
import jax.numpy as jnp
from jax import lax
from jax.experimental import pallas as pl
from jax.experimental.pallas import tpu as pltpu
from jax.sharding import PartitionSpec as P


STEPS = 4
KERR = 3
ADVANCE = 2
HALF = 0.5

D, E, H, EPS, CHI = 0, 3, 6, 9, 10
ALL = range(11)
NZL, NXL, NY = 8, 32, 128
XH = 4
ROWS = NXL + 2 * XH
EDGE = 24

RAW = [(c, 0) for c in range(H)] + [(c, p) for p in range(3) for c in (EPS, CHI)]
HI = RAW + [(H + c, 0) for c in range(3)] + [(c, p) for p in (1, 2) for c in range(EPS)]
LO = [(c, 7) for c in ALL] + [None, (H, 6), (H + 1, 6)]
HI_AT = {k: i for i, k in enumerate(HI)}
LO_AT = {k: i for i, k in enumerate(LO) if k}
NS, NR = len(HI), len(RAW)

FIRST = [(c, p) for p in range(5) for c in ALL] + [(E, 5), (E + 1, 5)]
SECOND = [(c, p) for p in (5, 6, 7) for c in ALL if (c, p) not in FIRST]

VM = pl.BlockSpec(memory_space=pltpu.VMEM)
HBM = pl.BlockSpec(memory_space=pltpu.HBM)
SM = pl.BlockSpec(memory_space=pltpu.SMEM)


def shape(*dims):
    return jax.ShapeDtypeStruct(dims, jnp.float32)


def rows(*parts):
    return jnp.concatenate(parts, axis=0)


def scalar(condition):
    return jnp.where(condition, 1.0, 0.0).astype(jnp.float32)


def position():
    gz, gx = lax.axis_index("gz"), lax.axis_index("gx")
    return gz, gx, lax.axis_size("gz") - 1, lax.axis_size("gx") - 1


def halo_row():
    return lax.broadcasted_iota(jnp.int32, (8, NY), 0)


def inside_x():
    _, gx, _, last = position()
    return jnp.where(halo_row() < XH, scalar(gx != last), scalar(gx != 0))


class Grid:
    def __init__(self, size, factor, fill):
        self.size, self.factor, self.fill = size, factor, fill
        self.where, self.level = {}, {}
        lane = lax.broadcasted_iota(jnp.int32, (size, NY), 1)
        self.last_y, self.first_y = lane == NY - 1, lane == 0

    def hold(self, comp, plane, read, level=0):
        self.where[(comp, plane)] = read
        self.level[(comp, plane)] = level

    def get(self, comp, plane, level=None):
        assert level is None or self.level[(comp, plane)] == level, (comp, plane)
        return self.where[(comp, plane)]()

    def put(self, ref, index, comp, plane, value, level):
        ref[index] = value
        self.hold(comp, plane, lambda: ref[index], level)

    def next_y(self, v):
        return jnp.where(self.last_y, 0.0, pltpu.roll(v, NY - 1, 1))

    def prev_y(self, v):
        return jnp.where(self.first_y, 0.0, pltpu.roll(v, 1, 1))

    def next_x(self, v):
        return pltpu.roll(v, self.size - 1, 0)

    def prev_x(self, v):
        return pltpu.roll(v, 1, 0)

    def step_h(self, n, p, comps, put):
        f = self.factor(p)
        ex, ey, ez = (self.get(E + c, p, n - 1) for c in range(3))
        new = {}
        if 0 in comps:
            eyn = self.get(E + 1, p + 1, n - 1)
            new[0] = (self.next_y(ez) - ez) - (eyn - ey)
        if 1 in comps:
            exn = self.get(E, p + 1, n - 1)
            new[1] = (exn - ex) - (self.next_x(ez) - ez)
        if 2 in comps:
            new[2] = (self.next_x(ey) - ey) - (self.next_y(ex) - ex)
        for c, curl in new.items():
            put(H + c, p, self.get(H + c, p, n - 1) - f * curl, n)

    def step_de(self, n, p, put):
        f = self.factor(p)
        hx, hy, hz = (self.get(H + c, p, n) for c in range(3))
        hxp, hyp = (self.get(H + c, p - 1, n) for c in range(2))
        dx = self.get(D, p, n - 1) + f * ((hz - self.prev_y(hz)) - (hy - hyp))
        dy = self.get(D + 1, p, n - 1) + f * ((hx - hxp) - (hz - self.prev_x(hz)))
        dz = self.get(D + 2, p, n - 1) + f * ((hy - self.prev_x(hy)) - (hx - self.prev_y(hx)))
        ex, ey, ez = (self.get(E + c, p, n - 1) for c in range(3))
        eps, chi = self.get(EPS, p), self.get(CHI, p)
        fill = self.fill(p)
        if fill is not None:
            eps = eps + fill
        if n == STEPS:
            dx, dy, dz, ex, ey, ez, eps, chi = (v[:NXL] for v in (dx, dy, dz, ex, ey, ez, eps, chi))
        inverse = 1.0 / (eps + chi * (ex * ex + ey * ey + ez * ez))
        squares = chi * (dx * dx + dy * dy + dz * dz)
        for _ in range(KERR - 1):
            inverse = 1.0 / (eps + squares * (inverse * inverse))
        for c, v in enumerate((dx, dy, dz)):
            put(D + c, p, v, n)
            put(E + c, p, v * inverse, n)

    def sweep(self, n, h_planes, de_planes, put):
        for p in range(-2, 11):
            if p in h_planes:
                self.step_h(n, p, range(3), put)
            if p in de_planes:
                self.step_de(n, p, put)


def own(fields, comp, plane):
    d, e, h, eps, chi = fields
    if comp < E:
        return d[comp, plane]
    if comp < H:
        return e[comp - E, plane]
    if comp < EPS:
        return h[comp - H, plane]
    return eps[plane] if comp == EPS else chi[plane]


def load(d, e, h, eps, chi, dv, ev, hv, epsv, chiv, ya, yb, yc, yd, sems):
    moves = [(a.at[c], b.at[c]) for a, b in ((d, dv), (e, ev), (h, hv)) for c in range(3)] + [(eps, epsv), (chi, chiv)]
    copies = [pltpu.make_async_copy(a, b, sems.at[i]) for i, (a, b) in enumerate(moves)]
    for c in copies:
        c.start()
    gz, gx, _, last = position()
    even, first_core = lax.rem(gx, 2) == 0, lax.rem(gz, 2) == 0
    keep = scalar(jnp.logical_and(gx != 0, gx != last))
    for c in copies:
        c.wait()
    fields = (dv, ev, hv, epsv, chiv)
    for units, a, b in ((FIRST, ya, yb), (SECOND, yc, yd)):
        for i, (comp, p) in enumerate(units):
            v = jnp.where(first_core, own(fields, comp, p), own(fields, comp, NZL - 1 - p))
            low, high = v[:XH], v[NXL - XH :]
            a[i] = jnp.where(even, high, low)
            b[i] = jnp.where(even, low, high) * keep


def mark(out):
    out[...] = inside_x()


def early(grid, put):
    grid.sweep(1, range(0, 5), range(1, 5), put)
    grid.sweep(2, range(1, 4), range(2, 4), put)
    grid.sweep(3, range(2, 3), (), put)


def lookup(classes, eps_table, chi_table, eps_in, chi_in):
    for out, table in ((eps_in, eps_table), (chi_in, chi_table)):
        for k in range(ADVANCE):
            picked = jnp.zeros((NXL, NY), jnp.float32)
            for label in range(table.shape[0]):
                picked = jnp.where(classes[k] == label, table[label], picked)
            out[k] = picked


def sent(grid, side, i):
    comp, plane = side[i]
    return grid.get(comp, plane)


def inner(d, e, h, eps, chi, fd, fe, fh, lo, out):
    fields = (d, e, h, eps, chi)
    grid = Grid(NXL, lambda p: HALF, lambda p: None)
    for comp in ALL:
        for p in range(NZL):
            grid.hold(comp, p, functools.partial(own, fields, comp, p))
    grid.step_h(1, 6, range(2), lambda c, p, v, n: grid.put(lo, c - H, c, p, v, n))

    def put(c, p, v, n):
        ref = (fd, fe, fh)[c // 3]
        grid.put(ref, (c % 3, p), c, p, v, n)

    early(grid, put)
    gz, _, last, _ = position()
    first_core = lax.rem(gz, 2) == 0
    keep = scalar(jnp.logical_and(gz != 0, gz != last))
    half = halo_row() < XH
    for i in range(NS):
        v = sent(grid, HI, i)
        if i < len(LO) and LO[i]:
            v = jnp.where(first_core, v, sent(grid, LO, i))
        v = v * keep
        out[24 * i : 24 * i + 8] = jnp.where(half, v[24:32], v[0:8])
        out[24 * i + 8 : 24 * i + 24] = v[8:24]
        if i < NR:
            out[24 * NS + 8 * i : 24 * NS + 8 * i + 8] = jnp.where(half, v[0:8], v[24:32])


def edge_grid(inside, fields, tile):
    f = rows(jnp.full((8, NY), HALF), inside * HALF, jnp.full((8, NY), HALF))
    none = jnp.zeros((8, NY), jnp.float32)
    fill = rows(none, 1.0 - inside, none)
    grid = Grid(EDGE, lambda p: f, lambda p: fill)

    def read(comp, p):
        v = own(fields, comp, p)
        return rows(v[24:32], tile(comp, p), v[0:8])

    for comp in ALL:
        for p in range(NZL):
            grid.hold(comp, p, functools.partial(read, comp, p))
    return grid


def joined(a, b):
    _, gx, _, _ = position()
    even = lax.rem(gx, 2) == 0
    return rows(jnp.where(even, a, b), jnp.where(even, b, a))


def edges(d, e, h, eps, chi, ra, rb, inside, cross, sd, se, sh, slo, tiles):
    fields = (d, e, h, eps, chi)
    gz, _, last, _ = position()
    keep = scalar(jnp.logical_and(gz != 0, gz != last))
    half = halo_row() < XH

    def pack(grid, side):
        for i, unit in enumerate(side):
            if unit:
                v = grid.get(*unit) * keep
                cross[8 * i : 8 * i + 8] = v[8:16]
                if i >= NR:
                    at = 8 * (NS + i - NR)
                    cross[at : at + 8] = jnp.where(half, v[16:24], v[0:8])

    @pl.when(lax.rem(gz, 2) == 0)
    def _():
        at = {k: i for i, k in enumerate(FIRST)}
        for i in range(len(FIRST)):
            tiles[i] = joined(ra[i], rb[i])
        grid = edge_grid(inside[...], fields, lambda comp, p: tiles[at[(comp, p)]])
        early(grid, lambda c, p, v, n: grid.put((sd, se, sh)[c // 3], (c % 3, p), c, p, v, n))
        pack(grid, HI)

    @pl.when(lax.rem(gz, 2) == 1)
    def _():
        at = {(c, NZL - 1 - p): i for i, (c, p) in enumerate(FIRST) if p < 2}
        for i in at.values():
            tiles[i] = joined(ra[i], rb[i])
        grid = edge_grid(inside[...], fields, lambda comp, p: tiles[at[(comp, p)]])
        grid.step_h(1, 6, range(2), lambda c, p, v, n: grid.put(slo, c - H, c, p, v, n))
        pack(grid, LO)


def merge(d, e, h, eps, chi, id_, ie, ih, ilo, ra, rb, rc, rd, inside, xt, fd, fe, fh, chip, sd, se, sh, slo):
    fields = (d, e, h, eps, chi)
    gz, _, _, _ = position()
    first_core = lax.rem(gz, 2) == 0
    for units, a, b in ((FIRST, ra, rb), (SECOND, rc, rd)):
        for i, (comp, p) in enumerate(units):
            xt[comp, jnp.where(first_core, p, NZL - 1 - p)] = joined(a[i], b[i])
    thin = edge_grid(inside[...], fields, lambda comp, p: xt[comp, p])
    thin.step_h(1, 6, range(2), lambda c, p, v, n: thin.put(slo, c - H, c, p, v, n))
    early(thin, lambda c, p, v, n: thin.put((sd, se, sh)[c // 3], (c % 3, p), c, p, v, n))
    half = halo_row() < XH

    def merged(v, w):
        return rows(jnp.where(half, w[16:24], v[0:8]), v[8:24], jnp.where(half, v[24:32], w[0:8]), w[8:16])

    grid = Grid(ROWS, None, None)
    hold_own(grid, fields, xt)
    for k, (v, w, ref) in enumerate(((id_, sd, fd), (ie, se, fe), (ih, sh, fh))):
        for p in EARLY[k]:
            for c in range(3):
                grid.put(ref, (c, p), 3 * k + c, p, merged(v[c, p], w[c, p]), 1)
    for c in range(2):
        grid.hold(H + c, 6, functools.partial(lambda a: merged(ilo[a], slo[a]), c))
    for i in range(NS):
        v = sent(grid, HI, i)
        if i < len(LO) and LO[i]:
            v = jnp.where(first_core, sent(grid, LO, i), v)
        chip[i] = v


def full_grid():
    gz, _, last, _ = position()
    up, down = scalar(gz != last), scalar(gz != 0)
    edge = inside_x()

    def inside(p):
        return up if p >= NZL else (down if p < 0 else None)

    def factor(p):
        z = inside(p)
        main, tile = jnp.full((NXL, NY), HALF, jnp.float32), edge * HALF
        return rows(main, tile) if z is None else rows(main * z, tile * z)

    def fill(p):
        z = inside(p)
        if z is None:
            return rows(jnp.zeros((NXL, NY), jnp.float32), 1.0 - edge)
        return rows(jnp.full((NXL, NY), 1.0 - z, jnp.float32), 1.0 - edge * z)

    return Grid(ROWS, factor, fill)


def hold_own(grid, fields, xt):
    for comp in ALL:
        for p in range(NZL):
            grid.hold(comp, p, functools.partial(lambda c, q: rows(own(fields, c, q), xt[c, q]), comp, p))


def hold_frames(grid, refs, levels):
    for k, ref in enumerate(refs):
        for p, level in levels[k].items():
            for c in range(3):
                grid.hold(3 * k + c, p, functools.partial(lambda r, a, b: r[a, b], ref, c, p), level)


EARLY = ({1: 1, 2: 2, 3: 2, 4: 1}, {1: 1, 2: 2, 3: 2, 4: 1}, {0: 1, 1: 2, 2: 3, 3: 2, 4: 1})
MIDDLE = ({3: 3, 4: 3, 5: 2, 6: 1}, {3: 3, 4: 3, 5: 2, 6: 1}, {3: 4, 4: 3, 5: 2, 6: 1})


def middle(d, e, h, eps, chi, xt, fd, fe, fh, gd, ge, gh):
    grid = full_grid()
    hold_own(grid, (d, e, h, eps, chi), xt)
    hold_frames(grid, (fd, fe, fh), EARLY)

    def put(c, p, v, n):
        grid.put((gd, ge, gh)[c // 3], (c % 3, p), c, p, v, n)

    grid.sweep(1, (5, 6), (5, 6), put)
    grid.sweep(2, (4, 5), (4, 5), put)
    grid.sweep(3, (3, 4), (3, 4), put)
    grid.sweep(4, (3,), (), put)


def complete(own_refs, xt, frames, more, above, below, scratch, outs, sems, coming):
    fields = own_refs
    grid = full_grid()
    hold_own(grid, fields, xt)
    hold_frames(grid, frames, EARLY)
    hold_frames(grid, more, MIDDLE)
    for side, at, shift in ((above, HI_AT, NZL), (below, LO_AT, -NZL)):
        if side is not None:
            for (comp, p), i in at.items():
                level = (p + (H <= comp < EPS)) if shift > 0 else int(p == 6)
                grid.hold(comp, p + shift, functools.partial(side, i), level)
    state, staged = scratch[:3], scratch[3:6]
    copies = []

    def send(o):
        for k in range(3):
            copies.append(pltpu.make_async_copy(staged[k].at[:, pl.ds(o, 1)], outs[k].at[:, pl.ds(o, 1)], sems.at[k, o]))
            copies[-1].start()

    def put(c, p, v, n):
        k = c // 3
        if n == STEPS and p >= ADVANCE:
            staged[k][c % 3, p - ADVANCE] = v[:NXL]
        if n < STEPS or k == 2:
            grid.put(state[k], (c % 3, p + 2), c, p, v, n)

    def last_sweep(h_planes, de_planes):
        for p in sorted(set(h_planes) | set(de_planes)):
            if p in h_planes:
                grid.step_h(STEPS, p, range(3), put)
            if p in de_planes:
                if p not in h_planes:
                    for c in range(3):
                        staged[2][c, p - ADVANCE] = grid.get(H + c, p, STEPS)[:NXL]
                grid.step_de(STEPS, p, put)
                send(p - ADVANCE)

    if below is not None:
        grid.sweep(1, (-1,), (-1, 0), put)
        grid.sweep(2, (-1, 0), (0, 1), put)
        grid.sweep(3, (0, 1), (1, 2), put)
        last_sweep((1, 2), (2, 3))
    if above is not None:
        for k, (comp, new) in enumerate(((EPS, coming and coming[0]), (CHI, coming and coming[1]))):
            for o in range(ADVANCE):
                v = grid.get(comp, NZL + o)[:NXL]
                if new is not None:
                    gz, _, last, _ = position()
                    v = jnp.where(gz == last, new[o], v)
                scratch[6 + k][o] = v
            copies.append(pltpu.make_async_copy(scratch[6 + k], outs[3 + k].at[pl.ds(NZL - ADVANCE, ADVANCE)], sems.at[3, k]))
            copies[-1].start()
        grid.sweep(1, (7,), (7, 8), put)
        grid.sweep(2, range(6, 9), range(6, 10), put)
        grid.sweep(3, range(5, 10), range(5, 11), put)
        last_sweep(range(4, 10), range(4, 10))
    for c in copies:
        c.wait()


def near(d, e, h, eps, chi, xt, fd, fe, fh, gd, ge, gh, cc, d_out, e_out, h_out, eps_out, chi_out, *rest):
    *scratch, sems = rest
    fields, frames, more = (d, e, h, eps, chi), (fd, fe, fh), (gd, ge, gh)
    outs = (d_out, e_out, h_out, eps_out, chi_out)
    gz, _, _, _ = position()
    keep = NZL - ADVANCE
    media = [
        pltpu.make_async_copy(a.at[pl.ds(ADVANCE, keep)], b.at[pl.ds(0, keep)], sems.at[3, 2 + k])
        for k, (a, b) in enumerate(((eps, eps_out), (chi, chi_out)))
    ]
    for c in media:
        c.start()

    @pl.when(lax.rem(gz, 2) == 0)
    def _():
        complete(fields, xt, frames, more, lambda i: cc[i], None, scratch, outs, sems, None)

    @pl.when(lax.rem(gz, 2) == 1)
    def _():
        complete(fields, xt, frames, more, None, lambda i: cc[i], scratch, outs, sems, None)

    for c in media:
        c.wait()


def far(d, e, h, eps, chi, xt, fd, fe, fh, gd, ge, gh, ca, cb, eps_in, chi_in, *rest):
    outs, scratch, sems = rest[5:10], rest[10:-1], rest[-1]
    fields, frames, more = (d, e, h, eps, chi), (fd, fe, fh), (gd, ge, gh)
    half = halo_row() < XH
    gz, _, _, _ = position()

    def cross(i):
        m = ca[24 * i : 24 * i + 8]
        x = ca[24 * NS + 8 * i : 24 * NS + 8 * i + 8] if i < NR else cb[8 * (NS + i - NR) : 8 * (NS + i - NR) + 8]
        return rows(jnp.where(half, x, m), ca[24 * i + 8 : 24 * i + 24], jnp.where(half, m, x), cb[8 * i : 8 * i + 8])

    @pl.when(lax.rem(gz, 2) == 0)
    def _():
        complete(fields, xt, frames, more, None, cross, scratch, outs, sems, None)

    @pl.when(lax.rem(gz, 2) == 1)
    def _():
        complete(fields, xt, frames, more, cross, None, scratch, outs, sems, (eps_in, chi_in))


def swapped(shard, axis, first):
    n = {a: lax.axis_size(a) for a in ("gz", "gx")}
    moves = []
    for z in range(n["gz"]):
        for x in range(n["gx"]):
            at = z if axis == "gz" else x
            to = at + 1 if at % 2 == first else at - 1
            if 0 <= to < n[axis]:
                other = (to, x) if axis == "gz" else (z, to)
            else:
                other = (z ^ 1, x) if axis == "gx" else (z, x ^ 1)
            moves.append((z * n["gx"] + x, other[0] * n["gx"] + other[1]))
    return lax.ppermute(shard, ("gz", "gx"), moves)


def call(body, inputs, out_shape, scratch=(), vmem=8, specs=None, out=VM, aliases=None):
    return pl.pallas_call(
        body,
        out_shape=out_shape,
        in_specs=[VM] * len(inputs) if specs is None else specs,
        out_specs=jax.tree.map(lambda _: out, out_shape),
        input_output_aliases=aliases or {},
        scratch_shapes=list(scratch),
        compiler_params=pltpu.CompilerParams(vmem_limit_bytes=vmem << 20),
    )(*inputs)


def on_device(d_field, e_field, h_field, permittivity, kerr_coeff, classes, eps_table, chi_table):
    field, medium = shape(3, NZL, NXL, NY), shape(NZL, NXL, NY)
    one, two = shape(len(FIRST), XH, NY), shape(len(SECOND), XH, NY)
    *fields, ya, yb, yc, yd = call(
        load,
        [pltpu.with_memory_space_constraint(a, pltpu.HBM) for a in (d_field, e_field, h_field, permittivity, kerr_coeff)],
        (field, field, field, medium, medium, one, one, two, two),
        [pltpu.SemaphoreType.DMA((11,))],
        specs=[HBM] * 5,
    )
    ra, rb = swapped(ya, "gx", 0), swapped(yb, "gx", 1)
    lo = shape(2, NXL, NY)
    *inside, za = call(inner, fields, (*[shape(3, 5, NXL, NY)] * 3, lo, shape(24 * NS + 8 * NR, NY)))
    ca = swapped(za, "gz", 1)
    rc, rd = swapped(yc, "gx", 0), swapped(yd, "gx", 1)
    (edge,) = call(mark, [], (shape(8, NY),))
    thin = [pltpu.VMEM((3, 5, EDGE, NY), jnp.float32)] * 3 + [pltpu.VMEM((2, EDGE, NY), jnp.float32)]
    (zb,) = call(
        edges,
        [*fields, ra, rb, edge],
        (shape(8 * (NS + NS - NR), NY),),
        [*thin, pltpu.VMEM((len(FIRST), 8, NY), jnp.float32)],
    )
    cb = swapped(zb, "gz", 1)
    coming = call(lookup, [classes, eps_table, chi_table], (shape(ADVANCE, NXL, NY),) * 2, specs=[VM, SM, SM])
    frames = [shape(3, 5, ROWS, NY)] * 3
    xt, *frames, zc = call(
        merge, [*fields, *inside, ra, rb, rc, rd, edge], (shape(11, NZL, 8, NY), *frames, shape(NS, ROWS, NY)), thin
    )
    cc = swapped(zc, "gz", 0)
    more = call(middle, [*fields, xt, *frames], (shape(3, 7, ROWS, NY),) * 3)
    scratch = [pltpu.VMEM((3, 13, ROWS, NY), jnp.float32)] * 3 + [pltpu.VMEM((3, NZL, NXL, NY), jnp.float32)] * 3
    scratch += [pltpu.VMEM((ADVANCE, NXL, NY), jnp.float32)] * 2 + [pltpu.SemaphoreType.DMA((4, NZL))]
    given = [*fields, xt, *frames, *more]
    results = (field, field, field, medium, medium)
    outs = call(near, [*given, cc], results, scratch, vmem=16, out=HBM)
    given += [ca, cb, *coming]
    n = len(given)
    return call(
        far,
        [*given, *outs],
        results,
        scratch,
        vmem=16,
        specs=[VM] * n + [HBM] * 5,
        out=HBM,
        aliases={n + k: k for k in range(5)},
    )


def solution(mesh):
    placed = (
        P(None, "gz", "gx", None),
        P(None, "gz", "gx", None),
        P(None, "gz", "gx", None),
        P("gz", "gx", None),
        P("gz", "gx", None),
        P(None, "gx", None),
        P(),
        P(),
    )
    return jax.shard_map(
        on_device,
        mesh=mesh,
        in_specs=placed,
        out_specs=placed[:5],
        check_vma=False,
    )
```

```python
import functools

import jax
import jax.numpy as jnp
from jax import lax
from jax.experimental import pallas as pl
from jax.experimental.pallas import tpu as pltpu
from jax.sharding import PartitionSpec as P


STEPS = 4
KERR = 3
ADVANCE = 2
HALF = 0.5

D, E, H, EPS, CHI = 0, 3, 6, 9, 10
ALL = range(11)
NZL, NXL, NY = 8, 32, 128
XH = 4
ROWS = NXL + 2 * XH
EDGE = 24

RAW = [(c, 0) for c in range(H)] + [(c, p) for p in range(3) for c in (EPS, CHI)]
HI = RAW + [(H + c, 0) for c in range(3)] + [(c, p) for p in (1, 2) for c in range(EPS)]
LO = [(c, 7) for c in ALL] + [None, (H, 6), (H + 1, 6)]
HI_AT = {k: i for i, k in enumerate(HI)}
LO_AT = {k: i for i, k in enumerate(LO) if k}
NS, NR = len(HI), len(RAW)

VM = pl.BlockSpec(memory_space=pltpu.VMEM)
HBM = pl.BlockSpec(memory_space=pltpu.HBM)
SM = pl.BlockSpec(memory_space=pltpu.SMEM)


def shape(*dims):
    return jax.ShapeDtypeStruct(dims, jnp.float32)


def rows(*parts):
    return jnp.concatenate(parts, axis=0)


def scalar(condition):
    return jnp.where(condition, 1.0, 0.0).astype(jnp.float32)


def position():
    gz, gx = lax.axis_index("gz"), lax.axis_index("gx")
    return gz, gx, lax.axis_size("gz") - 1, lax.axis_size("gx") - 1


def halo_row():
    return lax.broadcasted_iota(jnp.int32, (8, NY), 0)


def inside_x():
    _, gx, _, last = position()
    return jnp.where(halo_row() < XH, scalar(gx != last), scalar(gx != 0))


class Grid:
    def __init__(self, size, factor, fill):
        self.size, self.factor, self.fill = size, factor, fill
        self.where, self.level = {}, {}
        lane = lax.broadcasted_iota(jnp.int32, (size, NY), 1)
        self.last_y, self.first_y = lane == NY - 1, lane == 0

    def hold(self, comp, plane, read, level=0):
        self.where[(comp, plane)] = read
        self.level[(comp, plane)] = level

    def get(self, comp, plane, level=None):
        assert level is None or self.level[(comp, plane)] == level, (comp, plane)
        return self.where[(comp, plane)]()

    def put(self, ref, index, comp, plane, value, level):
        ref[index] = value
        self.hold(comp, plane, lambda: ref[index], level)

    def next_y(self, v):
        return jnp.where(self.last_y, 0.0, pltpu.roll(v, NY - 1, 1))

    def prev_y(self, v):
        return jnp.where(self.first_y, 0.0, pltpu.roll(v, 1, 1))

    def next_x(self, v):
        return pltpu.roll(v, self.size - 1, 0)

    def prev_x(self, v):
        return pltpu.roll(v, 1, 0)

    def step_h(self, n, p, comps, put):
        f = self.factor(p)
        ex, ey, ez = (self.get(E + c, p, n - 1) for c in range(3))
        new = {}
        if 0 in comps:
            eyn = self.get(E + 1, p + 1, n - 1)
            new[0] = (self.next_y(ez) - ez) - (eyn - ey)
        if 1 in comps:
            exn = self.get(E, p + 1, n - 1)
            new[1] = (exn - ex) - (self.next_x(ez) - ez)
        if 2 in comps:
            new[2] = (self.next_x(ey) - ey) - (self.next_y(ex) - ex)
        for c, curl in new.items():
            put(H + c, p, self.get(H + c, p, n - 1) - f * curl, n)

    def step_de(self, n, p, put):
        f = self.factor(p)
        hx, hy, hz = (self.get(H + c, p, n) for c in range(3))
        hxp, hyp = (self.get(H + c, p - 1, n) for c in range(2))
        dx = self.get(D, p, n - 1) + f * ((hz - self.prev_y(hz)) - (hy - hyp))
        dy = self.get(D + 1, p, n - 1) + f * ((hx - hxp) - (hz - self.prev_x(hz)))
        dz = self.get(D + 2, p, n - 1) + f * ((hy - self.prev_x(hy)) - (hx - self.prev_y(hx)))
        ex, ey, ez = (self.get(E + c, p, n - 1) for c in range(3))
        eps, chi = self.get(EPS, p), self.get(CHI, p)
        fill = self.fill(p)
        if fill is not None:
            eps = eps + fill
        if n == STEPS:
            dx, dy, dz, ex, ey, ez, eps, chi = (v[:NXL] for v in (dx, dy, dz, ex, ey, ez, eps, chi))
        inverse = 1.0 / (eps + chi * (ex * ex + ey * ey + ez * ez))
        squares = chi * (dx * dx + dy * dy + dz * dz)
        for _ in range(KERR - 1):
            inverse = 1.0 / (eps + squares * (inverse * inverse))
        for c, v in enumerate((dx, dy, dz)):
            put(D + c, p, v, n)
            put(E + c, p, v * inverse, n)

    def sweep(self, n, h_planes, de_planes, put):
        for p in range(-2, 11):
            if p in h_planes:
                self.step_h(n, p, range(3), put)
            if p in de_planes:
                self.step_de(n, p, put)


def own(fields, comp, plane):
    d, e, h, eps, chi = fields
    if comp < E:
        return d[comp, plane]
    if comp < H:
        return e[comp - E, plane]
    if comp < EPS:
        return h[comp - H, plane]
    return eps[plane] if comp == EPS else chi[plane]


def load(d, e, h, eps, chi, dv, ev, hv, epsv, chiv, ya, yb, sems):
    moves = [(a.at[c], b.at[c]) for a, b in ((d, dv), (e, ev), (h, hv)) for c in range(3)] + [(eps, epsv), (chi, chiv)]
    copies = [pltpu.make_async_copy(a, b, sems.at[i]) for i, (a, b) in enumerate(moves)]
    for c in copies:
        c.start()
    _, gx, _, last = position()
    even = lax.rem(gx, 2) == 0
    keep = scalar(jnp.logical_and(gx != 0, gx != last))
    for comp in ALL:
        copies[comp].wait()
        for p in range(NZL):
            v = own((dv, ev, hv, epsv, chiv), comp, p)
            low, high = v[:XH], v[NXL - XH :]
            ya[comp, p] = jnp.where(even, high, low)
            yb[comp, p] = jnp.where(even, low, high) * keep


def mark(out):
    out[...] = inside_x()


def early(grid, put):
    grid.sweep(1, range(0, 5), range(1, 5), put)
    grid.sweep(2, range(1, 4), range(2, 4), put)
    grid.sweep(3, range(2, 3), (), put)


def lookup(classes, table):
    labels = jnp.arange(table.shape[0], dtype=jnp.int32).reshape(-1, 1, 1, 1)
    picked = jnp.where(classes[None] == labels, table.reshape(-1, 1, 1, 1), jnp.float32(0.0))
    return jnp.sum(picked, axis=0)


def sent(grid, side, i):
    comp, plane = side[i]
    return grid.get(comp, plane)


def inner(d, e, h, eps, chi, fd, fe, fh, lo, out):
    fields = (d, e, h, eps, chi)
    grid = Grid(NXL, lambda p: HALF, lambda p: None)
    for comp in ALL:
        for p in range(NZL):
            grid.hold(comp, p, functools.partial(own, fields, comp, p))
    grid.step_h(1, 6, range(2), lambda c, p, v, n: grid.put(lo, c - H, c, p, v, n))

    def put(c, p, v, n):
        ref = (fd, fe, fh)[c // 3]
        grid.put(ref, (c % 3, p), c, p, v, n)

    early(grid, put)
    gz, _, last, _ = position()
    first_core = lax.rem(gz, 2) == 0
    keep = scalar(jnp.logical_and(gz != 0, gz != last))
    half = halo_row() < XH
    for i in range(NS):
        v = sent(grid, HI, i)
        if i < len(LO) and LO[i]:
            v = jnp.where(first_core, v, sent(grid, LO, i))
        v = v * keep
        out[24 * i : 24 * i + 8] = jnp.where(half, v[24:32], v[0:8])
        out[24 * i + 8 : 24 * i + 24] = v[8:24]
        if i < NR:
            out[24 * NS + 8 * i : 24 * NS + 8 * i + 8] = jnp.where(half, v[0:8], v[24:32])


def edge_grid(inside, fields, tile):
    f = rows(jnp.full((8, NY), HALF), inside * HALF, jnp.full((8, NY), HALF))
    none = jnp.zeros((8, NY), jnp.float32)
    fill = rows(none, 1.0 - inside, none)
    grid = Grid(EDGE, lambda p: f, lambda p: fill)

    def read(comp, p):
        v = own(fields, comp, p)
        return rows(v[24:32], tile(comp, p), v[0:8])

    for comp in ALL:
        for p in range(NZL):
            grid.hold(comp, p, functools.partial(read, comp, p))
    return grid


def joined(a, b):
    _, gx, _, _ = position()
    even = lax.rem(gx, 2) == 0
    return rows(jnp.where(even, a, b), jnp.where(even, b, a))


def edges(d, e, h, eps, chi, ra, rb, inside, xt, sd, se, sh, slo, cross):
    fields = (d, e, h, eps, chi)
    gz, _, last, _ = position()
    keep = scalar(jnp.logical_and(gz != 0, gz != last))
    half = halo_row() < XH
    for comp in ALL:
        for p in range(NZL):
            xt[comp, p] = joined(ra[comp, p], rb[comp, p])

    def pack(grid, side):
        for i, unit in enumerate(side):
            if unit:
                v = grid.get(*unit) * keep
                cross[8 * i : 8 * i + 8] = v[8:16]
                if i >= NR:
                    at = 8 * (NS + i - NR)
                    cross[at : at + 8] = jnp.where(half, v[16:24], v[0:8])

    @pl.when(lax.rem(gz, 2) == 0)
    def _():
        grid = edge_grid(inside[...], fields, lambda comp, p: xt[comp, p])
        early(grid, lambda c, p, v, n: grid.put((sd, se, sh)[c // 3], (c % 3, p), c, p, v, n))
        pack(grid, HI)

    @pl.when(lax.rem(gz, 2) == 1)
    def _():
        grid = edge_grid(inside[...], fields, lambda comp, p: xt[comp, p])
        grid.step_h(1, 6, range(2), lambda c, p, v, n: grid.put(slo, c - H, c, p, v, n))
        pack(grid, LO)


def merge(d, e, h, eps, chi, id_, ie, ih, ilo, xt, sd, se, sh, slo, inside, fd, fe, fh, chip, td, te, th, tlo):
    fields = (d, e, h, eps, chi)
    half = halo_row() < XH

    def merged(v, w):
        return rows(jnp.where(half, w[16:24], v[0:8]), v[8:24], jnp.where(half, v[24:32], w[0:8]), w[8:16])

    def join(sides, side):
        grid = Grid(ROWS, None, None)
        hold_own(grid, fields, xt)
        for k, (v, w, ref) in enumerate(((id_, sides[0], fd), (ie, sides[1], fe), (ih, sides[2], fh))):
            for p in EARLY[k]:
                for c in range(3):
                    grid.put(ref, (c, p), 3 * k + c, p, merged(v[c, p], w[c, p]), 1)
        for c in range(2):
            grid.hold(H + c, 6, functools.partial(lambda a: merged(ilo[a], tlo[a]), c))
        for i, unit in enumerate(side):
            if unit:
                chip[i] = grid.get(*unit)

    gz, _, _, _ = position()

    @pl.when(lax.rem(gz, 2) == 0)
    def _():
        grid = edge_grid(inside[...], fields, lambda comp, p: xt[comp, p])
        grid.step_h(1, 6, range(2), lambda c, p, v, n: grid.put(tlo, c - H, c, p, v, n))
        join((sd, se, sh), LO)

    @pl.when(lax.rem(gz, 2) == 1)
    def _():
        grid = edge_grid(inside[...], fields, lambda comp, p: xt[comp, p])
        early(grid, lambda c, p, v, n: grid.put((td, te, th)[c // 3], (c % 3, p), c, p, v, n))
        join((td, te, th), HI)


def full_grid():
    gz, _, last, _ = position()
    up, down = scalar(gz != last), scalar(gz != 0)
    edge = inside_x()

    def inside(p):
        return up if p >= NZL else (down if p < 0 else None)

    def factor(p):
        z = inside(p)
        main, tile = jnp.full((NXL, NY), HALF, jnp.float32), edge * HALF
        return rows(main, tile) if z is None else rows(main * z, tile * z)

    def fill(p):
        z = inside(p)
        if z is None:
            return rows(jnp.zeros((NXL, NY), jnp.float32), 1.0 - edge)
        return rows(jnp.full((NXL, NY), 1.0 - z, jnp.float32), 1.0 - edge * z)

    return Grid(ROWS, factor, fill)


def hold_own(grid, fields, xt):
    for comp in ALL:
        for p in range(NZL):
            grid.hold(comp, p, functools.partial(lambda c, q: rows(own(fields, c, q), xt[c, q]), comp, p))


def hold_frames(grid, refs, levels):
    for k, ref in enumerate(refs):
        for p, level in levels[k].items():
            for c in range(3):
                grid.hold(3 * k + c, p, functools.partial(lambda r, a, b: r[a, b], ref, c, p), level)


EARLY = ({1: 1, 2: 2, 3: 2, 4: 1}, {1: 1, 2: 2, 3: 2, 4: 1}, {0: 1, 1: 2, 2: 3, 3: 2, 4: 1})
MIDDLE = ({3: 3, 4: 3, 5: 2, 6: 1}, {3: 3, 4: 3, 5: 2, 6: 1}, {3: 4, 4: 3, 5: 2, 6: 1})


def middle(d, e, h, eps, chi, xt, fd, fe, fh, gd, ge, gh):
    grid = full_grid()
    hold_own(grid, (d, e, h, eps, chi), xt)
    hold_frames(grid, (fd, fe, fh), EARLY)

    def put(c, p, v, n):
        grid.put((gd, ge, gh)[c // 3], (c % 3, p), c, p, v, n)

    grid.sweep(1, (5, 6), (5, 6), put)
    grid.sweep(2, (4, 5), (4, 5), put)
    grid.sweep(3, (3, 4), (3, 4), put)
    grid.sweep(4, (3,), (), put)


def complete(fields, xt, frames, more, above, below, state, staged, media, coming, done):
    grid = full_grid()
    hold_own(grid, fields, xt)
    hold_frames(grid, frames, EARLY)
    hold_frames(grid, more, MIDDLE)
    for side, at, shift in ((above, HI_AT, NZL), (below, LO_AT, -NZL)):
        if side is not None:
            for (comp, p), i in at.items():
                level = (p + (H <= comp < EPS)) if shift > 0 else int(p == 6)
                grid.hold(comp, p + shift, functools.partial(side, i), level)

    def put(c, p, v, n):
        k = c // 3
        if n == STEPS and p >= ADVANCE:
            staged[k][c % 3, p - ADVANCE] = v[:NXL]
        if n < STEPS or k == 2:
            grid.put(state[k], (c % 3, p + 2), c, p, v, n)

    def last_sweep(h_planes, de_planes):
        for p in sorted(set(h_planes) | set(de_planes)):
            if p in h_planes:
                grid.step_h(STEPS, p, range(3), put)
            if p in de_planes:
                if p not in h_planes:
                    for c in range(3):
                        staged[2][c, p - ADVANCE] = grid.get(H + c, p, STEPS)[:NXL]
                grid.step_de(STEPS, p, put)
                for k in range(3):
                    done(k, p - ADVANCE, 1)

    if below is not None:
        grid.sweep(1, (-1,), (-1, 0), put)
        grid.sweep(2, (-1, 0), (0, 1), put)
        grid.sweep(3, (0, 1), (1, 2), put)
        last_sweep((1, 2), (2, 3))
    if above is not None:
        for k, comp in enumerate((EPS, CHI)):
            for o in range(ADVANCE):
                v = grid.get(comp, NZL + o)[:NXL]
                if coming is not None:
                    gz, _, last, _ = position()
                    v = jnp.where(gz == last, coming[k][o], v)
                media[k][o] = v
            done(3 + k, KEPT, ADVANCE)
        grid.sweep(1, (7,), (7, 8), put)
        grid.sweep(2, range(6, 9), range(6, 10), put)
        grid.sweep(3, range(5, 10), range(5, 11), put)
        last_sweep(range(4, 10), range(4, 10))


KEPT = NZL - ADVANCE
LOW, HIGH = (0, 2), (2, 6)


def near(d, e, h, eps, chi, xt, fd, fe, fh, gd, ge, gh, cc, nd, ne, nh, neps, nchi, *state):
    given = (d, e, h, eps, chi), xt, (fd, fe, fh), (gd, ge, gh)
    gz, _, _, _ = position()

    def done(k, o, n):
        pass

    @pl.when(lax.rem(gz, 2) == 0)
    def _():
        complete(*given, lambda i: cc[i], None, state, (nd, ne, nh), (neps, nchi), None, done)

    @pl.when(lax.rem(gz, 2) == 1)
    def _():
        complete(*given, None, lambda i: cc[i], state, (nd, ne, nh), (neps, nchi), None, done)


def far(d, e, h, eps, chi, xt, fd, fe, fh, gd, ge, gh, ca, cb, eps_in, chi_in, nd, ne, nh, neps, nchi, *rest):
    outs, state, staged, media, sems = rest[:5], rest[5:8], rest[8:11], rest[11:13], rest[13]
    given = (d, e, h, eps, chi), xt, (fd, fe, fh), (gd, ge, gh)
    half = halo_row() < XH
    gz, _, _, _ = position()

    def cross(i):
        m = ca[24 * i : 24 * i + 8]
        x = ca[24 * NS + 8 * i : 24 * NS + 8 * i + 8] if i < NR else cb[8 * (NS + i - NR) : 8 * (NS + i - NR) + 8]
        return rows(jnp.where(half, x, m), ca[24 * i + 8 : 24 * i + 24], jnp.where(half, m, x), cb[8 * i : 8 * i + 8])

    def run(above, below, made, new_media):
        copies = []

        def send(source, target):
            copies.append(pltpu.make_async_copy(source, target, sems.at[len(copies)]))
            copies[-1].start()

        def done(k, o, n):
            if k < 3:
                send(staged[k].at[:, pl.ds(o, n)], outs[k].at[:, pl.ds(o, n)])
            else:
                send(media[k - 3], outs[k].at[pl.ds(o, n)])

        o, n = made
        for a, b in zip((nd, ne, nh), outs):
            send(a.at[:, pl.ds(o, n)], b.at[:, pl.ds(o, n)])
        for a, b in zip((eps, chi), outs[3:]):
            send(a.at[pl.ds(ADVANCE, KEPT)], b.at[pl.ds(0, KEPT)])
        for a, b in zip(new_media, outs[3:]):
            send(a, b.at[pl.ds(KEPT, ADVANCE)])
        complete(*given, above, below, state, staged, media, (eps_in, chi_in), done)
        for c in copies:
            c.wait()

    @pl.when(lax.rem(gz, 2) == 0)
    def _():
        run(None, cross, HIGH, (neps, nchi))

    @pl.when(lax.rem(gz, 2) == 1)
    def _():
        run(cross, None, LOW, ())


def swapped(shard, axis, first):
    n = {a: lax.axis_size(a) for a in ("gz", "gx")}
    moves = []
    for z in range(n["gz"]):
        for x in range(n["gx"]):
            at = z if axis == "gz" else x
            to = at + 1 if at % 2 == first else at - 1
            if 0 <= to < n[axis]:
                other = (to, x) if axis == "gz" else (z, to)
            else:
                other = (z ^ 1, x) if axis == "gx" else (z, x ^ 1)
            moves.append((z * n["gx"] + x, other[0] * n["gx"] + other[1]))
    return lax.ppermute(shard, ("gz", "gx"), moves)


def call(body, inputs, out_shape, scratch=(), vmem=8, specs=None, out=VM, aliases=None):
    return pl.pallas_call(
        body,
        out_shape=out_shape,
        in_specs=[VM] * len(inputs) if specs is None else specs,
        out_specs=jax.tree.map(lambda _: out, out_shape),
        input_output_aliases=aliases or {},
        scratch_shapes=list(scratch),
        compiler_params=pltpu.CompilerParams(vmem_limit_bytes=vmem << 20),
    )(*inputs)


def on_device(d_field, e_field, h_field, permittivity, kerr_coeff, classes, eps_table, chi_table):
    field, medium = shape(3, NZL, NXL, NY), shape(NZL, NXL, NY)
    halo = shape(11, NZL, XH, NY)
    *fields, ya, yb = call(
        load,
        [pltpu.with_memory_space_constraint(a, pltpu.HBM) for a in (d_field, e_field, h_field, permittivity, kerr_coeff)],
        (field, field, field, medium, medium, halo, halo),
        [pltpu.SemaphoreType.DMA((11,))],
        specs=[HBM] * 5,
    )
    ra, rb = swapped(ya, "gx", 0), swapped(yb, "gx", 1)
    lo = shape(2, NXL, NY)
    *inside, za = call(inner, fields, (*[shape(3, 5, NXL, NY)] * 3, lo, shape(24 * NS + 8 * NR, NY)))
    ca = swapped(za, "gz", 1)
    (edge,) = call(mark, [], (shape(8, NY),))
    thin = [(3, 5, EDGE, NY)] * 3 + [(2, EDGE, NY)]
    xt, *outside, zb = call(
        edges,
        [*fields, ra, rb, edge],
        (shape(11, NZL, 8, NY), *[shape(*t) for t in thin], shape(8 * (NS + NS - NR), NY)),
    )
    cb = swapped(zb, "gz", 1)
    coming = lookup(classes, eps_table), lookup(classes, chi_table)
    *frames, zc = call(
        merge,
        [*fields, *inside, xt, *outside, edge],
        (*[shape(3, 5, ROWS, NY)] * 3, shape(NS, ROWS, NY)),
        [pltpu.VMEM(t, jnp.float32) for t in thin],
    )
    cc = swapped(zc, "gz", 0)
    more = call(middle, [*fields, xt, *frames], (shape(3, 7, ROWS, NY),) * 3)
    state = [pltpu.VMEM((3, 13, ROWS, NY), jnp.float32)] * 3
    given = [*fields, xt, *frames, *more]
    two = (ADVANCE, NXL, NY)
    made = call(near, [*given, cc], (field, field, field, shape(*two), shape(*two)), state, vmem=16)
    staged = [pltpu.VMEM(field.shape, jnp.float32)] * 3 + [pltpu.VMEM(two, jnp.float32)] * 2
    return call(
        far,
        [*given, ca, cb, *coming, *made],
        (field, field, field, medium, medium),
        [*state, *staged, pltpu.SemaphoreType.DMA((32,))],
        vmem=16,
        out=HBM,
    )


def solution(mesh):
    placed = (
        P(None, "gz", "gx", None),
        P(None, "gz", "gx", None),
        P(None, "gz", "gx", None),
        P("gz", "gx", None),
        P("gz", "gx", None),
        P(None, "gx", None),
        P(),
        P(),
    )
    return jax.shard_map(
        on_device,
        mesh=mesh,
        in_specs=placed,
        out_specs=placed[:5],
        check_vma=False,
    )
```

```python
import functools

import jax
import jax.numpy as jnp
from jax import lax
from jax.experimental import pallas as pl
from jax.experimental.pallas import tpu as pltpu
from jax.sharding import PartitionSpec as P


STEPS = 4
KERR = 3
ADVANCE = 2
HALF = 0.5

D, E, H, EPS, CHI = 0, 3, 6, 9, 10
ALL = range(11)
NZL, NXL, NY = 8, 32, 128
XH = 4
ROWS = NXL + 2 * XH
EDGE = 24

DP, HP, INV = 11, 14, 17
RAW = [(E + c, 0) for c in range(3)] + [(c, p) for p in range(3) for c in (EPS, CHI)]
HI = RAW + [(DP + c, p) for p in range(3) for c in range(3)] + [(HP + c, p) for p in range(2) for c in range(3)]
HI += [(INV, 1), (INV, 2)]
LO = [(c, 7) for c in ALL] + [(H, 6), (H + 1, 6)]
HI_AT = {k: i for i, k in enumerate(HI)}
LO_AT = {k: i for i, k in enumerate(LO)}
NS, NR = len(HI), len(RAW)

VM = pl.BlockSpec(memory_space=pltpu.VMEM)
HBM = pl.BlockSpec(memory_space=pltpu.HBM)
SM = pl.BlockSpec(memory_space=pltpu.SMEM)


def shape(*dims):
    return jax.ShapeDtypeStruct(dims, jnp.float32)


def rows(*parts):
    return jnp.concatenate(parts, axis=0)


def scalar(condition):
    return jnp.where(condition, 1.0, 0.0).astype(jnp.float32)


def position():
    gz, gx = lax.axis_index("gz"), lax.axis_index("gx")
    return gz, gx, lax.axis_size("gz") - 1, lax.axis_size("gx") - 1


def halo_row():
    return lax.broadcasted_iota(jnp.int32, (8, NY), 0)


def inside_x():
    _, gx, _, last = position()
    return jnp.where(halo_row() < XH, scalar(gx != last), scalar(gx != 0))


class Grid:
    def __init__(self, size, factor, fill):
        self.size, self.factor, self.fill = size, factor, fill
        self.where, self.level = {}, {}
        lane = lax.broadcasted_iota(jnp.int32, (size, NY), 1)
        self.last_y, self.first_y = lane == NY - 1, lane == 0

    def hold(self, comp, plane, read, level=0):
        self.where[(comp, plane)] = read
        self.level[(comp, plane)] = level

    def get(self, comp, plane, level=None):
        assert level is None or self.level[(comp, plane)] == level, (comp, plane)
        return self.where[(comp, plane)]()

    def put(self, ref, index, comp, plane, value, level):
        ref[index] = value
        self.hold(comp, plane, lambda: ref[index], level)

    def next_y(self, v):
        return jnp.where(self.last_y, 0.0, pltpu.roll(v, NY - 1, 1))

    def prev_y(self, v):
        return jnp.where(self.first_y, 0.0, pltpu.roll(v, 1, 1))

    def next_x(self, v):
        return pltpu.roll(v, self.size - 1, 0)

    def prev_x(self, v):
        return pltpu.roll(v, 1, 0)

    def step_h(self, n, p, comps, put):
        f = self.factor(p)
        ex, ey, ez = (self.get(E + c, p, n - 1) for c in range(3))
        if self.level.get((HP, p)) == n:
            hx, hy, hz = (self.get(HP + c, p) for c in range(3))
            put(H, p, hx - f * ((self.next_y(ez) - ez) + ey), n)
            put(H + 1, p, hy + f * (ex + (self.next_x(ez) - ez)), n)
            put(H + 2, p, hz - f * ((self.next_x(ey) - ey) - (self.next_y(ex) - ex)), n)
            return
        new = {}
        if 0 in comps:
            eyn = self.get(E + 1, p + 1, n - 1)
            new[0] = (self.next_y(ez) - ez) - (eyn - ey)
        if 1 in comps:
            exn = self.get(E, p + 1, n - 1)
            new[1] = (exn - ex) - (self.next_x(ez) - ez)
        if 2 in comps:
            new[2] = (self.next_x(ey) - ey) - (self.next_y(ex) - ex)
        for c, curl in new.items():
            put(H + c, p, self.get(H + c, p, n - 1) - f * curl, n)

    def medium(self, p):
        eps, fill = self.get(EPS, p), self.fill(p)
        return eps if fill is None else eps + fill, self.get(CHI, p)

    def first_inverse(self, n, p):
        ex, ey, ez = (self.get(E + c, p, n) for c in range(3))
        eps, chi = self.medium(p)
        return 1.0 / (eps + chi * (ex * ex + ey * ey + ez * ez))

    def derive(self):
        out = {}
        for p in range(3):
            f, n = self.factor(p), p + 1
            hx, hy, hz = (self.get(H + c, p, n) for c in range(3))
            dx, dy, dz = (self.get(D + c, p, n - 1) for c in range(3))
            out[(DP, p)] = dx + f * ((hz - self.prev_y(hz)) - hy)
            out[(DP + 1, p)] = dy + f * (hx - (hz - self.prev_x(hz)))
            out[(DP + 2, p)] = dz + f * ((hy - self.prev_x(hy)) - (hx - self.prev_y(hx)))
            if p < 2:
                out[(HP, p)] = hx + f * self.get(E + 1, p + 1, n)
                out[(HP + 1, p)] = hy - f * self.get(E, p + 1, n)
                out[(HP + 2, p)] = hz
            if p > 0:
                out[(INV, p)] = self.first_inverse(n - 1, p)
        return out

    def step_de(self, n, p, put):
        f = self.factor(p)
        hxp, hyp = (self.get(H + c, p - 1, n) for c in range(2))
        if self.level.get((DP, p)) == n:
            dx, dy, dz = (self.get(DP + c, p) for c in range(3))
            dx, dy = dx + f * hyp, dy - f * hxp
        else:
            hx, hy, hz = (self.get(H + c, p, n) for c in range(3))
            dx = self.get(D, p, n - 1) + f * ((hz - self.prev_y(hz)) - (hy - hyp))
            dy = self.get(D + 1, p, n - 1) + f * ((hx - hxp) - (hz - self.prev_x(hz)))
            dz = self.get(D + 2, p, n - 1) + f * ((hy - self.prev_x(hy)) - (hx - self.prev_y(hx)))
        eps, chi = self.medium(p)
        inverse = self.get(INV, p) if self.level.get((INV, p)) == n else self.first_inverse(n - 1, p)
        if n == STEPS:
            dx, dy, dz, eps, chi, inverse = (v[:NXL] for v in (dx, dy, dz, eps, chi, inverse))
        squares = chi * (dx * dx + dy * dy + dz * dz)
        for _ in range(KERR - 1):
            inverse = 1.0 / (eps + squares * (inverse * inverse))
        for c, v in enumerate((dx, dy, dz)):
            put(D + c, p, v, n)
            put(E + c, p, v * inverse, n)

    def sweep(self, n, h_planes, de_planes, put):
        for p in range(-2, 11):
            if p in h_planes:
                self.step_h(n, p, range(3), put)
            if p in de_planes:
                self.step_de(n, p, put)


def own(fields, comp, plane):
    d, e, h, eps, chi = fields
    if comp < E:
        return d[comp, plane]
    if comp < H:
        return e[comp - E, plane]
    if comp < EPS:
        return h[comp - H, plane]
    return eps[plane] if comp == EPS else chi[plane]


def load(d, e, h, eps, chi, dv, ev, hv, epsv, chiv, ya, yb, sems):
    moves = [(a.at[c], b.at[c]) for a, b in ((d, dv), (e, ev), (h, hv)) for c in range(3)] + [(eps, epsv), (chi, chiv)]
    copies = [pltpu.make_async_copy(a, b, sems.at[i]) for i, (a, b) in enumerate(moves)]
    for c in copies:
        c.start()
    _, gx, _, last = position()
    even = lax.rem(gx, 2) == 0
    keep = scalar(jnp.logical_and(gx != 0, gx != last))
    for comp in ALL:
        copies[comp].wait()
        for p in range(NZL):
            v = own((dv, ev, hv, epsv, chiv), comp, p)
            low, high = v[:XH], v[NXL - XH :]
            ya[comp, p] = jnp.where(even, high, low)
            yb[comp, p] = jnp.where(even, low, high) * keep


def mark(out):
    out[...] = inside_x()


def early(grid, put):
    grid.sweep(1, range(0, 5), range(1, 5), put)
    grid.sweep(2, range(1, 4), range(2, 4), put)
    grid.sweep(3, range(2, 3), (), put)


def lookup(classes, table):
    labels = jnp.arange(table.shape[0], dtype=jnp.int32).reshape(-1, 1, 1, 1)
    picked = jnp.where(classes[None] == labels, table.reshape(-1, 1, 1, 1), jnp.float32(0.0))
    return jnp.sum(picked, axis=0)


def payload(grid, side):
    made = grid.derive() if side is HI else {}
    return [made[k] if k in made else grid.get(*k) for k in side]


def inner(d, e, h, eps, chi, fd, fe, fh, lo, out):
    fields = (d, e, h, eps, chi)
    grid = Grid(NXL, lambda p: HALF, lambda p: None)
    for comp in ALL:
        for p in range(NZL):
            grid.hold(comp, p, functools.partial(own, fields, comp, p))
    grid.step_h(1, 6, range(2), lambda c, p, v, n: grid.put(lo, c - H, c, p, v, n))

    def put(c, p, v, n):
        ref = (fd, fe, fh)[c // 3]
        grid.put(ref, (c % 3, p), c, p, v, n)

    early(grid, put)
    gz, _, last, _ = position()
    first_core = lax.rem(gz, 2) == 0
    keep = scalar(jnp.logical_and(gz != 0, gz != last))
    half = halo_row() < XH
    low = payload(grid, LO)
    for i, v in enumerate(payload(grid, HI)):
        if i < len(LO):
            v = jnp.where(first_core, v, low[i])
        v = v * keep
        out[24 * i : 24 * i + 8] = jnp.where(half, v[24:32], v[0:8])
        out[24 * i + 8 : 24 * i + 24] = v[8:24]
        if i < NR:
            out[24 * NS + 8 * i : 24 * NS + 8 * i + 8] = jnp.where(half, v[0:8], v[24:32])


def edge_grid(inside, fields, tile):
    f = rows(jnp.full((8, NY), HALF), inside * HALF, jnp.full((8, NY), HALF))
    none = jnp.zeros((8, NY), jnp.float32)
    fill = rows(none, 1.0 - inside, none)
    grid = Grid(EDGE, lambda p: f, lambda p: fill)

    def read(comp, p):
        v = own(fields, comp, p)
        return rows(v[24:32], tile(comp, p), v[0:8])

    for comp in ALL:
        for p in range(NZL):
            grid.hold(comp, p, functools.partial(read, comp, p))
    return grid


def joined(a, b):
    _, gx, _, _ = position()
    even = lax.rem(gx, 2) == 0
    return rows(jnp.where(even, a, b), jnp.where(even, b, a))


def edges(d, e, h, eps, chi, ra, rb, inside, xt, sd, se, sh, slo, cross):
    fields = (d, e, h, eps, chi)
    gz, _, last, _ = position()
    keep = scalar(jnp.logical_and(gz != 0, gz != last))
    half = halo_row() < XH
    for comp in ALL:
        for p in range(NZL):
            xt[comp, p] = joined(ra[comp, p], rb[comp, p])

    def pack(grid, side):
        for i, v in enumerate(payload(grid, side)):
            v = v * keep
            cross[8 * i : 8 * i + 8] = v[8:16]
            if i >= NR:
                at = 8 * (NS + i - NR)
                cross[at : at + 8] = jnp.where(half, v[16:24], v[0:8])

    @pl.when(lax.rem(gz, 2) == 0)
    def _():
        grid = edge_grid(inside[...], fields, lambda comp, p: xt[comp, p])
        early(grid, lambda c, p, v, n: grid.put((sd, se, sh)[c // 3], (c % 3, p), c, p, v, n))
        pack(grid, HI)

    @pl.when(lax.rem(gz, 2) == 1)
    def _():
        grid = edge_grid(inside[...], fields, lambda comp, p: xt[comp, p])
        grid.step_h(1, 6, range(2), lambda c, p, v, n: grid.put(slo, c - H, c, p, v, n))
        pack(grid, LO)


def merge(d, e, h, eps, chi, id_, ie, ih, ilo, xt, sd, se, sh, slo, inside, fd, fe, fh, chip, td, te, th, tlo):
    fields = (d, e, h, eps, chi)
    half = halo_row() < XH

    def merged(v, w):
        return rows(jnp.where(half, w[16:24], v[0:8]), v[8:24], jnp.where(half, v[24:32], w[0:8]), w[8:16])

    def join(sides, side):
        grid = full_grid()
        hold_own(grid, fields, xt)
        for k, (v, w, ref) in enumerate(((id_, sides[0], fd), (ie, sides[1], fe), (ih, sides[2], fh))):
            for p, level in EARLY[k].items():
                for c in range(3):
                    grid.put(ref, (c, p), 3 * k + c, p, merged(v[c, p], w[c, p]), level)
        for c in range(2):
            grid.hold(H + c, 6, functools.partial(lambda a: merged(ilo[a], tlo[a]), c))
        for i, v in enumerate(payload(grid, side)):
            chip[i] = v

    gz, _, _, _ = position()

    @pl.when(lax.rem(gz, 2) == 0)
    def _():
        grid = edge_grid(inside[...], fields, lambda comp, p: xt[comp, p])
        grid.step_h(1, 6, range(2), lambda c, p, v, n: grid.put(tlo, c - H, c, p, v, n))
        join((sd, se, sh), LO)

    @pl.when(lax.rem(gz, 2) == 1)
    def _():
        grid = edge_grid(inside[...], fields, lambda comp, p: xt[comp, p])
        early(grid, lambda c, p, v, n: grid.put((td, te, th)[c // 3], (c % 3, p), c, p, v, n))
        join((td, te, th), HI)


def full_grid():
    gz, _, last, _ = position()
    up, down = scalar(gz != last), scalar(gz != 0)
    edge = inside_x()

    def inside(p):
        return up if p >= NZL else (down if p < 0 else None)

    def factor(p):
        z = inside(p)
        main, tile = jnp.full((NXL, NY), HALF, jnp.float32), edge * HALF
        return rows(main, tile) if z is None else rows(main * z, tile * z)

    def fill(p):
        z = inside(p)
        if z is None:
            return rows(jnp.zeros((NXL, NY), jnp.float32), 1.0 - edge)
        return rows(jnp.full((NXL, NY), 1.0 - z, jnp.float32), 1.0 - edge * z)

    return Grid(ROWS, factor, fill)


def hold_own(grid, fields, xt):
    for comp in ALL:
        for p in range(NZL):
            grid.hold(comp, p, functools.partial(lambda c, q: rows(own(fields, c, q), xt[c, q]), comp, p))


def hold_frames(grid, refs, levels):
    for k, ref in enumerate(refs):
        for p, level in levels[k].items():
            for c in range(3):
                grid.hold(3 * k + c, p, functools.partial(lambda r, a, b: r[a, b], ref, c, p), level)


EARLY = ({1: 1, 2: 2, 3: 2, 4: 1}, {1: 1, 2: 2, 3: 2, 4: 1}, {0: 1, 1: 2, 2: 3, 3: 2, 4: 1})
MIDDLE = ({3: 3, 4: 3, 5: 2, 6: 1}, {3: 3, 4: 3, 5: 2, 6: 1}, {3: 4, 4: 3, 5: 2, 6: 1})


def middle(d, e, h, eps, chi, xt, fd, fe, fh, gd, ge, gh):
    grid = full_grid()
    hold_own(grid, (d, e, h, eps, chi), xt)
    hold_frames(grid, (fd, fe, fh), EARLY)

    def put(c, p, v, n):
        grid.put((gd, ge, gh)[c // 3], (c % 3, p), c, p, v, n)

    grid.sweep(1, (5, 6), (5, 6), put)
    grid.sweep(2, (4, 5), (4, 5), put)
    grid.sweep(3, (3, 4), (3, 4), put)
    grid.sweep(4, (3,), (), put)


def complete(fields, xt, frames, more, above, below, state, staged, media, coming, done):
    grid = full_grid()
    hold_own(grid, fields, xt)
    hold_frames(grid, frames, EARLY)
    hold_frames(grid, more, MIDDLE)
    for side, at, shift in ((above, HI_AT, NZL), (below, LO_AT, -NZL)):
        if side is not None:
            for (comp, p), i in at.items():
                level = int(p == 6)
                if comp >= DP:
                    level = p + 2 if HP <= comp < INV else p + 1
                grid.hold(comp, p + shift, functools.partial(side, i), level)

    def put(c, p, v, n):
        k = c // 3
        if n == STEPS and p >= ADVANCE:
            staged[k][c % 3, p - ADVANCE] = v[:NXL]
        if n < STEPS or k == 2:
            grid.put(state[k], (c % 3, p + 2), c, p, v, n)

    def last_sweep(h_planes, de_planes):
        for p in sorted(set(h_planes) | set(de_planes)):
            if p in h_planes:
                grid.step_h(STEPS, p, range(3), put)
            if p in de_planes:
                if p not in h_planes:
                    for c in range(3):
                        staged[2][c, p - ADVANCE] = grid.get(H + c, p, STEPS)[:NXL]
                grid.step_de(STEPS, p, put)
                for k in range(3):
                    done(k, p - ADVANCE, 1)

    if below is not None:
        grid.sweep(1, (-1,), (-1, 0), put)
        grid.sweep(2, (-1, 0), (0, 1), put)
        grid.sweep(3, (0, 1), (1, 2), put)
        last_sweep((1, 2), (2, 3))
    if above is not None:
        for k, comp in enumerate((EPS, CHI)):
            for o in range(ADVANCE):
                v = grid.get(comp, NZL + o)[:NXL]
                if coming is not None:
                    gz, _, last, _ = position()
                    v = jnp.where(gz == last, coming[k][o], v)
                media[k][o] = v
            done(3 + k, KEPT, ADVANCE)
        grid.sweep(1, (7,), (7, 8), put)
        grid.sweep(2, range(6, 9), range(6, 10), put)
        grid.sweep(3, range(5, 10), range(5, 11), put)
        last_sweep(range(4, 10), range(4, 10))


KEPT = NZL - ADVANCE
LOW, HIGH = (0, 2), (2, 6)


def near(d, e, h, eps, chi, xt, fd, fe, fh, gd, ge, gh, cc, nd, ne, nh, neps, nchi, *state):
    given = (d, e, h, eps, chi), xt, (fd, fe, fh), (gd, ge, gh)
    gz, _, _, _ = position()

    def done(k, o, n):
        pass

    @pl.when(lax.rem(gz, 2) == 0)
    def _():
        complete(*given, lambda i: cc[i], None, state, (nd, ne, nh), (neps, nchi), None, done)

    @pl.when(lax.rem(gz, 2) == 1)
    def _():
        complete(*given, None, lambda i: cc[i], state, (nd, ne, nh), (neps, nchi), None, done)


def far(d, e, h, eps, chi, xt, fd, fe, fh, gd, ge, gh, ca, cb, eps_in, chi_in, nd, ne, nh, neps, nchi, *rest):
    outs, state, staged, media, sems = rest[:5], rest[5:8], rest[8:11], rest[11:13], rest[13]
    given = (d, e, h, eps, chi), xt, (fd, fe, fh), (gd, ge, gh)
    half = halo_row() < XH
    gz, _, _, _ = position()

    def cross(i):
        m = ca[24 * i : 24 * i + 8]
        x = ca[24 * NS + 8 * i : 24 * NS + 8 * i + 8] if i < NR else cb[8 * (NS + i - NR) : 8 * (NS + i - NR) + 8]
        return rows(jnp.where(half, x, m), ca[24 * i + 8 : 24 * i + 24], jnp.where(half, m, x), cb[8 * i : 8 * i + 8])

    def run(above, below, made, new_media):
        copies = []

        def send(source, target):
            copies.append(pltpu.make_async_copy(source, target, sems.at[len(copies)]))
            copies[-1].start()

        def done(k, o, n):
            if k < 3:
                send(staged[k].at[:, pl.ds(o, n)], outs[k].at[:, pl.ds(o, n)])
            else:
                send(media[k - 3], outs[k].at[pl.ds(o, n)])

        o, n = made
        for a, b in zip((nd, ne, nh), outs):
            send(a.at[:, pl.ds(o, n)], b.at[:, pl.ds(o, n)])
        for a, b in zip((eps, chi), outs[3:]):
            send(a.at[pl.ds(ADVANCE, KEPT)], b.at[pl.ds(0, KEPT)])
        for a, b in zip(new_media, outs[3:]):
            send(a, b.at[pl.ds(KEPT, ADVANCE)])
        complete(*given, above, below, state, staged, media, (eps_in, chi_in), done)
        for c in copies:
            c.wait()

    @pl.when(lax.rem(gz, 2) == 0)
    def _():
        run(None, cross, HIGH, (neps, nchi))

    @pl.when(lax.rem(gz, 2) == 1)
    def _():
        run(cross, None, LOW, ())


def swapped(shard, axis, first):
    n = {a: lax.axis_size(a) for a in ("gz", "gx")}
    moves = []
    for z in range(n["gz"]):
        for x in range(n["gx"]):
            at = z if axis == "gz" else x
            to = at + 1 if at % 2 == first else at - 1
            if 0 <= to < n[axis]:
                other = (to, x) if axis == "gz" else (z, to)
            else:
                other = (z ^ 1, x) if axis == "gx" else (z, x ^ 1)
            moves.append((z * n["gx"] + x, other[0] * n["gx"] + other[1]))
    return lax.ppermute(shard, ("gz", "gx"), moves)


def call(body, inputs, out_shape, scratch=(), vmem=8, specs=None, out=VM, aliases=None):
    return pl.pallas_call(
        body,
        out_shape=out_shape,
        in_specs=[VM] * len(inputs) if specs is None else specs,
        out_specs=jax.tree.map(lambda _: out, out_shape),
        input_output_aliases=aliases or {},
        scratch_shapes=list(scratch),
        compiler_params=pltpu.CompilerParams(vmem_limit_bytes=vmem << 20),
    )(*inputs)


def on_device(d_field, e_field, h_field, permittivity, kerr_coeff, classes, eps_table, chi_table):
    field, medium = shape(3, NZL, NXL, NY), shape(NZL, NXL, NY)
    halo = shape(11, NZL, XH, NY)
    *fields, ya, yb = call(
        load,
        [pltpu.with_memory_space_constraint(a, pltpu.HBM) for a in (d_field, e_field, h_field, permittivity, kerr_coeff)],
        (field, field, field, medium, medium, halo, halo),
        [pltpu.SemaphoreType.DMA((11,))],
        specs=[HBM] * 5,
    )
    ra, rb = swapped(ya, "gx", 0), swapped(yb, "gx", 1)
    lo = shape(2, NXL, NY)
    *inside, za = call(inner, fields, (*[shape(3, 5, NXL, NY)] * 3, lo, shape(24 * NS + 8 * NR, NY)))
    ca = swapped(za, "gz", 1)
    (edge,) = call(mark, [], (shape(8, NY),))
    thin = [(3, 5, EDGE, NY)] * 3 + [(2, EDGE, NY)]
    xt, *outside, zb = call(
        edges,
        [*fields, ra, rb, edge],
        (shape(11, NZL, 8, NY), *[shape(*t) for t in thin], shape(8 * (NS + NS - NR), NY)),
    )
    cb = swapped(zb, "gz", 1)
    coming = lookup(classes, eps_table), lookup(classes, chi_table)
    *frames, zc = call(
        merge,
        [*fields, *inside, xt, *outside, edge],
        (*[shape(3, 5, ROWS, NY)] * 3, shape(NS, ROWS, NY)),
        [pltpu.VMEM(t, jnp.float32) for t in thin],
    )
    cc = swapped(zc, "gz", 0)
    more = call(middle, [*fields, xt, *frames], (shape(3, 7, ROWS, NY),) * 3)
    state = [pltpu.VMEM((3, 13, ROWS, NY), jnp.float32)] * 3
    given = [*fields, xt, *frames, *more]
    two = (ADVANCE, NXL, NY)
    made = call(near, [*given, cc], (field, field, field, shape(*two), shape(*two)), state, vmem=16)
    staged = [pltpu.VMEM(field.shape, jnp.float32)] * 3 + [pltpu.VMEM(two, jnp.float32)] * 2
    return call(
        far,
        [*given, ca, cb, *coming, *made],
        (field, field, field, medium, medium),
        [*state, *staged, pltpu.SemaphoreType.DMA((32,))],
        vmem=16,
        out=HBM,
    )


def solution(mesh):
    placed = (
        P(None, "gz", "gx", None),
        P(None, "gz", "gx", None),
        P(None, "gz", "gx", None),
        P("gz", "gx", None),
        P("gz", "gx", None),
        P(None, "gx", None),
        P(),
        P(),
    )
    return jax.shard_map(
        on_device,
        mesh=mesh,
        in_specs=placed,
        out_specs=placed[:5],
        check_vma=False,
    )
```

```python
import functools

import jax
import jax.numpy as jnp
from jax import lax
from jax.experimental import pallas as pl
from jax.experimental.pallas import tpu as pltpu
from jax.sharding import PartitionSpec as P


STEPS = 4
KERR = 3
ADVANCE = 2
HALF = 0.5

D, E, H, EPS, CHI = 0, 3, 6, 9, 10
ALL = range(11)
NZL, NXL, NY = 8, 32, 128
XH = 4
ROWS = NXL + 2 * XH
EDGE = 24

DP, HP, INV = 11, 14, 17
RAW = [(E + c, 0) for c in range(3)] + [(c, p) for p in range(3) for c in (EPS, CHI)]
HI = RAW + [(DP + c, p) for p in range(3) for c in range(3)] + [(HP + c, p) for p in range(2) for c in range(3)]
HI += [(INV, 1), (INV, 2)]
LO = [(c, 7) for c in ALL] + [(H, 6), (H + 1, 6)]
HI_AT = {k: i for i, k in enumerate(HI)}
LO_AT = {k: i for i, k in enumerate(LO)}
NS, NR = len(HI), len(RAW)

FOUR, THREE = (E, E + 1, E + 2, H + 1, H + 2), (D, D + 1, D + 2, H, EPS, CHI)
NF = len(FOUR) * NZL * 4
NHALO = NF + len(THREE) * NZL * 3

VM = pl.BlockSpec(memory_space=pltpu.VMEM)
HBM = pl.BlockSpec(memory_space=pltpu.HBM)
SM = pl.BlockSpec(memory_space=pltpu.SMEM)


def shape(*dims):
    return jax.ShapeDtypeStruct(dims, jnp.float32)


def rows(*parts):
    return jnp.concatenate(parts, axis=0)


def scalar(condition):
    return jnp.where(condition, 1.0, 0.0).astype(jnp.float32)


def position():
    gz, gx = lax.axis_index("gz"), lax.axis_index("gx")
    return gz, gx, lax.axis_size("gz") - 1, lax.axis_size("gx") - 1


def halo_row():
    return lax.broadcasted_iota(jnp.int32, (8, NY), 0)


def inside_x():
    _, gx, _, last = position()
    return jnp.where(halo_row() < XH, scalar(gx != last), scalar(gx != 0))


class Grid:
    def __init__(self, size, factor, fill):
        self.size, self.factor, self.fill = size, factor, fill
        self.where, self.level = {}, {}
        lane = lax.broadcasted_iota(jnp.int32, (size, NY), 1)
        self.last_y, self.first_y = lane == NY - 1, lane == 0

    def hold(self, comp, plane, read, level=0):
        self.where[(comp, plane)] = read
        self.level[(comp, plane)] = level

    def get(self, comp, plane, level=None):
        assert level is None or self.level[(comp, plane)] == level, (comp, plane)
        return self.where[(comp, plane)]()

    def put(self, ref, index, comp, plane, value, level):
        ref[index] = value
        self.hold(comp, plane, lambda: ref[index], level)

    def next_y(self, v):
        return jnp.where(self.last_y, 0.0, pltpu.roll(v, NY - 1, 1))

    def prev_y(self, v):
        return jnp.where(self.first_y, 0.0, pltpu.roll(v, 1, 1))

    def next_x(self, v):
        return pltpu.roll(v, self.size - 1, 0)

    def prev_x(self, v):
        return pltpu.roll(v, 1, 0)

    def step_h(self, n, p, comps, put):
        f = self.factor(p)
        ex, ey, ez = (self.get(E + c, p, n - 1) for c in range(3))
        if self.level.get((HP, p)) == n:
            hx, hy, hz = (self.get(HP + c, p) for c in range(3))
            put(H, p, hx - f * ((self.next_y(ez) - ez) + ey), n)
            put(H + 1, p, hy + f * (ex + (self.next_x(ez) - ez)), n)
            put(H + 2, p, hz - f * ((self.next_x(ey) - ey) - (self.next_y(ex) - ex)), n)
            return
        new = {}
        if 0 in comps:
            eyn = self.get(E + 1, p + 1, n - 1)
            new[0] = (self.next_y(ez) - ez) - (eyn - ey)
        if 1 in comps:
            exn = self.get(E, p + 1, n - 1)
            new[1] = (exn - ex) - (self.next_x(ez) - ez)
        if 2 in comps:
            new[2] = (self.next_x(ey) - ey) - (self.next_y(ex) - ex)
        for c, curl in new.items():
            put(H + c, p, self.get(H + c, p, n - 1) - f * curl, n)

    def medium(self, p):
        eps, fill = self.get(EPS, p), self.fill(p)
        return eps if fill is None else eps + fill, self.get(CHI, p)

    def first_inverse(self, n, p):
        ex, ey, ez = (self.get(E + c, p, n) for c in range(3))
        eps, chi = self.medium(p)
        return 1.0 / (eps + chi * (ex * ex + ey * ey + ez * ez))

    def derive(self):
        out = {}
        for p in range(3):
            f, n = self.factor(p), p + 1
            hx, hy, hz = (self.get(H + c, p, n) for c in range(3))
            dx, dy, dz = (self.get(D + c, p, n - 1) for c in range(3))
            out[(DP, p)] = dx + f * ((hz - self.prev_y(hz)) - hy)
            out[(DP + 1, p)] = dy + f * (hx - (hz - self.prev_x(hz)))
            out[(DP + 2, p)] = dz + f * ((hy - self.prev_x(hy)) - (hx - self.prev_y(hx)))
            if p < 2:
                out[(HP, p)] = hx + f * self.get(E + 1, p + 1, n)
                out[(HP + 1, p)] = hy - f * self.get(E, p + 1, n)
                out[(HP + 2, p)] = hz
            if p > 0:
                out[(INV, p)] = self.first_inverse(n - 1, p)
        return out

    def step_de(self, n, p, put):
        f = self.factor(p)
        hxp, hyp = (self.get(H + c, p - 1, n) for c in range(2))
        if self.level.get((DP, p)) == n:
            dx, dy, dz = (self.get(DP + c, p) for c in range(3))
            dx, dy = dx + f * hyp, dy - f * hxp
        else:
            hx, hy, hz = (self.get(H + c, p, n) for c in range(3))
            dx = self.get(D, p, n - 1) + f * ((hz - self.prev_y(hz)) - (hy - hyp))
            dy = self.get(D + 1, p, n - 1) + f * ((hx - hxp) - (hz - self.prev_x(hz)))
            dz = self.get(D + 2, p, n - 1) + f * ((hy - self.prev_x(hy)) - (hx - self.prev_y(hx)))
        eps, chi = self.medium(p)
        inverse = self.get(INV, p) if self.level.get((INV, p)) == n else self.first_inverse(n - 1, p)
        if n == STEPS:
            dx, dy, dz, eps, chi, inverse = (v[:NXL] for v in (dx, dy, dz, eps, chi, inverse))
        squares = chi * (dx * dx + dy * dy + dz * dz)
        for _ in range(KERR - 1):
            inverse = 1.0 / (eps + squares * (inverse * inverse))
        for c, v in enumerate((dx, dy, dz)):
            put(D + c, p, v, n)
            put(E + c, p, v * inverse, n)

    def sweep(self, n, h_planes, de_planes, put):
        for p in range(-2, 11):
            if p in h_planes:
                self.step_h(n, p, range(3), put)
            if p in de_planes:
                self.step_de(n, p, put)


def own(fields, comp, plane):
    d, e, h, eps, chi = fields
    if comp < E:
        return d[comp, plane]
    if comp < H:
        return e[comp - E, plane]
    if comp < EPS:
        return h[comp - H, plane]
    return eps[plane] if comp == EPS else chi[plane]


def halo_slot(comp, p):
    if comp in FOUR:
        return (FOUR.index(comp) * NZL + p) * 4, 4
    return NF + (THREE.index(comp) * NZL + p) * 3, 3


def load(d, e, h, eps, chi, ya, yb, held, sems):
    parts = [r.at[c] for r in (d, e, h) for c in range(3)] + [eps, chi]
    copies = [
        [
            pltpu.make_async_copy(r.at[:, pl.ds(at, 8)], held.at[comp, :, pl.ds(k * 8, 8)], sems.at[comp, k])
            for k, at in enumerate((0, NXL - 8))
        ]
        for comp, r in enumerate(parts)
    ]
    for pair in copies:
        for c in pair:
            c.start()
    _, gx, _, last = position()
    even = lax.rem(gx, 2) == 0
    keep = scalar(jnp.logical_and(gx != 0, gx != last))
    for comp in ALL:
        for c in copies[comp]:
            c.wait()
        for p in range(NZL):
            at, n = halo_slot(comp, p)
            low, high = held[comp, p, 0:n], held[comp, p, 16 - n : 16]
            ya[at : at + n] = jnp.where(even, high, low)
            yb[at : at + n] = jnp.where(even, low, high) * keep


def mark(out):
    out[...] = inside_x()


def early(grid, put):
    grid.sweep(1, range(0, 5), range(1, 5), put)
    grid.sweep(2, range(1, 4), range(2, 4), put)
    grid.sweep(3, range(2, 3), (), put)


def lookup(classes, table):
    labels = jnp.arange(table.shape[0], dtype=jnp.int32).reshape(-1, 1, 1, 1)
    picked = jnp.where(classes[None] == labels, table.reshape(-1, 1, 1, 1), jnp.float32(0.0))
    return jnp.sum(picked, axis=0)


def payload(grid, side):
    made = grid.derive() if side is HI else {}
    return [made[k] if k in made else grid.get(*k) for k in side]


def inner(d, e, h, eps, chi, fd, fe, fh, lo, out):
    fields = (d, e, h, eps, chi)
    grid = Grid(NXL, lambda p: HALF, lambda p: None)
    for comp in ALL:
        for p in range(NZL):
            grid.hold(comp, p, functools.partial(own, fields, comp, p))
    grid.step_h(1, 6, range(2), lambda c, p, v, n: grid.put(lo, c - H, c, p, v, n))

    def put(c, p, v, n):
        ref = (fd, fe, fh)[c // 3]
        grid.put(ref, (c % 3, p), c, p, v, n)

    early(grid, put)
    gz, _, last, _ = position()
    first_core = lax.rem(gz, 2) == 0
    keep = scalar(jnp.logical_and(gz != 0, gz != last))
    half = halo_row() < XH
    low = payload(grid, LO)
    for i, v in enumerate(payload(grid, HI)):
        if i < len(LO):
            v = jnp.where(first_core, v, low[i])
        v = v * keep
        out[24 * i : 24 * i + 8] = jnp.where(half, v[24:32], v[0:8])
        out[24 * i + 8 : 24 * i + 24] = v[8:24]
        if i < NR:
            out[24 * NS + 8 * i : 24 * NS + 8 * i + 8] = jnp.where(half, v[0:8], v[24:32])


def edge_grid(inside, fields, tile):
    f = rows(jnp.full((8, NY), HALF), inside * HALF, jnp.full((8, NY), HALF))
    none = jnp.zeros((8, NY), jnp.float32)
    fill = rows(none, 1.0 - inside, none)
    grid = Grid(EDGE, lambda p: f, lambda p: fill)

    def read(comp, p):
        v = own(fields, comp, p)
        return rows(v[24:32], tile(comp, p), v[0:8])

    for comp in ALL:
        for p in range(NZL):
            grid.hold(comp, p, functools.partial(read, comp, p))
    return grid


def joined(a, b, comp, p):
    _, gx, _, _ = position()
    even = lax.rem(gx, 2) == 0
    at, n = halo_slot(comp, p)
    a, b = a[at : at + n], b[at : at + n]
    above, below = jnp.where(even, a, b), jnp.where(even, b, a)
    if n == 4:
        return rows(above, below)
    return rows(above, above[2:3], below[0:1], below)


def edges(d, e, h, eps, chi, ra, rb, inside, xt, sd, se, sh, slo, cross):
    fields = (d, e, h, eps, chi)
    gz, _, last, _ = position()
    keep = scalar(jnp.logical_and(gz != 0, gz != last))
    half = halo_row() < XH
    for comp in ALL:
        for p in range(NZL):
            xt[comp, p] = joined(ra, rb, comp, p)

    def pack(grid, side):
        for i, v in enumerate(payload(grid, side)):
            v = v * keep
            cross[8 * i : 8 * i + 8] = v[8:16]
            if i >= NR:
                at = 8 * (NS + i - NR)
                cross[at : at + 8] = jnp.where(half, v[16:24], v[0:8])

    @pl.when(lax.rem(gz, 2) == 0)
    def _():
        grid = edge_grid(inside[...], fields, lambda comp, p: xt[comp, p])
        early(grid, lambda c, p, v, n: grid.put((sd, se, sh)[c // 3], (c % 3, p), c, p, v, n))
        pack(grid, HI)

    @pl.when(lax.rem(gz, 2) == 1)
    def _():
        grid = edge_grid(inside[...], fields, lambda comp, p: xt[comp, p])
        grid.step_h(1, 6, range(2), lambda c, p, v, n: grid.put(slo, c - H, c, p, v, n))
        pack(grid, LO)


def merge(d, e, h, eps, chi, id_, ie, ih, ilo, xt, sd, se, sh, slo, inside, fd, fe, fh, chip, td, te, th, tlo):
    fields = (d, e, h, eps, chi)
    half = halo_row() < XH

    def merged(v, w):
        return rows(jnp.where(half, w[16:24], v[0:8]), v[8:24], jnp.where(half, v[24:32], w[0:8]), w[8:16])

    def join(sides, side):
        grid = full_grid()
        hold_own(grid, fields, xt)
        for k, (v, w, ref) in enumerate(((id_, sides[0], fd), (ie, sides[1], fe), (ih, sides[2], fh))):
            for p, level in EARLY[k].items():
                for c in range(3):
                    grid.put(ref, (c, p), 3 * k + c, p, merged(v[c, p], w[c, p]), level)
        for c in range(2):
            grid.hold(H + c, 6, functools.partial(lambda a: merged(ilo[a], tlo[a]), c))
        for i, v in enumerate(payload(grid, side)):
            chip[i] = v

    gz, _, _, _ = position()

    @pl.when(lax.rem(gz, 2) == 0)
    def _():
        grid = edge_grid(inside[...], fields, lambda comp, p: xt[comp, p])
        grid.step_h(1, 6, range(2), lambda c, p, v, n: grid.put(tlo, c - H, c, p, v, n))
        join((sd, se, sh), LO)

    @pl.when(lax.rem(gz, 2) == 1)
    def _():
        grid = edge_grid(inside[...], fields, lambda comp, p: xt[comp, p])
        early(grid, lambda c, p, v, n: grid.put((td, te, th)[c // 3], (c % 3, p), c, p, v, n))
        join((td, te, th), HI)


def full_grid():
    gz, _, last, _ = position()
    up, down = scalar(gz != last), scalar(gz != 0)
    edge = inside_x()

    def inside(p):
        return up if p >= NZL else (down if p < 0 else None)

    def factor(p):
        z = inside(p)
        main, tile = jnp.full((NXL, NY), HALF, jnp.float32), edge * HALF
        return rows(main, tile) if z is None else rows(main * z, tile * z)

    def fill(p):
        z = inside(p)
        if z is None:
            return rows(jnp.zeros((NXL, NY), jnp.float32), 1.0 - edge)
        return rows(jnp.full((NXL, NY), 1.0 - z, jnp.float32), 1.0 - edge * z)

    return Grid(ROWS, factor, fill)


def hold_own(grid, fields, xt):
    for comp in ALL:
        for p in range(NZL):
            grid.hold(comp, p, functools.partial(lambda c, q: rows(own(fields, c, q), xt[c, q]), comp, p))


def hold_frames(grid, refs, levels):
    for k, ref in enumerate(refs):
        for p, level in levels[k].items():
            for c in range(3):
                grid.hold(3 * k + c, p, functools.partial(lambda r, a, b: r[a, b], ref, c, p), level)


EARLY = ({1: 1, 2: 2, 3: 2, 4: 1}, {1: 1, 2: 2, 3: 2, 4: 1}, {0: 1, 1: 2, 2: 3, 3: 2, 4: 1})
MIDDLE = ({3: 3, 4: 3, 5: 2, 6: 1}, {3: 3, 4: 3, 5: 2, 6: 1}, {3: 4, 4: 3, 5: 2, 6: 1})


def middle(d, e, h, eps, chi, xt, fd, fe, fh, gd, ge, gh):
    grid = full_grid()
    hold_own(grid, (d, e, h, eps, chi), xt)
    hold_frames(grid, (fd, fe, fh), EARLY)

    def put(c, p, v, n):
        grid.put((gd, ge, gh)[c // 3], (c % 3, p), c, p, v, n)

    grid.sweep(1, (5, 6), (5, 6), put)
    grid.sweep(2, (4, 5), (4, 5), put)
    grid.sweep(3, (3, 4), (3, 4), put)
    grid.sweep(4, (3,), (), put)


def complete(fields, xt, frames, more, above, below, state, staged, media, coming, done):
    grid = full_grid()
    hold_own(grid, fields, xt)
    hold_frames(grid, frames, EARLY)
    hold_frames(grid, more, MIDDLE)
    for side, at, shift in ((above, HI_AT, NZL), (below, LO_AT, -NZL)):
        if side is not None:
            for (comp, p), i in at.items():
                level = int(p == 6)
                if comp >= DP:
                    level = p + 2 if HP <= comp < INV else p + 1
                grid.hold(comp, p + shift, functools.partial(side, i), level)

    def put(c, p, v, n):
        k = c // 3
        if n == STEPS and p >= ADVANCE:
            staged[k][c % 3, p - ADVANCE] = v[:NXL]
        if n < STEPS or k == 2:
            grid.put(state[k], (c % 3, p + 2), c, p, v, n)

    def last_sweep(h_planes, de_planes):
        for p in sorted(set(h_planes) | set(de_planes)):
            if p in h_planes:
                grid.step_h(STEPS, p, range(3), put)
            if p in de_planes:
                if p not in h_planes:
                    for c in range(3):
                        staged[2][c, p - ADVANCE] = grid.get(H + c, p, STEPS)[:NXL]
                grid.step_de(STEPS, p, put)
                for k in range(3):
                    done(k, p - ADVANCE, 1)

    if below is not None:
        grid.sweep(1, (-1,), (-1, 0), put)
        grid.sweep(2, (-1, 0), (0, 1), put)
        grid.sweep(3, (0, 1), (1, 2), put)
        last_sweep((1, 2), (2, 3))
    if above is not None:
        for k, comp in enumerate((EPS, CHI)):
            for o in range(ADVANCE):
                v = grid.get(comp, NZL + o)[:NXL]
                if coming is not None:
                    gz, _, last, _ = position()
                    v = jnp.where(gz == last, coming[k][o], v)
                media[k][o] = v
            done(3 + k, KEPT, ADVANCE)
        grid.sweep(1, (7,), (7, 8), put)
        grid.sweep(2, range(6, 9), range(6, 10), put)
        grid.sweep(3, range(5, 10), range(5, 11), put)
        last_sweep(range(4, 10), range(4, 10))


KEPT = NZL - ADVANCE


def run(given, above, below, coming, outs, scratch, also=()):
    state, staged, media, sems = scratch[:3], scratch[3:6], scratch[6:8], scratch[8]
    copies = []

    def send(source, target):
        copies.append(pltpu.make_async_copy(source, target, sems.at[len(copies)]))
        copies[-1].start()

    def done(k, o, n):
        if k < 3:
            send(staged[k].at[:, pl.ds(o, n)], outs[k].at[:, pl.ds(o, n)])
        else:
            send(media[k - 3], outs[k].at[pl.ds(o, n)])

    for a, b in also:
        send(a, b)
    complete(*given, above, below, state, staged, media, coming, done)
    for c in copies:
        c.wait()


def near(d, e, h, eps, chi, xt, fd, fe, fh, gd, ge, gh, cc, *rest):
    given = (d, e, h, eps, chi), xt, (fd, fe, fh), (gd, ge, gh)
    outs, scratch = rest[:5], rest[5:]
    also = [(a.at[pl.ds(ADVANCE, KEPT)], b.at[pl.ds(0, KEPT)]) for a, b in ((eps, outs[3]), (chi, outs[4]))]
    gz, _, _, _ = position()

    @pl.when(lax.rem(gz, 2) == 0)
    def _():
        run(given, lambda i: cc[i], None, None, outs, scratch, also)

    @pl.when(lax.rem(gz, 2) == 1)
    def _():
        run(given, None, lambda i: cc[i], None, outs, scratch, also)


def far(d, e, h, eps, chi, xt, fd, fe, fh, gd, ge, gh, ca, cb, eps_in, chi_in, *rest):
    given = (d, e, h, eps, chi), xt, (fd, fe, fh), (gd, ge, gh)
    outs, scratch = rest[5:10], rest[10:]
    half = halo_row() < XH
    gz, _, _, _ = position()

    def cross(i):
        m = ca[24 * i : 24 * i + 8]
        x = ca[24 * NS + 8 * i : 24 * NS + 8 * i + 8] if i < NR else cb[8 * (NS + i - NR) : 8 * (NS + i - NR) + 8]
        return rows(jnp.where(half, x, m), ca[24 * i + 8 : 24 * i + 24], jnp.where(half, m, x), cb[8 * i : 8 * i + 8])

    @pl.when(lax.rem(gz, 2) == 0)
    def _():
        run(given, None, cross, None, outs, scratch)

    @pl.when(lax.rem(gz, 2) == 1)
    def _():
        run(given, cross, None, (eps_in, chi_in), outs, scratch)


def swapped(shard, axis, first):
    n = {a: lax.axis_size(a) for a in ("gz", "gx")}
    moves = []
    for z in range(n["gz"]):
        for x in range(n["gx"]):
            at = z if axis == "gz" else x
            to = at + 1 if at % 2 == first else at - 1
            if 0 <= to < n[axis]:
                other = (to, x) if axis == "gz" else (z, to)
            else:
                other = (z ^ 1, x) if axis == "gx" else (z, x ^ 1)
            moves.append((z * n["gx"] + x, other[0] * n["gx"] + other[1]))
    return lax.ppermute(shard, ("gz", "gx"), moves)


def call(body, inputs, out_shape, scratch=(), vmem=8, specs=None, out=VM, aliases=None):
    return pl.pallas_call(
        body,
        out_shape=out_shape,
        in_specs=[VM] * len(inputs) if specs is None else specs,
        out_specs=jax.tree.map(lambda _: out, out_shape),
        input_output_aliases=aliases or {},
        scratch_shapes=list(scratch),
        compiler_params=pltpu.CompilerParams(vmem_limit_bytes=vmem << 20),
    )(*inputs)


def on_device(d_field, e_field, h_field, permittivity, kerr_coeff, classes, eps_table, chi_table):
    field, medium = shape(3, NZL, NXL, NY), shape(NZL, NXL, NY)
    fields = [d_field, e_field, h_field, permittivity, kerr_coeff]
    halo = shape(NHALO, NY)
    ya, yb = call(
        load,
        [pltpu.with_memory_space_constraint(a, pltpu.HBM) for a in fields],
        (halo, halo),
        [pltpu.VMEM((11, NZL, 16, NY), jnp.float32), pltpu.SemaphoreType.DMA((11, 2))],
        specs=[HBM] * 5,
    )
    ra, rb = swapped(ya, "gx", 0), swapped(yb, "gx", 1)
    lo = shape(2, NXL, NY)
    *inside, za = call(inner, fields, (*[shape(3, 5, NXL, NY)] * 3, lo, shape(24 * NS + 8 * NR, NY)))
    ca = swapped(za, "gz", 1)
    (edge,) = call(mark, [], (shape(8, NY),))
    thin = [(3, 5, EDGE, NY)] * 3 + [(2, EDGE, NY)]
    xt, *outside, zb = call(
        edges,
        [*fields, ra, rb, edge],
        (shape(11, NZL, 8, NY), *[shape(*t) for t in thin], shape(8 * (NS + NS - NR), NY)),
    )
    cb = swapped(zb, "gz", 1)
    coming = lookup(classes, eps_table), lookup(classes, chi_table)
    *frames, zc = call(
        merge,
        [*fields, *inside, xt, *outside, edge],
        (*[shape(3, 5, ROWS, NY)] * 3, shape(NS, ROWS, NY)),
        [pltpu.VMEM(t, jnp.float32) for t in thin],
    )
    cc = swapped(zc, "gz", 0)
    more = call(middle, [*fields, xt, *frames], (shape(3, 7, ROWS, NY),) * 3)
    state = [pltpu.VMEM((3, 13, ROWS, NY), jnp.float32)] * 3
    given = [*fields, xt, *frames, *more]
    two = (ADVANCE, NXL, NY)
    results = (field, field, field, medium, medium)
    scratch = state + [pltpu.VMEM(field.shape, jnp.float32)] * 3 + [pltpu.VMEM(two, jnp.float32)] * 2
    scratch += [pltpu.SemaphoreType.DMA((32,))]
    outs = call(near, [*given, cc], results, scratch, vmem=16, out=HBM)
    given += [ca, cb, *coming]
    n = len(given)
    return call(
        far,
        [*given, *outs],
        results,
        scratch,
        vmem=16,
        specs=[VM] * n + [HBM] * 5,
        out=HBM,
        aliases={n + k: k for k in range(5)},
    )


def solution(mesh):
    placed = (
        P(None, "gz", "gx", None),
        P(None, "gz", "gx", None),
        P(None, "gz", "gx", None),
        P("gz", "gx", None),
        P("gz", "gx", None),
        P(None, "gx", None),
        P(),
        P(),
    )
    return jax.shard_map(
        on_device,
        mesh=mesh,
        in_specs=placed,
        out_specs=placed[:5],
        check_vma=False,
    )
```

```python
import functools

import jax
import jax.numpy as jnp
from jax import lax
from jax.experimental import pallas as pl
from jax.experimental.pallas import tpu as pltpu
from jax.sharding import PartitionSpec as P


STEPS = 4
KERR = 3
ADVANCE = 2
HALF = 0.5

D, E, H, EPS, CHI = 0, 3, 6, 9, 10
ALL = range(11)
NZL, NXL, NY = 8, 32, 128
XH = 4
ROWS = NXL + 2 * XH
EDGE = 24

DP, HP, INV = 11, 14, 17
RAW = [(E + c, 0) for c in range(3)] + [(c, p) for p in range(3) for c in (EPS, CHI)]
HI = RAW + [(DP + c, p) for p in range(3) for c in range(3)] + [(HP + c, p) for p in range(2) for c in range(3)]
HI += [(INV, 1), (INV, 2)]
HI_ROWS = {8: range(8), 6: (0, 1, 2, 5, 6, 7), 4: (0, 1, 6, 7), 2: (0, 7)}
LO_ROWS = {8: range(8), 6: (0, 1, 2, 3, 6, 7), 4: (0, 1, 2, 7), 2: ()}


def slot_rows(comp, p):
    if (comp, p) == (E, 0):
        return 8
    level = p + (HP <= comp < INV)
    return 6 - 2 * p if comp < HP or comp >= INV else 6 - 2 * (level - 1)


WIDTH = [slot_rows(*k) for k in HI]
HALO_AT = [sum(WIDTH[:i]) for i in range(len(HI))]
LO = [None] * len(HI)
_wide = [i for i, n in enumerate(WIDTH) if n >= 6]
_thin = [i for i, n in enumerate(WIDTH) if n == 4]
for _k in [(E + c, 7) for c in range(3)] + [(H + c, 7) for c in range(3)]:
    LO[_wide.pop(0)] = _k
for _k in [(D + c, 7) for c in range(3)] + [(EPS, 7), (CHI, 7), (H, 6), (H + 1, 6)]:
    LO[_thin.pop(0)] = _k
HI_AT = {k: i for i, k in enumerate(HI)}
LO_AT = {k: i for i, k in enumerate(LO) if k}
NS, NR = len(HI), len(RAW)
NEW_AT = -(-sum(WIDTH) // 8) * 8
LATE = NEW_AT + 8 * (NS - NR)

FOUR, THREE = (E, E + 1, E + 2, H + 1, H + 2), (D, D + 1, D + 2, H, EPS, CHI)
NF = len(FOUR) * NZL * 4
NHALO = NF + len(THREE) * NZL * 3

VM = pl.BlockSpec(memory_space=pltpu.VMEM)
HBM = pl.BlockSpec(memory_space=pltpu.HBM)
SM = pl.BlockSpec(memory_space=pltpu.SMEM)


def shape(*dims):
    return jax.ShapeDtypeStruct(dims, jnp.float32)


def rows(*parts):
    return jnp.concatenate(parts, axis=0)


def scalar(condition):
    return jnp.where(condition, 1.0, 0.0).astype(jnp.float32)


def position():
    gz, gx = lax.axis_index("gz"), lax.axis_index("gx")
    return gz, gx, lax.axis_size("gz") - 1, lax.axis_size("gx") - 1


def halo_row():
    return lax.broadcasted_iota(jnp.int32, (8, NY), 0)


def inside_x():
    _, gx, _, last = position()
    return jnp.where(halo_row() < XH, scalar(gx != last), scalar(gx != 0))


class Grid:
    def __init__(self, size, factor, fill):
        self.size, self.factor, self.fill = size, factor, fill
        self.where, self.level = {}, {}
        lane = lax.broadcasted_iota(jnp.int32, (size, NY), 1)
        self.last_y, self.first_y = lane == NY - 1, lane == 0

    def hold(self, comp, plane, read, level=0):
        self.where[(comp, plane)] = read
        self.level[(comp, plane)] = level

    def get(self, comp, plane, level=None):
        assert level is None or self.level[(comp, plane)] == level, (comp, plane)
        return self.where[(comp, plane)]()

    def put(self, ref, index, comp, plane, value, level):
        ref[index] = value
        self.hold(comp, plane, lambda: ref[index], level)

    def next_y(self, v):
        return jnp.where(self.last_y, 0.0, pltpu.roll(v, NY - 1, 1))

    def prev_y(self, v):
        return jnp.where(self.first_y, 0.0, pltpu.roll(v, 1, 1))

    def next_x(self, v):
        return pltpu.roll(v, self.size - 1, 0)

    def prev_x(self, v):
        return pltpu.roll(v, 1, 0)

    def step_h(self, n, p, comps, put):
        f = self.factor(p)
        ex, ey, ez = (self.get(E + c, p, n - 1) for c in range(3))
        if self.level.get((HP, p)) == n:
            hx, hy, hz = (self.get(HP + c, p) for c in range(3))
            put(H, p, hx - f * ((self.next_y(ez) - ez) + ey), n)
            put(H + 1, p, hy + f * (ex + (self.next_x(ez) - ez)), n)
            put(H + 2, p, hz - f * ((self.next_x(ey) - ey) - (self.next_y(ex) - ex)), n)
            return
        new = {}
        if 0 in comps:
            eyn = self.get(E + 1, p + 1, n - 1)
            new[0] = (self.next_y(ez) - ez) - (eyn - ey)
        if 1 in comps:
            exn = self.get(E, p + 1, n - 1)
            new[1] = (exn - ex) - (self.next_x(ez) - ez)
        if 2 in comps:
            new[2] = (self.next_x(ey) - ey) - (self.next_y(ex) - ex)
        for c, curl in new.items():
            put(H + c, p, self.get(H + c, p, n - 1) - f * curl, n)

    def medium(self, p):
        eps, fill = self.get(EPS, p), self.fill(p)
        return eps if fill is None else eps + fill, self.get(CHI, p)

    def first_inverse(self, n, p):
        ex, ey, ez = (self.get(E + c, p, n) for c in range(3))
        eps, chi = self.medium(p)
        return 1.0 / (eps + chi * (ex * ex + ey * ey + ez * ez))

    def derive(self):
        out = {}
        for p in range(3):
            f, n = self.factor(p), p + 1
            hx, hy, hz = (self.get(H + c, p, n) for c in range(3))
            dx, dy, dz = (self.get(D + c, p, n - 1) for c in range(3))
            out[(DP, p)] = dx + f * ((hz - self.prev_y(hz)) - hy)
            out[(DP + 1, p)] = dy + f * (hx - (hz - self.prev_x(hz)))
            out[(DP + 2, p)] = dz + f * ((hy - self.prev_x(hy)) - (hx - self.prev_y(hx)))
            if p < 2:
                out[(HP, p)] = hx + f * self.get(E + 1, p + 1, n)
                out[(HP + 1, p)] = hy - f * self.get(E, p + 1, n)
                out[(HP + 2, p)] = hz
            if p > 0:
                out[(INV, p)] = self.first_inverse(n - 1, p)
        return out

    def step_de(self, n, p, put):
        f = self.factor(p)
        hxp, hyp = (self.get(H + c, p - 1, n) for c in range(2))
        if self.level.get((DP, p)) == n:
            dx, dy, dz = (self.get(DP + c, p) for c in range(3))
            dx, dy = dx + f * hyp, dy - f * hxp
        else:
            hx, hy, hz = (self.get(H + c, p, n) for c in range(3))
            dx = self.get(D, p, n - 1) + f * ((hz - self.prev_y(hz)) - (hy - hyp))
            dy = self.get(D + 1, p, n - 1) + f * ((hx - hxp) - (hz - self.prev_x(hz)))
            dz = self.get(D + 2, p, n - 1) + f * ((hy - self.prev_x(hy)) - (hx - self.prev_y(hx)))
        eps, chi = self.medium(p)
        inverse = self.get(INV, p) if self.level.get((INV, p)) == n else self.first_inverse(n - 1, p)
        if n == STEPS:
            dx, dy, dz, eps, chi, inverse = (v[:NXL] for v in (dx, dy, dz, eps, chi, inverse))
        squares = chi * (dx * dx + dy * dy + dz * dz)
        for _ in range(KERR - 1):
            inverse = 1.0 / (eps + squares * (inverse * inverse))
        for c, v in enumerate((dx, dy, dz)):
            put(D + c, p, v, n)
            put(E + c, p, v * inverse, n)

    def sweep(self, n, h_planes, de_planes, put):
        for p in range(-2, 11):
            if p in h_planes:
                self.step_h(n, p, range(3), put)
            if p in de_planes:
                self.step_de(n, p, put)


def own(fields, comp, plane):
    d, e, h, eps, chi = fields
    if comp < E:
        return d[comp, plane]
    if comp < H:
        return e[comp - E, plane]
    if comp < EPS:
        return h[comp - H, plane]
    return eps[plane] if comp == EPS else chi[plane]


def halo_slot(comp, p):
    if comp in FOUR:
        return (FOUR.index(comp) * NZL + p) * 4, 4
    return NF + (THREE.index(comp) * NZL + p) * 3, 3


def load(d, e, h, eps, chi, ya, yb, held, sems):
    parts = [r.at[c] for r in (d, e, h) for c in range(3)] + [eps, chi]
    copies = [
        [
            pltpu.make_async_copy(r.at[:, pl.ds(at, 8)], held.at[comp, :, pl.ds(k * 8, 8)], sems.at[comp, k])
            for k, at in enumerate((0, NXL - 8))
        ]
        for comp, r in enumerate(parts)
    ]
    for pair in copies:
        for c in pair:
            c.start()
    _, gx, _, last = position()
    even = lax.rem(gx, 2) == 0
    keep = scalar(jnp.logical_and(gx != 0, gx != last))
    for comp in ALL:
        for c in copies[comp]:
            c.wait()
        for p in range(NZL):
            at, n = halo_slot(comp, p)
            low, high = held[comp, p, 0:n], held[comp, p, 16 - n : 16]
            ya[at : at + n] = jnp.where(even, high, low)
            yb[at : at + n] = jnp.where(even, low, high) * keep


def mark(out):
    out[...] = inside_x()


def early(grid, put):
    grid.sweep(1, range(0, 5), range(1, 5), put)
    grid.sweep(2, range(1, 4), range(2, 4), put)
    grid.sweep(3, range(2, 3), (), put)


def lookup(classes, table):
    labels = jnp.arange(table.shape[0], dtype=jnp.int32).reshape(-1, 1, 1, 1)
    picked = jnp.where(classes[None] == labels, table.reshape(-1, 1, 1, 1), jnp.float32(0.0))
    return jnp.sum(picked, axis=0)


def payload(grid, side):
    made = grid.derive() if side is HI else {}
    return [k and (made[k] if k in made else grid.get(*k)) for k in side]


def inner(d, e, h, eps, chi, fd, fe, fh, lo, out):
    fields = (d, e, h, eps, chi)
    grid = Grid(NXL, lambda p: HALF, lambda p: None)
    for comp in ALL:
        for p in range(NZL):
            grid.hold(comp, p, functools.partial(own, fields, comp, p))
    grid.step_h(1, 6, range(2), lambda c, p, v, n: grid.put(lo, c - H, c, p, v, n))

    def put(c, p, v, n):
        ref = (fd, fe, fh)[c // 3]
        grid.put(ref, (c % 3, p), c, p, v, n)

    early(grid, put)
    gz, _, last, _ = position()
    first_core = lax.rem(gz, 2) == 0
    keep = scalar(jnp.logical_and(gz != 0, gz != last))
    half = halo_row() < XH
    low = payload(grid, LO)
    for i, v in enumerate(payload(grid, HI)):
        if low[i] is not None:
            v = jnp.where(first_core, v, low[i])
        v = v * keep
        out[24 * i : 24 * i + 8] = jnp.where(half, v[24:32], v[0:8])
        out[24 * i + 8 : 24 * i + 24] = v[8:24]
        if i < NR:
            out[24 * NS + 8 * i : 24 * NS + 8 * i + 8] = jnp.where(half, v[0:8], v[24:32])


def edge_grid(inside, fields, tile):
    f = rows(jnp.full((8, NY), HALF), inside * HALF, jnp.full((8, NY), HALF))
    none = jnp.zeros((8, NY), jnp.float32)
    fill = rows(none, 1.0 - inside, none)
    grid = Grid(EDGE, lambda p: f, lambda p: fill)

    def read(comp, p):
        v = own(fields, comp, p)
        return rows(v[24:32], tile(comp, p), v[0:8])

    for comp in ALL:
        for p in range(NZL):
            grid.hold(comp, p, functools.partial(read, comp, p))
    return grid


def joined(a, b, comp, p):
    _, gx, _, _ = position()
    even = lax.rem(gx, 2) == 0
    at, n = halo_slot(comp, p)
    a, b = a[at : at + n], b[at : at + n]
    above, below = jnp.where(even, a, b), jnp.where(even, b, a)
    if n == 4:
        return rows(above, below)
    return rows(above, above[2:3], below[0:1], below)


def edges(d, e, h, eps, chi, ra, rb, inside, xt, sd, se, sh, slo, cross):
    fields = (d, e, h, eps, chi)
    gz, _, last, _ = position()
    keep = scalar(jnp.logical_and(gz != 0, gz != last))
    half = halo_row() < XH
    for comp in ALL:
        for p in range(NZL):
            xt[comp, p] = joined(ra, rb, comp, p)

    def pack(grid, side, chosen):
        for i, v in enumerate(payload(grid, side)):
            if v is None:
                continue
            v = v * keep
            at, n = HALO_AT[i], WIDTH[i]
            runs = []
            for r in chosen[n]:
                if runs and runs[-1][1] == r:
                    runs[-1][1] = r + 1
                else:
                    runs.append([r, r + 1])
            for a, b in runs:
                cross[at : at + b - a] = v[8 + a : 8 + b]
                at += b - a
            if i >= NR:
                at = NEW_AT + 8 * (i - NR)
                cross[at : at + 8] = jnp.where(half, v[16:24], v[0:8])

    @pl.when(lax.rem(gz, 2) == 0)
    def _():
        grid = edge_grid(inside[...], fields, lambda comp, p: xt[comp, p])
        early(grid, lambda c, p, v, n: grid.put((sd, se, sh)[c // 3], (c % 3, p), c, p, v, n))
        pack(grid, HI, HI_ROWS)

    @pl.when(lax.rem(gz, 2) == 1)
    def _():
        grid = edge_grid(inside[...], fields, lambda comp, p: xt[comp, p])
        grid.step_h(1, 6, range(2), lambda c, p, v, n: grid.put(slo, c - H, c, p, v, n))
        pack(grid, LO, LO_ROWS)


def merge(d, e, h, eps, chi, id_, ie, ih, ilo, xt, sd, se, sh, slo, inside, fd, fe, fh, chip, td, te, th, tlo):
    fields = (d, e, h, eps, chi)
    half = halo_row() < XH

    def merged(v, w):
        return rows(jnp.where(half, w[16:24], v[0:8]), v[8:24], jnp.where(half, v[24:32], w[0:8]), w[8:16])

    def join(sides, side):
        grid = full_grid()
        hold_own(grid, fields, xt)
        for k, (v, w, ref) in enumerate(((id_, sides[0], fd), (ie, sides[1], fe), (ih, sides[2], fh))):
            for p, level in EARLY[k].items():
                for c in range(3):
                    grid.put(ref, (c, p), 3 * k + c, p, merged(v[c, p], w[c, p]), level)
        for c in range(2):
            grid.hold(H + c, 6, functools.partial(lambda a: merged(ilo[a], tlo[a]), c))
        for i, v in enumerate(payload(grid, side)):
            if v is not None:
                chip[i] = v

    gz, _, _, _ = position()

    @pl.when(lax.rem(gz, 2) == 0)
    def _():
        grid = edge_grid(inside[...], fields, lambda comp, p: xt[comp, p])
        grid.step_h(1, 6, range(2), lambda c, p, v, n: grid.put(tlo, c - H, c, p, v, n))
        join((sd, se, sh), LO)

    @pl.when(lax.rem(gz, 2) == 1)
    def _():
        grid = edge_grid(inside[...], fields, lambda comp, p: xt[comp, p])
        early(grid, lambda c, p, v, n: grid.put((td, te, th)[c // 3], (c % 3, p), c, p, v, n))
        join((td, te, th), HI)


def full_grid():
    gz, _, last, _ = position()
    up, down = scalar(gz != last), scalar(gz != 0)
    edge = inside_x()

    def inside(p):
        return up if p >= NZL else (down if p < 0 else None)

    def factor(p):
        z = inside(p)
        main, tile = jnp.full((NXL, NY), HALF, jnp.float32), edge * HALF
        return rows(main, tile) if z is None else rows(main * z, tile * z)

    def fill(p):
        z = inside(p)
        if z is None:
            return rows(jnp.zeros((NXL, NY), jnp.float32), 1.0 - edge)
        return rows(jnp.full((NXL, NY), 1.0 - z, jnp.float32), 1.0 - edge * z)

    return Grid(ROWS, factor, fill)


def hold_own(grid, fields, xt):
    for comp in ALL:
        for p in range(NZL):
            grid.hold(comp, p, functools.partial(lambda c, q: rows(own(fields, c, q), xt[c, q]), comp, p))


def hold_frames(grid, refs, levels):
    for k, ref in enumerate(refs):
        for p, level in levels[k].items():
            for c in range(3):
                grid.hold(3 * k + c, p, functools.partial(lambda r, a, b: r[a, b], ref, c, p), level)


EARLY = ({1: 1, 2: 2, 3: 2, 4: 1}, {1: 1, 2: 2, 3: 2, 4: 1}, {0: 1, 1: 2, 2: 3, 3: 2, 4: 1})
MIDDLE = ({3: 3, 4: 3, 5: 2, 6: 1}, {3: 3, 4: 3, 5: 2, 6: 1}, {3: 4, 4: 3, 5: 2, 6: 1})


def middle(d, e, h, eps, chi, xt, fd, fe, fh, gd, ge, gh):
    grid = full_grid()
    hold_own(grid, (d, e, h, eps, chi), xt)
    hold_frames(grid, (fd, fe, fh), EARLY)

    def put(c, p, v, n):
        grid.put((gd, ge, gh)[c // 3], (c % 3, p), c, p, v, n)

    grid.sweep(1, (5, 6), (5, 6), put)
    grid.sweep(2, (4, 5), (4, 5), put)
    grid.sweep(3, (3, 4), (3, 4), put)
    grid.sweep(4, (3,), (), put)


def complete(fields, xt, frames, more, above, below, state, staged, media, coming, done):
    grid = full_grid()
    hold_own(grid, fields, xt)
    hold_frames(grid, frames, EARLY)
    hold_frames(grid, more, MIDDLE)
    for side, at, shift in ((above, HI_AT, NZL), (below, LO_AT, -NZL)):
        if side is not None:
            for (comp, p), i in at.items():
                level = int(p == 6)
                if comp >= DP:
                    level = p + 2 if HP <= comp < INV else p + 1
                grid.hold(comp, p + shift, functools.partial(side, i), level)

    def put(c, p, v, n):
        k = c // 3
        if n == STEPS and p >= ADVANCE:
            staged[k][c % 3, p - ADVANCE] = v[:NXL]
        if n < STEPS or k == 2:
            grid.put(state[k], (c % 3, p + 2), c, p, v, n)

    def last_sweep(h_planes, de_planes):
        for p in sorted(set(h_planes) | set(de_planes)):
            if p in h_planes:
                grid.step_h(STEPS, p, range(3), put)
            if p in de_planes:
                if p not in h_planes:
                    for c in range(3):
                        staged[2][c, p - ADVANCE] = grid.get(H + c, p, STEPS)[:NXL]
                grid.step_de(STEPS, p, put)
                for k in range(3):
                    done(k, p - ADVANCE, 1)

    if below is not None:
        grid.sweep(1, (-1,), (-1, 0), put)
        grid.sweep(2, (-1, 0), (0, 1), put)
        grid.sweep(3, (0, 1), (1, 2), put)
        last_sweep((1, 2), (2, 3))
    if above is not None:
        for k, comp in enumerate((EPS, CHI)):
            for o in range(ADVANCE):
                v = grid.get(comp, NZL + o)[:NXL]
                if coming is not None:
                    gz, _, last, _ = position()
                    v = jnp.where(gz == last, coming[k][o], v)
                media[k][o] = v
            done(3 + k, KEPT, ADVANCE)
        grid.sweep(1, (7,), (7, 8), put)
        grid.sweep(2, range(6, 9), range(6, 10), put)
        grid.sweep(3, range(5, 10), range(5, 11), put)
        last_sweep(range(4, 10), range(4, 10))


KEPT = NZL - ADVANCE


def run(given, above, below, coming, outs, scratch, also=()):
    state, staged, media, sems = scratch[:3], scratch[3:6], scratch[6:8], scratch[8]
    copies = []

    def send(source, target):
        copies.append(pltpu.make_async_copy(source, target, sems.at[len(copies)]))
        copies[-1].start()

    def done(k, o, n):
        if k < 3:
            send(staged[k].at[:, pl.ds(o, n)], outs[k].at[:, pl.ds(o, n)])
        else:
            send(media[k - 3], outs[k].at[pl.ds(o, n)])

    for a, b in also:
        send(a, b)
    complete(*given, above, below, state, staged, media, coming, done)
    for c in copies:
        c.wait()


def near(d, e, h, eps, chi, xt, fd, fe, fh, gd, ge, gh, cc, *rest):
    given = (d, e, h, eps, chi), xt, (fd, fe, fh), (gd, ge, gh)
    outs, scratch = rest[:5], rest[5:]
    also = [(a.at[pl.ds(ADVANCE, KEPT)], b.at[pl.ds(0, KEPT)]) for a, b in ((eps, outs[3]), (chi, outs[4]))]
    gz, _, _, _ = position()

    @pl.when(lax.rem(gz, 2) == 0)
    def _():
        run(given, lambda i: cc[i], None, None, outs, scratch, also)

    @pl.when(lax.rem(gz, 2) == 1)
    def _():
        run(given, None, lambda i: cc[i], None, outs, scratch, also)


def far(d, e, h, eps, chi, xt, fd, fe, fh, gd, ge, gh, ca, cb, eps_in, chi_in, *rest):
    given = (d, e, h, eps, chi), xt, (fd, fe, fh), (gd, ge, gh)
    outs, scratch = rest[5:10], rest[10:]
    half = halo_row() < XH
    gz, _, _, _ = position()

    def cross(chosen, i):
        m = ca[24 * i : 24 * i + 8]
        x = ca[24 * NS + 8 * i : 24 * NS + 8 * i + 8] if i < NR else cb[NEW_AT + 8 * (i - NR) : NEW_AT + 8 * (i - NR) + 8]
        at, kept = HALO_AT[i], list(chosen[WIDTH[i]])
        v = cb[at : at + WIDTH[i]]
        if len(kept) < 8:
            near_row = [max([k for k in kept if k <= r], default=kept[0]) for r in range(8)]
            v = rows(*[v[kept.index(k) : kept.index(k) + 1] for k in near_row])
        return rows(jnp.where(half, x, m), ca[24 * i + 8 : 24 * i + 24], jnp.where(half, m, x), v)

    @pl.when(lax.rem(gz, 2) == 0)
    def _():
        run(given, None, functools.partial(cross, LO_ROWS), None, outs, scratch)

    @pl.when(lax.rem(gz, 2) == 1)
    def _():
        run(given, functools.partial(cross, HI_ROWS), None, (eps_in, chi_in), outs, scratch)


def swapped(shard, axis, first):
    n = {a: lax.axis_size(a) for a in ("gz", "gx")}
    moves = []
    for z in range(n["gz"]):
        for x in range(n["gx"]):
            at = z if axis == "gz" else x
            to = at + 1 if at % 2 == first else at - 1
            if 0 <= to < n[axis]:
                other = (to, x) if axis == "gz" else (z, to)
            else:
                other = (z ^ 1, x) if axis == "gx" else (z, x ^ 1)
            moves.append((z * n["gx"] + x, other[0] * n["gx"] + other[1]))
    return lax.ppermute(shard, ("gz", "gx"), moves)


def call(body, inputs, out_shape, scratch=(), vmem=8, specs=None, out=VM, aliases=None):
    return pl.pallas_call(
        body,
        out_shape=out_shape,
        in_specs=[VM] * len(inputs) if specs is None else specs,
        out_specs=jax.tree.map(lambda _: out, out_shape),
        input_output_aliases=aliases or {},
        scratch_shapes=list(scratch),
        compiler_params=pltpu.CompilerParams(vmem_limit_bytes=vmem << 20),
    )(*inputs)


def on_device(d_field, e_field, h_field, permittivity, kerr_coeff, classes, eps_table, chi_table):
    field, medium = shape(3, NZL, NXL, NY), shape(NZL, NXL, NY)
    fields = [d_field, e_field, h_field, permittivity, kerr_coeff]
    halo = shape(NHALO, NY)
    ya, yb = call(
        load,
        [pltpu.with_memory_space_constraint(a, pltpu.HBM) for a in fields],
        (halo, halo),
        [pltpu.VMEM((11, NZL, 16, NY), jnp.float32), pltpu.SemaphoreType.DMA((11, 2))],
        specs=[HBM] * 5,
    )
    ra, rb = swapped(ya, "gx", 0), swapped(yb, "gx", 1)
    lo = shape(2, NXL, NY)
    *inside, za = call(inner, fields, (*[shape(3, 5, NXL, NY)] * 3, lo, shape(24 * NS + 8 * NR, NY)))
    ca = swapped(za, "gz", 1)
    (edge,) = call(mark, [], (shape(8, NY),))
    thin = [(3, 5, EDGE, NY)] * 3 + [(2, EDGE, NY)]
    xt, *outside, zb = call(
        edges, [*fields, ra, rb, edge], (shape(11, NZL, 8, NY), *[shape(*t) for t in thin], shape(LATE, NY))
    )
    cb = swapped(zb, "gz", 1)
    coming = lookup(classes, eps_table), lookup(classes, chi_table)
    *frames, zc = call(
        merge,
        [*fields, *inside, xt, *outside, edge],
        (*[shape(3, 5, ROWS, NY)] * 3, shape(NS, ROWS, NY)),
        [pltpu.VMEM(t, jnp.float32) for t in thin],
    )
    cc = swapped(zc, "gz", 0)
    more = call(middle, [*fields, xt, *frames], (shape(3, 7, ROWS, NY),) * 3)
    state = [pltpu.VMEM((3, 13, ROWS, NY), jnp.float32)] * 3
    given = [*fields, xt, *frames, *more]
    two = (ADVANCE, NXL, NY)
    results = (field, field, field, medium, medium)
    scratch = state + [pltpu.VMEM(field.shape, jnp.float32)] * 3 + [pltpu.VMEM(two, jnp.float32)] * 2
    scratch += [pltpu.SemaphoreType.DMA((32,))]
    outs = call(near, [*given, cc], results, scratch, vmem=16, out=HBM)
    given += [ca, cb, *coming]
    n = len(given)
    return call(
        far,
        [*given, *outs],
        results,
        scratch,
        vmem=16,
        specs=[VM] * n + [HBM] * 5,
        out=HBM,
        aliases={n + k: k for k in range(5)},
    )


def solution(mesh):
    placed = (
        P(None, "gz", "gx", None),
        P(None, "gz", "gx", None),
        P(None, "gz", "gx", None),
        P("gz", "gx", None),
        P("gz", "gx", None),
        P(None, "gx", None),
        P(),
        P(),
    )
    return jax.shard_map(
        on_device,
        mesh=mesh,
        in_specs=placed,
        out_specs=placed[:5],
        check_vma=False,
    )
```

```python
import functools

import jax
import jax.numpy as jnp
from jax import lax
from jax.experimental import pallas as pl
from jax.experimental.pallas import tpu as pltpu
from jax.sharding import PartitionSpec as P


STEPS = 4
KERR = 3
ADVANCE = 2
HALF = 0.5

D, E, H, EPS, CHI = 0, 3, 6, 9, 10
ALL = range(11)
NZL, NXL, NY = 8, 32, 128
XH = 4
ROWS = NXL + 2 * XH
EDGE = 24

DP, HP, INV = 11, 14, 17
RAW = [(E + c, 0) for c in range(3)] + [(c, p) for p in range(3) for c in (EPS, CHI)]
HI = RAW + [(DP + c, p) for p in range(3) for c in range(3)] + [(HP + c, p) for p in range(2) for c in range(3)]
HI += [(INV, 1), (INV, 2)]
HI_ROWS = {8: range(8), 6: (0, 1, 2, 5, 6, 7), 4: (0, 1, 6, 7), 2: (0, 7)}
LO_ROWS = {8: range(8), 6: (0, 1, 2, 3, 6, 7), 4: (0, 1, 2, 7), 2: ()}


def slot_rows(comp, p):
    if (comp, p) == (E, 0):
        return 8
    level = p + (HP <= comp < INV)
    return 6 - 2 * p if comp < HP or comp >= INV else 6 - 2 * (level - 1)


WIDTH = [slot_rows(*k) for k in HI]
HALO_AT = [sum(WIDTH[:i]) for i in range(len(HI))]
LO = [None] * len(HI)
_wide = [i for i, n in enumerate(WIDTH) if n >= 6]
_thin = [i for i, n in enumerate(WIDTH) if n == 4]
for _k in [(E + c, 7) for c in range(3)] + [(H + c, 7) for c in range(3)]:
    LO[_wide.pop(0)] = _k
for _k in [(D + c, 7) for c in range(3)] + [(EPS, 7), (CHI, 7), (H, 6), (H + 1, 6)]:
    LO[_thin.pop(0)] = _k
HI_AT = {k: i for i, k in enumerate(HI)}
LO_AT = {k: i for i, k in enumerate(LO) if k}
NS, NR = len(HI), len(RAW)
NEW_AT = -(-sum(WIDTH) // 8) * 8
LATE = NEW_AT + 8 * (NS - NR)

FOUR, THREE = (E, E + 1, E + 2, H + 1, H + 2), (D, D + 1, D + 2, H, EPS, CHI)
NF = len(FOUR) * NZL * 4
NHALO = NF + len(THREE) * NZL * 3

VM = pl.BlockSpec(memory_space=pltpu.VMEM)
HBM = pl.BlockSpec(memory_space=pltpu.HBM)
SM = pl.BlockSpec(memory_space=pltpu.SMEM)


def shape(*dims):
    return jax.ShapeDtypeStruct(dims, jnp.float32)


def rows(*parts):
    return jnp.concatenate(parts, axis=0)


def scalar(condition):
    return jnp.where(condition, 1.0, 0.0).astype(jnp.float32)


def position():
    gz, gx = lax.axis_index("gz"), lax.axis_index("gx")
    return gz, gx, lax.axis_size("gz") - 1, lax.axis_size("gx") - 1


def halo_row():
    return lax.broadcasted_iota(jnp.int32, (8, NY), 0)


def inside_x():
    _, gx, _, last = position()
    return jnp.where(halo_row() < XH, scalar(gx != last), scalar(gx != 0))


class Grid:
    def __init__(self, size, factor, fill):
        self.size, self.factor, self.fill = size, factor, fill
        self.where, self.level = {}, {}
        lane = lax.broadcasted_iota(jnp.int32, (size, NY), 1)
        self.last_y, self.first_y = lane == NY - 1, lane == 0

    def hold(self, comp, plane, read, level=0):
        self.where[(comp, plane)] = read
        self.level[(comp, plane)] = level

    def get(self, comp, plane, level=None):
        assert level is None or self.level[(comp, plane)] == level, (comp, plane)
        return self.where[(comp, plane)]()

    def put(self, ref, index, comp, plane, value, level):
        ref[index] = value
        self.hold(comp, plane, lambda: ref[index], level)

    def next_y(self, v):
        return jnp.where(self.last_y, 0.0, pltpu.roll(v, NY - 1, 1))

    def prev_y(self, v):
        return jnp.where(self.first_y, 0.0, pltpu.roll(v, 1, 1))

    def next_x(self, v):
        return pltpu.roll(v, self.size - 1, 0)

    def prev_x(self, v):
        return pltpu.roll(v, 1, 0)

    def step_h(self, n, p, comps, put):
        f = self.factor(p)
        ex, ey, ez = (self.get(E + c, p, n - 1) for c in range(3))
        if self.level.get((HP, p)) == n:
            hx, hy, hz = (self.get(HP + c, p) for c in range(3))
            put(H, p, hx - f * ((self.next_y(ez) - ez) + ey), n)
            put(H + 1, p, hy + f * (ex + (self.next_x(ez) - ez)), n)
            put(H + 2, p, hz - f * ((self.next_x(ey) - ey) - (self.next_y(ex) - ex)), n)
            return
        new = {}
        if 0 in comps:
            eyn = self.get(E + 1, p + 1, n - 1)
            new[0] = (self.next_y(ez) - ez) - (eyn - ey)
        if 1 in comps:
            exn = self.get(E, p + 1, n - 1)
            new[1] = (exn - ex) - (self.next_x(ez) - ez)
        if 2 in comps:
            new[2] = (self.next_x(ey) - ey) - (self.next_y(ex) - ex)
        for c, curl in new.items():
            put(H + c, p, self.get(H + c, p, n - 1) - f * curl, n)

    def medium(self, p):
        eps, fill = self.get(EPS, p), self.fill(p)
        return eps if fill is None else eps + fill, self.get(CHI, p)

    def first_inverse(self, n, p):
        ex, ey, ez = (self.get(E + c, p, n) for c in range(3))
        eps, chi = self.medium(p)
        return 1.0 / (eps + chi * (ex * ex + ey * ey + ez * ez))

    def derive(self):
        out = {}
        for p in range(3):
            f, n = self.factor(p), p + 1
            hx, hy, hz = (self.get(H + c, p, n) for c in range(3))
            dx, dy, dz = (self.get(D + c, p, n - 1) for c in range(3))
            out[(DP, p)] = dx + f * ((hz - self.prev_y(hz)) - hy)
            out[(DP + 1, p)] = dy + f * (hx - (hz - self.prev_x(hz)))
            out[(DP + 2, p)] = dz + f * ((hy - self.prev_x(hy)) - (hx - self.prev_y(hx)))
            if p < 2:
                out[(HP, p)] = hx + f * self.get(E + 1, p + 1, n)
                out[(HP + 1, p)] = hy - f * self.get(E, p + 1, n)
                out[(HP + 2, p)] = hz
            if p > 0:
                out[(INV, p)] = self.first_inverse(n - 1, p)
        return out

    def step_de(self, n, p, put):
        f = self.factor(p)
        hxp, hyp = (self.get(H + c, p - 1, n) for c in range(2))
        if self.level.get((DP, p)) == n:
            dx, dy, dz = (self.get(DP + c, p) for c in range(3))
            dx, dy = dx + f * hyp, dy - f * hxp
        else:
            hx, hy, hz = (self.get(H + c, p, n) for c in range(3))
            dx = self.get(D, p, n - 1) + f * ((hz - self.prev_y(hz)) - (hy - hyp))
            dy = self.get(D + 1, p, n - 1) + f * ((hx - hxp) - (hz - self.prev_x(hz)))
            dz = self.get(D + 2, p, n - 1) + f * ((hy - self.prev_x(hy)) - (hx - self.prev_y(hx)))
        eps, chi = self.medium(p)
        inverse = self.get(INV, p) if self.level.get((INV, p)) == n else self.first_inverse(n - 1, p)
        if n == STEPS:
            dx, dy, dz, eps, chi, inverse = (v[:NXL] for v in (dx, dy, dz, eps, chi, inverse))
        squares = chi * (dx * dx + dy * dy + dz * dz)
        for _ in range(KERR - 1):
            inverse = 1.0 / (eps + squares * (inverse * inverse))
        for c, v in enumerate((dx, dy, dz)):
            put(D + c, p, v, n)
            put(E + c, p, v * inverse, n)

    def sweep(self, n, h_planes, de_planes, put):
        for p in range(-2, 11):
            if p in h_planes:
                self.step_h(n, p, range(3), put)
            if p in de_planes:
                self.step_de(n, p, put)


def own(fields, comp, plane):
    d, e, h, eps, chi = fields
    if comp < E:
        return d[comp, plane]
    if comp < H:
        return e[comp - E, plane]
    if comp < EPS:
        return h[comp - H, plane]
    return eps[plane] if comp == EPS else chi[plane]


def halo_slot(comp, p):
    if comp in FOUR:
        return (FOUR.index(comp) * NZL + p) * 4, 4
    return NF + (THREE.index(comp) * NZL + p) * 3, 3


def load(d, e, h, eps, chi, dv, ev, hv, epsv, chiv, ya, yb, sems):
    held = (dv, ev, hv, epsv, chiv)
    copies = [pltpu.make_async_copy(a, b, sems.at[i]) for i, (a, b) in enumerate(zip((d, e, h, eps, chi), held))]
    for c in copies:
        c.start()
    _, gx, _, last = position()
    even = lax.rem(gx, 2) == 0
    keep = scalar(jnp.logical_and(gx != 0, gx != last))
    for comps, copy in zip((range(D, E), range(E, H), range(H, EPS), (EPS,), (CHI,)), copies):
        copy.wait()
        for comp in comps:
            for p in range(NZL):
                at, n = halo_slot(comp, p)
                v = own(held, comp, p)
                low, high = v[0:n], v[NXL - n :]
                ya[at : at + n] = jnp.where(even, high, low)
                yb[at : at + n] = jnp.where(even, low, high) * keep


def mark(out):
    out[...] = inside_x()


def early(grid, put):
    grid.sweep(1, range(0, 5), range(1, 5), put)
    grid.sweep(2, range(1, 4), range(2, 4), put)
    grid.sweep(3, range(2, 3), (), put)


def lookup(classes, table):
    labels = jnp.arange(table.shape[0], dtype=jnp.int32).reshape(-1, 1, 1, 1)
    picked = jnp.where(classes[None] == labels, table.reshape(-1, 1, 1, 1), jnp.float32(0.0))
    return jnp.sum(picked, axis=0)


def payload(grid, side):
    made = grid.derive() if side is HI else {}
    return [k and (made[k] if k in made else grid.get(*k)) for k in side]


def inner(d, e, h, eps, chi, fd, fe, fh, lo, out):
    fields = (d, e, h, eps, chi)
    grid = Grid(NXL, lambda p: HALF, lambda p: None)
    for comp in ALL:
        for p in range(NZL):
            grid.hold(comp, p, functools.partial(own, fields, comp, p))
    grid.step_h(1, 6, range(2), lambda c, p, v, n: grid.put(lo, c - H, c, p, v, n))

    def put(c, p, v, n):
        ref = (fd, fe, fh)[c // 3]
        grid.put(ref, (c % 3, p), c, p, v, n)

    early(grid, put)
    gz, _, last, _ = position()
    first_core = lax.rem(gz, 2) == 0
    keep = scalar(jnp.logical_and(gz != 0, gz != last))
    half = halo_row() < XH
    low = payload(grid, LO)
    for i, v in enumerate(payload(grid, HI)):
        if low[i] is not None:
            v = jnp.where(first_core, v, low[i])
        v = v * keep
        out[24 * i : 24 * i + 8] = jnp.where(half, v[24:32], v[0:8])
        out[24 * i + 8 : 24 * i + 24] = v[8:24]
        if i < NR:
            out[24 * NS + 8 * i : 24 * NS + 8 * i + 8] = jnp.where(half, v[0:8], v[24:32])


def edge_grid(inside, fields, tile):
    f = rows(jnp.full((8, NY), HALF), inside * HALF, jnp.full((8, NY), HALF))
    none = jnp.zeros((8, NY), jnp.float32)
    fill = rows(none, 1.0 - inside, none)
    grid = Grid(EDGE, lambda p: f, lambda p: fill)

    def read(comp, p):
        v = own(fields, comp, p)
        return rows(v[24:32], tile(comp, p), v[0:8])

    for comp in ALL:
        for p in range(NZL):
            grid.hold(comp, p, functools.partial(read, comp, p))
    return grid


def joined(a, b, comp, p):
    _, gx, _, _ = position()
    even = lax.rem(gx, 2) == 0
    at, n = halo_slot(comp, p)
    a, b = a[at : at + n], b[at : at + n]
    above, below = jnp.where(even, a, b), jnp.where(even, b, a)
    if n == 4:
        return rows(above, below)
    return rows(above, above[2:3], below[0:1], below)


def edges(d, e, h, eps, chi, ra, rb, inside, xt, sd, se, sh, slo, cross):
    fields = (d, e, h, eps, chi)
    gz, _, last, _ = position()
    keep = scalar(jnp.logical_and(gz != 0, gz != last))
    half = halo_row() < XH
    for comp in ALL:
        for p in range(NZL):
            xt[comp, p] = joined(ra, rb, comp, p)

    def pack(grid, side, chosen):
        for i, v in enumerate(payload(grid, side)):
            if v is None:
                continue
            v = v * keep
            at, n = HALO_AT[i], WIDTH[i]
            runs = []
            for r in chosen[n]:
                if runs and runs[-1][1] == r:
                    runs[-1][1] = r + 1
                else:
                    runs.append([r, r + 1])
            for a, b in runs:
                cross[at : at + b - a] = v[8 + a : 8 + b]
                at += b - a
            if i >= NR:
                at = NEW_AT + 8 * (i - NR)
                cross[at : at + 8] = jnp.where(half, v[16:24], v[0:8])

    @pl.when(lax.rem(gz, 2) == 0)
    def _():
        grid = edge_grid(inside[...], fields, lambda comp, p: xt[comp, p])
        early(grid, lambda c, p, v, n: grid.put((sd, se, sh)[c // 3], (c % 3, p), c, p, v, n))
        pack(grid, HI, HI_ROWS)

    @pl.when(lax.rem(gz, 2) == 1)
    def _():
        grid = edge_grid(inside[...], fields, lambda comp, p: xt[comp, p])
        grid.step_h(1, 6, range(2), lambda c, p, v, n: grid.put(slo, c - H, c, p, v, n))
        pack(grid, LO, LO_ROWS)


def merge(d, e, h, eps, chi, id_, ie, ih, ilo, xt, sd, se, sh, slo, inside, fd, fe, fh, chip, td, te, th, tlo):
    fields = (d, e, h, eps, chi)
    half = halo_row() < XH

    def merged(v, w):
        return rows(jnp.where(half, w[16:24], v[0:8]), v[8:24], jnp.where(half, v[24:32], w[0:8]), w[8:16])

    def join(sides, side):
        grid = full_grid()
        hold_own(grid, fields, xt)
        for k, (v, w, ref) in enumerate(((id_, sides[0], fd), (ie, sides[1], fe), (ih, sides[2], fh))):
            for p, level in EARLY[k].items():
                for c in range(3):
                    grid.put(ref, (c, p), 3 * k + c, p, merged(v[c, p], w[c, p]), level)
        for c in range(2):
            grid.hold(H + c, 6, functools.partial(lambda a: merged(ilo[a], tlo[a]), c))
        for i, v in enumerate(payload(grid, side)):
            if v is not None:
                chip[i] = v

    gz, _, _, _ = position()

    @pl.when(lax.rem(gz, 2) == 0)
    def _():
        grid = edge_grid(inside[...], fields, lambda comp, p: xt[comp, p])
        grid.step_h(1, 6, range(2), lambda c, p, v, n: grid.put(tlo, c - H, c, p, v, n))
        join((sd, se, sh), LO)

    @pl.when(lax.rem(gz, 2) == 1)
    def _():
        grid = edge_grid(inside[...], fields, lambda comp, p: xt[comp, p])
        early(grid, lambda c, p, v, n: grid.put((td, te, th)[c // 3], (c % 3, p), c, p, v, n))
        join((td, te, th), HI)


def full_grid():
    gz, _, last, _ = position()
    up, down = scalar(gz != last), scalar(gz != 0)
    edge = inside_x()

    def inside(p):
        return up if p >= NZL else (down if p < 0 else None)

    def factor(p):
        z = inside(p)
        main, tile = jnp.full((NXL, NY), HALF, jnp.float32), edge * HALF
        return rows(main, tile) if z is None else rows(main * z, tile * z)

    def fill(p):
        z = inside(p)
        if z is None:
            return rows(jnp.zeros((NXL, NY), jnp.float32), 1.0 - edge)
        return rows(jnp.full((NXL, NY), 1.0 - z, jnp.float32), 1.0 - edge * z)

    return Grid(ROWS, factor, fill)


def hold_own(grid, fields, xt):
    for comp in ALL:
        for p in range(NZL):
            grid.hold(comp, p, functools.partial(lambda c, q: rows(own(fields, c, q), xt[c, q]), comp, p))


def hold_frames(grid, refs, levels, size=ROWS):
    for k, ref in enumerate(refs):
        for p, level in levels[k].items():
            for c in range(3):
                grid.hold(3 * k + c, p, functools.partial(lambda r, a, b: r[a, b, 0:size], ref, c, p), level)


EARLY = ({1: 1, 2: 2, 3: 2, 4: 1}, {1: 1, 2: 2, 3: 2, 4: 1}, {0: 1, 1: 2, 2: 3, 3: 2, 4: 1})
MIDDLE = ({3: 3, 4: 3, 5: 2, 6: 1}, {3: 3, 4: 3, 5: 2, 6: 1}, {3: 4, 4: 3, 5: 2, 6: 1})


def middle(d, e, h, eps, chi, xt, fd, fe, fh, gd, ge, gh):
    grid = full_grid()
    hold_own(grid, (d, e, h, eps, chi), xt)
    hold_frames(grid, (fd, fe, fh), EARLY)

    def put(c, p, v, n):
        grid.put((gd, ge, gh)[c // 3], (c % 3, p), c, p, v, n)

    grid.sweep(1, (5, 6), (5, 6), put)
    grid.sweep(2, (4, 5), (4, 5), put)
    grid.sweep(3, (3, 4), (3, 4), put)
    grid.sweep(4, (3,), (), put)


def hold_side(grid, high, read):
    at, shift = (HI_AT, NZL) if high else (LO_AT, -NZL)
    for (comp, p), i in at.items():
        level = int(p == 6)
        if comp >= DP:
            level = p + 2 if HP <= comp < INV else p + 1
        grid.hold(comp, p + shift, functools.partial(read, i), level)


def chain(grid, high, put, keep, done=lambda o: None):
    if high:
        grid.sweep(1, (7,), (7, 8), put)
        grid.sweep(2, range(6, 9), range(6, 10), put)
        grid.sweep(3, range(5, 10), range(5, 11), put)
        h_planes, de_planes = range(4, 10), range(4, 10)
    else:
        grid.sweep(1, (-1,), (-1, 0), put)
        grid.sweep(2, (-1, 0), (0, 1), put)
        grid.sweep(3, (0, 1), (1, 2), put)
        h_planes, de_planes = (1, 2), (2, 3)
    for p in sorted(set(h_planes) | set(de_planes)):
        if p in h_planes:
            grid.step_h(STEPS, p, range(3), put)
        if p in de_planes:
            if p not in h_planes:
                for c in range(3):
                    keep(c, p - ADVANCE, grid.get(H + c, p, STEPS))
            grid.step_de(STEPS, p, put)
            done(p - ADVANCE)


KEPT = NZL - ADVANCE


def near(d, e, h, eps, chi, xt, fd, fe, fh, gd, ge, gh, cc, nd, ne, nh, neps, nchi, *state):
    gz, _, _, _ = position()

    def side(high):
        grid = full_grid()
        hold_own(grid, (d, e, h, eps, chi), xt)
        hold_frames(grid, (fd, fe, fh), EARLY)
        hold_frames(grid, (gd, ge, gh), MIDDLE)
        hold_side(grid, high, lambda i: cc[i])

        def put(c, p, v, n):
            k = c // 3
            if n == STEPS and p >= ADVANCE:
                (nd, ne, nh)[k][c % 3, p - ADVANCE] = v[:NXL]
            if n < STEPS or k == 2:
                grid.put(state[k], (c % 3, p + 2), c, p, v, n)

        def keep(c, o, v):
            nh[c, o] = v[:NXL]

        chain(grid, high, put, keep)
        if high:
            for out, comp in ((neps, EPS), (nchi, CHI)):
                for o in range(ADVANCE):
                    out[o] = grid.get(comp, NZL + o)[:NXL]

    pl.when(lax.rem(gz, 2) == 0)(lambda: side(True))
    pl.when(lax.rem(gz, 2) == 1)(lambda: side(False))


def ahead(d, e, h, eps, chi, fd, fe, fh, gd, ge, gh, ca, eps_in, chi_in, ie, ih, od, oe, oh, oeps, ochi, sd):
    gz, _, last, _ = position()
    half = halo_row() < XH

    def read(i):
        m = ca[24 * i : 24 * i + 8]
        x = ca[24 * NS + 8 * i : 24 * NS + 8 * i + 8] if i < NR else m
        return rows(jnp.where(half, x, m), ca[24 * i + 8 : 24 * i + 24], jnp.where(half, m, x))

    def side(high):
        z = scalar(gz != last) if high else scalar(gz != 0)

        def own_plane(p):
            return 0 <= p < NZL

        grid = Grid(NXL, lambda p: HALF if own_plane(p) else HALF * z, lambda p: None if own_plane(p) else 1.0 - z)
        for comp in ALL:
            for p in range(NZL):
                grid.hold(comp, p, functools.partial(own, (d, e, h, eps, chi), comp, p))
        hold_frames(grid, (fd, fe, fh), EARLY, NXL)
        hold_frames(grid, (gd, ge, gh), MIDDLE, NXL)
        hold_side(grid, high, read)

        def put(c, p, v, n):
            k = c // 3
            if n == STEPS and p >= ADVANCE:
                (od, oe, oh)[k][c % 3, p - ADVANCE] = v
            if k == 2:
                grid.put(ih, (n - 1, c % 3, p + 2), c, p, v, n)
            elif n < STEPS and k == 1:
                grid.put(ie, (n - 1, c % 3, p + 2), c, p, v, n)
            elif n < STEPS:
                grid.put(sd, (c % 3, p + 2), c, p, v, n)

        def keep(c, o, v):
            oh[c, o] = v

        chain(grid, high, put, keep)
        if high:
            for out, comp, new in ((oeps, EPS, eps_in), (ochi, CHI, chi_in)):
                for o in range(ADVANCE):
                    out[o] = jnp.where(gz == last, new[o], grid.get(comp, NZL + o))

    pl.when(lax.rem(gz, 2) == 0)(lambda: side(False))
    pl.when(lax.rem(gz, 2) == 1)(lambda: side(True))


def far(d, e, h, eps, chi, xt, fd, fe, fh, gd, ge, gh, ca, cb, *rest):
    nd, ne, nh, neps, nchi, ie, ih, od, oe, oh, oeps, ochi = rest[:12]
    outs, state, edge, sems = rest[12:17], rest[17:20], rest[20:23], rest[23]
    half = halo_row() < XH
    gz, _, _, _ = position()

    def cross(chosen, i):
        m = ca[24 * i : 24 * i + 8]
        x = ca[24 * NS + 8 * i : 24 * NS + 8 * i + 8] if i < NR else cb[NEW_AT + 8 * (i - NR) : NEW_AT + 8 * (i - NR) + 8]
        at, kept = HALO_AT[i], list(chosen[WIDTH[i]])
        v = cb[at : at + WIDTH[i]]
        if len(kept) < 8:
            near_row = [max([k for k in kept if k <= r], default=kept[0]) for r in range(8)]
            v = rows(*[v[kept.index(k) : kept.index(k) + 1] for k in near_row])
        return rows(jnp.where(half, x, m), ca[24 * i + 8 : 24 * i + 24], jnp.where(half, m, x), v)

    def side(high):
        copies = []

        def send(source, target):
            copies.append(pltpu.make_async_copy(source, target, sems.at[len(copies)]))
            copies[-1].start()

        here, there = (pl.ds(ADVANCE, KEPT), pl.ds(0, ADVANCE)) if high else (pl.ds(0, ADVANCE), pl.ds(ADVANCE, KEPT))
        middle_rows = pl.ds(8, 16)
        for a, b, out in zip((nd, ne, nh), (od, oe, oh), outs):
            send(a.at[:, there], out.at[:, there])
            send(b.at[:, here, middle_rows], out.at[:, here, middle_rows])
        for a, new, out in zip((eps, chi), (oeps, ochi) if high else (neps, nchi), outs[3:]):
            send(a.at[pl.ds(ADVANCE, KEPT)], out.at[pl.ds(0, KEPT)])
            send(new, out.at[pl.ds(KEPT, ADVANCE)])

        grid = full_grid()
        hold_own(grid, (d, e, h, eps, chi), xt)
        hold_frames(grid, (fd, fe, fh), EARLY)
        hold_frames(grid, (gd, ge, gh), MIDDLE)
        hold_side(grid, high, functools.partial(cross, HI_ROWS if high else LO_ROWS))
        none = jnp.zeros((16, NY), jnp.float32)

        def result(k, c, o, v):
            edge[k][c, o, 0:8] = v[0:8]
            edge[k][c, o, 8:16] = v[24:32]

        def put(c, p, v, n):
            k, at = c // 3, (c % 3, p + 2)
            if n == STEPS and p >= ADVANCE:
                result(k, c % 3, p - ADVANCE, v)
            if n < STEPS or k == 2:
                ref, inner_ref = state[k], (None, ie, ih)[k]
                ref[(*at, slice(0, 8))] = v[0:8]
                ref[(*at, slice(8, 24))] = v[24:40]

                def read():
                    mid = none if inner_ref is None else inner_ref[(n - 1, *at, slice(8, 24))]
                    return rows(ref[(*at, slice(0, 8))], mid, ref[(*at, slice(8, 24))])

                grid.hold(c, p, read, n)

        def done(o):
            for k in range(3):
                for a, b in ((0, 0), (8, 24)):
                    send(edge[k].at[:, pl.ds(o, 1), pl.ds(a, 8)], outs[k].at[:, pl.ds(o, 1), pl.ds(b, 8)])

        chain(grid, high, put, functools.partial(result, 2), done)
        for c in copies:
            c.wait()

    pl.when(lax.rem(gz, 2) == 0)(lambda: side(False))
    pl.when(lax.rem(gz, 2) == 1)(lambda: side(True))


def swapped(shard, axis, first):
    n = {a: lax.axis_size(a) for a in ("gz", "gx")}
    moves = []
    for z in range(n["gz"]):
        for x in range(n["gx"]):
            at = z if axis == "gz" else x
            to = at + 1 if at % 2 == first else at - 1
            if 0 <= to < n[axis]:
                other = (to, x) if axis == "gz" else (z, to)
            else:
                other = (z ^ 1, x) if axis == "gx" else (z, x ^ 1)
            moves.append((z * n["gx"] + x, other[0] * n["gx"] + other[1]))
    return lax.ppermute(shard, ("gz", "gx"), moves)


def call(body, inputs, out_shape, scratch=(), vmem=8, specs=None, out=VM, aliases=None):
    return pl.pallas_call(
        body,
        out_shape=out_shape,
        in_specs=[VM] * len(inputs) if specs is None else specs,
        out_specs=jax.tree.map(lambda _: out, out_shape),
        input_output_aliases=aliases or {},
        scratch_shapes=list(scratch),
        compiler_params=pltpu.CompilerParams(vmem_limit_bytes=vmem << 20),
    )(*inputs)


def on_device(d_field, e_field, h_field, permittivity, kerr_coeff, classes, eps_table, chi_table):
    field, medium = shape(3, NZL, NXL, NY), shape(NZL, NXL, NY)
    halo = shape(NHALO, NY)
    *fields, ya, yb = call(
        load,
        [pltpu.with_memory_space_constraint(a, pltpu.HBM) for a in (d_field, e_field, h_field, permittivity, kerr_coeff)],
        (field, field, field, medium, medium, halo, halo),
        [pltpu.SemaphoreType.DMA((5,))],
        specs=[HBM] * 5,
    )
    ra, rb = swapped(ya, "gx", 0), swapped(yb, "gx", 1)
    lo = shape(2, NXL, NY)
    *inside, za = call(inner, fields, (*[shape(3, 5, NXL, NY)] * 3, lo, shape(24 * NS + 8 * NR, NY)))
    ca = swapped(za, "gz", 1)
    (edge,) = call(mark, [], (shape(8, NY),))
    thin = [(3, 5, EDGE, NY)] * 3 + [(2, EDGE, NY)]
    xt, *outside, zb = call(
        edges, [*fields, ra, rb, edge], (shape(11, NZL, 8, NY), *[shape(*t) for t in thin], shape(LATE, NY))
    )
    cb = swapped(zb, "gz", 1)
    coming = lookup(classes, eps_table), lookup(classes, chi_table)
    *frames, zc = call(
        merge,
        [*fields, *inside, xt, *outside, edge],
        (*[shape(3, 5, ROWS, NY)] * 3, shape(NS, ROWS, NY)),
        [pltpu.VMEM(t, jnp.float32) for t in thin],
    )
    cc = swapped(zc, "gz", 0)
    more = call(middle, [*fields, xt, *frames], (shape(3, 7, ROWS, NY),) * 3)
    state = [pltpu.VMEM((3, 13, ROWS, NY), jnp.float32)] * 3
    two = shape(ADVANCE, NXL, NY)
    made = call(near, [*fields, xt, *frames, *more, cc], (field, field, field, two, two), state, vmem=16)
    levels = shape(STEPS - 1, 3, 13, NXL, NY), shape(STEPS, 3, 13, NXL, NY)
    inside = call(
        ahead,
        [*fields, *frames, *more, ca, *coming],
        (*levels, field, field, field, two, two),
        [pltpu.VMEM((3, 13, NXL, NY), jnp.float32)],
        vmem=16,
    )
    thin = [pltpu.VMEM((3, 13, EDGE, NY), jnp.float32)] * 3 + [pltpu.VMEM((3, NZL, 16, NY), jnp.float32)] * 3
    return call(
        far,
        [*fields, xt, *frames, *more, ca, cb, *made, *inside],
        (field, field, field, medium, medium),
        [*thin, pltpu.SemaphoreType.DMA((48,))],
        vmem=16,
        out=HBM,
    )


def solution(mesh):
    placed = (
        P(None, "gz", "gx", None),
        P(None, "gz", "gx", None),
        P(None, "gz", "gx", None),
        P("gz", "gx", None),
        P("gz", "gx", None),
        P(None, "gx", None),
        P(),
        P(),
    )
    return jax.shard_map(
        on_device,
        mesh=mesh,
        in_specs=placed,
        out_specs=placed[:5],
        check_vma=False,
    )
```

```python
import functools

import jax
import jax.numpy as jnp
from jax import lax
from jax.experimental import pallas as pl
from jax.experimental.pallas import tpu as pltpu
from jax.sharding import PartitionSpec as P


STEPS = 4
KERR = 3
ADVANCE = 2
HALF = 0.5

D, E, H, EPS, CHI = 0, 3, 6, 9, 10
ALL = range(11)
NZL, NXL, NY = 8, 32, 128
XH = 4
ROWS = NXL + 2 * XH
EDGE = 24

DP, HP, INV = 11, 14, 17
RAW = [(E + c, 0) for c in range(3)] + [(c, p) for p in range(3) for c in (EPS, CHI)]
HI = RAW + [(DP + c, p) for p in range(3) for c in range(3)] + [(HP + c, p) for p in range(2) for c in range(3)]
HI += [(INV, 1), (INV, 2)]
HI_ROWS = {8: range(8), 6: (0, 1, 2, 5, 6, 7), 4: (0, 1, 6, 7), 2: (0, 7)}
LO_ROWS = {8: range(8), 6: (0, 1, 2, 3, 6, 7), 4: (0, 1, 2, 7), 2: ()}


def slot_rows(comp, p):
    if (comp, p) == (E, 0):
        return 8
    level = p + (HP <= comp < INV)
    return 6 - 2 * p if comp < HP or comp >= INV else 6 - 2 * (level - 1)


WIDTH = [slot_rows(*k) for k in HI]
HALO_AT = [sum(WIDTH[:i]) for i in range(len(HI))]
LO = [None] * len(HI)
_wide = [i for i, n in enumerate(WIDTH) if n >= 6]
_thin = [i for i, n in enumerate(WIDTH) if n == 4]
for _k in [(E + c, 7) for c in range(3)] + [(H + c, 7) for c in range(3)]:
    LO[_wide.pop(0)] = _k
for _k in [(D + c, 7) for c in range(3)] + [(EPS, 7), (CHI, 7), (H, 6), (H + 1, 6)]:
    LO[_thin.pop(0)] = _k
HI_AT = {k: i for i, k in enumerate(HI)}
LO_AT = {k: i for i, k in enumerate(LO) if k}
NS, NR = len(HI), len(RAW)
NEW_AT = -(-sum(WIDTH) // 8) * 8
LATE = NEW_AT + 8 * (NS - NR)

FOUR, THREE = (E, E + 1, E + 2, H + 1, H + 2), (D, D + 1, D + 2, H, EPS, CHI)
NF = len(FOUR) * NZL * 4
NHALO = NF + len(THREE) * NZL * 3

VM = pl.BlockSpec(memory_space=pltpu.VMEM)
HBM = pl.BlockSpec(memory_space=pltpu.HBM)
SM = pl.BlockSpec(memory_space=pltpu.SMEM)


def shape(*dims):
    return jax.ShapeDtypeStruct(dims, jnp.float32)


def rows(*parts):
    return jnp.concatenate(parts, axis=0)


def scalar(condition):
    return jnp.where(condition, 1.0, 0.0).astype(jnp.float32)


def position():
    gz, gx = lax.axis_index("gz"), lax.axis_index("gx")
    return gz, gx, lax.axis_size("gz") - 1, lax.axis_size("gx") - 1


def halo_row():
    return lax.broadcasted_iota(jnp.int32, (8, NY), 0)


def inside_x():
    _, gx, _, last = position()
    return jnp.where(halo_row() < XH, scalar(gx != last), scalar(gx != 0))


class Grid:
    def __init__(self, size, factor, fill):
        self.size, self.factor, self.fill = size, factor, fill
        self.where, self.level = {}, {}
        lane = lax.broadcasted_iota(jnp.int32, (size, NY), 1)
        self.last_y, self.first_y = lane == NY - 1, lane == 0

    def hold(self, comp, plane, read, level=0):
        self.where[(comp, plane)] = read
        self.level[(comp, plane)] = level

    def get(self, comp, plane, level=None):
        assert level is None or self.level[(comp, plane)] == level, (comp, plane)
        return self.where[(comp, plane)]()

    def put(self, ref, index, comp, plane, value, level):
        ref[index] = value
        self.hold(comp, plane, lambda: ref[index], level)

    def next_y(self, v):
        return jnp.where(self.last_y, 0.0, pltpu.roll(v, NY - 1, 1))

    def prev_y(self, v):
        return jnp.where(self.first_y, 0.0, pltpu.roll(v, 1, 1))

    def next_x(self, v):
        return pltpu.roll(v, self.size - 1, 0)

    def prev_x(self, v):
        return pltpu.roll(v, 1, 0)

    def step_h(self, n, p, comps, put):
        f = self.factor(p)
        ex, ey, ez = (self.get(E + c, p, n - 1) for c in range(3))
        if self.level.get((HP, p)) == n:
            hx, hy, hz = (self.get(HP + c, p) for c in range(3))
            put(H, p, hx - f * ((self.next_y(ez) - ez) + ey), n)
            put(H + 1, p, hy + f * (ex + (self.next_x(ez) - ez)), n)
            put(H + 2, p, hz - f * ((self.next_x(ey) - ey) - (self.next_y(ex) - ex)), n)
            return
        new = {}
        if 0 in comps:
            eyn = self.get(E + 1, p + 1, n - 1)
            new[0] = (self.next_y(ez) - ez) - (eyn - ey)
        if 1 in comps:
            exn = self.get(E, p + 1, n - 1)
            new[1] = (exn - ex) - (self.next_x(ez) - ez)
        if 2 in comps:
            new[2] = (self.next_x(ey) - ey) - (self.next_y(ex) - ex)
        for c, curl in new.items():
            put(H + c, p, self.get(H + c, p, n - 1) - f * curl, n)

    def medium(self, p):
        eps, fill = self.get(EPS, p), self.fill(p)
        return eps if fill is None else eps + fill, self.get(CHI, p)

    def first_inverse(self, n, p):
        ex, ey, ez = (self.get(E + c, p, n) for c in range(3))
        eps, chi = self.medium(p)
        return 1.0 / (eps + chi * (ex * ex + ey * ey + ez * ez))

    def derive(self):
        out = {}
        for p in range(3):
            f, n = self.factor(p), p + 1
            hx, hy, hz = (self.get(H + c, p, n) for c in range(3))
            dx, dy, dz = (self.get(D + c, p, n - 1) for c in range(3))
            out[(DP, p)] = dx + f * ((hz - self.prev_y(hz)) - hy)
            out[(DP + 1, p)] = dy + f * (hx - (hz - self.prev_x(hz)))
            out[(DP + 2, p)] = dz + f * ((hy - self.prev_x(hy)) - (hx - self.prev_y(hx)))
            if p < 2:
                out[(HP, p)] = hx + f * self.get(E + 1, p + 1, n)
                out[(HP + 1, p)] = hy - f * self.get(E, p + 1, n)
                out[(HP + 2, p)] = hz
            if p > 0:
                out[(INV, p)] = self.first_inverse(n - 1, p)
        return out

    def step_de(self, n, p, put):
        f = self.factor(p)
        hxp, hyp = (self.get(H + c, p - 1, n) for c in range(2))
        if self.level.get((DP, p)) == n:
            dx, dy, dz = (self.get(DP + c, p) for c in range(3))
            dx, dy = dx + f * hyp, dy - f * hxp
        else:
            hx, hy, hz = (self.get(H + c, p, n) for c in range(3))
            dx = self.get(D, p, n - 1) + f * ((hz - self.prev_y(hz)) - (hy - hyp))
            dy = self.get(D + 1, p, n - 1) + f * ((hx - hxp) - (hz - self.prev_x(hz)))
            dz = self.get(D + 2, p, n - 1) + f * ((hy - self.prev_x(hy)) - (hx - self.prev_y(hx)))
        eps, chi = self.medium(p)
        inverse = self.get(INV, p) if self.level.get((INV, p)) == n else self.first_inverse(n - 1, p)
        if n == STEPS:
            dx, dy, dz, eps, chi, inverse = (v[:NXL] for v in (dx, dy, dz, eps, chi, inverse))
        squares = chi * (dx * dx + dy * dy + dz * dz)
        for _ in range(KERR - 1):
            inverse = 1.0 / (eps + squares * (inverse * inverse))
        for c, v in enumerate((dx, dy, dz)):
            put(D + c, p, v, n)
            put(E + c, p, v * inverse, n)

    def sweep(self, n, h_planes, de_planes, put):
        for p in range(-2, 11):
            if p in h_planes:
                self.step_h(n, p, range(3), put)
            if p in de_planes:
                self.step_de(n, p, put)


def own(fields, comp, plane):
    d, e, h, eps, chi = fields
    if comp < E:
        return d[comp, plane]
    if comp < H:
        return e[comp - E, plane]
    if comp < EPS:
        return h[comp - H, plane]
    return eps[plane] if comp == EPS else chi[plane]


def halo_slot(comp, p):
    if comp in FOUR:
        return (FOUR.index(comp) * NZL + p) * 4, 4
    return NF + (THREE.index(comp) * NZL + p) * 3, 3


def load(d, e, h, eps, chi, dv, ev, hv, epsv, chiv, ya, yb, sems):
    held = (dv, ev, hv, epsv, chiv)
    copies = [pltpu.make_async_copy(a, b, sems.at[i]) for i, (a, b) in enumerate(zip((d, e, h, eps, chi), held))]
    for c in copies:
        c.start()
    _, gx, _, last = position()
    even = lax.rem(gx, 2) == 0
    keep = scalar(jnp.logical_and(gx != 0, gx != last))
    for comps, copy in zip((range(D, E), range(E, H), range(H, EPS), (EPS,), (CHI,)), copies):
        copy.wait()
        for comp in comps:
            for p in range(NZL):
                at, n = halo_slot(comp, p)
                v = own(held, comp, p)
                low, high = v[0:n], v[NXL - n :]
                ya[at : at + n] = jnp.where(even, high, low)
                yb[at : at + n] = jnp.where(even, low, high) * keep


def mark(out):
    out[...] = inside_x()


def early(grid, put):
    grid.sweep(1, range(0, 5), range(1, 5), put)
    grid.sweep(2, range(1, 4), range(2, 4), put)
    grid.sweep(3, range(2, 3), (), put)


def lookup(classes, table):
    labels = jnp.arange(table.shape[0], dtype=jnp.int32).reshape(-1, 1, 1, 1)
    picked = jnp.where(classes[None] == labels, table.reshape(-1, 1, 1, 1), jnp.float32(0.0))
    return jnp.sum(picked, axis=0)


def payload(grid, side):
    made = grid.derive() if side is HI else {}
    return [k and (made[k] if k in made else grid.get(*k)) for k in side]


def inner(d, e, h, eps, chi, fd, fe, fh, lo, out):
    fields = (d, e, h, eps, chi)
    grid = Grid(NXL, lambda p: HALF, lambda p: None)
    for comp in ALL:
        for p in range(NZL):
            grid.hold(comp, p, functools.partial(own, fields, comp, p))
    grid.step_h(1, 6, range(2), lambda c, p, v, n: grid.put(lo, c - H, c, p, v, n))

    def put(c, p, v, n):
        ref = (fd, fe, fh)[c // 3]
        grid.put(ref, (c % 3, p), c, p, v, n)

    early(grid, put)
    gz, _, last, _ = position()
    first_core = lax.rem(gz, 2) == 0
    keep = scalar(jnp.logical_and(gz != 0, gz != last))
    half = halo_row() < XH
    low = payload(grid, LO)
    for i, v in enumerate(payload(grid, HI)):
        if low[i] is not None:
            v = jnp.where(first_core, v, low[i])
        v = v * keep
        out[24 * i : 24 * i + 8] = jnp.where(half, v[24:32], v[0:8])
        out[24 * i + 8 : 24 * i + 24] = v[8:24]
        if i < NR:
            out[24 * NS + 8 * i : 24 * NS + 8 * i + 8] = jnp.where(half, v[0:8], v[24:32])


def edge_grid(inside, fields, tile):
    f = rows(jnp.full((8, NY), HALF), inside * HALF, jnp.full((8, NY), HALF))
    none = jnp.zeros((8, NY), jnp.float32)
    fill = rows(none, 1.0 - inside, none)
    grid = Grid(EDGE, lambda p: f, lambda p: fill)

    def read(comp, p):
        v = own(fields, comp, p)
        return rows(v[24:32], tile(comp, p), v[0:8])

    for comp in ALL:
        for p in range(NZL):
            grid.hold(comp, p, functools.partial(read, comp, p))
    return grid


def joined(a, b, comp, p):
    _, gx, _, _ = position()
    even = lax.rem(gx, 2) == 0
    at, n = halo_slot(comp, p)
    a, b = a[at : at + n], b[at : at + n]
    above, below = jnp.where(even, a, b), jnp.where(even, b, a)
    if n == 4:
        return rows(above, below)
    return rows(above, above[2:3], below[0:1], below)


def edges(d, e, h, eps, chi, ra, rb, inside, xt, sd, se, sh, slo, cross):
    fields = (d, e, h, eps, chi)
    gz, _, last, _ = position()
    keep = scalar(jnp.logical_and(gz != 0, gz != last))
    half = halo_row() < XH
    for comp in ALL:
        for p in range(NZL):
            xt[comp, p] = joined(ra, rb, comp, p)

    def pack(grid, side, chosen):
        for i, v in enumerate(payload(grid, side)):
            if v is None:
                continue
            v = v * keep
            at, n = HALO_AT[i], WIDTH[i]
            runs = []
            for r in chosen[n]:
                if runs and runs[-1][1] == r:
                    runs[-1][1] = r + 1
                else:
                    runs.append([r, r + 1])
            for a, b in runs:
                cross[at : at + b - a] = v[8 + a : 8 + b]
                at += b - a
            if i >= NR:
                at = NEW_AT + 8 * (i - NR)
                cross[at : at + 8] = jnp.where(half, v[16:24], v[0:8])

    @pl.when(lax.rem(gz, 2) == 0)
    def _():
        grid = edge_grid(inside[...], fields, lambda comp, p: xt[comp, p])
        early(grid, lambda c, p, v, n: grid.put((sd, se, sh)[c // 3], (c % 3, p), c, p, v, n))
        pack(grid, HI, HI_ROWS)

    @pl.when(lax.rem(gz, 2) == 1)
    def _():
        grid = edge_grid(inside[...], fields, lambda comp, p: xt[comp, p])
        grid.step_h(1, 6, range(2), lambda c, p, v, n: grid.put(slo, c - H, c, p, v, n))
        pack(grid, LO, LO_ROWS)


def merge(d, e, h, eps, chi, id_, ie, ih, ilo, xt, sd, se, sh, slo, inside, fd, fe, fh, chip, td, te, th, tlo):
    fields = (d, e, h, eps, chi)
    half = halo_row() < XH

    def merged(v, w):
        return rows(jnp.where(half, w[16:24], v[0:8]), v[8:24], jnp.where(half, v[24:32], w[0:8]), w[8:16])

    def join(sides, side):
        grid = full_grid()
        hold_own(grid, fields, xt)
        for k, (v, w, ref) in enumerate(((id_, sides[0], fd), (ie, sides[1], fe), (ih, sides[2], fh))):
            for p, level in EARLY[k].items():
                for c in range(3):
                    grid.put(ref, (c, p), 3 * k + c, p, merged(v[c, p], w[c, p]), level)
        for c in range(2):
            grid.hold(H + c, 6, functools.partial(lambda a: merged(ilo[a], tlo[a]), c))
        for i, v in enumerate(payload(grid, side)):
            if v is not None:
                chip[i] = v

    gz, _, _, _ = position()

    @pl.when(lax.rem(gz, 2) == 0)
    def _():
        grid = edge_grid(inside[...], fields, lambda comp, p: xt[comp, p])
        grid.step_h(1, 6, range(2), lambda c, p, v, n: grid.put(tlo, c - H, c, p, v, n))
        join((sd, se, sh), LO)

    @pl.when(lax.rem(gz, 2) == 1)
    def _():
        grid = edge_grid(inside[...], fields, lambda comp, p: xt[comp, p])
        early(grid, lambda c, p, v, n: grid.put((td, te, th)[c // 3], (c % 3, p), c, p, v, n))
        join((td, te, th), HI)


def full_grid():
    gz, _, last, _ = position()
    up, down = scalar(gz != last), scalar(gz != 0)
    edge = inside_x()

    def inside(p):
        return up if p >= NZL else (down if p < 0 else None)

    def factor(p):
        z = inside(p)
        main, tile = jnp.full((NXL, NY), HALF, jnp.float32), edge * HALF
        return rows(main, tile) if z is None else rows(main * z, tile * z)

    def fill(p):
        z = inside(p)
        if z is None:
            return rows(jnp.zeros((NXL, NY), jnp.float32), 1.0 - edge)
        return rows(jnp.full((NXL, NY), 1.0 - z, jnp.float32), 1.0 - edge * z)

    return Grid(ROWS, factor, fill)


def hold_own(grid, fields, xt):
    for comp in ALL:
        for p in range(NZL):
            grid.hold(comp, p, functools.partial(lambda c, q: rows(own(fields, c, q), xt[c, q]), comp, p))


def hold_frames(grid, refs, levels, size=ROWS):
    for k, ref in enumerate(refs):
        for p, level in levels[k].items():
            for c in range(3):
                grid.hold(3 * k + c, p, functools.partial(lambda r, a, b: r[a, b, 0:size], ref, c, p), level)


EARLY = ({1: 1, 2: 2, 3: 2, 4: 1}, {1: 1, 2: 2, 3: 2, 4: 1}, {0: 1, 1: 2, 2: 3, 3: 2, 4: 1})
MIDDLE = ({3: 3, 4: 3, 5: 2, 6: 1}, {3: 3, 4: 3, 5: 2, 6: 1}, {3: 4, 4: 3, 5: 2, 6: 1})


def middle(d, e, h, eps, chi, xt, fd, fe, fh, gd, ge, gh):
    grid = full_grid()
    hold_own(grid, (d, e, h, eps, chi), xt)
    hold_frames(grid, (fd, fe, fh), EARLY)

    def put(c, p, v, n):
        grid.put((gd, ge, gh)[c // 3], (c % 3, p), c, p, v, n)

    grid.sweep(1, (5, 6), (5, 6), put)
    grid.sweep(2, (4, 5), (4, 5), put)
    grid.sweep(3, (3, 4), (3, 4), put)
    grid.sweep(4, (3,), (), put)


def hold_side(grid, high, read):
    at, shift = (HI_AT, NZL) if high else (LO_AT, -NZL)
    for (comp, p), i in at.items():
        level = int(p == 6)
        if comp >= DP:
            level = p + 2 if HP <= comp < INV else p + 1
        grid.hold(comp, p + shift, functools.partial(read, i), level)


def chain(grid, high, put, keep, done=lambda o: None):
    if high:
        grid.sweep(1, (7,), (7, 8), put)
        grid.sweep(2, range(6, 9), range(6, 10), put)
        grid.sweep(3, range(5, 10), range(5, 11), put)
        h_planes, de_planes = range(4, 10), range(4, 10)
    else:
        grid.sweep(1, (-1,), (-1, 0), put)
        grid.sweep(2, (-1, 0), (0, 1), put)
        grid.sweep(3, (0, 1), (1, 2), put)
        h_planes, de_planes = (1, 2), (2, 3)
    for p in sorted(set(h_planes) | set(de_planes)):
        if p in h_planes:
            grid.step_h(STEPS, p, range(3), put)
        if p in de_planes:
            if p not in h_planes:
                for c in range(3):
                    keep(c, p - ADVANCE, grid.get(H + c, p, STEPS))
            grid.step_de(STEPS, p, put)
            done(p - ADVANCE)


KEPT = NZL - ADVANCE


def near(d, e, h, eps, chi, xt, fd, fe, fh, gd, ge, gh, cc, nd, ne, nh, neps, nchi, *state):
    gz, _, _, _ = position()

    def side(high):
        grid = full_grid()
        hold_own(grid, (d, e, h, eps, chi), xt)
        hold_frames(grid, (fd, fe, fh), EARLY)
        hold_frames(grid, (gd, ge, gh), MIDDLE)
        hold_side(grid, high, lambda i: cc[i])

        def put(c, p, v, n):
            k = c // 3
            if n == STEPS and p >= ADVANCE:
                (nd, ne, nh)[k][c % 3, p - ADVANCE] = v[:NXL]
            if n < STEPS or k == 2:
                grid.put(state[k], (c % 3, p + 2), c, p, v, n)

        def keep(c, o, v):
            nh[c, o] = v[:NXL]

        chain(grid, high, put, keep)
        if high:
            for out, comp in ((neps, EPS), (nchi, CHI)):
                for o in range(ADVANCE):
                    out[o] = grid.get(comp, NZL + o)[:NXL]

    pl.when(lax.rem(gz, 2) == 0)(lambda: side(True))
    pl.when(lax.rem(gz, 2) == 1)(lambda: side(False))


def ahead(d, e, h, eps, chi, fd, fe, fh, gd, ge, gh, ca, eps_in, chi_in, nd, ne, nh, neps, nchi, *rest):
    outs, (ie, ih, od, oe, oh, oeps, ochi, sd, sems) = rest[:5], rest[5:]
    gz, _, last, _ = position()
    half = halo_row() < XH

    def read(i):
        m = ca[24 * i : 24 * i + 8]
        x = ca[24 * NS + 8 * i : 24 * NS + 8 * i + 8] if i < NR else m
        return rows(jnp.where(half, x, m), ca[24 * i + 8 : 24 * i + 24], jnp.where(half, m, x))

    def side(high):
        there = pl.ds(0, ADVANCE) if high else pl.ds(ADVANCE, KEPT)
        moves = [(a.at[:, there], b.at[:, there]) for a, b in zip((nd, ne, nh), outs)]
        moves += [(a.at[pl.ds(ADVANCE, KEPT)], b.at[pl.ds(0, KEPT)]) for a, b in zip((eps, chi), outs[3:])]
        if not high:
            moves += [(a, b.at[pl.ds(KEPT, ADVANCE)]) for a, b in zip((neps, nchi), outs[3:])]
        copies = [pltpu.make_async_copy(a, b, sems.at[i]) for i, (a, b) in enumerate(moves)]
        for c in copies:
            c.start()
        z = scalar(gz != last) if high else scalar(gz != 0)

        def own_plane(p):
            return 0 <= p < NZL

        grid = Grid(NXL, lambda p: HALF if own_plane(p) else HALF * z, lambda p: None if own_plane(p) else 1.0 - z)
        for comp in ALL:
            for p in range(NZL):
                grid.hold(comp, p, functools.partial(own, (d, e, h, eps, chi), comp, p))
        hold_frames(grid, (fd, fe, fh), EARLY, NXL)
        hold_frames(grid, (gd, ge, gh), MIDDLE, NXL)
        hold_side(grid, high, read)

        def put(c, p, v, n):
            k = c // 3
            if n == STEPS and p >= ADVANCE:
                (od, oe, oh)[k][c % 3, p - ADVANCE] = v
            if k == 2:
                grid.put(ih, (n - 1, c % 3, p + 2), c, p, v, n)
            elif n < STEPS and k == 1:
                grid.put(ie, (n - 1, c % 3, p + 2), c, p, v, n)
            elif n < STEPS:
                grid.put(sd, (c % 3, p + 2), c, p, v, n)

        def keep(c, o, v):
            oh[c, o] = v

        chain(grid, high, put, keep)
        if high:
            for out, comp, new in ((oeps, EPS, eps_in), (ochi, CHI, chi_in)):
                for o in range(ADVANCE):
                    out[o] = jnp.where(gz == last, new[o], grid.get(comp, NZL + o))
        for c in copies:
            c.wait()

    pl.when(lax.rem(gz, 2) == 0)(lambda: side(False))
    pl.when(lax.rem(gz, 2) == 1)(lambda: side(True))


def far(d, e, h, eps, chi, xt, fd, fe, fh, gd, ge, gh, ca, cb, *rest):
    ie, ih, od, oe, oh, oeps, ochi = rest[:7]
    outs, state, edge, sems = rest[12:17], rest[17:20], rest[20:23], rest[23]
    half = halo_row() < XH
    gz, _, _, _ = position()

    def cross(chosen, i):
        m = ca[24 * i : 24 * i + 8]
        x = ca[24 * NS + 8 * i : 24 * NS + 8 * i + 8] if i < NR else cb[NEW_AT + 8 * (i - NR) : NEW_AT + 8 * (i - NR) + 8]
        at, kept = HALO_AT[i], list(chosen[WIDTH[i]])
        v = cb[at : at + WIDTH[i]]
        if len(kept) < 8:
            near_row = [max([k for k in kept if k <= r], default=kept[0]) for r in range(8)]
            v = rows(*[v[kept.index(k) : kept.index(k) + 1] for k in near_row])
        return rows(jnp.where(half, x, m), ca[24 * i + 8 : 24 * i + 24], jnp.where(half, m, x), v)

    def side(high):
        copies = []

        def send(source, target):
            copies.append(pltpu.make_async_copy(source, target, sems.at[len(copies)]))
            copies[-1].start()

        here = pl.ds(ADVANCE, KEPT) if high else pl.ds(0, ADVANCE)
        for a, out in zip((od, oe, oh), outs):
            send(a.at[:, here, pl.ds(8, 16)], out.at[:, here, pl.ds(8, 16)])
        if high:
            for a, out in zip((oeps, ochi), outs[3:]):
                send(a, out.at[pl.ds(KEPT, ADVANCE)])

        grid = full_grid()
        hold_own(grid, (d, e, h, eps, chi), xt)
        hold_frames(grid, (fd, fe, fh), EARLY)
        hold_frames(grid, (gd, ge, gh), MIDDLE)
        hold_side(grid, high, functools.partial(cross, HI_ROWS if high else LO_ROWS))
        none = jnp.zeros((16, NY), jnp.float32)

        def result(k, c, o, v):
            edge[k][c, o, 0:8] = v[0:8]
            edge[k][c, o, 8:16] = v[24:32]

        def put(c, p, v, n):
            k, at = c // 3, (c % 3, p + 2)
            if n == STEPS and p >= ADVANCE:
                result(k, c % 3, p - ADVANCE, v)
            if n < STEPS or k == 2:
                ref, inner_ref = state[k], (None, ie, ih)[k]
                ref[(*at, slice(0, 8))] = v[0:8]
                ref[(*at, slice(8, 24))] = v[24:40]

                def read():
                    mid = none if inner_ref is None else inner_ref[(n - 1, *at, slice(8, 24))]
                    return rows(ref[(*at, slice(0, 8))], mid, ref[(*at, slice(8, 24))])

                grid.hold(c, p, read, n)

        def done(o):
            for k in range(3):
                for a, b in ((0, 0), (8, 24)):
                    send(edge[k].at[:, pl.ds(o, 1), pl.ds(a, 8)], outs[k].at[:, pl.ds(o, 1), pl.ds(b, 8)])

        chain(grid, high, put, functools.partial(result, 2), done)
        for c in copies:
            c.wait()

    pl.when(lax.rem(gz, 2) == 0)(lambda: side(False))
    pl.when(lax.rem(gz, 2) == 1)(lambda: side(True))


def swapped(shard, axis, first):
    n = {a: lax.axis_size(a) for a in ("gz", "gx")}
    moves = []
    for z in range(n["gz"]):
        for x in range(n["gx"]):
            at = z if axis == "gz" else x
            to = at + 1 if at % 2 == first else at - 1
            if 0 <= to < n[axis]:
                other = (to, x) if axis == "gz" else (z, to)
            else:
                other = (z ^ 1, x) if axis == "gx" else (z, x ^ 1)
            moves.append((z * n["gx"] + x, other[0] * n["gx"] + other[1]))
    return lax.ppermute(shard, ("gz", "gx"), moves)


def call(body, inputs, out_shape, scratch=(), vmem=8, specs=None, out=VM, aliases=None):
    return pl.pallas_call(
        body,
        out_shape=out_shape,
        in_specs=[VM] * len(inputs) if specs is None else specs,
        out_specs=out if isinstance(out, tuple) else (out,) * len(out_shape),
        input_output_aliases=aliases or {},
        scratch_shapes=list(scratch),
        compiler_params=pltpu.CompilerParams(vmem_limit_bytes=vmem << 20),
    )(*inputs)


def on_device(d_field, e_field, h_field, permittivity, kerr_coeff, classes, eps_table, chi_table):
    field, medium = shape(3, NZL, NXL, NY), shape(NZL, NXL, NY)
    halo = shape(NHALO, NY)
    *fields, ya, yb = call(
        load,
        [pltpu.with_memory_space_constraint(a, pltpu.HBM) for a in (d_field, e_field, h_field, permittivity, kerr_coeff)],
        (field, field, field, medium, medium, halo, halo),
        [pltpu.SemaphoreType.DMA((5,))],
        specs=[HBM] * 5,
    )
    ra, rb = swapped(ya, "gx", 0), swapped(yb, "gx", 1)
    lo = shape(2, NXL, NY)
    *inside, za = call(inner, fields, (*[shape(3, 5, NXL, NY)] * 3, lo, shape(24 * NS + 8 * NR, NY)))
    ca = swapped(za, "gz", 1)
    (edge,) = call(mark, [], (shape(8, NY),))
    thin = [(3, 5, EDGE, NY)] * 3 + [(2, EDGE, NY)]
    xt, *outside, zb = call(
        edges, [*fields, ra, rb, edge], (shape(11, NZL, 8, NY), *[shape(*t) for t in thin], shape(LATE, NY))
    )
    cb = swapped(zb, "gz", 1)
    coming = lookup(classes, eps_table), lookup(classes, chi_table)
    *frames, zc = call(
        merge,
        [*fields, *inside, xt, *outside, edge],
        (*[shape(3, 5, ROWS, NY)] * 3, shape(NS, ROWS, NY)),
        [pltpu.VMEM(t, jnp.float32) for t in thin],
    )
    cc = swapped(zc, "gz", 0)
    more = call(middle, [*fields, xt, *frames], (shape(3, 7, ROWS, NY),) * 3)
    state = [pltpu.VMEM((3, 13, ROWS, NY), jnp.float32)] * 3
    two = shape(ADVANCE, NXL, NY)
    made = call(near, [*fields, xt, *frames, *more, cc], (field, field, field, two, two), state, vmem=16)
    levels = shape(STEPS - 1, 3, 13, NXL, NY), shape(STEPS, 3, 13, NXL, NY)
    results = (field, field, field, medium, medium)
    *outs, ie, ih, od, oe, oh, oeps, ochi = call(
        ahead,
        [*fields, *frames, *more, ca, *coming, *made],
        (*results, *levels, field, field, field, two, two),
        [pltpu.VMEM((3, 13, NXL, NY), jnp.float32), pltpu.SemaphoreType.DMA((8,))],
        vmem=16,
        out=(HBM,) * 5 + (VM,) * 7,
    )
    thin = [pltpu.VMEM((3, 13, EDGE, NY), jnp.float32)] * 3 + [pltpu.VMEM((3, NZL, 16, NY), jnp.float32)] * 3
    given = [*fields, xt, *frames, *more, ca, cb, ie, ih, od, oe, oh, oeps, ochi]
    n = len(given)
    return call(
        far,
        [*given, *outs],
        results,
        [*thin, pltpu.SemaphoreType.DMA((48,))],
        vmem=16,
        specs=[VM] * n + [HBM] * 5,
        out=HBM,
        aliases={n + k: k for k in range(5)},
    )


def solution(mesh):
    placed = (
        P(None, "gz", "gx", None),
        P(None, "gz", "gx", None),
        P(None, "gz", "gx", None),
        P("gz", "gx", None),
        P("gz", "gx", None),
        P(None, "gx", None),
        P(),
        P(),
    )
    return jax.shard_map(
        on_device,
        mesh=mesh,
        in_specs=placed,
        out_specs=placed[:5],
        check_vma=False,
    )
```

```python
import functools

import jax
import jax.numpy as jnp
from jax import lax
from jax.experimental import pallas as pl
from jax.experimental.pallas import tpu as pltpu
from jax.sharding import PartitionSpec as P


STEPS = 4
KERR = 3
ADVANCE = 2
HALF = 0.5

D, E, H, EPS, CHI = 0, 3, 6, 9, 10
ALL = range(11)
NZL, NXL, NY = 8, 32, 128
XH = 4
ROWS = NXL + 2 * XH
EDGE = 24

DP, HP, INV = 11, 14, 17
RAW = [(E + c, 0) for c in range(3)] + [(c, p) for p in range(3) for c in (EPS, CHI)]
HI = RAW + [(DP + c, p) for p in range(3) for c in range(3)] + [(HP + c, p) for p in range(2) for c in range(3)]
HI += [(INV, 1), (INV, 2)]
HI_ROWS = {8: range(8), 6: (0, 1, 2, 5, 6, 7), 4: (0, 1, 6, 7), 2: (0, 7)}
LO_ROWS = {8: range(8), 6: (0, 1, 2, 3, 6, 7), 4: (0, 1, 2, 7), 2: ()}


def slot_rows(comp, p):
    if (comp, p) == (E, 0):
        return 8
    level = p + (HP <= comp < INV)
    return 6 - 2 * p if comp < HP or comp >= INV else 6 - 2 * (level - 1)


WIDTH = [slot_rows(*k) for k in HI]
HALO_AT = [sum(WIDTH[:i]) for i in range(len(HI))]
LO = [None] * len(HI)
_wide = [i for i, n in enumerate(WIDTH) if n >= 6]
_thin = [i for i, n in enumerate(WIDTH) if n == 4]
for _k in [(E + c, 7) for c in range(3)] + [(H + c, 7) for c in range(3)]:
    LO[_wide.pop(0)] = _k
for _k in [(D + c, 7) for c in range(3)] + [(EPS, 7), (CHI, 7), (H, 6), (H + 1, 6)]:
    LO[_thin.pop(0)] = _k
HI_AT = {k: i for i, k in enumerate(HI)}
LO_AT = {k: i for i, k in enumerate(LO) if k}
NS, NR = len(HI), len(RAW)
NEW_AT = -(-sum(WIDTH) // 8) * 8
LATE = NEW_AT + 8 * (NS - NR)

FOUR, THREE = (E, E + 1, E + 2, H + 1, H + 2), (D, D + 1, D + 2, H, EPS, CHI)
NF = len(FOUR) * NZL * 4
NHALO = NF + len(THREE) * NZL * 3

VM = pl.BlockSpec(memory_space=pltpu.VMEM)
HBM = pl.BlockSpec(memory_space=pltpu.HBM)
SM = pl.BlockSpec(memory_space=pltpu.SMEM)


def shape(*dims):
    return jax.ShapeDtypeStruct(dims, jnp.float32)


def rows(*parts):
    return jnp.concatenate(parts, axis=0)


def scalar(condition):
    return jnp.where(condition, 1.0, 0.0).astype(jnp.float32)


def position():
    gz, gx = lax.axis_index("gz"), lax.axis_index("gx")
    return gz, gx, lax.axis_size("gz") - 1, lax.axis_size("gx") - 1


def halo_row():
    return lax.broadcasted_iota(jnp.int32, (8, NY), 0)


def inside_x():
    _, gx, _, last = position()
    return jnp.where(halo_row() < XH, scalar(gx != last), scalar(gx != 0))


class Grid:
    def __init__(self, size, factor, fill):
        self.size, self.factor, self.fill = size, factor, fill
        self.where, self.level = {}, {}
        lane = lax.broadcasted_iota(jnp.int32, (size, NY), 1)
        self.last_y, self.first_y = lane == NY - 1, lane == 0

    def hold(self, comp, plane, read, level=0):
        self.where[(comp, plane)] = read
        self.level[(comp, plane)] = level

    def get(self, comp, plane, level=None):
        assert level is None or self.level[(comp, plane)] == level, (comp, plane)
        return self.where[(comp, plane)]()

    def put(self, ref, index, comp, plane, value, level):
        ref[index] = value
        self.hold(comp, plane, lambda: ref[index], level)

    def next_y(self, v):
        return jnp.where(self.last_y, 0.0, pltpu.roll(v, NY - 1, 1))

    def prev_y(self, v):
        return jnp.where(self.first_y, 0.0, pltpu.roll(v, 1, 1))

    def next_x(self, v):
        return pltpu.roll(v, self.size - 1, 0)

    def prev_x(self, v):
        return pltpu.roll(v, 1, 0)

    def step_h(self, n, p, comps, put):
        f = self.factor(p)
        ex, ey, ez = (self.get(E + c, p, n - 1) for c in range(3))
        if self.level.get((HP, p)) == n:
            hx, hy, hz = (self.get(HP + c, p) for c in range(3))
            put(H, p, hx - f * ((self.next_y(ez) - ez) + ey), n)
            put(H + 1, p, hy + f * (ex + (self.next_x(ez) - ez)), n)
            put(H + 2, p, hz - f * ((self.next_x(ey) - ey) - (self.next_y(ex) - ex)), n)
            return
        new = {}
        if 0 in comps:
            eyn = self.get(E + 1, p + 1, n - 1)
            new[0] = (self.next_y(ez) - ez) - (eyn - ey)
        if 1 in comps:
            exn = self.get(E, p + 1, n - 1)
            new[1] = (exn - ex) - (self.next_x(ez) - ez)
        if 2 in comps:
            new[2] = (self.next_x(ey) - ey) - (self.next_y(ex) - ex)
        for c, curl in new.items():
            put(H + c, p, self.get(H + c, p, n - 1) - f * curl, n)

    def medium(self, p):
        eps, fill = self.get(EPS, p), self.fill(p)
        return eps if fill is None else eps + fill, self.get(CHI, p)

    def first_inverse(self, n, p):
        ex, ey, ez = (self.get(E + c, p, n) for c in range(3))
        eps, chi = self.medium(p)
        return 1.0 / (eps + chi * (ex * ex + ey * ey + ez * ez))

    def derive(self):
        out = {}
        for p in range(3):
            f, n = self.factor(p), p + 1
            hx, hy, hz = (self.get(H + c, p, n) for c in range(3))
            dx, dy, dz = (self.get(D + c, p, n - 1) for c in range(3))
            out[(DP, p)] = dx + f * ((hz - self.prev_y(hz)) - hy)
            out[(DP + 1, p)] = dy + f * (hx - (hz - self.prev_x(hz)))
            out[(DP + 2, p)] = dz + f * ((hy - self.prev_x(hy)) - (hx - self.prev_y(hx)))
            if p < 2:
                out[(HP, p)] = hx + f * self.get(E + 1, p + 1, n)
                out[(HP + 1, p)] = hy - f * self.get(E, p + 1, n)
                out[(HP + 2, p)] = hz
            if p > 0:
                out[(INV, p)] = self.first_inverse(n - 1, p)
        return out

    def step_de(self, n, p, put):
        f = self.factor(p)
        hxp, hyp = (self.get(H + c, p - 1, n) for c in range(2))
        if self.level.get((DP, p)) == n:
            dx, dy, dz = (self.get(DP + c, p) for c in range(3))
            dx, dy = dx + f * hyp, dy - f * hxp
        else:
            hx, hy, hz = (self.get(H + c, p, n) for c in range(3))
            dx = self.get(D, p, n - 1) + f * ((hz - self.prev_y(hz)) - (hy - hyp))
            dy = self.get(D + 1, p, n - 1) + f * ((hx - hxp) - (hz - self.prev_x(hz)))
            dz = self.get(D + 2, p, n - 1) + f * ((hy - self.prev_x(hy)) - (hx - self.prev_y(hx)))
        eps, chi = self.medium(p)
        inverse = self.get(INV, p) if self.level.get((INV, p)) == n else self.first_inverse(n - 1, p)
        if n == STEPS:
            dx, dy, dz, eps, chi, inverse = (v[:NXL] for v in (dx, dy, dz, eps, chi, inverse))
        squares = chi * (dx * dx + dy * dy + dz * dz)
        for _ in range(KERR - 1):
            inverse = 1.0 / (eps + squares * (inverse * inverse))
        for c, v in enumerate((dx, dy, dz)):
            put(D + c, p, v, n)
            put(E + c, p, v * inverse, n)

    def sweep(self, n, h_planes, de_planes, put):
        for p in range(-2, 11):
            if p in h_planes:
                self.step_h(n, p, range(3), put)
            if p in de_planes:
                self.step_de(n, p, put)


def own(fields, comp, plane):
    d, e, h, eps, chi = fields
    if comp < E:
        return d[comp, plane]
    if comp < H:
        return e[comp - E, plane]
    if comp < EPS:
        return h[comp - H, plane]
    return eps[plane] if comp == EPS else chi[plane]


def halo_slot(comp, p):
    if comp in FOUR:
        return (FOUR.index(comp) * NZL + p) * 4, 4
    return NF + (THREE.index(comp) * NZL + p) * 3, 3


def load(d, e, h, eps, chi, dv, ev, hv, epsv, chiv, ya, yb, sems):
    held = (dv, ev, hv, epsv, chiv)
    copies = [pltpu.make_async_copy(a, b, sems.at[i]) for i, (a, b) in enumerate(zip((d, e, h, eps, chi), held))]
    for c in copies:
        c.start()
    _, gx, _, last = position()
    even = lax.rem(gx, 2) == 0
    keep = scalar(jnp.logical_and(gx != 0, gx != last))
    for comps, copy in zip((range(D, E), range(E, H), range(H, EPS), (EPS,), (CHI,)), copies):
        copy.wait()
        for comp in comps:
            for p in range(NZL):
                at, n = halo_slot(comp, p)
                v = own(held, comp, p)
                low, high = v[0:n], v[NXL - n :]
                ya[at : at + n] = jnp.where(even, high, low)
                yb[at : at + n] = jnp.where(even, low, high) * keep


def mark(out):
    out[...] = inside_x()


def early(grid, put):
    grid.sweep(1, range(0, 5), range(1, 5), put)
    grid.sweep(2, range(1, 4), range(2, 4), put)
    grid.sweep(3, range(2, 3), (), put)


def lookup(classes, table):
    labels = jnp.arange(table.shape[0], dtype=jnp.int32).reshape(-1, 1, 1, 1)
    picked = jnp.where(classes[None] == labels, table.reshape(-1, 1, 1, 1), jnp.float32(0.0))
    return jnp.sum(picked, axis=0)


def payload(grid, side):
    made = grid.derive() if side is HI else {}
    return [k and (made[k] if k in made else grid.get(*k)) for k in side]


def inner(d, e, h, eps, chi, fd, fe, fh, lo, out):
    fields = (d, e, h, eps, chi)
    grid = Grid(NXL, lambda p: HALF, lambda p: None)
    for comp in ALL:
        for p in range(NZL):
            grid.hold(comp, p, functools.partial(own, fields, comp, p))
    grid.step_h(1, 6, range(2), lambda c, p, v, n: grid.put(lo, c - H, c, p, v, n))

    def put(c, p, v, n):
        ref = (fd, fe, fh)[c // 3]
        grid.put(ref, (c % 3, p), c, p, v, n)

    early(grid, put)
    gz, _, last, _ = position()
    first_core = lax.rem(gz, 2) == 0
    keep = scalar(jnp.logical_and(gz != 0, gz != last))
    half = halo_row() < XH
    low = payload(grid, LO)
    for i, v in enumerate(payload(grid, HI)):
        if low[i] is not None:
            v = jnp.where(first_core, v, low[i])
        v = v * keep
        out[24 * i : 24 * i + 8] = jnp.where(half, v[24:32], v[0:8])
        out[24 * i + 8 : 24 * i + 24] = v[8:24]
        if i < NR:
            out[24 * NS + 8 * i : 24 * NS + 8 * i + 8] = jnp.where(half, v[0:8], v[24:32])


def edge_grid(inside, fields, tile):
    f = rows(jnp.full((8, NY), HALF), inside * HALF, jnp.full((8, NY), HALF))
    none = jnp.zeros((8, NY), jnp.float32)
    fill = rows(none, 1.0 - inside, none)
    grid = Grid(EDGE, lambda p: f, lambda p: fill)

    def read(comp, p):
        v = own(fields, comp, p)
        return rows(v[24:32], tile(comp, p), v[0:8])

    for comp in ALL:
        for p in range(NZL):
            grid.hold(comp, p, functools.partial(read, comp, p))
    return grid


def joined(a, b, comp, p):
    _, gx, _, _ = position()
    even = lax.rem(gx, 2) == 0
    at, n = halo_slot(comp, p)
    a, b = a[at : at + n], b[at : at + n]
    above, below = jnp.where(even, a, b), jnp.where(even, b, a)
    if n == 4:
        return rows(above, below)
    return rows(above, above[2:3], below[0:1], below)


def edges(d, e, h, eps, chi, ra, rb, inside, xt, sd, se, sh, slo, cross):
    fields = (d, e, h, eps, chi)
    gz, _, last, _ = position()
    keep = scalar(jnp.logical_and(gz != 0, gz != last))
    half = halo_row() < XH
    for comp in ALL:
        for p in range(NZL):
            xt[comp, p] = joined(ra, rb, comp, p)

    def pack(grid, side, chosen):
        for i, v in enumerate(payload(grid, side)):
            if v is None:
                continue
            v = v * keep
            at, n = HALO_AT[i], WIDTH[i]
            runs = []
            for r in chosen[n]:
                if runs and runs[-1][1] == r:
                    runs[-1][1] = r + 1
                else:
                    runs.append([r, r + 1])
            for a, b in runs:
                cross[at : at + b - a] = v[8 + a : 8 + b]
                at += b - a
            if i >= NR:
                at = NEW_AT + 8 * (i - NR)
                cross[at : at + 8] = jnp.where(half, v[16:24], v[0:8])

    @pl.when(lax.rem(gz, 2) == 0)
    def _():
        grid = edge_grid(inside[...], fields, lambda comp, p: xt[comp, p])
        early(grid, lambda c, p, v, n: grid.put((sd, se, sh)[c // 3], (c % 3, p), c, p, v, n))
        pack(grid, HI, HI_ROWS)

    @pl.when(lax.rem(gz, 2) == 1)
    def _():
        grid = edge_grid(inside[...], fields, lambda comp, p: xt[comp, p])
        grid.step_h(1, 6, range(2), lambda c, p, v, n: grid.put(slo, c - H, c, p, v, n))
        pack(grid, LO, LO_ROWS)


def merge(d, e, h, eps, chi, id_, ie, ih, ilo, xt, sd, se, sh, slo, inside, fd, fe, fh, chip, td, te, th, tlo):
    fields = (d, e, h, eps, chi)
    half = halo_row() < XH

    def merged(v, w):
        return rows(jnp.where(half, w[16:24], v[0:8]), v[8:24], jnp.where(half, v[24:32], w[0:8]), w[8:16])

    def join(sides, side):
        grid = full_grid()
        hold_own(grid, fields, xt)
        for k, (v, w, ref) in enumerate(((id_, sides[0], fd), (ie, sides[1], fe), (ih, sides[2], fh))):
            for p, level in EARLY[k].items():
                for c in range(3):
                    grid.put(ref, (c, p), 3 * k + c, p, merged(v[c, p], w[c, p]), level)
        for c in range(2):
            grid.hold(H + c, 6, functools.partial(lambda a: merged(ilo[a], tlo[a]), c))
        for i, v in enumerate(payload(grid, side)):
            if v is not None:
                chip[i] = v

    gz, _, _, _ = position()

    @pl.when(lax.rem(gz, 2) == 0)
    def _():
        grid = edge_grid(inside[...], fields, lambda comp, p: xt[comp, p])
        grid.step_h(1, 6, range(2), lambda c, p, v, n: grid.put(tlo, c - H, c, p, v, n))
        join((sd, se, sh), LO)

    @pl.when(lax.rem(gz, 2) == 1)
    def _():
        grid = edge_grid(inside[...], fields, lambda comp, p: xt[comp, p])
        early(grid, lambda c, p, v, n: grid.put((td, te, th)[c // 3], (c % 3, p), c, p, v, n))
        join((td, te, th), HI)


def full_grid():
    gz, _, last, _ = position()
    up, down = scalar(gz != last), scalar(gz != 0)
    edge = inside_x()

    def inside(p):
        return up if p >= NZL else (down if p < 0 else None)

    def factor(p):
        z = inside(p)
        main, tile = jnp.full((NXL, NY), HALF, jnp.float32), edge * HALF
        return rows(main, tile) if z is None else rows(main * z, tile * z)

    def fill(p):
        z = inside(p)
        if z is None:
            return rows(jnp.zeros((NXL, NY), jnp.float32), 1.0 - edge)
        return rows(jnp.full((NXL, NY), 1.0 - z, jnp.float32), 1.0 - edge * z)

    return Grid(ROWS, factor, fill)


def hold_own(grid, fields, xt):
    for comp in ALL:
        for p in range(NZL):
            grid.hold(comp, p, functools.partial(lambda c, q: rows(own(fields, c, q), xt[c, q]), comp, p))


def hold_frames(grid, refs, levels, size=ROWS):
    for k, ref in enumerate(refs):
        for p, level in levels[k].items():
            for c in range(3):
                grid.hold(3 * k + c, p, functools.partial(lambda r, a, b: r[a, b, 0:size], ref, c, p), level)


EARLY = ({1: 1, 2: 2, 3: 2, 4: 1}, {1: 1, 2: 2, 3: 2, 4: 1}, {0: 1, 1: 2, 2: 3, 3: 2, 4: 1})
MIDDLE = ({3: 3, 4: 3, 5: 2, 6: 1}, {3: 3, 4: 3, 5: 2, 6: 1}, {3: 4, 4: 3, 5: 2, 6: 1})


def middle(d, e, h, eps, chi, xt, fd, fe, fh, gd, ge, gh):
    grid = full_grid()
    hold_own(grid, (d, e, h, eps, chi), xt)
    hold_frames(grid, (fd, fe, fh), EARLY)

    def put(c, p, v, n):
        grid.put((gd, ge, gh)[c // 3], (c % 3, p), c, p, v, n)

    grid.sweep(1, (5, 6), (5, 6), put)
    grid.sweep(2, (4, 5), (4, 5), put)
    grid.sweep(3, (3, 4), (3, 4), put)
    grid.sweep(4, (3,), (), put)


def hold_side(grid, high, read):
    at, shift = (HI_AT, NZL) if high else (LO_AT, -NZL)
    for (comp, p), i in at.items():
        level = int(p == 6)
        if comp >= DP:
            level = p + 2 if HP <= comp < INV else p + 1
        grid.hold(comp, p + shift, functools.partial(read, i), level)


def chain(grid, high, put, keep, done=lambda o: None):
    if high:
        grid.sweep(1, (7,), (7, 8), put)
        grid.sweep(2, range(6, 9), range(6, 10), put)
        grid.sweep(3, range(5, 10), range(5, 11), put)
        h_planes, de_planes = range(4, 10), range(4, 10)
    else:
        grid.sweep(1, (-1,), (-1, 0), put)
        grid.sweep(2, (-1, 0), (0, 1), put)
        grid.sweep(3, (0, 1), (1, 2), put)
        h_planes, de_planes = (1, 2), (2, 3)
    for p in sorted(set(h_planes) | set(de_planes)):
        if p in h_planes:
            grid.step_h(STEPS, p, range(3), put)
        if p in de_planes:
            if p not in h_planes:
                for c in range(3):
                    keep(c, p - ADVANCE, grid.get(H + c, p, STEPS))
            grid.step_de(STEPS, p, put)
            done(p - ADVANCE)


KEPT = NZL - ADVANCE


def near(d, e, h, eps, chi, xt, fd, fe, fh, gd, ge, gh, cc, nd, ne, nh, neps, nchi, *state):
    gz, _, _, _ = position()

    def side(high):
        grid = full_grid()
        hold_own(grid, (d, e, h, eps, chi), xt)
        hold_frames(grid, (fd, fe, fh), EARLY)
        hold_frames(grid, (gd, ge, gh), MIDDLE)
        hold_side(grid, high, lambda i: cc[i])

        def put(c, p, v, n):
            k = c // 3
            if n == STEPS and p >= ADVANCE:
                (nd, ne, nh)[k][c % 3, p - ADVANCE] = v[:NXL]
            if n < STEPS or k == 2:
                grid.put(state[k], (c % 3, p + 2), c, p, v, n)

        def keep(c, o, v):
            nh[c, o] = v[:NXL]

        chain(grid, high, put, keep)
        if high:
            for out, comp in ((neps, EPS), (nchi, CHI)):
                for o in range(ADVANCE):
                    out[o] = grid.get(comp, NZL + o)[:NXL]

    pl.when(lax.rem(gz, 2) == 0)(lambda: side(True))
    pl.when(lax.rem(gz, 2) == 1)(lambda: side(False))


def ahead(d, e, h, eps, chi, fd, fe, fh, gd, ge, gh, ca, eps_in, chi_in, ie, ih, od, oe, oh, oeps, ochi, sd):
    gz, _, last, _ = position()
    half = halo_row() < XH

    def read(i):
        m = ca[24 * i : 24 * i + 8]
        x = ca[24 * NS + 8 * i : 24 * NS + 8 * i + 8] if i < NR else m
        return rows(jnp.where(half, x, m), ca[24 * i + 8 : 24 * i + 24], jnp.where(half, m, x))

    def side(high):
        z = scalar(gz != last) if high else scalar(gz != 0)

        def own_plane(p):
            return 0 <= p < NZL

        grid = Grid(NXL, lambda p: HALF if own_plane(p) else HALF * z, lambda p: None if own_plane(p) else 1.0 - z)
        for comp in ALL:
            for p in range(NZL):
                grid.hold(comp, p, functools.partial(own, (d, e, h, eps, chi), comp, p))
        hold_frames(grid, (fd, fe, fh), EARLY, NXL)
        hold_frames(grid, (gd, ge, gh), MIDDLE, NXL)
        hold_side(grid, high, read)

        def put(c, p, v, n):
            k = c // 3
            if n == STEPS and p >= ADVANCE:
                (od, oe, oh)[k][c % 3, p - ADVANCE] = v
            if k == 2:
                grid.put(ih, (n - 1, c % 3, p + 2), c, p, v, n)
            elif n < STEPS and k == 1:
                grid.put(ie, (n - 1, c % 3, p + 2), c, p, v, n)
            elif n < STEPS:
                grid.put(sd, (c % 3, p + 2), c, p, v, n)

        def keep(c, o, v):
            oh[c, o] = v

        chain(grid, high, put, keep)
        if high:
            for out, comp, new in ((oeps, EPS, eps_in), (ochi, CHI, chi_in)):
                for o in range(ADVANCE):
                    out[o] = jnp.where(gz == last, new[o], grid.get(comp, NZL + o))

    pl.when(lax.rem(gz, 2) == 0)(lambda: side(False))
    pl.when(lax.rem(gz, 2) == 1)(lambda: side(True))


def far(d, e, h, eps, chi, xt, fd, fe, fh, gd, ge, gh, ca, cb, *rest):
    nd, ne, nh, neps, nchi, ie, ih, od, oe, oh, oeps, ochi = rest[:12]
    outs, state, staged, sems = rest[12:17], rest[17:20], rest[20:23], rest[23]
    half = halo_row() < XH
    gz, _, _, _ = position()

    def cross(chosen, i):
        m = ca[24 * i : 24 * i + 8]
        x = ca[24 * NS + 8 * i : 24 * NS + 8 * i + 8] if i < NR else cb[NEW_AT + 8 * (i - NR) : NEW_AT + 8 * (i - NR) + 8]
        at, kept = HALO_AT[i], list(chosen[WIDTH[i]])
        v = cb[at : at + WIDTH[i]]
        if len(kept) < 8:
            near_row = [max([k for k in kept if k <= r], default=kept[0]) for r in range(8)]
            v = rows(*[v[kept.index(k) : kept.index(k) + 1] for k in near_row])
        return rows(jnp.where(half, x, m), ca[24 * i + 8 : 24 * i + 24], jnp.where(half, m, x), v)

    def side(high):
        copies = []

        def send(source, target):
            copies.append(pltpu.make_async_copy(source, target, sems.at[len(copies)]))
            copies[-1].start()

        there = pl.ds(0, ADVANCE) if high else pl.ds(ADVANCE, KEPT)
        for a, out in zip((nd, ne, nh), outs):
            send(a.at[:, there], out.at[:, there])
        for a, new, out in zip((eps, chi), (oeps, ochi) if high else (neps, nchi), outs[3:]):
            send(a.at[pl.ds(ADVANCE, KEPT)], out.at[pl.ds(0, KEPT)])
            send(new, out.at[pl.ds(KEPT, ADVANCE)])

        grid = full_grid()
        hold_own(grid, (d, e, h, eps, chi), xt)
        hold_frames(grid, (fd, fe, fh), EARLY)
        hold_frames(grid, (gd, ge, gh), MIDDLE)
        hold_side(grid, high, functools.partial(cross, HI_ROWS if high else LO_ROWS))
        none = jnp.zeros((16, NY), jnp.float32)

        def result(k, c, o, v):
            staged[k][c, o, 0:8] = v[0:8]
            staged[k][c, o, 8:24] = (od, oe, oh)[k][c, o, 8:24]
            staged[k][c, o, 24:32] = v[24:32]

        def put(c, p, v, n):
            k, at = c // 3, (c % 3, p + 2)
            if n == STEPS and p >= ADVANCE:
                result(k, c % 3, p - ADVANCE, v)
            if n < STEPS or k == 2:
                ref, inner_ref = state[k], (None, ie, ih)[k]
                ref[(*at, slice(0, 8))] = v[0:8]
                ref[(*at, slice(8, 24))] = v[24:40]

                def read():
                    mid = none if inner_ref is None else inner_ref[(n - 1, *at, slice(8, 24))]
                    return rows(ref[(*at, slice(0, 8))], mid, ref[(*at, slice(8, 24))])

                grid.hold(c, p, read, n)

        def done(o):
            batch = {4: 3, 7: 3, 1: 2}.get(o)
            if batch:
                some = pl.ds(o + 1 - batch, batch)
                for k in range(3):
                    send(staged[k].at[:, some], outs[k].at[:, some])

        chain(grid, high, put, functools.partial(result, 2), done)
        for c in copies:
            c.wait()

    pl.when(lax.rem(gz, 2) == 0)(lambda: side(False))
    pl.when(lax.rem(gz, 2) == 1)(lambda: side(True))


def swapped(shard, axis, first):
    n = {a: lax.axis_size(a) for a in ("gz", "gx")}
    moves = []
    for z in range(n["gz"]):
        for x in range(n["gx"]):
            at = z if axis == "gz" else x
            to = at + 1 if at % 2 == first else at - 1
            if 0 <= to < n[axis]:
                other = (to, x) if axis == "gz" else (z, to)
            else:
                other = (z ^ 1, x) if axis == "gx" else (z, x ^ 1)
            moves.append((z * n["gx"] + x, other[0] * n["gx"] + other[1]))
    return lax.ppermute(shard, ("gz", "gx"), moves)


def call(body, inputs, out_shape, scratch=(), vmem=8, specs=None, out=VM, aliases=None):
    return pl.pallas_call(
        body,
        out_shape=out_shape,
        in_specs=[VM] * len(inputs) if specs is None else specs,
        out_specs=jax.tree.map(lambda _: out, out_shape),
        input_output_aliases=aliases or {},
        scratch_shapes=list(scratch),
        compiler_params=pltpu.CompilerParams(vmem_limit_bytes=vmem << 20),
    )(*inputs)


def on_device(d_field, e_field, h_field, permittivity, kerr_coeff, classes, eps_table, chi_table):
    field, medium = shape(3, NZL, NXL, NY), shape(NZL, NXL, NY)
    halo = shape(NHALO, NY)
    *fields, ya, yb = call(
        load,
        [pltpu.with_memory_space_constraint(a, pltpu.HBM) for a in (d_field, e_field, h_field, permittivity, kerr_coeff)],
        (field, field, field, medium, medium, halo, halo),
        [pltpu.SemaphoreType.DMA((5,))],
        specs=[HBM] * 5,
    )
    ra, rb = swapped(ya, "gx", 0), swapped(yb, "gx", 1)
    lo = shape(2, NXL, NY)
    *inside, za = call(inner, fields, (*[shape(3, 5, NXL, NY)] * 3, lo, shape(24 * NS + 8 * NR, NY)))
    ca = swapped(za, "gz", 1)
    (edge,) = call(mark, [], (shape(8, NY),))
    thin = [(3, 5, EDGE, NY)] * 3 + [(2, EDGE, NY)]
    xt, *outside, zb = call(
        edges, [*fields, ra, rb, edge], (shape(11, NZL, 8, NY), *[shape(*t) for t in thin], shape(LATE, NY))
    )
    cb = swapped(zb, "gz", 1)
    coming = lookup(classes, eps_table), lookup(classes, chi_table)
    *frames, zc = call(
        merge,
        [*fields, *inside, xt, *outside, edge],
        (*[shape(3, 5, ROWS, NY)] * 3, shape(NS, ROWS, NY)),
        [pltpu.VMEM(t, jnp.float32) for t in thin],
    )
    cc = swapped(zc, "gz", 0)
    more = call(middle, [*fields, xt, *frames], (shape(3, 7, ROWS, NY),) * 3)
    state = [pltpu.VMEM((3, 13, ROWS, NY), jnp.float32)] * 3
    two = shape(ADVANCE, NXL, NY)
    made = call(near, [*fields, xt, *frames, *more, cc], (field, field, field, two, two), state, vmem=16)
    levels = shape(STEPS - 1, 3, 13, NXL, NY), shape(STEPS, 3, 13, NXL, NY)
    inside = call(
        ahead,
        [*fields, *frames, *more, ca, *coming],
        (*levels, field, field, field, two, two),
        [pltpu.VMEM((3, 13, NXL, NY), jnp.float32)],
        vmem=16,
    )
    thin = [pltpu.VMEM((3, 13, EDGE, NY), jnp.float32)] * 3 + [pltpu.VMEM(field.shape, jnp.float32)] * 3
    return call(
        far,
        [*fields, xt, *frames, *more, ca, cb, *made, *inside],
        (field, field, field, medium, medium),
        [*thin, pltpu.SemaphoreType.DMA((48,))],
        vmem=16,
        out=HBM,
    )


def solution(mesh):
    placed = (
        P(None, "gz", "gx", None),
        P(None, "gz", "gx", None),
        P(None, "gz", "gx", None),
        P("gz", "gx", None),
        P("gz", "gx", None),
        P(None, "gx", None),
        P(),
        P(),
    )
    return jax.shard_map(
        on_device,
        mesh=mesh,
        in_specs=placed,
        out_specs=placed[:5],
        check_vma=False,
    )
```

```python
import functools

import jax
import jax.numpy as jnp
from jax import lax
from jax.experimental import pallas as pl
from jax.experimental.pallas import tpu as pltpu
from jax.sharding import PartitionSpec as P


STEPS = 4
KERR = 3
ADVANCE = 2
HALF = 0.5

D, E, H, EPS, CHI = 0, 3, 6, 9, 10
ALL = range(11)
NZL, NXL, NY = 8, 32, 128
XH = 4
ROWS = NXL + 2 * XH
EDGE = 24

DP, HP, INV = 11, 14, 17
RAW = [(E + c, 0) for c in range(3)] + [(c, p) for p in range(3) for c in (EPS, CHI)]
HI = RAW + [(DP + c, p) for p in range(3) for c in range(3)] + [(HP + c, p) for p in range(2) for c in range(3)]
HI += [(INV, 1), (INV, 2)]
HI_ROWS = {8: range(8), 6: (0, 1, 2, 5, 6, 7), 4: (0, 1, 6, 7), 2: (0, 7)}
LO_ROWS = {8: range(8), 6: (0, 1, 2, 3, 6, 7), 4: (0, 1, 2, 7), 2: ()}


def slot_rows(comp, p):
    if (comp, p) == (E, 0):
        return 8
    level = p + (HP <= comp < INV)
    return 6 - 2 * p if comp < HP or comp >= INV else 6 - 2 * (level - 1)


WIDTH = [slot_rows(*k) for k in HI]
HALO_AT = [sum(WIDTH[:i]) for i in range(len(HI))]
LO = [None] * len(HI)
_wide = [i for i, n in enumerate(WIDTH) if n >= 6]
_thin = [i for i, n in enumerate(WIDTH) if n == 4]
for _k in [(E + c, 7) for c in range(3)] + [(H + c, 7) for c in range(3)]:
    LO[_wide.pop(0)] = _k
for _k in [(D + c, 7) for c in range(3)] + [(EPS, 7), (CHI, 7), (H, 6), (H + 1, 6)]:
    LO[_thin.pop(0)] = _k
HI_AT = {k: i for i, k in enumerate(HI)}
LO_AT = {k: i for i, k in enumerate(LO) if k}
NS = len(HI)


def late_rows(comp, p):
    if comp < DP:
        return 0
    return p if comp == INV else p + 1


LATE_N = [late_rows(*k) for k in HI]
EARLY_AT = [24 * NS + sum(8 - 2 * n for n in LATE_N[:i]) for i in range(NS + 1)]
LATE_AT = [sum(WIDTH) + sum(2 * n for n in LATE_N[:i]) for i in range(NS + 1)]
EARLY_ROWS, LATE_ROWS = (-(-at[-1] // 8) * 8 for at in (EARLY_AT, LATE_AT))

FOUR, THREE = (E, E + 1, E + 2, H + 1, H + 2), (D, D + 1, D + 2, H, EPS, CHI)
NF = len(FOUR) * NZL * 4
NHALO = NF + len(THREE) * NZL * 3

VM = pl.BlockSpec(memory_space=pltpu.VMEM)
HBM = pl.BlockSpec(memory_space=pltpu.HBM)
SM = pl.BlockSpec(memory_space=pltpu.SMEM)


def shape(*dims):
    return jax.ShapeDtypeStruct(dims, jnp.float32)


def rows(*parts):
    return jnp.concatenate(parts, axis=0)


def scalar(condition):
    return jnp.where(condition, 1.0, 0.0).astype(jnp.float32)


def position():
    gz, gx = lax.axis_index("gz"), lax.axis_index("gx")
    return gz, gx, lax.axis_size("gz") - 1, lax.axis_size("gx") - 1


def halo_row():
    return lax.broadcasted_iota(jnp.int32, (8, NY), 0)


def inside_x():
    _, gx, _, last = position()
    return jnp.where(halo_row() < XH, scalar(gx != last), scalar(gx != 0))


class Grid:
    def __init__(self, size, factor, fill):
        self.size, self.factor, self.fill = size, factor, fill
        self.where, self.level = {}, {}
        lane = lax.broadcasted_iota(jnp.int32, (size, NY), 1)
        self.last_y, self.first_y = lane == NY - 1, lane == 0

    def hold(self, comp, plane, read, level=0):
        self.where[(comp, plane)] = read
        self.level[(comp, plane)] = level

    def get(self, comp, plane, level=None):
        assert level is None or self.level[(comp, plane)] == level, (comp, plane)
        return self.where[(comp, plane)]()

    def put(self, ref, index, comp, plane, value, level):
        ref[index] = value
        self.hold(comp, plane, lambda: ref[index], level)

    def next_y(self, v):
        return jnp.where(self.last_y, 0.0, pltpu.roll(v, NY - 1, 1))

    def prev_y(self, v):
        return jnp.where(self.first_y, 0.0, pltpu.roll(v, 1, 1))

    def next_x(self, v):
        return pltpu.roll(v, self.size - 1, 0)

    def prev_x(self, v):
        return pltpu.roll(v, 1, 0)

    def step_h(self, n, p, comps, put):
        f = self.factor(p)
        ex, ey, ez = (self.get(E + c, p, n - 1) for c in range(3))
        if self.level.get((HP, p)) == n:
            hx, hy, hz = (self.get(HP + c, p) for c in range(3))
            put(H, p, hx - f * ((self.next_y(ez) - ez) + ey), n)
            put(H + 1, p, hy + f * (ex + (self.next_x(ez) - ez)), n)
            put(H + 2, p, hz - f * ((self.next_x(ey) - ey) - (self.next_y(ex) - ex)), n)
            return
        new = {}
        if 0 in comps:
            eyn = self.get(E + 1, p + 1, n - 1)
            new[0] = (self.next_y(ez) - ez) - (eyn - ey)
        if 1 in comps:
            exn = self.get(E, p + 1, n - 1)
            new[1] = (exn - ex) - (self.next_x(ez) - ez)
        if 2 in comps:
            new[2] = (self.next_x(ey) - ey) - (self.next_y(ex) - ex)
        for c, curl in new.items():
            put(H + c, p, self.get(H + c, p, n - 1) - f * curl, n)

    def medium(self, p):
        eps, fill = self.get(EPS, p), self.fill(p)
        return eps if fill is None else eps + fill, self.get(CHI, p)

    def first_inverse(self, n, p):
        ex, ey, ez = (self.get(E + c, p, n) for c in range(3))
        eps, chi = self.medium(p)
        return 1.0 / (eps + chi * (ex * ex + ey * ey + ez * ez))

    def derive(self):
        out = {}
        for p in range(3):
            f, n = self.factor(p), p + 1
            hx, hy, hz = (self.get(H + c, p, n) for c in range(3))
            dx, dy, dz = (self.get(D + c, p, n - 1) for c in range(3))
            out[(DP, p)] = dx + f * ((hz - self.prev_y(hz)) - hy)
            out[(DP + 1, p)] = dy + f * (hx - (hz - self.prev_x(hz)))
            out[(DP + 2, p)] = dz + f * ((hy - self.prev_x(hy)) - (hx - self.prev_y(hx)))
            if p < 2:
                out[(HP, p)] = hx + f * self.get(E + 1, p + 1, n)
                out[(HP + 1, p)] = hy - f * self.get(E, p + 1, n)
                out[(HP + 2, p)] = hz
            if p > 0:
                out[(INV, p)] = self.first_inverse(n - 1, p)
        return out

    def step_de(self, n, p, put):
        f = self.factor(p)
        hxp, hyp = (self.get(H + c, p - 1, n) for c in range(2))
        if self.level.get((DP, p)) == n:
            dx, dy, dz = (self.get(DP + c, p) for c in range(3))
            dx, dy = dx + f * hyp, dy - f * hxp
        else:
            hx, hy, hz = (self.get(H + c, p, n) for c in range(3))
            dx = self.get(D, p, n - 1) + f * ((hz - self.prev_y(hz)) - (hy - hyp))
            dy = self.get(D + 1, p, n - 1) + f * ((hx - hxp) - (hz - self.prev_x(hz)))
            dz = self.get(D + 2, p, n - 1) + f * ((hy - self.prev_x(hy)) - (hx - self.prev_y(hx)))
        eps, chi = self.medium(p)
        inverse = self.get(INV, p) if self.level.get((INV, p)) == n else self.first_inverse(n - 1, p)
        if n == STEPS:
            dx, dy, dz, eps, chi, inverse = (v[:NXL] for v in (dx, dy, dz, eps, chi, inverse))
        squares = chi * (dx * dx + dy * dy + dz * dz)
        for _ in range(KERR - 1):
            inverse = 1.0 / (eps + squares * (inverse * inverse))
        for c, v in enumerate((dx, dy, dz)):
            put(D + c, p, v, n)
            put(E + c, p, v * inverse, n)

    def sweep(self, n, h_planes, de_planes, put):
        for p in range(-2, 11):
            if p in h_planes:
                self.step_h(n, p, range(3), put)
            if p in de_planes:
                self.step_de(n, p, put)


def own(fields, comp, plane):
    d, e, h, eps, chi = fields
    if comp < E:
        return d[comp, plane]
    if comp < H:
        return e[comp - E, plane]
    if comp < EPS:
        return h[comp - H, plane]
    return eps[plane] if comp == EPS else chi[plane]


def halo_slot(comp, p):
    if comp in FOUR:
        return (FOUR.index(comp) * NZL + p) * 4, 4
    return NF + (THREE.index(comp) * NZL + p) * 3, 3


def load(d, e, h, eps, chi, dv, ev, hv, epsv, chiv, ya, yb, sems):
    held = (dv, ev, hv, epsv, chiv)
    copies = [pltpu.make_async_copy(a, b, sems.at[i]) for i, (a, b) in enumerate(zip((d, e, h, eps, chi), held))]
    for c in copies:
        c.start()
    _, gx, _, last = position()
    even = lax.rem(gx, 2) == 0
    keep = scalar(jnp.logical_and(gx != 0, gx != last))
    for comps, copy in zip((range(D, E), range(E, H), range(H, EPS), (EPS,), (CHI,)), copies):
        copy.wait()
        for comp in comps:
            for p in range(NZL):
                at, n = halo_slot(comp, p)
                v = own(held, comp, p)
                low, high = v[0:n], v[NXL - n :]
                ya[at : at + n] = jnp.where(even, high, low)
                yb[at : at + n] = jnp.where(even, low, high) * keep


def mark(out):
    out[...] = inside_x()


def early(grid, put):
    grid.sweep(1, range(0, 5), range(1, 5), put)
    grid.sweep(2, range(1, 4), range(2, 4), put)
    grid.sweep(3, range(2, 3), (), put)


def lookup(classes, table):
    labels = jnp.arange(table.shape[0], dtype=jnp.int32).reshape(-1, 1, 1, 1)
    picked = jnp.where(classes[None] == labels, table.reshape(-1, 1, 1, 1), jnp.float32(0.0))
    return jnp.sum(picked, axis=0)


def payload(grid, side):
    made = grid.derive() if side is HI else {}
    return [k and (made[k] if k in made else grid.get(*k)) for k in side]


def inner(d, e, h, eps, chi, fd, fe, fh, lo, out):
    fields = (d, e, h, eps, chi)
    grid = Grid(NXL, lambda p: HALF, lambda p: None)
    for comp in ALL:
        for p in range(NZL):
            grid.hold(comp, p, functools.partial(own, fields, comp, p))
    grid.step_h(1, 6, range(2), lambda c, p, v, n: grid.put(lo, c - H, c, p, v, n))

    def put(c, p, v, n):
        ref = (fd, fe, fh)[c // 3]
        grid.put(ref, (c % 3, p), c, p, v, n)

    early(grid, put)
    gz, _, last, _ = position()
    first_core = lax.rem(gz, 2) == 0
    keep = scalar(jnp.logical_and(gz != 0, gz != last))
    half = halo_row() < XH
    low = payload(grid, LO)
    for i, v in enumerate(payload(grid, HI)):
        if low[i] is not None:
            v = jnp.where(first_core, v, low[i])
        v = v * keep
        out[24 * i : 24 * i + 8] = jnp.where(half, v[24:32], v[0:8])
        out[24 * i + 8 : 24 * i + 24] = v[8:24]
        n = LATE_N[i]
        out[EARLY_AT[i] : EARLY_AT[i + 1]] = jnp.where(half, v[0:8], v[24:32])[n : 8 - n]


def edge_grid(inside, fields, tile):
    f = rows(jnp.full((8, NY), HALF), inside * HALF, jnp.full((8, NY), HALF))
    none = jnp.zeros((8, NY), jnp.float32)
    fill = rows(none, 1.0 - inside, none)
    grid = Grid(EDGE, lambda p: f, lambda p: fill)

    def read(comp, p):
        v = own(fields, comp, p)
        return rows(v[24:32], tile(comp, p), v[0:8])

    for comp in ALL:
        for p in range(NZL):
            grid.hold(comp, p, functools.partial(read, comp, p))
    return grid


def joined(a, b, comp, p):
    _, gx, _, _ = position()
    even = lax.rem(gx, 2) == 0
    at, n = halo_slot(comp, p)
    a, b = a[at : at + n], b[at : at + n]
    above, below = jnp.where(even, a, b), jnp.where(even, b, a)
    if n == 4:
        return rows(above, below)
    return rows(above, above[2:3], below[0:1], below)


def edges(d, e, h, eps, chi, ra, rb, inside, xt, sd, se, sh, slo, cross):
    fields = (d, e, h, eps, chi)
    gz, _, last, _ = position()
    keep = scalar(jnp.logical_and(gz != 0, gz != last))
    half = halo_row() < XH
    for comp in ALL:
        for p in range(NZL):
            xt[comp, p] = joined(ra, rb, comp, p)

    def pack(grid, side, chosen):
        for i, v in enumerate(payload(grid, side)):
            if v is None:
                continue
            v = v * keep
            at, n = HALO_AT[i], WIDTH[i]
            runs = []
            for r in chosen[n]:
                if runs and runs[-1][1] == r:
                    runs[-1][1] = r + 1
                else:
                    runs.append([r, r + 1])
            for a, b in runs:
                cross[at : at + b - a] = v[8 + a : 8 + b]
                at += b - a
            n = LATE_N[i]
            if n:
                at = LATE_AT[i]
                cross[at : at + n] = v[16 : 16 + n]
                cross[at + n : at + 2 * n] = v[8 - n : 8]

    @pl.when(lax.rem(gz, 2) == 0)
    def _():
        grid = edge_grid(inside[...], fields, lambda comp, p: xt[comp, p])
        early(grid, lambda c, p, v, n: grid.put((sd, se, sh)[c // 3], (c % 3, p), c, p, v, n))
        pack(grid, HI, HI_ROWS)

    @pl.when(lax.rem(gz, 2) == 1)
    def _():
        grid = edge_grid(inside[...], fields, lambda comp, p: xt[comp, p])
        grid.step_h(1, 6, range(2), lambda c, p, v, n: grid.put(slo, c - H, c, p, v, n))
        pack(grid, LO, LO_ROWS)


def merge(d, e, h, eps, chi, id_, ie, ih, ilo, xt, sd, se, sh, slo, inside, fd, fe, fh, chip, td, te, th, tlo):
    fields = (d, e, h, eps, chi)
    half = halo_row() < XH

    def merged(v, w):
        return rows(jnp.where(half, w[16:24], v[0:8]), v[8:24], jnp.where(half, v[24:32], w[0:8]), w[8:16])

    def join(sides, side):
        grid = full_grid()
        hold_own(grid, fields, xt)
        for k, (v, w, ref) in enumerate(((id_, sides[0], fd), (ie, sides[1], fe), (ih, sides[2], fh))):
            for p, level in EARLY[k].items():
                for c in range(3):
                    grid.put(ref, (c, p), 3 * k + c, p, merged(v[c, p], w[c, p]), level)
        for c in range(2):
            grid.hold(H + c, 6, functools.partial(lambda a: merged(ilo[a], tlo[a]), c))
        for i, v in enumerate(payload(grid, side)):
            if v is not None:
                chip[i] = v

    gz, _, _, _ = position()

    @pl.when(lax.rem(gz, 2) == 0)
    def _():
        grid = edge_grid(inside[...], fields, lambda comp, p: xt[comp, p])
        grid.step_h(1, 6, range(2), lambda c, p, v, n: grid.put(tlo, c - H, c, p, v, n))
        join((sd, se, sh), LO)

    @pl.when(lax.rem(gz, 2) == 1)
    def _():
        grid = edge_grid(inside[...], fields, lambda comp, p: xt[comp, p])
        early(grid, lambda c, p, v, n: grid.put((td, te, th)[c // 3], (c % 3, p), c, p, v, n))
        join((td, te, th), HI)


def full_grid():
    gz, _, last, _ = position()
    up, down = scalar(gz != last), scalar(gz != 0)
    edge = inside_x()

    def inside(p):
        return up if p >= NZL else (down if p < 0 else None)

    def factor(p):
        z = inside(p)
        main, tile = jnp.full((NXL, NY), HALF, jnp.float32), edge * HALF
        return rows(main, tile) if z is None else rows(main * z, tile * z)

    def fill(p):
        z = inside(p)
        if z is None:
            return rows(jnp.zeros((NXL, NY), jnp.float32), 1.0 - edge)
        return rows(jnp.full((NXL, NY), 1.0 - z, jnp.float32), 1.0 - edge * z)

    return Grid(ROWS, factor, fill)


def hold_own(grid, fields, xt):
    for comp in ALL:
        for p in range(NZL):
            grid.hold(comp, p, functools.partial(lambda c, q: rows(own(fields, c, q), xt[c, q]), comp, p))


def hold_frames(grid, refs, levels, size=ROWS):
    for k, ref in enumerate(refs):
        for p, level in levels[k].items():
            for c in range(3):
                grid.hold(3 * k + c, p, functools.partial(lambda r, a, b: r[a, b, 0:size], ref, c, p), level)


EARLY = ({1: 1, 2: 2, 3: 2, 4: 1}, {1: 1, 2: 2, 3: 2, 4: 1}, {0: 1, 1: 2, 2: 3, 3: 2, 4: 1})
MIDDLE = ({3: 3, 4: 3, 5: 2, 6: 1}, {3: 3, 4: 3, 5: 2, 6: 1}, {3: 4, 4: 3, 5: 2, 6: 1})


def middle(d, e, h, eps, chi, xt, fd, fe, fh, gd, ge, gh):
    grid = full_grid()
    hold_own(grid, (d, e, h, eps, chi), xt)
    hold_frames(grid, (fd, fe, fh), EARLY)

    def put(c, p, v, n):
        grid.put((gd, ge, gh)[c // 3], (c % 3, p), c, p, v, n)

    grid.sweep(1, (5, 6), (5, 6), put)
    grid.sweep(2, (4, 5), (4, 5), put)
    grid.sweep(3, (3, 4), (3, 4), put)
    grid.sweep(4, (3,), (), put)


def hold_side(grid, high, read):
    at, shift = (HI_AT, NZL) if high else (LO_AT, -NZL)
    for (comp, p), i in at.items():
        level = int(p == 6)
        if comp >= DP:
            level = p + 2 if HP <= comp < INV else p + 1
        grid.hold(comp, p + shift, functools.partial(read, i), level)


def chain(grid, high, put, keep, done=lambda o: None):
    if high:
        grid.sweep(1, (7,), (7, 8), put)
        grid.sweep(2, range(6, 9), range(6, 10), put)
        grid.sweep(3, range(5, 10), range(5, 11), put)
        h_planes, de_planes = range(4, 10), range(4, 10)
    else:
        grid.sweep(1, (-1,), (-1, 0), put)
        grid.sweep(2, (-1, 0), (0, 1), put)
        grid.sweep(3, (0, 1), (1, 2), put)
        h_planes, de_planes = (1, 2), (2, 3)
    for p in sorted(set(h_planes) | set(de_planes)):
        if p in h_planes:
            grid.step_h(STEPS, p, range(3), put)
        if p in de_planes:
            if p not in h_planes:
                for c in range(3):
                    keep(c, p - ADVANCE, grid.get(H + c, p, STEPS))
            grid.step_de(STEPS, p, put)
            done(p - ADVANCE)


KEPT = NZL - ADVANCE


def near(d, e, h, eps, chi, xt, fd, fe, fh, gd, ge, gh, cc, nd, ne, nh, neps, nchi, *state):
    gz, _, _, _ = position()

    def side(high):
        grid = full_grid()
        hold_own(grid, (d, e, h, eps, chi), xt)
        hold_frames(grid, (fd, fe, fh), EARLY)
        hold_frames(grid, (gd, ge, gh), MIDDLE)
        hold_side(grid, high, lambda i: cc[i])

        def put(c, p, v, n):
            k = c // 3
            if n == STEPS and p >= ADVANCE:
                (nd, ne, nh)[k][c % 3, p - ADVANCE] = v[:NXL]
            if n < STEPS or k == 2:
                grid.put(state[k], (c % 3, p + 2), c, p, v, n)

        def keep(c, o, v):
            nh[c, o] = v[:NXL]

        chain(grid, high, put, keep)
        if high:
            for out, comp in ((neps, EPS), (nchi, CHI)):
                for o in range(ADVANCE):
                    out[o] = grid.get(comp, NZL + o)[:NXL]

    pl.when(lax.rem(gz, 2) == 0)(lambda: side(True))
    pl.when(lax.rem(gz, 2) == 1)(lambda: side(False))


def ahead(d, e, h, eps, chi, fd, fe, fh, gd, ge, gh, ca, eps_in, chi_in, ie, ih, od, oe, oh, oeps, ochi, sd):
    gz, _, last, _ = position()
    half = halo_row() < XH

    def read(i):
        m = ca[24 * i : 24 * i + 8]
        x = m if LATE_N[i] else ca[EARLY_AT[i] : EARLY_AT[i + 1]]
        return rows(jnp.where(half, x, m), ca[24 * i + 8 : 24 * i + 24], jnp.where(half, m, x))

    def side(high):
        z = scalar(gz != last) if high else scalar(gz != 0)

        def own_plane(p):
            return 0 <= p < NZL

        grid = Grid(NXL, lambda p: HALF if own_plane(p) else HALF * z, lambda p: None if own_plane(p) else 1.0 - z)
        for comp in ALL:
            for p in range(NZL):
                grid.hold(comp, p, functools.partial(own, (d, e, h, eps, chi), comp, p))
        hold_frames(grid, (fd, fe, fh), EARLY, NXL)
        hold_frames(grid, (gd, ge, gh), MIDDLE, NXL)
        hold_side(grid, high, read)

        def put(c, p, v, n):
            k = c // 3
            if n == STEPS and p >= ADVANCE:
                (od, oe, oh)[k][c % 3, p - ADVANCE] = v
            if k == 2:
                grid.put(ih, (n - 1, c % 3, p + 2), c, p, v, n)
            elif n < STEPS and k == 1:
                grid.put(ie, (n - 1, c % 3, p + 2), c, p, v, n)
            elif n < STEPS:
                grid.put(sd, (c % 3, p + 2), c, p, v, n)

        def keep(c, o, v):
            oh[c, o] = v

        chain(grid, high, put, keep)
        if high:
            for out, comp, new in ((oeps, EPS, eps_in), (ochi, CHI, chi_in)):
                for o in range(ADVANCE):
                    out[o] = jnp.where(gz == last, new[o], grid.get(comp, NZL + o))

    pl.when(lax.rem(gz, 2) == 0)(lambda: side(False))
    pl.when(lax.rem(gz, 2) == 1)(lambda: side(True))


def far(d, e, h, eps, chi, xt, fd, fe, fh, gd, ge, gh, ca, cb, *rest):
    nd, ne, nh, neps, nchi, ie, ih, od, oe, oh, oeps, ochi = rest[:12]
    outs, state, edge, sems = rest[12:17], rest[17:20], rest[20:23], rest[23]
    half = halo_row() < XH
    gz, _, _, _ = position()

    def cross(chosen, i):
        m = ca[24 * i : 24 * i + 8]
        x, n = ca[EARLY_AT[i] : EARLY_AT[i + 1]], LATE_N[i]
        if n:
            x = rows(cb[LATE_AT[i] : LATE_AT[i] + n], x, cb[LATE_AT[i] + n : LATE_AT[i] + 2 * n])
        at, kept = HALO_AT[i], list(chosen[WIDTH[i]])
        v = cb[at : at + WIDTH[i]]
        if len(kept) < 8:
            near_row = [max([k for k in kept if k <= r], default=kept[0]) for r in range(8)]
            v = rows(*[v[kept.index(k) : kept.index(k) + 1] for k in near_row])
        return rows(jnp.where(half, x, m), ca[24 * i + 8 : 24 * i + 24], jnp.where(half, m, x), v)

    def side(high):
        copies = []

        def send(source, target):
            copies.append(pltpu.make_async_copy(source, target, sems.at[len(copies)]))
            copies[-1].start()

        here, there = (pl.ds(ADVANCE, KEPT), pl.ds(0, ADVANCE)) if high else (pl.ds(0, ADVANCE), pl.ds(ADVANCE, KEPT))
        middle_rows = pl.ds(8, 16)
        for a, b, out in zip((nd, ne, nh), (od, oe, oh), outs):
            send(a.at[:, there], out.at[:, there])
            send(b.at[:, here, middle_rows], out.at[:, here, middle_rows])
        for a, new, out in zip((eps, chi), (oeps, ochi) if high else (neps, nchi), outs[3:]):
            send(a.at[pl.ds(ADVANCE, KEPT)], out.at[pl.ds(0, KEPT)])
            send(new, out.at[pl.ds(KEPT, ADVANCE)])

        grid = full_grid()
        hold_own(grid, (d, e, h, eps, chi), xt)
        hold_frames(grid, (fd, fe, fh), EARLY)
        hold_frames(grid, (gd, ge, gh), MIDDLE)
        hold_side(grid, high, functools.partial(cross, HI_ROWS if high else LO_ROWS))
        none = jnp.zeros((16, NY), jnp.float32)

        def result(k, c, o, v):
            edge[k][c, o, 0:8] = v[0:8]
            edge[k][c, o, 8:16] = v[24:32]

        def put(c, p, v, n):
            k, at = c // 3, (c % 3, p + 2)
            if n == STEPS and p >= ADVANCE:
                result(k, c % 3, p - ADVANCE, v)
            if n < STEPS or k == 2:
                ref, inner_ref = state[k], (None, ie, ih)[k]
                ref[(*at, slice(0, 8))] = v[0:8]
                ref[(*at, slice(8, 24))] = v[24:40]

                def read():
                    mid = none if inner_ref is None else inner_ref[(n - 1, *at, slice(8, 24))]
                    return rows(ref[(*at, slice(0, 8))], mid, ref[(*at, slice(8, 24))])

                grid.hold(c, p, read, n)

        def done(o):
            for k in range(3):
                for a, b in ((0, 0), (8, 24)):
                    send(edge[k].at[:, pl.ds(o, 1), pl.ds(a, 8)], outs[k].at[:, pl.ds(o, 1), pl.ds(b, 8)])

        chain(grid, high, put, functools.partial(result, 2), done)
        for c in copies:
            c.wait()

    pl.when(lax.rem(gz, 2) == 0)(lambda: side(False))
    pl.when(lax.rem(gz, 2) == 1)(lambda: side(True))


def swapped(shard, axis, first):
    n = {a: lax.axis_size(a) for a in ("gz", "gx")}
    moves = []
    for z in range(n["gz"]):
        for x in range(n["gx"]):
            at = z if axis == "gz" else x
            to = at + 1 if at % 2 == first else at - 1
            if 0 <= to < n[axis]:
                other = (to, x) if axis == "gz" else (z, to)
            else:
                other = (z ^ 1, x) if axis == "gx" else (z, x ^ 1)
            moves.append((z * n["gx"] + x, other[0] * n["gx"] + other[1]))
    return lax.ppermute(shard, ("gz", "gx"), moves)


def call(body, inputs, out_shape, scratch=(), vmem=8, specs=None, out=VM, aliases=None):
    return pl.pallas_call(
        body,
        out_shape=out_shape,
        in_specs=[VM] * len(inputs) if specs is None else specs,
        out_specs=jax.tree.map(lambda _: out, out_shape),
        input_output_aliases=aliases or {},
        scratch_shapes=list(scratch),
        compiler_params=pltpu.CompilerParams(vmem_limit_bytes=vmem << 20),
    )(*inputs)


def on_device(d_field, e_field, h_field, permittivity, kerr_coeff, classes, eps_table, chi_table):
    field, medium = shape(3, NZL, NXL, NY), shape(NZL, NXL, NY)
    halo = shape(NHALO, NY)
    *fields, ya, yb = call(
        load,
        [pltpu.with_memory_space_constraint(a, pltpu.HBM) for a in (d_field, e_field, h_field, permittivity, kerr_coeff)],
        (field, field, field, medium, medium, halo, halo),
        [pltpu.SemaphoreType.DMA((5,))],
        specs=[HBM] * 5,
    )
    ra, rb = swapped(ya, "gx", 0), swapped(yb, "gx", 1)
    lo = shape(2, NXL, NY)
    *inside, za = call(inner, fields, (*[shape(3, 5, NXL, NY)] * 3, lo, shape(EARLY_ROWS, NY)))
    ca = swapped(za, "gz", 1)
    (edge,) = call(mark, [], (shape(8, NY),))
    thin = [(3, 5, EDGE, NY)] * 3 + [(2, EDGE, NY)]
    xt, *outside, zb = call(
        edges, [*fields, ra, rb, edge], (shape(11, NZL, 8, NY), *[shape(*t) for t in thin], shape(LATE_ROWS, NY))
    )
    cb = swapped(zb, "gz", 1)
    coming = lookup(classes, eps_table), lookup(classes, chi_table)
    *frames, zc = call(
        merge,
        [*fields, *inside, xt, *outside, edge],
        (*[shape(3, 5, ROWS, NY)] * 3, shape(NS, ROWS, NY)),
        [pltpu.VMEM(t, jnp.float32) for t in thin],
    )
    cc = swapped(zc, "gz", 0)
    more = call(middle, [*fields, xt, *frames], (shape(3, 7, ROWS, NY),) * 3)
    state = [pltpu.VMEM((3, 13, ROWS, NY), jnp.float32)] * 3
    two = shape(ADVANCE, NXL, NY)
    made = call(near, [*fields, xt, *frames, *more, cc], (field, field, field, two, two), state, vmem=16)
    levels = shape(STEPS - 1, 3, 13, NXL, NY), shape(STEPS, 3, 13, NXL, NY)
    inside = call(
        ahead,
        [*fields, *frames, *more, ca, *coming],
        (*levels, field, field, field, two, two),
        [pltpu.VMEM((3, 13, NXL, NY), jnp.float32)],
        vmem=16,
    )
    thin = [pltpu.VMEM((3, 13, EDGE, NY), jnp.float32)] * 3 + [pltpu.VMEM((3, NZL, 16, NY), jnp.float32)] * 3
    return call(
        far,
        [*fields, xt, *frames, *more, ca, cb, *made, *inside],
        (field, field, field, medium, medium),
        [*thin, pltpu.SemaphoreType.DMA((48,))],
        vmem=16,
        out=HBM,
    )


def solution(mesh):
    placed = (
        P(None, "gz", "gx", None),
        P(None, "gz", "gx", None),
        P(None, "gz", "gx", None),
        P("gz", "gx", None),
        P("gz", "gx", None),
        P(None, "gx", None),
        P(),
        P(),
    )
    return jax.shard_map(
        on_device,
        mesh=mesh,
        in_specs=placed,
        out_specs=placed[:5],
        check_vma=False,
    )
```

```python
import functools

import jax
import jax.numpy as jnp
from jax import lax
from jax.experimental import pallas as pl
from jax.experimental.pallas import tpu as pltpu
from jax.sharding import PartitionSpec as P


STEPS = 4
KERR = 3
ADVANCE = 2
HALF = 0.5

D, E, H, EPS, CHI = 0, 3, 6, 9, 10
ALL = range(11)
NZL, NXL, NY = 8, 32, 128
XH = 4
ROWS = NXL + 2 * XH
EDGE = 24

DP, HP, INV = 11, 14, 17
RAW = [(E + c, 0) for c in range(3)] + [(c, p) for p in range(3) for c in (EPS, CHI)]
HI = RAW + [(DP + c, p) for p in range(3) for c in range(3)] + [(HP + c, p) for p in range(2) for c in range(3)]
HI += [(INV, 1), (INV, 2)]
HI_ROWS = {8: range(8), 6: (0, 1, 2, 5, 6, 7), 4: (0, 1, 6, 7), 2: (0, 7)}
LO_ROWS = {8: range(8), 6: (0, 1, 2, 3, 6, 7), 4: (0, 1, 2, 7), 2: ()}


def slot_rows(comp, p):
    if (comp, p) == (E, 0):
        return 8
    level = p + (HP <= comp < INV)
    return 6 - 2 * p if comp < HP or comp >= INV else 6 - 2 * (level - 1)


WIDTH = [slot_rows(*k) for k in HI]
HALO_AT = [sum(WIDTH[:i]) for i in range(len(HI))]
LO = [None] * len(HI)
_wide = [i for i, n in enumerate(WIDTH) if n >= 6]
_thin = [i for i, n in enumerate(WIDTH) if n == 4]
for _k in [(E + c, 7) for c in range(3)] + [(H + c, 7) for c in range(3)]:
    LO[_wide.pop(0)] = _k
for _k in [(D + c, 7) for c in range(3)] + [(EPS, 7), (CHI, 7), (H, 6), (H + 1, 6)]:
    LO[_thin.pop(0)] = _k
HI_AT = {k: i for i, k in enumerate(HI)}
LO_AT = {k: i for i, k in enumerate(LO) if k}
NS = len(HI)


def late_rows(comp, p):
    if comp < DP:
        return 0
    if comp < HP:
        return 4
    return p if comp == INV else p + 1


LATE_N = [late_rows(*k) for k in HI]
EARLY_AT = [24 * NS + sum(8 - 2 * n for n in LATE_N[:i]) for i in range(NS + 1)]
LATE_AT = [sum(WIDTH) + sum(2 * n for n in LATE_N[:i]) for i in range(NS + 1)]
EARLY_ROWS, LATE_ROWS = (-(-at[-1] // 8) * 8 for at in (EARLY_AT, LATE_AT))

FOUR, THREE = (E, E + 1, E + 2, H + 1, H + 2), (D, D + 1, D + 2, H, EPS, CHI)
NF = len(FOUR) * NZL * 4
NHALO = NF + len(THREE) * NZL * 3

VM = pl.BlockSpec(memory_space=pltpu.VMEM)
HBM = pl.BlockSpec(memory_space=pltpu.HBM)
SM = pl.BlockSpec(memory_space=pltpu.SMEM)


def shape(*dims):
    return jax.ShapeDtypeStruct(dims, jnp.float32)


def rows(*parts):
    return jnp.concatenate(parts, axis=0)


def scalar(condition):
    return jnp.where(condition, 1.0, 0.0).astype(jnp.float32)


def position():
    gz, gx = lax.axis_index("gz"), lax.axis_index("gx")
    return gz, gx, lax.axis_size("gz") - 1, lax.axis_size("gx") - 1


def halo_row():
    return lax.broadcasted_iota(jnp.int32, (8, NY), 0)


def inside_x():
    _, gx, _, last = position()
    return jnp.where(halo_row() < XH, scalar(gx != last), scalar(gx != 0))


class Grid:
    def __init__(self, size, factor, fill):
        self.size, self.factor, self.fill = size, factor, fill
        self.where, self.level = {}, {}
        lane = lax.broadcasted_iota(jnp.int32, (size, NY), 1)
        self.last_y, self.first_y = lane == NY - 1, lane == 0

    def hold(self, comp, plane, read, level=0):
        self.where[(comp, plane)] = read
        self.level[(comp, plane)] = level

    def get(self, comp, plane, level=None):
        assert level is None or self.level[(comp, plane)] == level, (comp, plane)
        return self.where[(comp, plane)]()

    def put(self, ref, index, comp, plane, value, level):
        ref[index] = value
        self.hold(comp, plane, lambda: ref[index], level)

    def next_y(self, v):
        return jnp.where(self.last_y, 0.0, pltpu.roll(v, NY - 1, 1))

    def prev_y(self, v):
        return jnp.where(self.first_y, 0.0, pltpu.roll(v, 1, 1))

    def next_x(self, v):
        return pltpu.roll(v, self.size - 1, 0)

    def prev_x(self, v):
        return pltpu.roll(v, 1, 0)

    def step_h(self, n, p, comps, put):
        f = self.factor(p)
        ex, ey, ez = (self.get(E + c, p, n - 1) for c in range(3))
        if self.level.get((HP, p)) == n:
            hx, hy, hz = (self.get(HP + c, p) for c in range(3))
            put(H, p, hx - f * ((self.next_y(ez) - ez) + ey), n)
            put(H + 1, p, hy + f * (ex + (self.next_x(ez) - ez)), n)
            put(H + 2, p, hz - f * ((self.next_x(ey) - ey) - (self.next_y(ex) - ex)), n)
            return
        new = {}
        if 0 in comps:
            eyn = self.get(E + 1, p + 1, n - 1)
            new[0] = (self.next_y(ez) - ez) - (eyn - ey)
        if 1 in comps:
            exn = self.get(E, p + 1, n - 1)
            new[1] = (exn - ex) - (self.next_x(ez) - ez)
        if 2 in comps:
            new[2] = (self.next_x(ey) - ey) - (self.next_y(ex) - ex)
        for c, curl in new.items():
            put(H + c, p, self.get(H + c, p, n - 1) - f * curl, n)

    def medium(self, p):
        eps, fill = self.get(EPS, p), self.fill(p)
        return eps if fill is None else eps + fill, self.get(CHI, p)

    def first_inverse(self, n, p):
        ex, ey, ez = (self.get(E + c, p, n) for c in range(3))
        eps, chi = self.medium(p)
        return 1.0 / (eps + chi * (ex * ex + ey * ey + ez * ez))

    def derive(self):
        out = {}
        for p in range(3):
            f, n = self.factor(p), p + 1
            hx, hy, hz = (self.get(H + c, p, n) for c in range(3))
            dx, dy, dz = (self.get(D + c, p, n - 1) for c in range(3))
            out[(DP, p)] = dx + f * ((hz - self.prev_y(hz)) - hy)
            out[(DP + 1, p)] = dy + f * (hx - (hz - self.prev_x(hz)))
            out[(DP + 2, p)] = dz + f * ((hy - self.prev_x(hy)) - (hx - self.prev_y(hx)))
            if p < 2:
                out[(HP, p)] = hx + f * self.get(E + 1, p + 1, n)
                out[(HP + 1, p)] = hy - f * self.get(E, p + 1, n)
                out[(HP + 2, p)] = hz
            if p > 0:
                out[(INV, p)] = self.first_inverse(n - 1, p)
        return out

    def step_de(self, n, p, put):
        f = self.factor(p)
        hxp, hyp = (self.get(H + c, p - 1, n) for c in range(2))
        if self.level.get((DP, p)) == n:
            dx, dy, dz = (self.get(DP + c, p) for c in range(3))
            dx, dy = dx + f * hyp, dy - f * hxp
        else:
            hx, hy, hz = (self.get(H + c, p, n) for c in range(3))
            dx = self.get(D, p, n - 1) + f * ((hz - self.prev_y(hz)) - (hy - hyp))
            dy = self.get(D + 1, p, n - 1) + f * ((hx - hxp) - (hz - self.prev_x(hz)))
            dz = self.get(D + 2, p, n - 1) + f * ((hy - self.prev_x(hy)) - (hx - self.prev_y(hx)))
        eps, chi = self.medium(p)
        inverse = self.get(INV, p) if self.level.get((INV, p)) == n else self.first_inverse(n - 1, p)
        if n == STEPS:
            dx, dy, dz, eps, chi, inverse = (v[:NXL] for v in (dx, dy, dz, eps, chi, inverse))
        squares = chi * (dx * dx + dy * dy + dz * dz)
        for _ in range(KERR - 1):
            inverse = 1.0 / (eps + squares * (inverse * inverse))
        for c, v in enumerate((dx, dy, dz)):
            put(D + c, p, v, n)
            put(E + c, p, v * inverse, n)

    def sweep(self, n, h_planes, de_planes, put):
        for p in range(-2, 11):
            if p in h_planes:
                self.step_h(n, p, range(3), put)
            if p in de_planes:
                self.step_de(n, p, put)


def own(fields, comp, plane):
    d, e, h, eps, chi = fields
    if comp < E:
        return d[comp, plane]
    if comp < H:
        return e[comp - E, plane]
    if comp < EPS:
        return h[comp - H, plane]
    return eps[plane] if comp == EPS else chi[plane]


def halo_slot(comp, p):
    if comp in FOUR:
        return (FOUR.index(comp) * NZL + p) * 4, 4
    return NF + (THREE.index(comp) * NZL + p) * 3, 3


def load(d, e, h, eps, chi, dv, ev, hv, epsv, chiv, ya, yb, sems):
    held = (dv, ev, hv, epsv, chiv)
    copies = [pltpu.make_async_copy(a, b, sems.at[i]) for i, (a, b) in enumerate(zip((d, e, h, eps, chi), held))]
    for c in copies:
        c.start()
    _, gx, _, last = position()
    even = lax.rem(gx, 2) == 0
    keep = scalar(jnp.logical_and(gx != 0, gx != last))
    for comps, copy in zip((range(D, E), range(E, H), range(H, EPS), (EPS,), (CHI,)), copies):
        copy.wait()
        for comp in comps:
            for p in range(NZL):
                at, n = halo_slot(comp, p)
                v = own(held, comp, p)
                low, high = v[0:n], v[NXL - n :]
                ya[at : at + n] = jnp.where(even, high, low)
                yb[at : at + n] = jnp.where(even, low, high) * keep


def mark(out):
    out[...] = inside_x()


def early(grid, put):
    grid.sweep(1, range(0, 5), range(1, 5), put)
    grid.sweep(2, range(1, 4), range(2, 4), put)
    grid.sweep(3, range(2, 3), (), put)


def lookup(classes, table):
    labels = jnp.arange(table.shape[0], dtype=jnp.int32).reshape(-1, 1, 1, 1)
    picked = jnp.where(classes[None] == labels, table.reshape(-1, 1, 1, 1), jnp.float32(0.0))
    return jnp.sum(picked, axis=0)


def payload(grid, side):
    made = grid.derive() if side is HI else {}
    return [k and (made[k] if k in made else grid.get(*k)) for k in side]


def inner(d, e, h, eps, chi, fd, fe, fh, lo, out):
    fields = (d, e, h, eps, chi)
    grid = Grid(NXL, lambda p: HALF, lambda p: None)
    for comp in ALL:
        for p in range(NZL):
            grid.hold(comp, p, functools.partial(own, fields, comp, p))
    grid.step_h(1, 6, range(2), lambda c, p, v, n: grid.put(lo, c - H, c, p, v, n))

    def put(c, p, v, n):
        ref = (fd, fe, fh)[c // 3]
        grid.put(ref, (c % 3, p), c, p, v, n)

    early(grid, put)
    gz, _, last, _ = position()
    first_core = lax.rem(gz, 2) == 0
    keep = scalar(jnp.logical_and(gz != 0, gz != last))
    half = halo_row() < XH
    low = payload(grid, LO)
    for i, v in enumerate(payload(grid, HI)):
        if low[i] is not None:
            v = jnp.where(first_core, v, low[i])
        v = v * keep
        out[24 * i : 24 * i + 8] = jnp.where(half, v[24:32], v[0:8])
        out[24 * i + 8 : 24 * i + 24] = v[8:24]
        n = LATE_N[i]
        if n < 4:
            out[EARLY_AT[i] : EARLY_AT[i + 1]] = jnp.where(half, v[0:8], v[24:32])[n : 8 - n]


def edge_grid(inside, fields, tile):
    f = rows(jnp.full((8, NY), HALF), inside * HALF, jnp.full((8, NY), HALF))
    none = jnp.zeros((8, NY), jnp.float32)
    fill = rows(none, 1.0 - inside, none)
    grid = Grid(EDGE, lambda p: f, lambda p: fill)

    def read(comp, p):
        v = own(fields, comp, p)
        return rows(v[24:32], tile(comp, p), v[0:8])

    for comp in ALL:
        for p in range(NZL):
            grid.hold(comp, p, functools.partial(read, comp, p))
    return grid


def joined(a, b, comp, p):
    _, gx, _, _ = position()
    even = lax.rem(gx, 2) == 0
    at, n = halo_slot(comp, p)
    a, b = a[at : at + n], b[at : at + n]
    above, below = jnp.where(even, a, b), jnp.where(even, b, a)
    if n == 4:
        return rows(above, below)
    return rows(above, above[2:3], below[0:1], below)


def edges(d, e, h, eps, chi, ra, rb, inside, xt, sd, se, sh, slo, cross):
    fields = (d, e, h, eps, chi)
    gz, _, last, _ = position()
    keep = scalar(jnp.logical_and(gz != 0, gz != last))
    half = halo_row() < XH
    for comp in ALL:
        for p in range(NZL):
            xt[comp, p] = joined(ra, rb, comp, p)

    def pack(grid, side, chosen):
        for i, v in enumerate(payload(grid, side)):
            if v is None:
                continue
            v = v * keep
            at, n = HALO_AT[i], WIDTH[i]
            runs = []
            for r in chosen[n]:
                if runs and runs[-1][1] == r:
                    runs[-1][1] = r + 1
                else:
                    runs.append([r, r + 1])
            for a, b in runs:
                cross[at : at + b - a] = v[8 + a : 8 + b]
                at += b - a
            n = LATE_N[i]
            if n:
                at = LATE_AT[i]
                cross[at : at + n] = v[16 : 16 + n]
                cross[at + n : at + 2 * n] = v[8 - n : 8]

    @pl.when(lax.rem(gz, 2) == 0)
    def _():
        grid = edge_grid(inside[...], fields, lambda comp, p: xt[comp, p])
        early(grid, lambda c, p, v, n: grid.put((sd, se, sh)[c // 3], (c % 3, p), c, p, v, n))
        pack(grid, HI, HI_ROWS)

    @pl.when(lax.rem(gz, 2) == 1)
    def _():
        grid = edge_grid(inside[...], fields, lambda comp, p: xt[comp, p])
        grid.step_h(1, 6, range(2), lambda c, p, v, n: grid.put(slo, c - H, c, p, v, n))
        pack(grid, LO, LO_ROWS)


def merge(d, e, h, eps, chi, id_, ie, ih, ilo, xt, sd, se, sh, slo, inside, fd, fe, fh, chip, td, te, th, tlo):
    fields = (d, e, h, eps, chi)
    half = halo_row() < XH

    def merged(v, w):
        return rows(jnp.where(half, w[16:24], v[0:8]), v[8:24], jnp.where(half, v[24:32], w[0:8]), w[8:16])

    def join(sides, side):
        grid = full_grid()
        hold_own(grid, fields, xt)
        for k, (v, w, ref) in enumerate(((id_, sides[0], fd), (ie, sides[1], fe), (ih, sides[2], fh))):
            for p, level in EARLY[k].items():
                for c in range(3):
                    grid.put(ref, (c, p), 3 * k + c, p, merged(v[c, p], w[c, p]), level)
        for c in range(2):
            grid.hold(H + c, 6, functools.partial(lambda a: merged(ilo[a], tlo[a]), c))
        for i, v in enumerate(payload(grid, side)):
            if v is not None:
                chip[i] = v

    gz, _, _, _ = position()

    @pl.when(lax.rem(gz, 2) == 0)
    def _():
        grid = edge_grid(inside[...], fields, lambda comp, p: xt[comp, p])
        grid.step_h(1, 6, range(2), lambda c, p, v, n: grid.put(tlo, c - H, c, p, v, n))
        join((sd, se, sh), LO)

    @pl.when(lax.rem(gz, 2) == 1)
    def _():
        grid = edge_grid(inside[...], fields, lambda comp, p: xt[comp, p])
        early(grid, lambda c, p, v, n: grid.put((td, te, th)[c // 3], (c % 3, p), c, p, v, n))
        join((td, te, th), HI)


def full_grid():
    gz, _, last, _ = position()
    up, down = scalar(gz != last), scalar(gz != 0)
    edge = inside_x()

    def inside(p):
        return up if p >= NZL else (down if p < 0 else None)

    def factor(p):
        z = inside(p)
        main, tile = jnp.full((NXL, NY), HALF, jnp.float32), edge * HALF
        return rows(main, tile) if z is None else rows(main * z, tile * z)

    def fill(p):
        z = inside(p)
        if z is None:
            return rows(jnp.zeros((NXL, NY), jnp.float32), 1.0 - edge)
        return rows(jnp.full((NXL, NY), 1.0 - z, jnp.float32), 1.0 - edge * z)

    return Grid(ROWS, factor, fill)


def hold_own(grid, fields, xt):
    for comp in ALL:
        for p in range(NZL):
            grid.hold(comp, p, functools.partial(lambda c, q: rows(own(fields, c, q), xt[c, q]), comp, p))


def hold_frames(grid, refs, levels, size=ROWS):
    for k, ref in enumerate(refs):
        for p, level in levels[k].items():
            for c in range(3):
                grid.hold(3 * k + c, p, functools.partial(lambda r, a, b: r[a, b, 0:size], ref, c, p), level)


EARLY = ({1: 1, 2: 2, 3: 2, 4: 1}, {1: 1, 2: 2, 3: 2, 4: 1}, {0: 1, 1: 2, 2: 3, 3: 2, 4: 1})
MIDDLE = ({3: 3, 4: 3, 5: 2, 6: 1}, {3: 3, 4: 3, 5: 2, 6: 1}, {3: 4, 4: 3, 5: 2, 6: 1})


def middle(d, e, h, eps, chi, xt, fd, fe, fh, gd, ge, gh):
    grid = full_grid()
    hold_own(grid, (d, e, h, eps, chi), xt)
    hold_frames(grid, (fd, fe, fh), EARLY)

    def put(c, p, v, n):
        grid.put((gd, ge, gh)[c // 3], (c % 3, p), c, p, v, n)

    grid.sweep(1, (5, 6), (5, 6), put)
    grid.sweep(2, (4, 5), (4, 5), put)
    grid.sweep(3, (3, 4), (3, 4), put)
    grid.sweep(4, (3,), (), put)


def hold_side(grid, high, read):
    at, shift = (HI_AT, NZL) if high else (LO_AT, -NZL)
    for (comp, p), i in at.items():
        level = int(p == 6)
        if comp >= DP:
            level = p + 2 if HP <= comp < INV else p + 1
        grid.hold(comp, p + shift, functools.partial(read, i), level)


def stages(grid, high, put, keep, done=lambda o: None):
    if high:
        first = ((7,), (7, 8)), (range(6, 9), range(6, 10)), (range(5, 10), range(5, 11))
        h_planes, de_planes = range(4, 10), range(4, 10)
    else:
        first = ((-1,), (-1, 0)), ((-1, 0), (0, 1)), ((0, 1), (1, 2))
        h_planes, de_planes = (1, 2), (2, 3)
    for n, (hs, des) in enumerate(first, 1):
        grid.sweep(n, hs, des, put)
        yield n
    for p in sorted(set(h_planes) | set(de_planes)):
        if p in h_planes:
            grid.step_h(STEPS, p, range(3), put)
        if p in de_planes:
            if p not in h_planes:
                for c in range(3):
                    keep(c, p - ADVANCE, grid.get(H + c, p, STEPS))
            grid.step_de(STEPS, p, put)
            done(p - ADVANCE)
    yield STEPS


def chain(*args):
    for _ in stages(*args):
        pass


KEPT = NZL - ADVANCE


def near_side(given, high, cc, made, state):
    fields, xt, frames, more = given
    grid = full_grid()
    hold_own(grid, fields, xt)
    hold_frames(grid, frames, EARLY)
    hold_frames(grid, more, MIDDLE)
    hold_side(grid, high, lambda i: cc[i])

    def put(c, p, v, n):
        k = c // 3
        if n == STEPS and p >= ADVANCE:
            made[k][c % 3, p - ADVANCE] = v[:NXL]
        if n < STEPS or k == 2:
            grid.put(state[k], (c % 3, p + 2), c, p, v, n)

    def keep(c, o, v):
        made[2][c, o] = v[:NXL]

    return grid, stages(grid, high, put, keep)


def near(d, e, h, eps, chi, xt, fd, fe, fh, gd, ge, gh, cc, nd, ne, nh, neps, nchi, *state):
    gz, _, _, _ = position()

    @pl.when(lax.rem(gz, 2) == 0)
    def _():
        grid, parts = near_side(((d, e, h, eps, chi), xt, (fd, fe, fh), (gd, ge, gh)), True, cc, (nd, ne, nh), state)
        for _ in parts:
            pass
        for out, comp in ((neps, EPS), (nchi, CHI)):
            for o in range(ADVANCE):
                out[o] = grid.get(comp, NZL + o)[:NXL]


def ahead(d, e, h, eps, chi, xt, fd, fe, fh, gd, ge, gh, ca, cc, eps_in, chi_in, ie, ih, od, oe, oh, oeps, ochi, sd, *state):
    gz, _, last, _ = position()
    half = halo_row() < XH

    def read(i):
        m = ca[24 * i : 24 * i + 8]
        x = m if LATE_N[i] else ca[EARLY_AT[i] : EARLY_AT[i + 1]]
        return rows(jnp.where(half, x, m), ca[24 * i + 8 : 24 * i + 24], jnp.where(half, m, x))

    def side(high):
        z = scalar(gz != last) if high else scalar(gz != 0)

        def own_plane(p):
            return 0 <= p < NZL

        grid = Grid(NXL, lambda p: HALF if own_plane(p) else HALF * z, lambda p: None if own_plane(p) else 1.0 - z)
        for comp in ALL:
            for p in range(NZL):
                grid.hold(comp, p, functools.partial(own, (d, e, h, eps, chi), comp, p))
        hold_frames(grid, (fd, fe, fh), EARLY, NXL)
        hold_frames(grid, (gd, ge, gh), MIDDLE, NXL)
        hold_side(grid, high, read)

        def put(c, p, v, n):
            k = c // 3
            if n == STEPS and p >= ADVANCE:
                (od, oe, oh)[k][c % 3, p - ADVANCE] = v
            if k == 2:
                grid.put(ih, (n - 1, c % 3, p + 2), c, p, v, n)
            elif n < STEPS and k == 1:
                grid.put(ie, (n - 1, c % 3, p + 2), c, p, v, n)
            elif n < STEPS:
                grid.put(sd, (c % 3, p + 2), c, p, v, n)

        def keep(c, o, v):
            oh[c, o] = v

        parts = stages(grid, high, put, keep)
        if high:
            _, others = near_side(((d, e, h, eps, chi), xt, (fd, fe, fh), (gd, ge, gh)), False, cc, (od, oe, oh), state)
            for _ in zip(others, parts):
                pass
        else:
            for _ in parts:
                pass
        if high:
            for out, comp, new in ((oeps, EPS, eps_in), (ochi, CHI, chi_in)):
                for o in range(ADVANCE):
                    out[o] = jnp.where(gz == last, new[o], grid.get(comp, NZL + o))

    pl.when(lax.rem(gz, 2) == 0)(lambda: side(False))
    pl.when(lax.rem(gz, 2) == 1)(lambda: side(True))


def far(d, e, h, eps, chi, xt, fd, fe, fh, gd, ge, gh, ca, cb, *rest):
    nd, ne, nh, neps, nchi, ie, ih, od, oe, oh, oeps, ochi = rest[:12]
    outs, state, edge, sems = rest[12:17], rest[17:20], rest[20:23], rest[23]
    half = halo_row() < XH
    gz, _, _, _ = position()

    def cross(chosen, i):
        m = ca[24 * i : 24 * i + 8]
        n = LATE_N[i]
        parts = [ca[EARLY_AT[i] : EARLY_AT[i + 1]]] if n < 4 else []
        if n:
            parts = [cb[LATE_AT[i] : LATE_AT[i] + n], *parts, cb[LATE_AT[i] + n : LATE_AT[i] + 2 * n]]
        x = rows(*parts)
        at, kept = HALO_AT[i], list(chosen[WIDTH[i]])
        v = cb[at : at + WIDTH[i]]
        if len(kept) < 8:
            near_row = [max([k for k in kept if k <= r], default=kept[0]) for r in range(8)]
            v = rows(*[v[kept.index(k) : kept.index(k) + 1] for k in near_row])
        return rows(jnp.where(half, x, m), ca[24 * i + 8 : 24 * i + 24], jnp.where(half, m, x), v)

    def side(high):
        copies = []

        def send(source, target):
            copies.append(pltpu.make_async_copy(source, target, sems.at[len(copies)]))
            copies[-1].start()

        here, there = (pl.ds(ADVANCE, KEPT), pl.ds(0, ADVANCE)) if high else (pl.ds(0, ADVANCE), pl.ds(ADVANCE, KEPT))
        middle_rows = pl.ds(8, 16)
        for a, b, out in zip((od, oe, oh) if high else (nd, ne, nh), (od, oe, oh), outs):
            send(a.at[:, there], out.at[:, there])
            send(b.at[:, here, middle_rows], out.at[:, here, middle_rows])
        for a, new, out in zip((eps, chi), (oeps, ochi) if high else (neps, nchi), outs[3:]):
            send(a.at[pl.ds(ADVANCE, KEPT)], out.at[pl.ds(0, KEPT)])
            send(new, out.at[pl.ds(KEPT, ADVANCE)])

        grid = full_grid()
        hold_own(grid, (d, e, h, eps, chi), xt)
        hold_frames(grid, (fd, fe, fh), EARLY)
        hold_frames(grid, (gd, ge, gh), MIDDLE)
        hold_side(grid, high, functools.partial(cross, HI_ROWS if high else LO_ROWS))
        none = jnp.zeros((16, NY), jnp.float32)

        def result(k, c, o, v):
            edge[k][c, o, 0:8] = v[0:8]
            edge[k][c, o, 8:16] = v[24:32]

        def put(c, p, v, n):
            k, at = c // 3, (c % 3, p + 2)
            if n == STEPS and p >= ADVANCE:
                result(k, c % 3, p - ADVANCE, v)
            if n < STEPS or k == 2:
                ref, inner_ref = state[k], (None, ie, ih)[k]
                ref[(*at, slice(0, 8))] = v[0:8]
                ref[(*at, slice(8, 24))] = v[24:40]

                def read():
                    mid = none if inner_ref is None else inner_ref[(n - 1, *at, slice(8, 24))]
                    return rows(ref[(*at, slice(0, 8))], mid, ref[(*at, slice(8, 24))])

                grid.hold(c, p, read, n)

        def done(o):
            for k in range(3):
                for a, b in ((0, 0), (8, 24)):
                    send(edge[k].at[:, pl.ds(o, 1), pl.ds(a, 8)], outs[k].at[:, pl.ds(o, 1), pl.ds(b, 8)])

        chain(grid, high, put, functools.partial(result, 2), done)
        for c in copies:
            c.wait()

    pl.when(lax.rem(gz, 2) == 0)(lambda: side(False))
    pl.when(lax.rem(gz, 2) == 1)(lambda: side(True))


def swapped(shard, axis, first):
    n = {a: lax.axis_size(a) for a in ("gz", "gx")}
    moves = []
    for z in range(n["gz"]):
        for x in range(n["gx"]):
            at = z if axis == "gz" else x
            to = at + 1 if at % 2 == first else at - 1
            if 0 <= to < n[axis]:
                other = (to, x) if axis == "gz" else (z, to)
            else:
                other = (z ^ 1, x) if axis == "gx" else (z, x ^ 1)
            moves.append((z * n["gx"] + x, other[0] * n["gx"] + other[1]))
    return lax.ppermute(shard, ("gz", "gx"), moves)


def call(body, inputs, out_shape, scratch=(), vmem=8, specs=None, out=VM, aliases=None):
    return pl.pallas_call(
        body,
        out_shape=out_shape,
        in_specs=[VM] * len(inputs) if specs is None else specs,
        out_specs=jax.tree.map(lambda _: out, out_shape),
        input_output_aliases=aliases or {},
        scratch_shapes=list(scratch),
        compiler_params=pltpu.CompilerParams(vmem_limit_bytes=vmem << 20),
    )(*inputs)


def on_device(d_field, e_field, h_field, permittivity, kerr_coeff, classes, eps_table, chi_table):
    field, medium = shape(3, NZL, NXL, NY), shape(NZL, NXL, NY)
    halo = shape(NHALO, NY)
    *fields, ya, yb = call(
        load,
        [pltpu.with_memory_space_constraint(a, pltpu.HBM) for a in (d_field, e_field, h_field, permittivity, kerr_coeff)],
        (field, field, field, medium, medium, halo, halo),
        [pltpu.SemaphoreType.DMA((5,))],
        specs=[HBM] * 5,
    )
    ra, rb = swapped(ya, "gx", 0), swapped(yb, "gx", 1)
    lo = shape(2, NXL, NY)
    *inside, za = call(inner, fields, (*[shape(3, 5, NXL, NY)] * 3, lo, shape(EARLY_ROWS, NY)))
    ca = swapped(za, "gz", 1)
    (edge,) = call(mark, [], (shape(8, NY),))
    thin = [(3, 5, EDGE, NY)] * 3 + [(2, EDGE, NY)]
    xt, *outside, zb = call(
        edges, [*fields, ra, rb, edge], (shape(11, NZL, 8, NY), *[shape(*t) for t in thin], shape(LATE_ROWS, NY))
    )
    cb = swapped(zb, "gz", 1)
    coming = lookup(classes, eps_table), lookup(classes, chi_table)
    *frames, zc = call(
        merge,
        [*fields, *inside, xt, *outside, edge],
        (*[shape(3, 5, ROWS, NY)] * 3, shape(NS, ROWS, NY)),
        [pltpu.VMEM(t, jnp.float32) for t in thin],
    )
    cc = swapped(zc, "gz", 0)
    more = call(middle, [*fields, xt, *frames], (shape(3, 7, ROWS, NY),) * 3)
    state = [pltpu.VMEM((3, 13, ROWS, NY), jnp.float32)] * 3
    two = shape(ADVANCE, NXL, NY)
    made = call(near, [*fields, xt, *frames, *more, cc], (field, field, field, two, two), state, vmem=16)
    levels = shape(STEPS - 1, 3, 13, NXL, NY), shape(STEPS, 3, 13, NXL, NY)
    inside = call(
        ahead,
        [*fields, xt, *frames, *more, ca, cc, *coming],
        (*levels, field, field, field, two, two),
        [pltpu.VMEM((3, 13, NXL, NY), jnp.float32), *state],
        vmem=16,
    )
    thin = [pltpu.VMEM((3, 13, EDGE, NY), jnp.float32)] * 3 + [pltpu.VMEM((3, NZL, 16, NY), jnp.float32)] * 3
    return call(
        far,
        [*fields, xt, *frames, *more, ca, cb, *made, *inside],
        (field, field, field, medium, medium),
        [*thin, pltpu.SemaphoreType.DMA((48,))],
        vmem=16,
        out=HBM,
    )


def solution(mesh):
    placed = (
        P(None, "gz", "gx", None),
        P(None, "gz", "gx", None),
        P(None, "gz", "gx", None),
        P("gz", "gx", None),
        P("gz", "gx", None),
        P(None, "gx", None),
        P(),
        P(),
    )
    return jax.shard_map(
        on_device,
        mesh=mesh,
        in_specs=placed,
        out_specs=placed[:5],
        check_vma=False,
    )
```

```python
import functools

import jax
import jax.numpy as jnp
from jax import lax
from jax.experimental import pallas as pl
from jax.experimental.pallas import tpu as pltpu
from jax.sharding import PartitionSpec as P


STEPS = 4
KERR = 3
ADVANCE = 2
HALF = 0.5

D, E, H, EPS, CHI = 0, 3, 6, 9, 10
ALL = range(11)
NZL, NXL, NY = 8, 32, 128
XH = 4
ROWS = NXL + 2 * XH
EDGE = 24

DP, HP, INV = 11, 14, 17
RAW = [(E + c, 0) for c in range(3)] + [(c, p) for p in range(3) for c in (EPS, CHI)]
HI = RAW + [(DP + c, p) for p in range(3) for c in range(3)] + [(HP + c, p) for p in range(2) for c in range(3)]
HI += [(INV, 1), (INV, 2)]
HI_ROWS = {8: range(8), 6: (0, 1, 2, 5, 6, 7), 4: (0, 1, 6, 7), 2: (0, 7)}
LO_ROWS = {8: range(8), 6: (0, 1, 2, 3, 6, 7), 4: (0, 1, 2, 7), 2: ()}


def slot_rows(comp, p):
    if (comp, p) == (E, 0):
        return 8
    level = p + (HP <= comp < INV)
    return 6 - 2 * p if comp < HP or comp >= INV else 6 - 2 * (level - 1)


WIDTH = [slot_rows(*k) for k in HI]
HALO_AT = [sum(WIDTH[:i]) for i in range(len(HI))]
LO = [None] * len(HI)
_wide = [i for i, n in enumerate(WIDTH) if n >= 6]
_thin = [i for i, n in enumerate(WIDTH) if n == 4]
for _k in [(E + c, 7) for c in range(3)] + [(H + c, 7) for c in range(3)]:
    LO[_wide.pop(0)] = _k
for _k in [(D + c, 7) for c in range(3)] + [(EPS, 7), (CHI, 7), (H, 6), (H + 1, 6)]:
    LO[_thin.pop(0)] = _k
HI_AT = {k: i for i, k in enumerate(HI)}
LO_AT = {k: i for i, k in enumerate(LO) if k}
NS = len(HI)


def late_rows(comp, p):
    if comp < DP:
        return 0
    if comp < HP:
        return 4
    return p if comp == INV else p + 1


LATE_N = [late_rows(*k) for k in HI]
EARLY_AT = [24 * NS + sum(8 - 2 * n for n in LATE_N[:i]) for i in range(NS + 1)]
LATE_AT = [sum(WIDTH) + sum(2 * n for n in LATE_N[:i]) for i in range(NS + 1)]
EARLY_ROWS, LATE_ROWS = (-(-at[-1] // 8) * 8 for at in (EARLY_AT, LATE_AT))

FOUR, THREE = (E, E + 1, E + 2, H + 1, H + 2), (D, D + 1, D + 2, H, EPS, CHI)
NF = len(FOUR) * NZL * 4
NHALO = NF + len(THREE) * NZL * 3

VM = pl.BlockSpec(memory_space=pltpu.VMEM)
HBM = pl.BlockSpec(memory_space=pltpu.HBM)
SM = pl.BlockSpec(memory_space=pltpu.SMEM)


def shape(*dims):
    return jax.ShapeDtypeStruct(dims, jnp.float32)


def rows(*parts):
    return jnp.concatenate(parts, axis=0)


def scalar(condition):
    return jnp.where(condition, 1.0, 0.0).astype(jnp.float32)


def position():
    gz, gx = lax.axis_index("gz"), lax.axis_index("gx")
    return gz, gx, lax.axis_size("gz") - 1, lax.axis_size("gx") - 1


def halo_row():
    return lax.broadcasted_iota(jnp.int32, (8, NY), 0)


def inside_x():
    _, gx, _, last = position()
    return jnp.where(halo_row() < XH, scalar(gx != last), scalar(gx != 0))


class Grid:
    def __init__(self, size, factor, fill):
        self.size, self.factor, self.fill = size, factor, fill
        self.where, self.level = {}, {}
        lane = lax.broadcasted_iota(jnp.int32, (size, NY), 1)
        self.last_y, self.first_y = lane == NY - 1, lane == 0

    def hold(self, comp, plane, read, level=0):
        self.where[(comp, plane)] = read
        self.level[(comp, plane)] = level

    def get(self, comp, plane, level=None):
        assert level is None or self.level[(comp, plane)] == level, (comp, plane)
        return self.where[(comp, plane)]()

    def put(self, ref, index, comp, plane, value, level):
        ref[index] = value
        self.hold(comp, plane, lambda: ref[index], level)

    def next_y(self, v):
        return jnp.where(self.last_y, 0.0, pltpu.roll(v, NY - 1, 1))

    def prev_y(self, v):
        return jnp.where(self.first_y, 0.0, pltpu.roll(v, 1, 1))

    def next_x(self, v):
        return pltpu.roll(v, self.size - 1, 0)

    def prev_x(self, v):
        return pltpu.roll(v, 1, 0)

    def step_h(self, n, p, comps, put):
        f = self.factor(p)
        ex, ey, ez = (self.get(E + c, p, n - 1) for c in range(3))
        if self.level.get((HP, p)) == n:
            hx, hy, hz = (self.get(HP + c, p) for c in range(3))
            put(H, p, hx - f * ((self.next_y(ez) - ez) + ey), n)
            put(H + 1, p, hy + f * (ex + (self.next_x(ez) - ez)), n)
            put(H + 2, p, hz - f * ((self.next_x(ey) - ey) - (self.next_y(ex) - ex)), n)
            return
        new = {}
        if 0 in comps:
            eyn = self.get(E + 1, p + 1, n - 1)
            new[0] = (self.next_y(ez) - ez) - (eyn - ey)
        if 1 in comps:
            exn = self.get(E, p + 1, n - 1)
            new[1] = (exn - ex) - (self.next_x(ez) - ez)
        if 2 in comps:
            new[2] = (self.next_x(ey) - ey) - (self.next_y(ex) - ex)
        for c, curl in new.items():
            put(H + c, p, self.get(H + c, p, n - 1) - f * curl, n)

    def medium(self, p):
        eps, fill = self.get(EPS, p), self.fill(p)
        return eps if fill is None else eps + fill, self.get(CHI, p)

    def first_inverse(self, n, p):
        ex, ey, ez = (self.get(E + c, p, n) for c in range(3))
        eps, chi = self.medium(p)
        return 1.0 / (eps + chi * (ex * ex + ey * ey + ez * ez))

    def derive(self):
        out = {}
        for p in range(3):
            f, n = self.factor(p), p + 1
            hx, hy, hz = (self.get(H + c, p, n) for c in range(3))
            dx, dy, dz = (self.get(D + c, p, n - 1) for c in range(3))
            out[(DP, p)] = dx + f * ((hz - self.prev_y(hz)) - hy)
            out[(DP + 1, p)] = dy + f * (hx - (hz - self.prev_x(hz)))
            out[(DP + 2, p)] = dz + f * ((hy - self.prev_x(hy)) - (hx - self.prev_y(hx)))
            if p < 2:
                out[(HP, p)] = hx + f * self.get(E + 1, p + 1, n)
                out[(HP + 1, p)] = hy - f * self.get(E, p + 1, n)
                out[(HP + 2, p)] = hz
            if p > 0:
                out[(INV, p)] = self.first_inverse(n - 1, p)
        return out

    def step_de(self, n, p, put):
        f = self.factor(p)
        hxp, hyp = (self.get(H + c, p - 1, n) for c in range(2))
        if self.level.get((DP, p)) == n:
            dx, dy, dz = (self.get(DP + c, p) for c in range(3))
            dx, dy = dx + f * hyp, dy - f * hxp
        else:
            hx, hy, hz = (self.get(H + c, p, n) for c in range(3))
            dx = self.get(D, p, n - 1) + f * ((hz - self.prev_y(hz)) - (hy - hyp))
            dy = self.get(D + 1, p, n - 1) + f * ((hx - hxp) - (hz - self.prev_x(hz)))
            dz = self.get(D + 2, p, n - 1) + f * ((hy - self.prev_x(hy)) - (hx - self.prev_y(hx)))
        eps, chi = self.medium(p)
        inverse = self.get(INV, p) if self.level.get((INV, p)) == n else self.first_inverse(n - 1, p)
        if n == STEPS:
            dx, dy, dz, eps, chi, inverse = (v[:NXL] for v in (dx, dy, dz, eps, chi, inverse))
        squares = chi * (dx * dx + dy * dy + dz * dz)
        for _ in range(KERR - 1):
            inverse = 1.0 / (eps + squares * (inverse * inverse))
        for c, v in enumerate((dx, dy, dz)):
            put(D + c, p, v, n)
            put(E + c, p, v * inverse, n)

    def sweep(self, n, h_planes, de_planes, put):
        for p in range(-2, 11):
            if p in h_planes:
                self.step_h(n, p, range(3), put)
            if p in de_planes:
                self.step_de(n, p, put)


def own(fields, comp, plane):
    d, e, h, eps, chi = fields
    if comp < E:
        return d[comp, plane]
    if comp < H:
        return e[comp - E, plane]
    if comp < EPS:
        return h[comp - H, plane]
    return eps[plane] if comp == EPS else chi[plane]


def halo_slot(comp, p):
    if comp in FOUR:
        return (FOUR.index(comp) * NZL + p) * 4, 4
    return NF + (THREE.index(comp) * NZL + p) * 3, 3


def load(d, e, h, eps, chi, dv, ev, hv, epsv, chiv, ya, yb, sems):
    held = (dv, ev, hv, epsv, chiv)
    copies = [pltpu.make_async_copy(a, b, sems.at[i]) for i, (a, b) in enumerate(zip((d, e, h, eps, chi), held))]
    for c in copies:
        c.start()
    _, gx, _, last = position()
    even = lax.rem(gx, 2) == 0
    keep = scalar(jnp.logical_and(gx != 0, gx != last))
    for comps, copy in zip((range(D, E), range(E, H), range(H, EPS), (EPS,), (CHI,)), copies):
        copy.wait()
        for comp in comps:
            for p in range(NZL):
                at, n = halo_slot(comp, p)
                v = own(held, comp, p)
                low, high = v[0:n], v[NXL - n :]
                ya[at : at + n] = jnp.where(even, high, low)
                yb[at : at + n] = jnp.where(even, low, high) * keep


def mark(out):
    out[...] = inside_x()


def early(grid, put):
    grid.sweep(1, range(0, 5), range(1, 5), put)
    grid.sweep(2, range(1, 4), range(2, 4), put)
    grid.sweep(3, range(2, 3), (), put)


def lookup(classes, table):
    labels = jnp.arange(table.shape[0], dtype=jnp.int32).reshape(-1, 1, 1, 1)
    picked = jnp.where(classes[None] == labels, table.reshape(-1, 1, 1, 1), jnp.float32(0.0))
    return jnp.sum(picked, axis=0)


def payload(grid, side):
    made = grid.derive() if side is HI else {}
    return [k and (made[k] if k in made else grid.get(*k)) for k in side]


def inner(fields, side, fd, fe, fh, lo, out):
    grid = Grid(NXL, lambda p: HALF, lambda p: None)
    for comp in ALL:
        for p in range(NZL):
            grid.hold(comp, p, functools.partial(own, fields, comp, p))
    grid.step_h(1, 6, range(2), lambda c, p, v, n: grid.put(lo, c - H, c, p, v, n))
    early(grid, lambda c, p, v, n: grid.put((fd, fe, fh)[c // 3], (c % 3, p), c, p, v, n))
    gz, _, last, _ = position()
    keep = scalar(jnp.logical_and(gz != 0, gz != last))
    half = halo_row() < XH
    for i, v in enumerate(payload(grid, side)):
        if v is None:
            continue
        v = v * keep
        out[24 * i : 24 * i + 8] = jnp.where(half, v[24:32], v[0:8])
        out[24 * i + 8 : 24 * i + 24] = v[8:24]
        n = LATE_N[i]
        if n < 4:
            out[EARLY_AT[i] : EARLY_AT[i + 1]] = jnp.where(half, v[0:8], v[24:32])[n : 8 - n]


def sooner(d, e, h, eps, chi, *out):
    gz, _, _, _ = position()
    pl.when(lax.rem(gz, 2) == 1)(lambda: inner((d, e, h, eps, chi), LO, *out))


def later(d, e, h, eps, chi, *refs):
    had, out = refs[:5], refs[5:]
    gz, _, _, _ = position()
    pl.when(lax.rem(gz, 2) == 0)(lambda: inner((d, e, h, eps, chi), HI, *out))

    @pl.when(lax.rem(gz, 2) == 1)
    def _():
        for a, b in zip(had, out):
            b[...] = a[...]


def edge_grid(inside, fields, tile):
    f = rows(jnp.full((8, NY), HALF), inside * HALF, jnp.full((8, NY), HALF))
    none = jnp.zeros((8, NY), jnp.float32)
    fill = rows(none, 1.0 - inside, none)
    grid = Grid(EDGE, lambda p: f, lambda p: fill)

    def read(comp, p):
        v = own(fields, comp, p)
        return rows(v[24:32], tile(comp, p), v[0:8])

    for comp in ALL:
        for p in range(NZL):
            grid.hold(comp, p, functools.partial(read, comp, p))
    return grid


def joined(a, b, comp, p):
    _, gx, _, _ = position()
    even = lax.rem(gx, 2) == 0
    at, n = halo_slot(comp, p)
    a, b = a[at : at + n], b[at : at + n]
    above, below = jnp.where(even, a, b), jnp.where(even, b, a)
    if n == 4:
        return rows(above, below)
    return rows(above, above[2:3], below[0:1], below)


def edges(d, e, h, eps, chi, ra, rb, inside, xt, sd, se, sh, slo, cross):
    fields = (d, e, h, eps, chi)
    gz, _, last, _ = position()
    keep = scalar(jnp.logical_and(gz != 0, gz != last))
    half = halo_row() < XH
    for comp in ALL:
        for p in range(NZL):
            xt[comp, p] = joined(ra, rb, comp, p)

    def pack(grid, side, chosen):
        for i, v in enumerate(payload(grid, side)):
            if v is None:
                continue
            v = v * keep
            at, n = HALO_AT[i], WIDTH[i]
            runs = []
            for r in chosen[n]:
                if runs and runs[-1][1] == r:
                    runs[-1][1] = r + 1
                else:
                    runs.append([r, r + 1])
            for a, b in runs:
                cross[at : at + b - a] = v[8 + a : 8 + b]
                at += b - a
            n = LATE_N[i]
            if n:
                at = LATE_AT[i]
                cross[at : at + n] = v[16 : 16 + n]
                cross[at + n : at + 2 * n] = v[8 - n : 8]

    @pl.when(lax.rem(gz, 2) == 0)
    def _():
        grid = edge_grid(inside[...], fields, lambda comp, p: xt[comp, p])
        early(grid, lambda c, p, v, n: grid.put((sd, se, sh)[c // 3], (c % 3, p), c, p, v, n))
        pack(grid, HI, HI_ROWS)

    @pl.when(lax.rem(gz, 2) == 1)
    def _():
        grid = edge_grid(inside[...], fields, lambda comp, p: xt[comp, p])
        grid.step_h(1, 6, range(2), lambda c, p, v, n: grid.put(slo, c - H, c, p, v, n))
        pack(grid, LO, LO_ROWS)


def merge(d, e, h, eps, chi, id_, ie, ih, ilo, xt, sd, se, sh, slo, inside, fd, fe, fh, chip, td, te, th, tlo):
    fields = (d, e, h, eps, chi)
    half = halo_row() < XH

    def merged(v, w):
        return rows(jnp.where(half, w[16:24], v[0:8]), v[8:24], jnp.where(half, v[24:32], w[0:8]), w[8:16])

    def join(sides, side):
        grid = full_grid()
        hold_own(grid, fields, xt)
        for k, (v, w, ref) in enumerate(((id_, sides[0], fd), (ie, sides[1], fe), (ih, sides[2], fh))):
            for p, level in EARLY[k].items():
                for c in range(3):
                    grid.put(ref, (c, p), 3 * k + c, p, merged(v[c, p], w[c, p]), level)
        for c in range(2):
            grid.hold(H + c, 6, functools.partial(lambda a: merged(ilo[a], tlo[a]), c))
        for i, v in enumerate(payload(grid, side)):
            if v is not None:
                chip[i] = v

    gz, _, _, _ = position()

    @pl.when(lax.rem(gz, 2) == 0)
    def _():
        grid = edge_grid(inside[...], fields, lambda comp, p: xt[comp, p])
        grid.step_h(1, 6, range(2), lambda c, p, v, n: grid.put(tlo, c - H, c, p, v, n))
        join((sd, se, sh), LO)

    @pl.when(lax.rem(gz, 2) == 1)
    def _():
        grid = edge_grid(inside[...], fields, lambda comp, p: xt[comp, p])
        early(grid, lambda c, p, v, n: grid.put((td, te, th)[c // 3], (c % 3, p), c, p, v, n))
        join((td, te, th), HI)


def full_grid():
    gz, _, last, _ = position()
    up, down = scalar(gz != last), scalar(gz != 0)
    edge = inside_x()

    def inside(p):
        return up if p >= NZL else (down if p < 0 else None)

    def factor(p):
        z = inside(p)
        main, tile = jnp.full((NXL, NY), HALF, jnp.float32), edge * HALF
        return rows(main, tile) if z is None else rows(main * z, tile * z)

    def fill(p):
        z = inside(p)
        if z is None:
            return rows(jnp.zeros((NXL, NY), jnp.float32), 1.0 - edge)
        return rows(jnp.full((NXL, NY), 1.0 - z, jnp.float32), 1.0 - edge * z)

    return Grid(ROWS, factor, fill)


def hold_own(grid, fields, xt):
    for comp in ALL:
        for p in range(NZL):
            grid.hold(comp, p, functools.partial(lambda c, q: rows(own(fields, c, q), xt[c, q]), comp, p))


def hold_frames(grid, refs, levels, size=ROWS):
    for k, ref in enumerate(refs):
        for p, level in levels[k].items():
            for c in range(3):
                grid.hold(3 * k + c, p, functools.partial(lambda r, a, b: r[a, b, 0:size], ref, c, p), level)


EARLY = ({1: 1, 2: 2, 3: 2, 4: 1}, {1: 1, 2: 2, 3: 2, 4: 1}, {0: 1, 1: 2, 2: 3, 3: 2, 4: 1})
MIDDLE = ({3: 3, 4: 3, 5: 2, 6: 1}, {3: 3, 4: 3, 5: 2, 6: 1}, {3: 4, 4: 3, 5: 2, 6: 1})


def middle(d, e, h, eps, chi, xt, fd, fe, fh, gd, ge, gh):
    grid = full_grid()
    hold_own(grid, (d, e, h, eps, chi), xt)
    hold_frames(grid, (fd, fe, fh), EARLY)

    def put(c, p, v, n):
        grid.put((gd, ge, gh)[c // 3], (c % 3, p), c, p, v, n)

    grid.sweep(1, (5, 6), (5, 6), put)
    grid.sweep(2, (4, 5), (4, 5), put)
    grid.sweep(3, (3, 4), (3, 4), put)
    grid.sweep(4, (3,), (), put)


def hold_side(grid, high, read):
    at, shift = (HI_AT, NZL) if high else (LO_AT, -NZL)
    for (comp, p), i in at.items():
        level = int(p == 6)
        if comp >= DP:
            level = p + 2 if HP <= comp < INV else p + 1
        grid.hold(comp, p + shift, functools.partial(read, i), level)


def stages(grid, high, put, keep, done=lambda o: None):
    if high:
        first = ((7,), (7, 8)), (range(6, 9), range(6, 10)), (range(5, 10), range(5, 11))
        h_planes, de_planes = range(4, 10), range(4, 10)
    else:
        first = ((-1,), (-1, 0)), ((-1, 0), (0, 1)), ((0, 1), (1, 2))
        h_planes, de_planes = (1, 2), (2, 3)
    for n, (hs, des) in enumerate(first, 1):
        grid.sweep(n, hs, des, put)
        yield n
    for p in sorted(set(h_planes) | set(de_planes)):
        if p in h_planes:
            grid.step_h(STEPS, p, range(3), put)
        if p in de_planes:
            if p not in h_planes:
                for c in range(3):
                    keep(c, p - ADVANCE, grid.get(H + c, p, STEPS))
            grid.step_de(STEPS, p, put)
            done(p - ADVANCE)
    yield STEPS


def chain(*args):
    for _ in stages(*args):
        pass


KEPT = NZL - ADVANCE


def near_side(given, high, cc, made, state):
    fields, xt, frames, more = given
    grid = full_grid()
    hold_own(grid, fields, xt)
    hold_frames(grid, frames, EARLY)
    hold_frames(grid, more, MIDDLE)
    hold_side(grid, high, lambda i: cc[i])

    def put(c, p, v, n):
        k = c // 3
        if n == STEPS and p >= ADVANCE:
            made[k][c % 3, p - ADVANCE] = v[:NXL]
        if n < STEPS or k == 2:
            grid.put(state[k], (c % 3, p + 2), c, p, v, n)

    def keep(c, o, v):
        made[2][c, o] = v[:NXL]

    return grid, stages(grid, high, put, keep)


def near(d, e, h, eps, chi, xt, fd, fe, fh, gd, ge, gh, cc, nd, ne, nh, neps, nchi, *state):
    gz, _, _, _ = position()

    @pl.when(lax.rem(gz, 2) == 0)
    def _():
        grid, parts = near_side(((d, e, h, eps, chi), xt, (fd, fe, fh), (gd, ge, gh)), True, cc, (nd, ne, nh), state)
        for _ in parts:
            pass
        for out, comp in ((neps, EPS), (nchi, CHI)):
            for o in range(ADVANCE):
                out[o] = grid.get(comp, NZL + o)[:NXL]


def ahead(d, e, h, eps, chi, xt, fd, fe, fh, gd, ge, gh, ca, cc, eps_in, chi_in, ie, ih, od, oe, oh, oeps, ochi, sd, *state):
    gz, _, last, _ = position()
    half = halo_row() < XH

    def read(i):
        m = ca[24 * i : 24 * i + 8]
        x = m if LATE_N[i] else ca[EARLY_AT[i] : EARLY_AT[i + 1]]
        return rows(jnp.where(half, x, m), ca[24 * i + 8 : 24 * i + 24], jnp.where(half, m, x))

    def side(high):
        z = scalar(gz != last) if high else scalar(gz != 0)

        def own_plane(p):
            return 0 <= p < NZL

        grid = Grid(NXL, lambda p: HALF if own_plane(p) else HALF * z, lambda p: None if own_plane(p) else 1.0 - z)
        for comp in ALL:
            for p in range(NZL):
                grid.hold(comp, p, functools.partial(own, (d, e, h, eps, chi), comp, p))
        hold_frames(grid, (fd, fe, fh), EARLY, NXL)
        hold_frames(grid, (gd, ge, gh), MIDDLE, NXL)
        hold_side(grid, high, read)

        def put(c, p, v, n):
            k = c // 3
            if n == STEPS and p >= ADVANCE:
                (od, oe, oh)[k][c % 3, p - ADVANCE] = v
            if k == 2:
                grid.put(ih, (n - 1, c % 3, p + 2), c, p, v, n)
            elif n < STEPS and k == 1:
                grid.put(ie, (n - 1, c % 3, p + 2), c, p, v, n)
            elif n < STEPS:
                grid.put(sd, (c % 3, p + 2), c, p, v, n)

        def keep(c, o, v):
            oh[c, o] = v

        parts = stages(grid, high, put, keep)
        if high:
            _, others = near_side(((d, e, h, eps, chi), xt, (fd, fe, fh), (gd, ge, gh)), False, cc, (od, oe, oh), state)
            for _ in zip(others, parts):
                pass
        else:
            for _ in parts:
                pass
        if high:
            for out, comp, new in ((oeps, EPS, eps_in), (ochi, CHI, chi_in)):
                for o in range(ADVANCE):
                    out[o] = jnp.where(gz == last, new[o], grid.get(comp, NZL + o))

    pl.when(lax.rem(gz, 2) == 0)(lambda: side(False))
    pl.when(lax.rem(gz, 2) == 1)(lambda: side(True))


def far(d, e, h, eps, chi, xt, fd, fe, fh, gd, ge, gh, ca, cb, *rest):
    nd, ne, nh, neps, nchi, ie, ih, od, oe, oh, oeps, ochi = rest[:12]
    outs, state, edge, sems = rest[12:17], rest[17:20], rest[20:23], rest[23]
    half = halo_row() < XH
    gz, _, _, _ = position()

    def cross(chosen, i):
        m = ca[24 * i : 24 * i + 8]
        n = LATE_N[i]
        parts = [ca[EARLY_AT[i] : EARLY_AT[i + 1]]] if n < 4 else []
        if n:
            parts = [cb[LATE_AT[i] : LATE_AT[i] + n], *parts, cb[LATE_AT[i] + n : LATE_AT[i] + 2 * n]]
        x = rows(*parts)
        at, kept = HALO_AT[i], list(chosen[WIDTH[i]])
        v = cb[at : at + WIDTH[i]]
        if len(kept) < 8:
            near_row = [max([k for k in kept if k <= r], default=kept[0]) for r in range(8)]
            v = rows(*[v[kept.index(k) : kept.index(k) + 1] for k in near_row])
        return rows(jnp.where(half, x, m), ca[24 * i + 8 : 24 * i + 24], jnp.where(half, m, x), v)

    def side(high):
        copies = []

        def send(source, target):
            copies.append(pltpu.make_async_copy(source, target, sems.at[len(copies)]))
            copies[-1].start()

        here, there = (pl.ds(ADVANCE, KEPT), pl.ds(0, ADVANCE)) if high else (pl.ds(0, ADVANCE), pl.ds(ADVANCE, KEPT))
        middle_rows = pl.ds(8, 16)
        for a, b, out in zip((od, oe, oh) if high else (nd, ne, nh), (od, oe, oh), outs):
            send(a.at[:, there], out.at[:, there])
            send(b.at[:, here, middle_rows], out.at[:, here, middle_rows])
        for a, new, out in zip((eps, chi), (oeps, ochi) if high else (neps, nchi), outs[3:]):
            send(a.at[pl.ds(ADVANCE, KEPT)], out.at[pl.ds(0, KEPT)])
            send(new, out.at[pl.ds(KEPT, ADVANCE)])

        grid = full_grid()
        hold_own(grid, (d, e, h, eps, chi), xt)
        hold_frames(grid, (fd, fe, fh), EARLY)
        hold_frames(grid, (gd, ge, gh), MIDDLE)
        hold_side(grid, high, functools.partial(cross, HI_ROWS if high else LO_ROWS))
        none = jnp.zeros((16, NY), jnp.float32)

        def result(k, c, o, v):
            edge[k][c, o, 0:8] = v[0:8]
            edge[k][c, o, 8:16] = v[24:32]

        def put(c, p, v, n):
            k, at = c // 3, (c % 3, p + 2)
            if n == STEPS and p >= ADVANCE:
                result(k, c % 3, p - ADVANCE, v)
            if n < STEPS or k == 2:
                ref, inner_ref = state[k], (None, ie, ih)[k]
                ref[(*at, slice(0, 8))] = v[0:8]
                ref[(*at, slice(8, 24))] = v[24:40]

                def read():
                    mid = none if inner_ref is None else inner_ref[(n - 1, *at, slice(8, 24))]
                    return rows(ref[(*at, slice(0, 8))], mid, ref[(*at, slice(8, 24))])

                grid.hold(c, p, read, n)

        def done(o):
            for k in range(3):
                for a, b in ((0, 0), (8, 24)):
                    send(edge[k].at[:, pl.ds(o, 1), pl.ds(a, 8)], outs[k].at[:, pl.ds(o, 1), pl.ds(b, 8)])

        chain(grid, high, put, functools.partial(result, 2), done)
        for c in copies:
            c.wait()

    pl.when(lax.rem(gz, 2) == 0)(lambda: side(False))
    pl.when(lax.rem(gz, 2) == 1)(lambda: side(True))


def swapped(shard, axis, first):
    n = {a: lax.axis_size(a) for a in ("gz", "gx")}
    moves = []
    for z in range(n["gz"]):
        for x in range(n["gx"]):
            at = z if axis == "gz" else x
            to = at + 1 if at % 2 == first else at - 1
            if 0 <= to < n[axis]:
                other = (to, x) if axis == "gz" else (z, to)
            else:
                other = (z ^ 1, x) if axis == "gx" else (z, x ^ 1)
            moves.append((z * n["gx"] + x, other[0] * n["gx"] + other[1]))
    return lax.ppermute(shard, ("gz", "gx"), moves)


def call(body, inputs, out_shape, scratch=(), vmem=8, specs=None, out=VM, aliases=None):
    return pl.pallas_call(
        body,
        out_shape=out_shape,
        in_specs=[VM] * len(inputs) if specs is None else specs,
        out_specs=jax.tree.map(lambda _: out, out_shape),
        input_output_aliases=aliases or {},
        scratch_shapes=list(scratch),
        compiler_params=pltpu.CompilerParams(vmem_limit_bytes=vmem << 20),
    )(*inputs)


def on_device(d_field, e_field, h_field, permittivity, kerr_coeff, classes, eps_table, chi_table):
    field, medium = shape(3, NZL, NXL, NY), shape(NZL, NXL, NY)
    halo = shape(NHALO, NY)
    *fields, ya, yb = call(
        load,
        [pltpu.with_memory_space_constraint(a, pltpu.HBM) for a in (d_field, e_field, h_field, permittivity, kerr_coeff)],
        (field, field, field, medium, medium, halo, halo),
        [pltpu.SemaphoreType.DMA((5,))],
        specs=[HBM] * 5,
    )
    kinds = (*[shape(3, 5, NXL, NY)] * 3, shape(2, NXL, NY), shape(EARLY_ROWS, NY))
    had = call(sooner, fields, kinds)
    ra, rb = swapped(ya, "gx", 0), swapped(yb, "gx", 1)
    *inside, za = call(later, [*fields, *had], kinds)
    ca = swapped(za, "gz", 1)
    (edge,) = call(mark, [], (shape(8, NY),))
    thin = [(3, 5, EDGE, NY)] * 3 + [(2, EDGE, NY)]
    xt, *outside, zb = call(
        edges, [*fields, ra, rb, edge], (shape(11, NZL, 8, NY), *[shape(*t) for t in thin], shape(LATE_ROWS, NY))
    )
    cb = swapped(zb, "gz", 1)
    coming = lookup(classes, eps_table), lookup(classes, chi_table)
    *frames, zc = call(
        merge,
        [*fields, *inside, xt, *outside, edge],
        (*[shape(3, 5, ROWS, NY)] * 3, shape(NS, ROWS, NY)),
        [pltpu.VMEM(t, jnp.float32) for t in thin],
    )
    cc = swapped(zc, "gz", 0)
    more = call(middle, [*fields, xt, *frames], (shape(3, 7, ROWS, NY),) * 3)
    state = [pltpu.VMEM((3, 13, ROWS, NY), jnp.float32)] * 3
    two = shape(ADVANCE, NXL, NY)
    made = call(near, [*fields, xt, *frames, *more, cc], (field, field, field, two, two), state, vmem=16)
    levels = shape(STEPS - 1, 3, 13, NXL, NY), shape(STEPS, 3, 13, NXL, NY)
    inside = call(
        ahead,
        [*fields, xt, *frames, *more, ca, cc, *coming],
        (*levels, field, field, field, two, two),
        [pltpu.VMEM((3, 13, NXL, NY), jnp.float32), *state],
        vmem=16,
    )
    thin = [pltpu.VMEM((3, 13, EDGE, NY), jnp.float32)] * 3 + [pltpu.VMEM((3, NZL, 16, NY), jnp.float32)] * 3
    return call(
        far,
        [*fields, xt, *frames, *more, ca, cb, *made, *inside],
        (field, field, field, medium, medium),
        [*thin, pltpu.SemaphoreType.DMA((48,))],
        vmem=16,
        out=HBM,
    )


def solution(mesh):
    placed = (
        P(None, "gz", "gx", None),
        P(None, "gz", "gx", None),
        P(None, "gz", "gx", None),
        P("gz", "gx", None),
        P("gz", "gx", None),
        P(None, "gx", None),
        P(),
        P(),
    )
    return jax.shard_map(
        on_device,
        mesh=mesh,
        in_specs=placed,
        out_specs=placed[:5],
        check_vma=False,
    )
```

```python
import functools

import jax
import jax.numpy as jnp
from jax import lax
from jax.experimental import pallas as pl
from jax.experimental.pallas import tpu as pltpu
from jax.sharding import PartitionSpec as P


STEPS = 4
KERR = 3
ADVANCE = 2
HALF = 0.5

D, E, H, EPS, CHI = 0, 3, 6, 9, 10
ALL = range(11)
NZL, NXL, NY = 8, 32, 128
XH = 4
ROWS = NXL + 2 * XH
EDGE = 24

DP, HP, INV = 11, 14, 17
RAW = [(E + c, 0) for c in range(3)] + [(c, p) for p in range(3) for c in (EPS, CHI)]
HI = RAW + [(DP + c, p) for p in range(3) for c in range(3)] + [(HP + c, p) for p in range(2) for c in range(3)]
HI += [(INV, 1), (INV, 2)]
HI_ROWS = {8: range(8), 6: (0, 1, 2, 5, 6, 7), 4: (0, 1, 6, 7), 2: (0, 7)}
LO_ROWS = {8: range(8), 6: (0, 1, 2, 3, 6, 7), 4: (0, 1, 2, 7), 2: ()}


def slot_rows(comp, p):
    if (comp, p) == (E, 0):
        return 8
    level = p + (HP <= comp < INV)
    return 6 - 2 * p if comp < HP or comp >= INV else 6 - 2 * (level - 1)


WIDTH = [slot_rows(*k) for k in HI]
HALO_AT = [sum(WIDTH[:i]) for i in range(len(HI))]
LO = [None] * len(HI)
_wide = [i for i, n in enumerate(WIDTH) if n >= 6]
_thin = [i for i, n in enumerate(WIDTH) if n == 4]
for _k in [(E + c, 7) for c in range(3)] + [(H + c, 7) for c in range(3)]:
    LO[_wide.pop(0)] = _k
for _k in [(D + c, 7) for c in range(3)] + [(EPS, 7), (CHI, 7), (H, 6), (H + 1, 6)]:
    LO[_thin.pop(0)] = _k
HI_AT = {k: i for i, k in enumerate(HI)}
LO_AT = {k: i for i, k in enumerate(LO) if k}
NS = len(HI)


def late_rows(comp, p):
    if comp < DP:
        return 0
    if comp < HP:
        return 4
    return p if comp == INV else p + 1


LATE_N = [late_rows(*k) for k in HI]
EARLY_AT = [24 * NS + sum(8 - 2 * n for n in LATE_N[:i]) for i in range(NS + 1)]
LATE_AT = [sum(WIDTH) + sum(2 * n for n in LATE_N[:i]) for i in range(NS + 1)]
EARLY_ROWS, LATE_ROWS = (-(-at[-1] // 8) * 8 + 8 for at in (EARLY_AT, LATE_AT))

FOUR, THREE = (E, E + 1, E + 2, H + 1, H + 2), (D, D + 1, D + 2, H, EPS, CHI)
NF = 8 + len(FOUR) * NZL * 4
NHALO = NF + len(THREE) * NZL * 3 + 8

VM = pl.BlockSpec(memory_space=pltpu.VMEM)
HBM = pl.BlockSpec(memory_space=pltpu.HBM)
SM = pl.BlockSpec(memory_space=pltpu.SMEM)


def shape(*dims):
    return jax.ShapeDtypeStruct(dims, jnp.float32)


def rows(*parts):
    return jnp.concatenate(parts, axis=0)


def scalar(condition):
    return jnp.where(condition, 1.0, 0.0).astype(jnp.float32)


def position():
    gz, gx = lax.axis_index("gz"), lax.axis_index("gx")
    return gz, gx, lax.axis_size("gz") - 1, lax.axis_size("gx") - 1


def halo_row():
    return lax.broadcasted_iota(jnp.int32, (8, NY), 0)


def inside_x():
    _, gx, _, last = position()
    return jnp.where(halo_row() < XH, scalar(gx != last), scalar(gx != 0))


class Grid:
    def __init__(self, size, factor, fill):
        self.size, self.factor, self.fill = size, factor, fill
        self.where, self.level = {}, {}
        lane = lax.broadcasted_iota(jnp.int32, (size, NY), 1)
        self.last_y, self.first_y = lane == NY - 1, lane == 0

    def hold(self, comp, plane, read, level=0):
        self.where[(comp, plane)] = read
        self.level[(comp, plane)] = level

    def get(self, comp, plane, level=None):
        assert level is None or self.level[(comp, plane)] == level, (comp, plane)
        return self.where[(comp, plane)]()

    def put(self, ref, index, comp, plane, value, level):
        ref[index] = value
        self.hold(comp, plane, lambda: ref[index], level)

    def next_y(self, v):
        return jnp.where(self.last_y, 0.0, pltpu.roll(v, NY - 1, 1))

    def prev_y(self, v):
        return jnp.where(self.first_y, 0.0, pltpu.roll(v, 1, 1))

    def next_x(self, v):
        return pltpu.roll(v, self.size - 1, 0)

    def prev_x(self, v):
        return pltpu.roll(v, 1, 0)

    def step_h(self, n, p, comps, put):
        f = self.factor(p)
        ex, ey, ez = (self.get(E + c, p, n - 1) for c in range(3))
        if self.level.get((HP, p)) == n:
            hx, hy, hz = (self.get(HP + c, p) for c in range(3))
            put(H, p, hx - f * ((self.next_y(ez) - ez) + ey), n)
            put(H + 1, p, hy + f * (ex + (self.next_x(ez) - ez)), n)
            put(H + 2, p, hz - f * ((self.next_x(ey) - ey) - (self.next_y(ex) - ex)), n)
            return
        new = {}
        if 0 in comps:
            eyn = self.get(E + 1, p + 1, n - 1)
            new[0] = (self.next_y(ez) - ez) - (eyn - ey)
        if 1 in comps:
            exn = self.get(E, p + 1, n - 1)
            new[1] = (exn - ex) - (self.next_x(ez) - ez)
        if 2 in comps:
            new[2] = (self.next_x(ey) - ey) - (self.next_y(ex) - ex)
        for c, curl in new.items():
            put(H + c, p, self.get(H + c, p, n - 1) - f * curl, n)

    def medium(self, p):
        eps, fill = self.get(EPS, p), self.fill(p)
        return eps if fill is None else eps + fill, self.get(CHI, p)

    def first_inverse(self, n, p):
        ex, ey, ez = (self.get(E + c, p, n) for c in range(3))
        eps, chi = self.medium(p)
        return 1.0 / (eps + chi * (ex * ex + ey * ey + ez * ez))

    def derive(self):
        out = {}
        for p in range(3):
            f, n = self.factor(p), p + 1
            hx, hy, hz = (self.get(H + c, p, n) for c in range(3))
            dx, dy, dz = (self.get(D + c, p, n - 1) for c in range(3))
            out[(DP, p)] = dx + f * ((hz - self.prev_y(hz)) - hy)
            out[(DP + 1, p)] = dy + f * (hx - (hz - self.prev_x(hz)))
            out[(DP + 2, p)] = dz + f * ((hy - self.prev_x(hy)) - (hx - self.prev_y(hx)))
            if p < 2:
                out[(HP, p)] = hx + f * self.get(E + 1, p + 1, n)
                out[(HP + 1, p)] = hy - f * self.get(E, p + 1, n)
                out[(HP + 2, p)] = hz
            if p > 0:
                out[(INV, p)] = self.first_inverse(n - 1, p)
        return out

    def step_de(self, n, p, put):
        f = self.factor(p)
        hxp, hyp = (self.get(H + c, p - 1, n) for c in range(2))
        if self.level.get((DP, p)) == n:
            dx, dy, dz = (self.get(DP + c, p) for c in range(3))
            dx, dy = dx + f * hyp, dy - f * hxp
        else:
            hx, hy, hz = (self.get(H + c, p, n) for c in range(3))
            dx = self.get(D, p, n - 1) + f * ((hz - self.prev_y(hz)) - (hy - hyp))
            dy = self.get(D + 1, p, n - 1) + f * ((hx - hxp) - (hz - self.prev_x(hz)))
            dz = self.get(D + 2, p, n - 1) + f * ((hy - self.prev_x(hy)) - (hx - self.prev_y(hx)))
        eps, chi = self.medium(p)
        inverse = self.get(INV, p) if self.level.get((INV, p)) == n else self.first_inverse(n - 1, p)
        if n == STEPS:
            dx, dy, dz, eps, chi, inverse = (v[:NXL] for v in (dx, dy, dz, eps, chi, inverse))
        squares = chi * (dx * dx + dy * dy + dz * dz)
        for _ in range(KERR - 1):
            inverse = 1.0 / (eps + squares * (inverse * inverse))
        for c, v in enumerate((dx, dy, dz)):
            put(D + c, p, v, n)
            put(E + c, p, v * inverse, n)

    def sweep(self, n, h_planes, de_planes, put):
        for p in range(-2, 11):
            if p in h_planes:
                self.step_h(n, p, range(3), put)
            if p in de_planes:
                self.step_de(n, p, put)


def own(fields, comp, plane):
    d, e, h, eps, chi = fields
    if comp < E:
        return d[comp, plane]
    if comp < H:
        return e[comp - E, plane]
    if comp < EPS:
        return h[comp - H, plane]
    return eps[plane] if comp == EPS else chi[plane]


def halo_slot(comp, p):
    if comp in FOUR:
        return 8 + (FOUR.index(comp) * NZL + p) * 4, 4
    return NF + (THREE.index(comp) * NZL + p) * 3, 3


def load(d, e, h, eps, chi, dv, ev, hv, epsv, chiv, ya, yb, sems):
    held = (dv, ev, hv, epsv, chiv)
    copies = [pltpu.make_async_copy(a, b, sems.at[i]) for i, (a, b) in enumerate(zip((d, e, h, eps, chi), held))]
    for c in copies:
        c.start()
    _, gx, _, last = position()
    even = lax.rem(gx, 2) == 0
    keep = scalar(jnp.logical_and(gx != 0, gx != last))
    for comps, copy in zip((range(D, E), range(E, H), range(H, EPS), (EPS,), (CHI,)), copies):
        copy.wait()
        for comp in comps:
            for p in range(NZL):
                at, n = halo_slot(comp, p)
                v = own(held, comp, p)
                low, high = v[0:n], v[NXL - n :]
                ya[at : at + n] = jnp.where(even, high, low)
                yb[at : at + n] = jnp.where(even, low, high) * keep


def mark(out):
    out[...] = inside_x()


def early(grid, put):
    grid.sweep(1, range(0, 5), range(1, 5), put)
    grid.sweep(2, range(1, 4), range(2, 4), put)
    grid.sweep(3, range(2, 3), (), put)


def lookup(classes, table):
    labels = jnp.arange(table.shape[0], dtype=jnp.int32).reshape(-1, 1, 1, 1)
    picked = jnp.where(classes[None] == labels, table.reshape(-1, 1, 1, 1), jnp.float32(0.0))
    return jnp.sum(picked, axis=0)


def payload(grid, side):
    made = grid.derive() if side is HI else {}
    return [k and (made[k] if k in made else grid.get(*k)) for k in side]


def inner(d, e, h, eps, chi, fd, fe, fh, lo, out):
    fields = (d, e, h, eps, chi)
    grid = Grid(NXL, lambda p: HALF, lambda p: None)
    for comp in ALL:
        for p in range(NZL):
            grid.hold(comp, p, functools.partial(own, fields, comp, p))
    grid.step_h(1, 6, range(2), lambda c, p, v, n: grid.put(lo, c - H, c, p, v, n))

    def put(c, p, v, n):
        ref = (fd, fe, fh)[c // 3]
        grid.put(ref, (c % 3, p), c, p, v, n)

    early(grid, put)
    gz, _, last, _ = position()
    first_core = lax.rem(gz, 2) == 0
    keep = scalar(jnp.logical_and(gz != 0, gz != last))
    half = halo_row() < XH
    low = payload(grid, LO)
    for i, v in enumerate(payload(grid, HI)):
        if low[i] is not None:
            v = jnp.where(first_core, v, low[i])
        v = v * keep
        out[24 * i : 24 * i + 8] = jnp.where(half, v[24:32], v[0:8])
        out[24 * i + 8 : 24 * i + 24] = v[8:24]
        n = LATE_N[i]
        if n < 4:
            out[EARLY_AT[i] : EARLY_AT[i + 1]] = jnp.where(half, v[0:8], v[24:32])[n : 8 - n]


def edge_grid(inside, fields, tile):
    f = rows(jnp.full((8, NY), HALF), inside * HALF, jnp.full((8, NY), HALF))
    none = jnp.zeros((8, NY), jnp.float32)
    fill = rows(none, 1.0 - inside, none)
    grid = Grid(EDGE, lambda p: f, lambda p: fill)

    def read(comp, p):
        v = own(fields, comp, p)
        return rows(v[24:32], tile(comp, p), v[0:8])

    for comp in ALL:
        for p in range(NZL):
            grid.hold(comp, p, functools.partial(read, comp, p))
    return grid


def joined(a, b, comp, p):
    _, gx, _, _ = position()
    even = lax.rem(gx, 2) == 0
    at, n = halo_slot(comp, p)
    a, b = a[at : at + n], b[at : at + n]
    above, below = jnp.where(even, a, b), jnp.where(even, b, a)
    if n == 4:
        return rows(above, below)
    return rows(above, above[2:3], below[0:1], below)


def edges(d, e, h, eps, chi, ra, rb, inside, xt, sd, se, sh, slo, cross):
    fields = (d, e, h, eps, chi)
    gz, _, last, _ = position()
    keep = scalar(jnp.logical_and(gz != 0, gz != last))
    half = halo_row() < XH
    for comp in ALL:
        for p in range(NZL):
            xt[comp, p] = joined(ra, rb, comp, p)

    def pack(grid, side, chosen):
        for i, v in enumerate(payload(grid, side)):
            if v is None:
                continue
            v = v * keep
            at, n = HALO_AT[i], WIDTH[i]
            runs = []
            for r in chosen[n]:
                if runs and runs[-1][1] == r:
                    runs[-1][1] = r + 1
                else:
                    runs.append([r, r + 1])
            for a, b in runs:
                cross[at : at + b - a] = v[8 + a : 8 + b]
                at += b - a
            n = LATE_N[i]
            if n:
                at = LATE_AT[i]
                cross[at : at + n] = v[16 : 16 + n]
                cross[at + n : at + 2 * n] = v[8 - n : 8]

    @pl.when(lax.rem(gz, 2) == 0)
    def _():
        grid = edge_grid(inside[...], fields, lambda comp, p: xt[comp, p])
        early(grid, lambda c, p, v, n: grid.put((sd, se, sh)[c // 3], (c % 3, p), c, p, v, n))
        pack(grid, HI, HI_ROWS)

    @pl.when(lax.rem(gz, 2) == 1)
    def _():
        grid = edge_grid(inside[...], fields, lambda comp, p: xt[comp, p])
        grid.step_h(1, 6, range(2), lambda c, p, v, n: grid.put(slo, c - H, c, p, v, n))
        pack(grid, LO, LO_ROWS)


def merge(d, e, h, eps, chi, id_, ie, ih, ilo, xt, sd, se, sh, slo, inside, fd, fe, fh, chip, td, te, th, tlo):
    fields = (d, e, h, eps, chi)
    half = halo_row() < XH

    def merged(v, w):
        return rows(jnp.where(half, w[16:24], v[0:8]), v[8:24], jnp.where(half, v[24:32], w[0:8]), w[8:16])

    def join(sides, side):
        grid = full_grid()
        hold_own(grid, fields, xt)
        for k, (v, w, ref) in enumerate(((id_, sides[0], fd), (ie, sides[1], fe), (ih, sides[2], fh))):
            for p, level in EARLY[k].items():
                for c in range(3):
                    grid.put(ref, (c, p), 3 * k + c, p, merged(v[c, p], w[c, p]), level)
        for c in range(2):
            grid.hold(H + c, 6, functools.partial(lambda a: merged(ilo[a], tlo[a]), c))
        for i, v in enumerate(payload(grid, side)):
            if v is not None:
                chip[i] = v

    gz, _, _, _ = position()

    @pl.when(lax.rem(gz, 2) == 0)
    def _():
        grid = edge_grid(inside[...], fields, lambda comp, p: xt[comp, p])
        grid.step_h(1, 6, range(2), lambda c, p, v, n: grid.put(tlo, c - H, c, p, v, n))
        join((sd, se, sh), LO)

    @pl.when(lax.rem(gz, 2) == 1)
    def _():
        grid = edge_grid(inside[...], fields, lambda comp, p: xt[comp, p])
        early(grid, lambda c, p, v, n: grid.put((td, te, th)[c // 3], (c % 3, p), c, p, v, n))
        join((td, te, th), HI)


def full_grid():
    gz, _, last, _ = position()
    up, down = scalar(gz != last), scalar(gz != 0)
    edge = inside_x()

    def inside(p):
        return up if p >= NZL else (down if p < 0 else None)

    def factor(p):
        z = inside(p)
        main, tile = jnp.full((NXL, NY), HALF, jnp.float32), edge * HALF
        return rows(main, tile) if z is None else rows(main * z, tile * z)

    def fill(p):
        z = inside(p)
        if z is None:
            return rows(jnp.zeros((NXL, NY), jnp.float32), 1.0 - edge)
        return rows(jnp.full((NXL, NY), 1.0 - z, jnp.float32), 1.0 - edge * z)

    return Grid(ROWS, factor, fill)


def hold_own(grid, fields, xt):
    for comp in ALL:
        for p in range(NZL):
            grid.hold(comp, p, functools.partial(lambda c, q: rows(own(fields, c, q), xt[c, q]), comp, p))


def hold_frames(grid, refs, levels, size=ROWS):
    for k, ref in enumerate(refs):
        for p, level in levels[k].items():
            for c in range(3):
                grid.hold(3 * k + c, p, functools.partial(lambda r, a, b: r[a, b, 0:size], ref, c, p), level)


EARLY = ({1: 1, 2: 2, 3: 2, 4: 1}, {1: 1, 2: 2, 3: 2, 4: 1}, {0: 1, 1: 2, 2: 3, 3: 2, 4: 1})
MIDDLE = ({3: 3, 4: 3, 5: 2, 6: 1}, {3: 3, 4: 3, 5: 2, 6: 1}, {3: 4, 4: 3, 5: 2, 6: 1})


def middle(d, e, h, eps, chi, xt, fd, fe, fh, gd, ge, gh):
    grid = full_grid()
    hold_own(grid, (d, e, h, eps, chi), xt)
    hold_frames(grid, (fd, fe, fh), EARLY)

    def put(c, p, v, n):
        grid.put((gd, ge, gh)[c // 3], (c % 3, p), c, p, v, n)

    grid.sweep(1, (5, 6), (5, 6), put)
    grid.sweep(2, (4, 5), (4, 5), put)
    grid.sweep(3, (3, 4), (3, 4), put)
    grid.sweep(4, (3,), (), put)


def hold_side(grid, high, read):
    at, shift = (HI_AT, NZL) if high else (LO_AT, -NZL)
    for (comp, p), i in at.items():
        level = int(p == 6)
        if comp >= DP:
            level = p + 2 if HP <= comp < INV else p + 1
        grid.hold(comp, p + shift, functools.partial(read, i), level)


def stages(grid, high, put, keep, done=lambda o: None):
    if high:
        first = ((7,), (7, 8)), (range(6, 9), range(6, 10)), (range(5, 10), range(5, 11))
        h_planes, de_planes = range(4, 10), range(4, 10)
    else:
        first = ((-1,), (-1, 0)), ((-1, 0), (0, 1)), ((0, 1), (1, 2))
        h_planes, de_planes = (1, 2), (2, 3)
    for n, (hs, des) in enumerate(first, 1):
        grid.sweep(n, hs, des, put)
        yield n
    for p in sorted(set(h_planes) | set(de_planes)):
        if p in h_planes:
            grid.step_h(STEPS, p, range(3), put)
        if p in de_planes:
            if p not in h_planes:
                for c in range(3):
                    keep(c, p - ADVANCE, grid.get(H + c, p, STEPS))
            grid.step_de(STEPS, p, put)
            done(p - ADVANCE)
    yield STEPS


def chain(*args):
    for _ in stages(*args):
        pass


KEPT = NZL - ADVANCE


def near_side(given, high, cc, made, state):
    fields, xt, frames, more = given
    grid = full_grid()
    hold_own(grid, fields, xt)
    hold_frames(grid, frames, EARLY)
    hold_frames(grid, more, MIDDLE)
    hold_side(grid, high, lambda i: cc[i])

    def put(c, p, v, n):
        k = c // 3
        if n == STEPS and p >= ADVANCE:
            made[k][c % 3, p - ADVANCE] = v[:NXL]
        if n < STEPS or k == 2:
            grid.put(state[k], (c % 3, p + 2), c, p, v, n)

    def keep(c, o, v):
        made[2][c, o] = v[:NXL]

    return grid, stages(grid, high, put, keep)


def near(d, e, h, eps, chi, xt, fd, fe, fh, gd, ge, gh, cc, nd, ne, nh, neps, nchi, *state):
    gz, _, _, _ = position()

    @pl.when(lax.rem(gz, 2) == 0)
    def _():
        grid, parts = near_side(((d, e, h, eps, chi), xt, (fd, fe, fh), (gd, ge, gh)), True, cc, (nd, ne, nh), state)
        for _ in parts:
            pass
        for out, comp in ((neps, EPS), (nchi, CHI)):
            for o in range(ADVANCE):
                out[o] = grid.get(comp, NZL + o)[:NXL]


def ahead(d, e, h, eps, chi, xt, fd, fe, fh, gd, ge, gh, ca, cc, eps_in, chi_in, ie, ih, od, oe, oh, oeps, ochi, sd, *state):
    gz, _, last, _ = position()
    half = halo_row() < XH

    def read(i):
        m = ca[24 * i : 24 * i + 8]
        x = m if LATE_N[i] else ca[EARLY_AT[i] : EARLY_AT[i + 1]]
        return rows(jnp.where(half, x, m), ca[24 * i + 8 : 24 * i + 24], jnp.where(half, m, x))

    def side(high):
        z = scalar(gz != last) if high else scalar(gz != 0)

        def own_plane(p):
            return 0 <= p < NZL

        grid = Grid(NXL, lambda p: HALF if own_plane(p) else HALF * z, lambda p: None if own_plane(p) else 1.0 - z)
        for comp in ALL:
            for p in range(NZL):
                grid.hold(comp, p, functools.partial(own, (d, e, h, eps, chi), comp, p))
        hold_frames(grid, (fd, fe, fh), EARLY, NXL)
        hold_frames(grid, (gd, ge, gh), MIDDLE, NXL)
        hold_side(grid, high, read)

        def put(c, p, v, n):
            k = c // 3
            if n == STEPS and p >= ADVANCE:
                (od, oe, oh)[k][c % 3, p - ADVANCE] = v
            if k == 2:
                grid.put(ih, (n - 1, c % 3, p + 2), c, p, v, n)
            elif n < STEPS and k == 1:
                grid.put(ie, (n - 1, c % 3, p + 2), c, p, v, n)
            elif n < STEPS:
                grid.put(sd, (c % 3, p + 2), c, p, v, n)

        def keep(c, o, v):
            oh[c, o] = v

        parts = stages(grid, high, put, keep)
        if high:
            _, others = near_side(((d, e, h, eps, chi), xt, (fd, fe, fh), (gd, ge, gh)), False, cc, (od, oe, oh), state)
            for _ in zip(others, parts):
                pass
        else:
            for _ in parts:
                pass
        if high:
            for out, comp, new in ((oeps, EPS, eps_in), (ochi, CHI, chi_in)):
                for o in range(ADVANCE):
                    out[o] = jnp.where(gz == last, new[o], grid.get(comp, NZL + o))

    pl.when(lax.rem(gz, 2) == 0)(lambda: side(False))
    pl.when(lax.rem(gz, 2) == 1)(lambda: side(True))


def far(d, e, h, eps, chi, xt, fd, fe, fh, gd, ge, gh, ca, cb, *rest):
    nd, ne, nh, neps, nchi, ie, ih, od, oe, oh, oeps, ochi = rest[:12]
    outs, state, edge, sems = rest[12:17], rest[17:20], rest[20:23], rest[23]
    half = halo_row() < XH
    gz, _, _, _ = position()

    def cross(chosen, i):
        m = ca[24 * i : 24 * i + 8]
        n = LATE_N[i]
        parts = [ca[EARLY_AT[i] : EARLY_AT[i + 1]]] if n < 4 else []
        if n:
            parts = [cb[LATE_AT[i] : LATE_AT[i] + n], *parts, cb[LATE_AT[i] + n : LATE_AT[i] + 2 * n]]
        x = rows(*parts)
        at, kept = HALO_AT[i], list(chosen[WIDTH[i]])
        v = cb[at : at + WIDTH[i]]
        if len(kept) < 8:
            near_row = [max([k for k in kept if k <= r], default=kept[0]) for r in range(8)]
            v = rows(*[v[kept.index(k) : kept.index(k) + 1] for k in near_row])
        return rows(jnp.where(half, x, m), ca[24 * i + 8 : 24 * i + 24], jnp.where(half, m, x), v)

    def side(high):
        copies = []

        def send(source, target):
            copies.append(pltpu.make_async_copy(source, target, sems.at[len(copies)]))
            copies[-1].start()

        here, there = (pl.ds(ADVANCE, KEPT), pl.ds(0, ADVANCE)) if high else (pl.ds(0, ADVANCE), pl.ds(ADVANCE, KEPT))
        middle_rows = pl.ds(8, 16)
        for a, b, out in zip((od, oe, oh) if high else (nd, ne, nh), (od, oe, oh), outs):
            send(a.at[:, there], out.at[:, there])
            send(b.at[:, here, middle_rows], out.at[:, here, middle_rows])
        for a, new, out in zip((eps, chi), (oeps, ochi) if high else (neps, nchi), outs[3:]):
            send(a.at[pl.ds(ADVANCE, KEPT)], out.at[pl.ds(0, KEPT)])
            send(new, out.at[pl.ds(KEPT, ADVANCE)])

        grid = full_grid()
        hold_own(grid, (d, e, h, eps, chi), xt)
        hold_frames(grid, (fd, fe, fh), EARLY)
        hold_frames(grid, (gd, ge, gh), MIDDLE)
        hold_side(grid, high, functools.partial(cross, HI_ROWS if high else LO_ROWS))
        none = jnp.zeros((16, NY), jnp.float32)

        def result(k, c, o, v):
            edge[k][c, o, 0:8] = v[0:8]
            edge[k][c, o, 8:16] = v[24:32]

        def put(c, p, v, n):
            k, at = c // 3, (c % 3, p + 2)
            if n == STEPS and p >= ADVANCE:
                result(k, c % 3, p - ADVANCE, v)
            if n < STEPS or k == 2:
                ref, inner_ref = state[k], (None, ie, ih)[k]
                ref[(*at, slice(0, 8))] = v[0:8]
                ref[(*at, slice(8, 24))] = v[24:40]

                def read():
                    mid = none if inner_ref is None else inner_ref[(n - 1, *at, slice(8, 24))]
                    return rows(ref[(*at, slice(0, 8))], mid, ref[(*at, slice(8, 24))])

                grid.hold(c, p, read, n)

        def done(o):
            for k in range(3):
                for a, b in ((0, 0), (8, 24)):
                    send(edge[k].at[:, pl.ds(o, 1), pl.ds(a, 8)], outs[k].at[:, pl.ds(o, 1), pl.ds(b, 8)])

        chain(grid, high, put, functools.partial(result, 2), done)
        for c in copies:
            c.wait()

    pl.when(lax.rem(gz, 2) == 0)(lambda: side(False))
    pl.when(lax.rem(gz, 2) == 1)(lambda: side(True))


def swapped(shard, axis, first):
    n = {a: lax.axis_size(a) for a in ("gz", "gx")}
    moves = []
    for z in range(n["gz"]):
        for x in range(n["gx"]):
            at = z if axis == "gz" else x
            to = at + 1 if at % 2 == first else at - 1
            if 0 <= to < n[axis]:
                other = (to, x) if axis == "gz" else (z, to)
            else:
                other = (z ^ 1, x) if axis == "gx" else (z, x ^ 1)
            moves.append((z * n["gx"] + x, other[0] * n["gx"] + other[1]))
    return lax.ppermute(shard, ("gz", "gx"), moves)


def call(body, inputs, out_shape, scratch=(), vmem=8, specs=None, out=VM, aliases=None):
    return pl.pallas_call(
        body,
        out_shape=out_shape,
        in_specs=[VM] * len(inputs) if specs is None else specs,
        out_specs=jax.tree.map(lambda _: out, out_shape),
        input_output_aliases=aliases or {},
        scratch_shapes=list(scratch),
        compiler_params=pltpu.CompilerParams(vmem_limit_bytes=vmem << 20),
    )(*inputs)


def on_device(d_field, e_field, h_field, permittivity, kerr_coeff, classes, eps_table, chi_table):
    field, medium = shape(3, NZL, NXL, NY), shape(NZL, NXL, NY)
    halo = shape(NHALO, NY)
    *fields, ya, yb = call(
        load,
        [pltpu.with_memory_space_constraint(a, pltpu.HBM) for a in (d_field, e_field, h_field, permittivity, kerr_coeff)],
        (field, field, field, medium, medium, halo, halo),
        [pltpu.SemaphoreType.DMA((5,))],
        specs=[HBM] * 5,
    )
    ra, rb = swapped(ya, "gx", 0), swapped(yb, "gx", 1)
    lo = shape(2, NXL, NY)
    *inside, za = call(inner, fields, (*[shape(3, 5, NXL, NY)] * 3, lo, shape(EARLY_ROWS, NY)))
    ca = swapped(za, "gz", 1)
    (edge,) = call(mark, [], (shape(8, NY),))
    thin = [(3, 5, EDGE, NY)] * 3 + [(2, EDGE, NY)]
    xt, *outside, zb = call(
        edges, [*fields, ra, rb, edge], (shape(11, NZL, 8, NY), *[shape(*t) for t in thin], shape(LATE_ROWS, NY))
    )
    cb = swapped(zb, "gz", 1)
    coming = lookup(classes, eps_table), lookup(classes, chi_table)
    *frames, zc = call(
        merge,
        [*fields, *inside, xt, *outside, edge],
        (*[shape(3, 5, ROWS, NY)] * 3, shape(NS, ROWS, NY)),
        [pltpu.VMEM(t, jnp.float32) for t in thin],
    )
    cc = swapped(zc, "gz", 0)
    more = call(middle, [*fields, xt, *frames], (shape(3, 7, ROWS, NY),) * 3)
    state = [pltpu.VMEM((3, 13, ROWS, NY), jnp.float32)] * 3
    two = shape(ADVANCE, NXL, NY)
    made = call(near, [*fields, xt, *frames, *more, cc], (field, field, field, two, two), state, vmem=16)
    levels = shape(STEPS - 1, 3, 13, NXL, NY), shape(STEPS, 3, 13, NXL, NY)
    inside = call(
        ahead,
        [*fields, xt, *frames, *more, ca, cc, *coming],
        (*levels, field, field, field, two, two),
        [pltpu.VMEM((3, 13, NXL, NY), jnp.float32), *state],
        vmem=16,
    )
    thin = [pltpu.VMEM((3, 13, EDGE, NY), jnp.float32)] * 3 + [pltpu.VMEM((3, NZL, 16, NY), jnp.float32)] * 3
    return call(
        far,
        [*fields, xt, *frames, *more, ca, cb, *made, *inside],
        (field, field, field, medium, medium),
        [*thin, pltpu.SemaphoreType.DMA((48,))],
        vmem=16,
        out=HBM,
    )


def solution(mesh):
    placed = (
        P(None, "gz", "gx", None),
        P(None, "gz", "gx", None),
        P(None, "gz", "gx", None),
        P("gz", "gx", None),
        P("gz", "gx", None),
        P(None, "gx", None),
        P(),
        P(),
    )
    return jax.shard_map(
        on_device,
        mesh=mesh,
        in_specs=placed,
        out_specs=placed[:5],
        check_vma=False,
    )
```
